32 devices in a mesh: fsdp: 8 (over y, x, core), tp: 4 (over z).
Axes of the slice: x: 2, y: 2, z: 4, core: 2. Of those that a mesh axis runs over, the one named last changes fastest.
Arguments:
- block_in: bfloat16 [16, 1024, 3072], P('fsdp', 'tp'), may hold values from -6 to 6
- out_cotangent: bfloat16 [16, 1024, 3072], P('fsdp', 'tp'), may hold values from -6 to 6
- segment_ids: int32 [16, 1024], P('fsdp', 'tp'), may hold values from 0 to 3, as said below
- doc_positions: int32 [16, 1024], P('fsdp', 'tp'), may hold values from 0 to 799, as said below
- norm1_gain: bfloat16 [3072], replicated, may hold values from 0.5 to 1.5
- qkv_weight: bfloat16 [3072, 3, 3072], P('fsdp', None, 'tp'), may hold values from -0.5 to 0.5
- out_weight: bfloat16 [3072, 3072], P(('tp', 'fsdp')), may hold values from -0.875 to 0.875
- norm2_gain: bfloat16 [3072], replicated, may hold values from 0.5 to 1.5
- gate_up_weight: bfloat16 [3072, 2, 8192], P('fsdp', None, 'tp'), may hold values from -0.109375 to 0.109375
- down_weight: bfloat16 [8192, 3072], P(('tp', 'fsdp')), may hold values from -0.0625 to 0.0625
Outputs:
- block_out: bfloat16 [16, 1024, 3072], P('fsdp', 'tp')
- in_grad: float32 [16, 1024, 3072], P('fsdp', 'tp')
- norm1_gain_grad: float32 [3072], P(('fsdp', 'tp'))
- qkv_weight_grad: float32 [3072, 3, 3072], P('fsdp', None, 'tp')
- out_weight_grad: float32 [3072, 3072], P(('tp', 'fsdp'))
- norm2_gain_grad: float32 [3072], P(('fsdp', 'tp'))
- gate_up_weight_grad: float32 [3072, 2, 8192], P('fsdp', None, 'tp')
- down_weight_grad: float32 [8192, 3072], P(('tp', 'fsdp'))
The draws below stay inside these ranges and needn't reach their ends.
Inputs may be any that keep to these rules, and one draw needn't show every extreme that they name: `segment_ids`: within each sequence the numbers start at 0, never fall and rise by at most one from a token to the next; every document has 60 to 800 tokens, and the first document of each sequence has 800. `doc_positions`: 0 at the first token of each document, else one more than at the token before.
All inputs are finite; a program needn't handle non-finite values.
Results may differ from the reference program's by a relative error of at most 0.017.
Values may be sent and summed in bfloat16 or wider, within the bound.
A program may use at most 256 MiB of HBM per device.

```python
import jax
import jax.numpy as jnp
from jax import lax

D = 3072
HEADS = 32
HD = 96
FF = 8192
SEQ = 1024
DOC_MIN = 60
DOC_MAX = 800
SEQS = 16


def doc_layout(key):
    doc_count = SEQ // DOC_MIN + 1
    dense_row = jax.random.randint(jax.random.fold_in(key, 5), (), 0, SEQS).astype(jnp.int32)

    def one_row(row_key, row_index):
        lengths = jax.random.randint(row_key, (doc_count,), DOC_MIN, DOC_MAX - DOC_MIN + 1).astype(jnp.int32)
        lengths = jnp.where(row_index == dense_row, DOC_MIN, lengths).astype(jnp.int32)
        lengths = jnp.where(jnp.arange(doc_count) == 0, DOC_MAX, lengths).astype(jnp.int32)
        doc_ends = jnp.cumsum(lengths).astype(jnp.int32)
        doc_ends = jnp.where(doc_ends > SEQ - DOC_MIN, SEQ + 1, doc_ends).astype(jnp.int32)
        places = jnp.arange(SEQ).astype(jnp.int32)
        segment = jnp.sum((doc_ends[None, :] <= places[:, None]).astype(jnp.int32), axis=1).astype(jnp.int32)
        starts = jnp.concatenate([jnp.zeros((1,), jnp.int32), doc_ends])
        doc_start = jnp.take(starts, segment)
        return (segment, (places - doc_start).astype(jnp.int32))
    return jax.vmap(one_row)(jax.random.split(key, SEQS), jnp.arange(SEQS).astype(jnp.int32))


def draw_segment_ids(key, part):
    return doc_layout(jax.random.fold_in(key, 11))[0]


def draw_doc_positions(key, part):
    return doc_layout(jax.random.fold_in(key, 11))[1]


def draw_qkv_weight(key, part):
    base_draw = jax.random.normal(key, (D, 3, D), jnp.float32) * D ** (-0.5)
    return jnp.clip(base_draw, -0.5, 0.5).astype(jnp.bfloat16)


def block_levels(rng, dims, cuts, smallest, largest):
    factor_of = 1.0
    for position, parts in cuts:
        steps = jax.random.uniform(jax.random.fold_in(jax.random.fold_in(rng, 6), position), (parts,), jnp.float32, smallest / len(cuts), largest / len(cuts))
        factor_of = factor_of * jnp.repeat(jnp.exp(steps), dims[position] // parts).reshape((-1,) + (1,) * (len(dims) - 1 - position))
    return factor_of


def bell_draw(key, extent, width, reach, cuts=(), kind=jnp.bfloat16):
    array = width * jax.random.normal(key, extent, jnp.float32)
    if cuts:
        array = array * block_levels(key, extent, cuts, -0.22, 0.18)
    return jnp.clip(array, -reach, reach).astype(kind)


def setup_inputs(seed: int = 0) -> dict:
    splits = jax.random.split(jax.random.key(seed), 11)
    block_in = bell_draw(splits[0], (SEQS, SEQ, D), 1.0, 6.0, ((0, 8), (1, 4)))
    out_cotangent = bell_draw(splits[1], (SEQS, SEQ, D), 1.0, 6.0, ((0, 8), (1, 4)))
    segment_ids = draw_segment_ids(jax.random.fold_in(splits[10], 71), 0)
    doc_positions = draw_doc_positions(jax.random.fold_in(splits[10], 71), 0)
    norm1_gain = jnp.clip(1.0 + 0.1 * jax.random.normal(splits[4], (D,), jnp.float32), 0.5, 1.5).astype(jnp.bfloat16)
    qkv_weight = draw_qkv_weight(jax.random.fold_in(splits[10], 71), 0)
    out_weight = bell_draw(splits[6], (D, D), (D // 64) ** -0.5, 0.875, ((0, 32),))
    norm2_gain = jnp.clip(1.0 + 0.1 * jax.random.normal(splits[7], (D,), jnp.float32), 0.5, 1.5).astype(jnp.bfloat16)
    gate_up_weight = bell_draw(splits[8], (D, 2, FF), D ** -0.5, 0.109375, ((0, 8), (2, 4)))
    down_weight = bell_draw(splits[9], (FF, D), FF ** -0.5, 0.0625, ((0, 32),))
    return {"block_in": block_in, "out_cotangent": out_cotangent, "segment_ids": segment_ids, "doc_positions": doc_positions, "norm1_gain": norm1_gain, "qkv_weight": qkv_weight, "out_weight": out_weight, "norm2_gain": norm2_gain, "gate_up_weight": gate_up_weight, "down_weight": down_weight}


@jax.custom_vjp
def low(v):
    return lax.optimization_barrier(v.astype(jnp.bfloat16)).astype(jnp.float32)

@jax.custom_vjp
def low_back(v):
    return v

def low_keep(v):
    return (low(v), None)

def low_pass(kept, grad):
    return (grad,)

def back_keep(v):
    return (v, None)

def back_low(kept, grad):
    return (low(grad),)
low.defvjp(low_keep, low_pass)
low_back.defvjp(back_keep, back_low)
rms_epsilon = 1e-05
rope_theta = 10000.0
masked_score = -1e+30

def rope_tables(positions):
    half_width = HD // 2
    frequency = rope_theta ** (-(jnp.arange(half_width, dtype=jnp.float32) * 2.0 / HD))
    angles = positions.astype(jnp.float32)[:, None] * frequency[None, :]
    return (jnp.cos(angles)[:, None, :], jnp.sin(angles)[:, None, :])

def rotate(values, cosine_part, sine_part):
    half_width = values.shape[-1] // 2
    lead_half = values[..., :half_width]
    tail_half = values[..., half_width:]
    return jnp.concatenate([lead_half * cosine_part - tail_half * sine_part, tail_half * cosine_part + lead_half * sine_part], axis=-1)

def rms_scale(stream):
    return lax.rsqrt(lax.optimization_barrier(jnp.mean(stream * stream, axis=-1, keepdims=True)) + rms_epsilon)

def attend(queries, key_rows, value_rows, segments):
    block_rows = min(SEQ, 512)
    tiles = SEQ // block_rows
    positions = jnp.arange(SEQ).astype(jnp.int32)

    def query_block(packed):
        query_tile, segment_tile, index_tile = packed
        scores = jnp.einsum('qhd,khd->hqk', query_tile, key_rows, precision=lax.Precision.HIGHEST) * HD ** (-0.5)
        scores = low_back(scores)
        allowed = (segment_tile[:, None] == segments[None, :]) & (index_tile[:, None] >= positions[None, :])
        scores = jnp.where(allowed[None], scores, masked_score)
        row_max = lax.optimization_barrier(jnp.max(scores, axis=-1, keepdims=True))
        exponent = jnp.exp(scores - row_max)
        probs = exponent / lax.optimization_barrier(jnp.sum(exponent, axis=-1, keepdims=True))
        return jnp.einsum('hqk,khd->qhd', low(probs), value_rows, precision=lax.Precision.HIGHEST)
    mixed = lax.map(jax.checkpoint(query_block), (queries.reshape(tiles, block_rows, HEADS, HD), segments.reshape(tiles, block_rows), positions.reshape(tiles, block_rows)))
    return mixed.reshape(SEQ, D)

def layer(stream, segments, positions, weights):
    gain_one, qkv_matrix, out_matrix, gain_two, gate_up_matrix, down_matrix = weights
    scale_one = rms_scale(stream)
    normed_one = low(stream * scale_one * gain_one)
    projected = low_back(jnp.einsum('sd,dtc->stc', normed_one, qkv_matrix, precision=lax.Precision.HIGHEST))
    cosine_part, sine_part = rope_tables(positions)
    queries = low(rotate(projected[:, 0].reshape(SEQ, HEADS, HD), cosine_part, sine_part))
    key_rows = low(rotate(projected[:, 1].reshape(SEQ, HEADS, HD), cosine_part, sine_part))
    value_rows = low(projected[:, 2].reshape(SEQ, HEADS, HD))
    attn_heads = low(low_back(attend(queries, key_rows, value_rows, segments)))
    attn_branch = low_back(jnp.dot(attn_heads, out_matrix, precision=lax.Precision.HIGHEST))
    middle = stream + attn_branch
    scale_two = rms_scale(middle)
    normed_two = low(middle * scale_two * gain_two)
    gate_up = low_back(jnp.einsum('sd,dtf->stf', normed_two, gate_up_matrix, precision=lax.Precision.HIGHEST))
    activated = low(jax.nn.silu(gate_up[:, 0]) * gate_up[:, 1])
    mlp_branch = low_back(jnp.dot(activated, down_matrix, precision=lax.Precision.HIGHEST))
    return middle + mlp_branch

def reference(block_in, out_cotangent, segment_ids, doc_positions, norm1_gain, qkv_weight, out_weight, norm2_gain, gate_up_weight, down_weight):
    params = (norm1_gain.astype(jnp.float32), qkv_weight.astype(jnp.float32), out_weight.astype(jnp.float32), norm2_gain.astype(jnp.float32), gate_up_weight.astype(jnp.float32), down_weight.astype(jnp.float32))

    def forward(stream_all, weights):

        def one_sequence(packed):
            stream, segments, positions = packed
            return layer(stream, segments, positions, weights)
        return lax.map(jax.checkpoint(one_sequence), (stream_all, segment_ids, doc_positions))
    block_out, pullback = jax.vjp(forward, block_in.astype(jnp.float32), params)
    in_grad, weight_grads = pullback(out_cotangent.astype(jnp.float32))
    return (block_out.astype(jnp.bfloat16), in_grad, weight_grads[0], weight_grads[1], weight_grads[2], weight_grads[3], weight_grads[4], weight_grads[5])
```

```python
import functools

import jax
import jax.numpy as jnp
from jax import lax
from jax.experimental import pallas as pl
from jax.experimental.pallas import tpu as pltpu
from jax.sharding import PartitionSpec as P

D = 3072
HD = 96


rms_epsilon = 1e-05
rope_theta = 10000.0
masked_score = -1e30
LOG2E = 1.4426950408889634


def rope_tables(positions, head_size):
    half_width = head_size // 2
    frequency = rope_theta ** (-(jnp.arange(half_width, dtype=jnp.float32) * 2.0 / head_size))
    angles = positions.astype(jnp.float32)[:, None] * frequency[None, :]
    return (jnp.cos(angles)[:, None, :], jnp.sin(angles)[:, None, :])


def rotate(values, cosine_part, sine_part):
    half_width = values.shape[-1] // 2
    lead_half = values[..., :half_width]
    tail_half = values[..., half_width:]
    return jnp.concatenate(
        [
            lead_half * cosine_part - tail_half * sine_part,
            tail_half * cosine_part + lead_half * sine_part,
        ],
        axis=-1,
    )


def unrotate(values, cosine_part, sine_part):
    half_width = values.shape[-1] // 2
    lead_half = values[..., :half_width]
    tail_half = values[..., half_width:]
    return jnp.concatenate(
        [
            lead_half * cosine_part + tail_half * sine_part,
            tail_half * cosine_part - lead_half * sine_part,
        ],
        axis=-1,
    )


def rms_scale(stream):
    return lax.rsqrt(jnp.mean(stream * stream, axis=-1, keepdims=True) + rms_epsilon)


def norm_back(stream, scale_rows, gain_vec, grad_rows):
    gained_grad = gain_vec * grad_rows
    input_grad = scale_rows * gained_grad - stream * scale_rows**3 * jnp.mean(
        gained_grad * stream, axis=-1, keepdims=True
    )
    return (input_grad, jnp.sum(grad_rows * stream * scale_rows, axis=0))


def allowed_mask(segment_tile, index_tile, segments):
    columns = jnp.arange(segments.shape[0], dtype=jnp.int32)
    return (segment_tile[:, None] == segments[None, :]) & (index_tile[:, None] >= columns[None, :])


def masked_scores(query_tile, key_rows, segment_tile, index_tile, segments, scale_value):
    scores = (
        jnp.einsum("qhd,khd->hqk", query_tile, key_rows, preferred_element_type=jnp.float32)
        * scale_value
    )
    return jnp.where(allowed_mask(segment_tile, index_tile, segments)[None], scores, masked_score)


def attention_forward(queries, key_rows, value_rows, segments, block_rows):
    seq_len, head_count, head_size = queries.shape
    tiles = seq_len // block_rows
    scale_value = head_size ** (-0.5)
    positions = jnp.arange(seq_len, dtype=jnp.int32)

    def query_block(packed):
        query_tile, segment_tile, index_tile = packed
        scores = masked_scores(
            query_tile, key_rows, segment_tile, index_tile, segments, scale_value
        )
        row_max = jnp.max(scores, axis=-1, keepdims=True)
        exponent = jnp.exp(scores - row_max)
        row_total = jnp.sum(exponent, axis=-1, keepdims=True)
        probs_low = (exponent / row_total).astype(jnp.bfloat16)
        mixed = jnp.einsum(
            "hqk,khd->qhd", probs_low, value_rows, preferred_element_type=jnp.float32
        )
        return (mixed, (row_max + jnp.log(row_total))[..., 0])

    mixed, log_total = lax.map(
        query_block,
        (
            queries.reshape(tiles, block_rows, head_count, head_size),
            segments.reshape(tiles, block_rows),
            positions.reshape(tiles, block_rows),
        ),
    )
    return (mixed.reshape(seq_len, head_count * head_size), log_total)


def attention_backward(queries, key_rows, value_rows, segments, log_total, out_grad, block_rows):
    seq_len, head_count, head_size = queries.shape
    tiles = seq_len // block_rows
    scale_value = head_size ** (-0.5)
    positions = jnp.arange(seq_len, dtype=jnp.int32)

    def query_block(carry, packed):
        key_acc, value_acc = carry
        query_tile, segment_tile, index_tile, total_tile, grad_tile = packed
        scores = masked_scores(
            query_tile, key_rows, segment_tile, index_tile, segments, scale_value
        )
        probs = jnp.exp(scores - total_tile[..., None])
        probs_low = probs.astype(jnp.bfloat16)
        prob_grad = jnp.einsum(
            "qhd,khd->hqk", grad_tile, value_rows, preferred_element_type=jnp.float32
        )
        score_grad = (
            probs * (prob_grad - jnp.sum(probs * prob_grad, axis=-1, keepdims=True))
        ).astype(jnp.bfloat16)
        query_grad = (
            jnp.einsum("hqk,khd->qhd", score_grad, key_rows, preferred_element_type=jnp.float32)
            * scale_value
        )
        key_acc = (
            key_acc
            + jnp.einsum("hqk,qhd->khd", score_grad, query_tile, preferred_element_type=jnp.float32)
            * scale_value
        )
        value_acc = value_acc + jnp.einsum(
            "hqk,qhd->khd", probs_low, grad_tile, preferred_element_type=jnp.float32
        )
        return ((key_acc, value_acc), query_grad)

    start_acc = (jnp.zeros(queries.shape, jnp.float32), jnp.zeros(queries.shape, jnp.float32))
    (key_grad, value_grad), query_grad = lax.scan(
        query_block,
        start_acc,
        (
            queries.reshape(tiles, block_rows, head_count, head_size),
            segments.reshape(tiles, block_rows),
            positions.reshape(tiles, block_rows),
            log_total,
            out_grad.reshape(tiles, block_rows, head_count, head_size),
        ),
    )
    return (query_grad.reshape(seq_len, head_count, head_size), key_grad, value_grad)


def gather_attention(qkv_weight, out_weight):
    return (
        lax.all_gather(qkv_weight, "fsdp", axis=0, tiled=True),
        lax.all_gather(out_weight, "fsdp", axis=0, tiled=True),
    )


def gather_feedforward(gate_up_weight, down_weight):
    return (
        lax.all_gather(gate_up_weight, "fsdp", axis=0, tiled=True),
        lax.all_gather(down_weight, "fsdp", axis=0, tiled=True),
    )


def per_device(
    block_in,
    out_cotangent,
    segment_ids,
    doc_positions,
    norm1_gain,
    qkv_weight,
    out_weight,
    norm2_gain,
    gate_up_weight,
    down_weight,
):
    micro_count = block_in.shape[0]
    fsdp_count = lax.axis_size("fsdp")
    segment_full, position_full = (
        lax.all_gather(segment_ids, "tp", axis=1, tiled=True),
        lax.all_gather(doc_positions, "tp", axis=1, tiled=True),
    )
    seq_len = segment_full.shape[1]
    block_rows = min(seq_len, 512)
    gain_one = norm1_gain.astype(jnp.float32)
    gain_two = norm2_gain.astype(jnp.float32)
    local_cols = qkv_weight.shape[2]
    local_units = gate_up_weight.shape[2]
    heads_local = local_cols // HD
    grad_qkv = jnp.zeros((D, 3, local_cols), jnp.float32)
    grad_out = jnp.zeros((out_weight.shape[0] * fsdp_count, D), jnp.float32)
    grad_gate_up = jnp.zeros((D, 2, local_units), jnp.float32)
    grad_down = jnp.zeros((down_weight.shape[0] * fsdp_count, D), jnp.float32)
    gain_one_acc = jnp.zeros((D,), jnp.float32)
    gain_two_acc = jnp.zeros((D,), jnp.float32)
    outputs = []
    input_grads = []
    for micro_index in range(micro_count):
        weights_fwd = (
            gather_attention(qkv_weight, out_weight),
            gather_feedforward(gate_up_weight, down_weight),
        )
        (qkv_full, out_full), (gate_up_full, down_full) = weights_fwd
        stream = block_in[micro_index].astype(jnp.float32)
        segment_row = segment_full[micro_index]
        cosine_part, sine_part = rope_tables(position_full[micro_index], HD)
        scale_one = rms_scale(stream)
        normed_one = (stream * scale_one * gain_one).astype(jnp.bfloat16)
        normed_one_full = lax.all_gather(normed_one, "tp", axis=0, tiled=True)
        projected = jnp.einsum(
            "sd,dtc->stc", normed_one_full, qkv_full, preferred_element_type=jnp.float32
        )
        queries = rotate(
            projected[:, 0].reshape(seq_len, heads_local, HD), cosine_part, sine_part
        ).astype(jnp.bfloat16)
        key_rows = rotate(
            projected[:, 1].reshape(seq_len, heads_local, HD), cosine_part, sine_part
        ).astype(jnp.bfloat16)
        value_rows = projected[:, 2].reshape(seq_len, heads_local, HD).astype(jnp.bfloat16)
        mixed, log_total = attention_forward(queries, key_rows, value_rows, segment_row, block_rows)
        attn_heads = mixed.astype(jnp.bfloat16)
        attn_term = jnp.dot(attn_heads, out_full, preferred_element_type=jnp.float32)
        attn_branch = lax.psum_scatter(attn_term, "tp", scatter_dimension=0, tiled=True)
        middle = stream + attn_branch
        scale_two = rms_scale(middle)
        normed_two = (middle * scale_two * gain_two).astype(jnp.bfloat16)
        normed_two_full = lax.all_gather(normed_two, "tp", axis=0, tiled=True)
        gate_up = jnp.einsum(
            "sd,dtf->stf", normed_two_full, gate_up_full, preferred_element_type=jnp.float32
        )
        gate_rows = gate_up[:, 0]
        up_rows = gate_up[:, 1]
        sigmoid_gate = jax.nn.sigmoid(gate_rows)
        silu_gate = gate_rows * sigmoid_gate
        activated = (silu_gate * up_rows).astype(jnp.bfloat16)
        mlp_term = jnp.dot(activated, down_full, preferred_element_type=jnp.float32)
        mlp_branch = lax.psum_scatter(
            mlp_term.astype(jnp.bfloat16), "tp", scatter_dimension=0, tiled=True
        ).astype(jnp.float32)
        outputs.append((middle + mlp_branch).astype(jnp.bfloat16))
        (qkv_back, out_back), (gate_up_back, down_back) = weights_fwd
        cotangent = out_cotangent[micro_index].astype(jnp.float32)
        cotangent_full = lax.all_gather(out_cotangent[micro_index], "tp", axis=0, tiled=True)
        grad_down = grad_down + jnp.einsum(
            "sf,sd->fd", activated, cotangent_full, preferred_element_type=jnp.float32
        )
        act_grad = jnp.einsum(
            "sd,fd->sf", cotangent_full, down_back, preferred_element_type=jnp.float32
        )
        gate_grad = act_grad * up_rows * sigmoid_gate * (1.0 + gate_rows * (1.0 - sigmoid_gate))
        up_grad = act_grad * silu_gate
        gate_up_grad = jnp.stack([gate_grad, up_grad], axis=1).astype(jnp.bfloat16)
        grad_gate_up = grad_gate_up + jnp.einsum(
            "sd,stf->dtf", normed_two_full, gate_up_grad, preferred_element_type=jnp.float32
        )
        normed_two_term = jnp.einsum(
            "stf,dtf->sd", gate_up_grad, gate_up_back, preferred_element_type=jnp.float32
        )
        normed_two_grad = lax.psum_scatter(normed_two_term, "tp", scatter_dimension=0, tiled=True)
        middle_back, gain_two_term = norm_back(middle, scale_two, gain_two, normed_two_grad)
        gain_two_acc = gain_two_acc + gain_two_term
        middle_grad = cotangent + middle_back
        attn_grad_full = lax.all_gather(middle_grad.astype(jnp.bfloat16), "tp", axis=0, tiled=True)
        grad_out = grad_out + jnp.einsum(
            "sc,sd->cd", attn_heads, attn_grad_full, preferred_element_type=jnp.float32
        )
        heads_grad = jnp.einsum(
            "sd,cd->sc", attn_grad_full, out_back, preferred_element_type=jnp.float32
        ).astype(jnp.bfloat16)
        query_grad, key_grad, value_grad = attention_backward(
            queries,
            key_rows,
            value_rows,
            segment_row,
            log_total,
            heads_grad.reshape(seq_len, heads_local, HD),
            block_rows,
        )
        projected_grad = jnp.stack(
            [
                unrotate(query_grad, cosine_part, sine_part).reshape(seq_len, local_cols),
                unrotate(key_grad, cosine_part, sine_part).reshape(seq_len, local_cols),
                value_grad.reshape(seq_len, local_cols),
            ],
            axis=1,
        ).astype(jnp.bfloat16)
        grad_qkv = grad_qkv + jnp.einsum(
            "sd,stc->dtc", normed_one_full, projected_grad, preferred_element_type=jnp.float32
        )
        normed_one_term = jnp.einsum(
            "stc,dtc->sd", projected_grad, qkv_back, preferred_element_type=jnp.float32
        )
        normed_one_grad = lax.psum_scatter(
            normed_one_term.astype(jnp.bfloat16), "tp", scatter_dimension=0, tiled=True
        ).astype(jnp.float32)
        stream_back, gain_one_term = norm_back(stream, scale_one, gain_one, normed_one_grad)
        gain_one_acc = gain_one_acc + gain_one_term
        input_grads.append(middle_grad + stream_back)
    owned_grads = (
        lax.psum_scatter(
            grad_qkv.astype(jnp.bfloat16), "fsdp", scatter_dimension=0, tiled=True
        ).astype(jnp.float32),
        lax.psum_scatter(
            grad_out.astype(jnp.bfloat16), "fsdp", scatter_dimension=0, tiled=True
        ).astype(jnp.float32),
        lax.psum_scatter(
            grad_gate_up.astype(jnp.bfloat16), "fsdp", scatter_dimension=0, tiled=True
        ).astype(jnp.float32),
        lax.psum_scatter(
            grad_down.astype(jnp.bfloat16), "fsdp", scatter_dimension=0, tiled=True
        ).astype(jnp.float32),
    )
    owned_gains = (
        lax.psum_scatter(gain_one_acc, ("fsdp", "tp"), scatter_dimension=0, tiled=True),
        lax.psum_scatter(gain_two_acc, ("fsdp", "tp"), scatter_dimension=0, tiled=True),
    )
    return (
        jnp.stack(outputs),
        jnp.stack(input_grads),
        owned_gains[0],
        owned_grads[0],
        owned_grads[1],
        owned_gains[1],
        owned_grads[2],
        owned_grads[3],
    )


HEAD_GROUP = 4
FIRST_DOC = 800


def dot_nt(left, right):
    return lax.dot_general(left, right, (((1,), (1,)), ((), ())), preferred_element_type=jnp.float32)


def dot_tn(left, right):
    return lax.dot_general(left, right, (((0,), (0,)), ((), ())), preferred_element_type=jnp.float32)


def dot_nn(left, right):
    return lax.dot_general(left, right, (((1,), (0,)), ((), ())), preferred_element_type=jnp.float32)


def swap_halves(values):
    lanes = lax.broadcasted_iota(jnp.int32, values.shape, 1)
    width = values.shape[1]
    return jnp.where(
        lanes % HD < HD // 2,
        pltpu.roll(values, width - HD // 2, 1),
        pltpu.roll(values, HD // 2, 1),
    )


def causal_mask(rows, columns):
    row_ids = lax.broadcasted_iota(jnp.int32, (rows, columns), 0)
    column_ids = lax.broadcasted_iota(jnp.int32, (rows, columns), 1)
    return row_ids >= column_ids


def tail_mask(reach):
    rows = reach.shape[0]
    row_ids = lax.broadcasted_iota(jnp.int32, (rows, rows), 0)
    column_ids = lax.broadcasted_iota(jnp.int32, (rows, rows), 1)
    return (row_ids >= column_ids) & (row_ids - column_ids <= reach)


def halves(slot_ref, quarter):
    first = slot_ref[0]
    return (
        pl.multiple_of(first * quarter, quarter),
        pl.multiple_of((1 - first) * quarter, quarter),
    )


def load_rotated(offsets, quarter, q_ref, k_ref, v_ref, cos_ref, sin_ref, qr_ref, kr_ref, vr_ref):
    for place, offset in enumerate(offsets):
        rows = pl.ds(offset, quarter)
        target = pl.ds(place * quarter, quarter)
        cosine, sine = cos_ref[rows, :], sin_ref[rows, :]
        q_raw, k_raw = q_ref[rows, :], k_ref[rows, :]
        qr_ref[target, :] = (q_raw * cosine + swap_halves(q_raw) * sine).astype(jnp.bfloat16)
        kr_ref[target, :] = (k_raw * cosine + swap_halves(k_raw) * sine).astype(jnp.bfloat16)
        vr_ref[target, :] = v_ref[rows, :].astype(jnp.bfloat16)


def softmax_mix(query, pieces, factor):
    scores = []
    for keys, _, mask in pieces:
        score = dot_nt(query, keys)
        scores.append(score if mask is None else jnp.where(mask, score, masked_score))
    top = functools.reduce(jnp.maximum, [jnp.max(s, axis=-1, keepdims=True) for s in scores])
    weights = [jnp.exp2((s - top) * factor) for s in scores]
    total = functools.reduce(jnp.add, [jnp.sum(w, axis=-1, keepdims=True) for w in weights])
    inverse = 1.0 / total
    mixed = functools.reduce(
        jnp.add,
        [dot_nn((w * inverse).astype(jnp.bfloat16), piece[1]) for w, piece in zip(weights, pieces)],
    )
    return mixed, top * factor + jnp.log2(total)


def head_slice(head):
    return slice(head * HD, (head + 1) * HD)


def forward_first(
    slot_ref, q_ref, k_ref, v_ref, cos_ref, sin_ref, qr_ref, kr_ref, vr_ref, o_ref, lse_ref
):
    half = q_ref.shape[0]
    quarter = half // 2
    offsets = halves(slot_ref, quarter)
    load_rotated(offsets, quarter, q_ref, k_ref, v_ref, cos_ref, sin_ref, qr_ref, kr_ref, vr_ref)
    factor = HD ** (-0.5) * LOG2E
    mask = causal_mask(quarter, quarter)
    for head in range(HEAD_GROUP):
        cols = head_slice(head)
        early, late = slice(0, quarter), slice(quarter, half)
        k_early, v_early = kr_ref[early, cols], vr_ref[early, cols]
        mixed, lse = softmax_mix(qr_ref[early, cols], [(k_early, v_early, mask)], factor)
        o_ref[pl.ds(offsets[0], quarter), cols] = mixed.astype(jnp.bfloat16)
        lse_ref[0, early, head : head + 1] = lse
        mixed, lse = softmax_mix(
            qr_ref[late, cols],
            [(k_early, v_early, None), (kr_ref[late, cols], vr_ref[late, cols], mask)],
            factor,
        )
        o_ref[pl.ds(offsets[1], quarter), cols] = mixed.astype(jnp.bfloat16)
        lse_ref[0, late, head : head + 1] = lse


def forward_second(
    slot_ref, q_ref, k_ref, v_ref, cos_ref, sin_ref, ka_ref, va_ref, pos_ref,
    qr_ref, kr_ref, vr_ref, o_ref, lse_ref,
):
    half = q_ref.shape[0]
    quarter = half // 2
    cut = FIRST_DOC - half
    spill = cut - quarter
    offsets = halves(slot_ref, quarter)
    load_rotated(offsets, quarter, q_ref, k_ref, v_ref, cos_ref, sin_ref, qr_ref, kr_ref, vr_ref)
    factor = HD ** (-0.5) * LOG2E
    mask = causal_mask(cut, cut)
    mask_tail = tail_mask(pos_ref[pl.ds(offsets[1] + spill, half - cut), :])
    for head in range(HEAD_GROUP):
        cols = head_slice(head)
        early, late = slice(0, cut), slice(cut, half)
        mixed, lse = softmax_mix(
            qr_ref[early, cols],
            [
                (ka_ref[:, cols], va_ref[:, cols], None),
                (kr_ref[early, cols], vr_ref[early, cols], mask),
            ],
            factor,
        )
        low = mixed.astype(jnp.bfloat16)
        o_ref[pl.ds(offsets[0], quarter), cols] = low[:quarter]
        o_ref[pl.ds(offsets[1], spill), cols] = low[quarter:]
        lse_ref[0, early, head : head + 1] = lse
        mixed, lse = softmax_mix(
            qr_ref[late, cols], [(kr_ref[late, cols], vr_ref[late, cols], mask_tail)], factor
        )
        o_ref[pl.ds(offsets[1] + spill, half - cut), cols] = mixed.astype(jnp.bfloat16)
        lse_ref[0, late, head : head + 1] = lse


def backward_both(
    slot_ref, qa_ref, ka_ref, va_ref, qb_ref, kb_ref, vb_ref, ga_ref, gb_ref, la_ref, lb_ref,
    cosa_ref, sina_ref, cosb_ref, sinb_ref, pos_ref,
    dqa_ref, dka_ref, dva_ref, dqb_ref, dkb_ref, dvb_ref,
    go_a, go_b, tqa, tka, tva, tqb, tkb, tvb,
):
    half = qa_ref.shape[0]
    quarter = half // 2
    cut = FIRST_DOC - half
    spill = cut - quarter
    offsets = halves(slot_ref, quarter)
    scale_value = HD ** (-0.5)
    factor = scale_value * LOG2E
    for place, offset in enumerate(offsets):
        target, rows = pl.ds(place * quarter, quarter), pl.ds(offset, quarter)
        go_a[target, :] = ga_ref[rows, :]
        go_b[target, :] = gb_ref[rows, :]
    mask = causal_mask(quarter, quarter)
    mask_cut = causal_mask(cut, cut)
    mask_tail = tail_mask(pos_ref[pl.ds(offsets[1] + spill, half - cut), :])
    for accumulator in (tka, tva, tkb, tvb):
        accumulator[...] = jnp.zeros_like(accumulator)

    def attend(query, grad, lse, pieces):
        weights, weight_grads = [], []
        for k_ref, v_ref, rows, cols, mask, _, _ in pieces:
            weight = jnp.exp2(dot_nt(query, k_ref[rows, cols]) * factor - lse)
            weights.append(weight if mask is None else jnp.where(mask, weight, 0.0))
            weight_grads.append(dot_nt(grad, v_ref[rows, cols]))
        shared = functools.reduce(
            jnp.add,
            [jnp.sum(w * g, axis=-1, keepdims=True) for w, g in zip(weights, weight_grads)],
        )
        query_grad = None
        for weight, weight_grad, piece in zip(weights, weight_grads, pieces):
            k_ref, v_ref, rows, cols, _, tk, tv = piece
            score_grad = (weight * (weight_grad - shared)).astype(jnp.bfloat16)
            term = dot_nn(score_grad, k_ref[rows, cols])
            query_grad = term if query_grad is None else query_grad + term
            tk[rows, cols] += dot_tn(score_grad, query)
            tv[rows, cols] += dot_tn(weight.astype(jnp.bfloat16), grad)
        return query_grad

    for head in range(HEAD_GROUP):
        cols = head_slice(head)
        lane = slice(head, head + 1)
        early, late, whole = slice(0, quarter), slice(quarter, half), slice(0, half)
        tqa[early, cols] = attend(
            qa_ref[early, cols], go_a[early, cols], la_ref[0, early, lane],
            [(ka_ref, va_ref, early, cols, mask, tka, tva)],
        )
        tqa[late, cols] = attend(
            qa_ref[late, cols], go_a[late, cols], la_ref[0, late, lane],
            [
                (ka_ref, va_ref, early, cols, None, tka, tva),
                (ka_ref, va_ref, late, cols, mask, tka, tva),
            ],
        )
        early, late = slice(0, cut), slice(cut, half)
        tqb[early, cols] = attend(
            qb_ref[early, cols], go_b[early, cols], lb_ref[0, early, lane],
            [
                (ka_ref, va_ref, whole, cols, None, tka, tva),
                (kb_ref, vb_ref, early, cols, mask_cut, tkb, tvb),
            ],
        )
        tqb[late, cols] = attend(
            qb_ref[late, cols], go_b[late, cols], lb_ref[0, late, lane],
            [(kb_ref, vb_ref, late, cols, mask_tail, tkb, tvb)],
        )
    for place, offset in enumerate(offsets):
        source, rows = pl.ds(place * quarter, quarter), pl.ds(offset, quarter)
        for total, cos_ref, sin_ref, out_ref in (
            (tqa, cosa_ref, sina_ref, dqa_ref),
            (tka, cosa_ref, sina_ref, dka_ref),
            (tqb, cosb_ref, sinb_ref, dqb_ref),
            (tkb, cosb_ref, sinb_ref, dkb_ref),
        ):
            grad = total[source, :] * scale_value
            out_ref[rows, :] = (
                grad * cos_ref[rows, :] - swap_halves(grad) * sin_ref[rows, :]
            ).astype(jnp.bfloat16)
        dva_ref[rows, :] = tva[source, :].astype(jnp.bfloat16)
        dvb_ref[rows, :] = tvb[source, :].astype(jnp.bfloat16)


def kernel_params():
    return pltpu.CompilerParams(
        dimension_semantics=("arbitrary", "arbitrary"), vmem_limit_bytes=40 * 1024 * 1024
    )


def attention_call(kernel, slot, arrays, kinds, outs, scratch, flops):
    rows, heads_local = arrays[-1].shape[0], outs[1]
    half = rows // 2
    groups = heads_local // HEAD_GROUP
    width = HEAD_GROUP * HD

    def spec(kind):
        if kind == "table":
            return pl.BlockSpec((half, width), lambda s, g, _: (s, 0))
        if kind == "column":
            return pl.BlockSpec((half, 1), lambda s, g, _: (s, 0))
        if kind == "lse":
            return pl.BlockSpec((1, half, HEAD_GROUP), lambda s, g, _: (g, s, 0))
        shift = kind * groups
        return pl.BlockSpec((half, width), lambda s, g, _: (s, shift + g))

    def shape(kind):
        if kind == "lse":
            return jax.ShapeDtypeStruct((groups, rows, HEAD_GROUP), jnp.float32)
        return jax.ShapeDtypeStruct((rows, heads_local * HD), jnp.bfloat16)

    return pl.pallas_call(
        kernel,
        out_shape=[shape(kind) for kind in outs[0]],
        grid_spec=pltpu.PrefetchScalarGridSpec(
            num_scalar_prefetch=1,
            grid=(rows // half, groups),
            in_specs=[spec(kind) for kind in kinds],
            out_specs=[spec(kind) for kind in outs[0]],
            scratch_shapes=scratch(half, width),
        ),
        compiler_params=kernel_params(),
        cost_estimate=pl.CostEstimate(
            flops=flops, bytes_accessed=rows * heads_local * HD * 20, transcendentals=flops // 400
        ),
    )(slot, *arrays)


def backward_scratch(half, width):
    return [pltpu.VMEM((half, width), jnp.bfloat16)] * 2 + [
        pltpu.VMEM((half, width), jnp.float32)
    ] * 6


def no_scratch(half, width):
    return []


def wide_tables(positions):
    half_width = HD // 2
    frequency = rope_theta ** (-(jnp.arange(half_width, dtype=jnp.float32) * 2.0 / HD))
    angles = positions.astype(jnp.float32)[:, None] * frequency[None, :]
    cosine, sine = jnp.cos(angles), jnp.sin(angles)
    return (
        jnp.concatenate([cosine, cosine] * HEAD_GROUP, axis=-1),
        jnp.concatenate([-sine, sine] * HEAD_GROUP, axis=-1),
    )


def paired_device(
    block_in,
    out_cotangent,
    segment_ids,
    doc_positions,
    norm1_gain,
    qkv_weight,
    out_weight,
    norm2_gain,
    gate_up_weight,
    down_weight,
):
    fsdp_count, tp_count = lax.axis_size("fsdp"), lax.axis_size("tp")
    core = lax.axis_index("fsdp") % 2
    lane_z = lax.axis_index("tp")
    near, far = lane_z % 2, lane_z // 2
    slot = jnp.reshape(near, (1,)).astype(jnp.int32)
    core_pairs = [(i, i ^ 1) for i in range(fsdp_count)]
    near_pairs = [(i, i ^ 1) for i in range(tp_count)]
    far_pairs = [(i, i ^ 2) for i in range(tp_count)]
    plane_groups = [list(range(first, fsdp_count, 2)) for first in range(2)]
    rows = block_in.shape[1]
    local_cols = qkv_weight.shape[2]
    heads_local = local_cols // HD
    gain_one = norm1_gain.astype(jnp.float32)
    gain_two = norm2_gain.astype(jnp.float32)

    def swap_core(value):
        return lax.ppermute(value, "fsdp", core_pairs)

    def swap_near(value):
        return lax.ppermute(value, "tp", near_pairs)

    def swap_far(value):
        return lax.ppermute(value, "tp", far_pairs)

    def spread_tokens(value):
        keep = lax.dynamic_index_in_dim(value, far, 0, keepdims=False)
        got = swap_far(lax.dynamic_index_in_dim(value, 1 - far, 0, keepdims=False))
        return jnp.where(far == 0, keep, got), jnp.where(far == 0, got, keep)

    def return_tokens(first, second, link_type, final_type):
        keep = jnp.where(far == 0, first, second)
        got = swap_far(jnp.where(far == 0, second, first).astype(link_type))
        keep, got = keep.astype(final_type), got.astype(final_type)
        return jnp.stack([jnp.where(far == 0, keep, got), jnp.where(far == 0, got, keep)])

    def gather_tokens(value):
        both = jnp.concatenate([value, swap_near(value)], axis=0)
        return jnp.concatenate([both, swap_core(both)], axis=0)

    def scatter_tokens(term):
        half = term.shape[0] // 2
        quarter = half // 2
        summed = term[:half].astype(jnp.float32) + swap_core(term[half:]).astype(jnp.float32)
        return summed[:quarter] + swap_near(summed[quarter:].astype(jnp.bfloat16)).astype(
            jnp.float32
        )

    def gather_weight(weight):
        other = swap_far(weight)
        mine = jnp.where(core == far, weight, other)
        sibling = swap_core(jnp.where(core == far, other, weight))
        pair = jnp.concatenate(
            [jnp.where(core == 0, mine, sibling), jnp.where(core == 0, sibling, mine)], axis=0
        )
        return lax.all_gather(pair, "fsdp", axis=0, tiled=True, axis_index_groups=plane_groups)

    def scatter_weight(grad):
        pair = lax.psum_scatter(
            grad, "fsdp", scatter_dimension=0, tiled=True, axis_index_groups=plane_groups
        )
        count = pair.shape[0] // 2
        even, odd = pair[:count], pair[count:]
        mine = jnp.where(core == 0, even, odd)
        got = swap_core(jnp.where(core == 0, odd, even))
        keep = jnp.where(core == far, mine, got)
        sent = swap_far(jnp.where(core == far, got, mine))
        return keep.astype(jnp.float32) + sent.astype(jnp.float32)

    qkv_full = gather_weight(qkv_weight.reshape(qkv_weight.shape[0], 3 * local_cols))
    out_full = gather_weight(out_weight)
    gate_up_full = gather_weight(gate_up_weight)
    down_full = gather_weight(down_weight)

    streams = spread_tokens(block_in)
    positions = [gather_tokens(part) for part in spread_tokens(doc_positions)]
    tables = [wide_tables(part) for part in positions]
    reach = positions[1].astype(jnp.int32)[:, None]

    normed_one_full, saved, attn_outs, lses = [], [], [], []
    scales_one = []
    streams = [part.astype(jnp.float32) for part in streams]
    for part in range(2):
        stream = streams[part]
        scale_one = rms_scale(stream)
        scales_one.append(scale_one)
        normed = (stream * scale_one * gain_one).astype(jnp.bfloat16)
        normed_one_full.append(gather_tokens(normed))
    count = normed_one_full[0].shape[0]
    pair_flops = 2 * heads_local * count * count * HD // 2
    for part in range(2):
        projected = jnp.dot(
            normed_one_full[part], qkv_full, preferred_element_type=jnp.float32
        )
        cosine, sine = tables[part]
        arrays = [projected, projected, projected, cosine, sine]
        kinds = [0, 1, 2, "table", "table"]
        if part == 0:
            kernel = forward_first
        else:
            kernel = forward_second
            arrays += [saved[0][1], saved[0][2], reach]
            kinds += [0, 0, "column"]
        results = attention_call(
            kernel, slot, arrays, kinds, ([0, 0, 0, 0, "lse"], heads_local), no_scratch, pair_flops
        )
        saved.append(results[:3])
        attn_outs.append(results[3])
        lses.append(results[4])

    cotangents = [part for part in spread_tokens(out_cotangent)]
    cotangent_full = [gather_tokens(part) for part in cotangents]
    middles, scales_two, normed_two_full = [], [], []
    for part in range(2):
        term = jnp.dot(attn_outs[part], out_full, preferred_element_type=jnp.float32)
        middle = streams[part] + scatter_tokens(term.astype(jnp.bfloat16))
        scale_two = rms_scale(middle)
        normed = (middle * scale_two * gain_two).astype(jnp.bfloat16)
        middles.append(middle)
        scales_two.append(scale_two)
        normed_two_full.append(gather_tokens(normed))

    outputs, middle_grads, attn_grad_full = [], [], []
    grad_down = grad_gate_up = grad_out = None
    gain_two_acc = 0.0
    for part in range(2):
        gate_up = jnp.einsum(
            "sd,dtf->stf", normed_two_full[part], gate_up_full, preferred_element_type=jnp.float32
        )
        gate_rows, up_rows = gate_up[:, 0], gate_up[:, 1]
        sigmoid_gate = jax.nn.sigmoid(gate_rows)
        silu_gate = gate_rows * sigmoid_gate
        activated = (silu_gate * up_rows).astype(jnp.bfloat16)
        term = jnp.einsum(
            "sf,sd->fd", activated, cotangent_full[part], preferred_element_type=jnp.float32
        )
        grad_down = term if part == 0 else grad_down + term
        act_grad = jnp.einsum(
            "sd,fd->sf", cotangent_full[part], down_full, preferred_element_type=jnp.float32
        )
        gate_grad = act_grad * up_rows * sigmoid_gate * (1.0 + gate_rows * (1.0 - sigmoid_gate))
        up_grad = act_grad * silu_gate
        gate_up_grad = jnp.stack([gate_grad, up_grad], axis=1).astype(jnp.bfloat16)
        term = jnp.einsum(
            "sd,stf->dtf", normed_two_full[part], gate_up_grad, preferred_element_type=jnp.float32
        )
        grad_gate_up = term if part == 0 else grad_gate_up + term
        term = jnp.einsum(
            "stf,dtf->sd", gate_up_grad, gate_up_full, preferred_element_type=jnp.float32
        )
        normed_two_grad = scatter_tokens(term.astype(jnp.bfloat16))
        mlp_term = jnp.dot(activated, down_full, preferred_element_type=jnp.float32)
        mlp_branch = scatter_tokens(mlp_term.astype(jnp.bfloat16))
        outputs.append((middles[part] + mlp_branch).astype(jnp.bfloat16))
        middle_back, gain_two_term = norm_back(
            middles[part], scales_two[part], gain_two, normed_two_grad
        )
        gain_two_acc = gain_two_acc + gain_two_term
        middle_grad = cotangents[part].astype(jnp.float32) + middle_back
        middle_grads.append(middle_grad)
        attn_grad_full.append(gather_tokens(middle_grad.astype(jnp.bfloat16)))
    down_owned = scatter_weight(grad_down.astype(jnp.bfloat16))
    gate_up_owned = scatter_weight(grad_gate_up.astype(jnp.bfloat16))

    head_grads = []
    for part in range(2):
        term = jnp.einsum(
            "sc,sd->cd", attn_outs[part], attn_grad_full[part], preferred_element_type=jnp.float32
        )
        grad_out = term if part == 0 else grad_out + term
        head_grads.append(
            jnp.einsum(
                "sd,cd->sc", attn_grad_full[part], out_full, preferred_element_type=jnp.float32
            ).astype(jnp.bfloat16)
        )
    out_owned = scatter_weight(grad_out.astype(jnp.bfloat16))
    grads = attention_call(
        backward_both,
        slot,
        [*saved[0], *saved[1], *head_grads, *lses, *tables[0], *tables[1], reach],
        [0] * 8 + ["lse"] * 2 + ["table"] * 4 + ["column"],
        ([0] * 6, heads_local),
        backward_scratch,
        pair_flops * 5,
    )
    input_grads = []
    grad_qkv = None
    gain_one_acc = 0.0
    for part in range(2):
        projected_grad = jnp.concatenate(grads[3 * part : 3 * part + 3], axis=1)
        term = jnp.einsum(
            "sd,sc->dc", normed_one_full[part], projected_grad, preferred_element_type=jnp.float32
        )
        grad_qkv = term if part == 0 else grad_qkv + term
        term = jnp.einsum(
            "sc,dc->sd", projected_grad, qkv_full, preferred_element_type=jnp.float32
        )
        normed_one_grad = scatter_tokens(term.astype(jnp.bfloat16))
        stream_back, gain_one_term = norm_back(
            streams[part], scales_one[part], gain_one, normed_one_grad
        )
        gain_one_acc = gain_one_acc + gain_one_term
        input_grads.append(middle_grads[part] + stream_back)
    qkv_owned = scatter_weight(grad_qkv.astype(jnp.bfloat16))
    gains = lax.psum_scatter(
        jnp.stack([gain_one_acc, gain_two_acc], axis=1),
        ("fsdp", "tp"),
        scatter_dimension=0,
        tiled=True,
    )
    return (
        return_tokens(outputs[0], outputs[1], jnp.bfloat16, jnp.bfloat16),
        return_tokens(input_grads[0], input_grads[1], jnp.bfloat16, jnp.float32),
        gains[:, 0],
        qkv_owned.reshape(qkv_weight.shape),
        out_owned,
        gains[:, 1],
        gate_up_owned,
        down_owned,
    )


def solution(mesh):
    sizes = (mesh.shape["fsdp"], mesh.shape["tp"])
    body = paired_device if sizes == (8, 4) else per_device
    in_specs = (
        P("fsdp", "tp", None),
        P("fsdp", "tp", None),
        P("fsdp", "tp"),
        P("fsdp", "tp"),
        P(),
        P("fsdp", None, "tp"),
        P(("tp", "fsdp"), None),
        P(),
        P("fsdp", None, "tp"),
        P(("tp", "fsdp"), None),
    )
    out_specs = (
        P("fsdp", "tp", None),
        P("fsdp", "tp", None),
        P(("fsdp", "tp")),
        P("fsdp", None, "tp"),
        P(("tp", "fsdp"), None),
        P(("fsdp", "tp")),
        P("fsdp", None, "tp"),
        P(("tp", "fsdp"), None),
    )
    return jax.shard_map(
        body, mesh=mesh, in_specs=in_specs, out_specs=out_specs, check_vma=False
    )
```

```python
import functools

import jax
import jax.numpy as jnp
from jax import lax
from jax.experimental import pallas as pl
from jax.experimental.pallas import tpu as pltpu
from jax.sharding import PartitionSpec as P

D = 3072
HD = 96


rms_epsilon = 1e-05
rope_theta = 10000.0
masked_score = -1e30
LOG2E = 1.4426950408889634


def rope_tables(positions, head_size):
    half_width = head_size // 2
    frequency = rope_theta ** (-(jnp.arange(half_width, dtype=jnp.float32) * 2.0 / head_size))
    angles = positions.astype(jnp.float32)[:, None] * frequency[None, :]
    return (jnp.cos(angles)[:, None, :], jnp.sin(angles)[:, None, :])


def rotate(values, cosine_part, sine_part):
    half_width = values.shape[-1] // 2
    lead_half = values[..., :half_width]
    tail_half = values[..., half_width:]
    return jnp.concatenate(
        [
            lead_half * cosine_part - tail_half * sine_part,
            tail_half * cosine_part + lead_half * sine_part,
        ],
        axis=-1,
    )


def unrotate(values, cosine_part, sine_part):
    half_width = values.shape[-1] // 2
    lead_half = values[..., :half_width]
    tail_half = values[..., half_width:]
    return jnp.concatenate(
        [
            lead_half * cosine_part + tail_half * sine_part,
            tail_half * cosine_part - lead_half * sine_part,
        ],
        axis=-1,
    )


def rms_scale(stream):
    return lax.rsqrt(jnp.mean(stream * stream, axis=-1, keepdims=True) + rms_epsilon)


def norm_back(stream, scale_rows, gain_vec, grad_rows):
    gained_grad = gain_vec * grad_rows
    input_grad = scale_rows * gained_grad - stream * scale_rows**3 * jnp.mean(
        gained_grad * stream, axis=-1, keepdims=True
    )
    return (input_grad, jnp.sum(grad_rows * stream * scale_rows, axis=0))


def allowed_mask(segment_tile, index_tile, segments):
    columns = jnp.arange(segments.shape[0], dtype=jnp.int32)
    return (segment_tile[:, None] == segments[None, :]) & (index_tile[:, None] >= columns[None, :])


def masked_scores(query_tile, key_rows, segment_tile, index_tile, segments, scale_value):
    scores = (
        jnp.einsum("qhd,khd->hqk", query_tile, key_rows, preferred_element_type=jnp.float32)
        * scale_value
    )
    return jnp.where(allowed_mask(segment_tile, index_tile, segments)[None], scores, masked_score)


def attention_forward(queries, key_rows, value_rows, segments, block_rows):
    seq_len, head_count, head_size = queries.shape
    tiles = seq_len // block_rows
    scale_value = head_size ** (-0.5)
    positions = jnp.arange(seq_len, dtype=jnp.int32)

    def query_block(packed):
        query_tile, segment_tile, index_tile = packed
        scores = masked_scores(
            query_tile, key_rows, segment_tile, index_tile, segments, scale_value
        )
        row_max = jnp.max(scores, axis=-1, keepdims=True)
        exponent = jnp.exp(scores - row_max)
        row_total = jnp.sum(exponent, axis=-1, keepdims=True)
        probs_low = (exponent / row_total).astype(jnp.bfloat16)
        mixed = jnp.einsum(
            "hqk,khd->qhd", probs_low, value_rows, preferred_element_type=jnp.float32
        )
        return (mixed, (row_max + jnp.log(row_total))[..., 0])

    mixed, log_total = lax.map(
        query_block,
        (
            queries.reshape(tiles, block_rows, head_count, head_size),
            segments.reshape(tiles, block_rows),
            positions.reshape(tiles, block_rows),
        ),
    )
    return (mixed.reshape(seq_len, head_count * head_size), log_total)


def attention_backward(queries, key_rows, value_rows, segments, log_total, out_grad, block_rows):
    seq_len, head_count, head_size = queries.shape
    tiles = seq_len // block_rows
    scale_value = head_size ** (-0.5)
    positions = jnp.arange(seq_len, dtype=jnp.int32)

    def query_block(carry, packed):
        key_acc, value_acc = carry
        query_tile, segment_tile, index_tile, total_tile, grad_tile = packed
        scores = masked_scores(
            query_tile, key_rows, segment_tile, index_tile, segments, scale_value
        )
        probs = jnp.exp(scores - total_tile[..., None])
        probs_low = probs.astype(jnp.bfloat16)
        prob_grad = jnp.einsum(
            "qhd,khd->hqk", grad_tile, value_rows, preferred_element_type=jnp.float32
        )
        score_grad = (
            probs * (prob_grad - jnp.sum(probs * prob_grad, axis=-1, keepdims=True))
        ).astype(jnp.bfloat16)
        query_grad = (
            jnp.einsum("hqk,khd->qhd", score_grad, key_rows, preferred_element_type=jnp.float32)
            * scale_value
        )
        key_acc = (
            key_acc
            + jnp.einsum("hqk,qhd->khd", score_grad, query_tile, preferred_element_type=jnp.float32)
            * scale_value
        )
        value_acc = value_acc + jnp.einsum(
            "hqk,qhd->khd", probs_low, grad_tile, preferred_element_type=jnp.float32
        )
        return ((key_acc, value_acc), query_grad)

    start_acc = (jnp.zeros(queries.shape, jnp.float32), jnp.zeros(queries.shape, jnp.float32))
    (key_grad, value_grad), query_grad = lax.scan(
        query_block,
        start_acc,
        (
            queries.reshape(tiles, block_rows, head_count, head_size),
            segments.reshape(tiles, block_rows),
            positions.reshape(tiles, block_rows),
            log_total,
            out_grad.reshape(tiles, block_rows, head_count, head_size),
        ),
    )
    return (query_grad.reshape(seq_len, head_count, head_size), key_grad, value_grad)


def gather_attention(qkv_weight, out_weight):
    return (
        lax.all_gather(qkv_weight, "fsdp", axis=0, tiled=True),
        lax.all_gather(out_weight, "fsdp", axis=0, tiled=True),
    )


def gather_feedforward(gate_up_weight, down_weight):
    return (
        lax.all_gather(gate_up_weight, "fsdp", axis=0, tiled=True),
        lax.all_gather(down_weight, "fsdp", axis=0, tiled=True),
    )


def per_device(
    block_in,
    out_cotangent,
    segment_ids,
    doc_positions,
    norm1_gain,
    qkv_weight,
    out_weight,
    norm2_gain,
    gate_up_weight,
    down_weight,
):
    micro_count = block_in.shape[0]
    fsdp_count = lax.axis_size("fsdp")
    segment_full, position_full = (
        lax.all_gather(segment_ids, "tp", axis=1, tiled=True),
        lax.all_gather(doc_positions, "tp", axis=1, tiled=True),
    )
    seq_len = segment_full.shape[1]
    block_rows = min(seq_len, 512)
    gain_one = norm1_gain.astype(jnp.float32)
    gain_two = norm2_gain.astype(jnp.float32)
    local_cols = qkv_weight.shape[2]
    local_units = gate_up_weight.shape[2]
    heads_local = local_cols // HD
    grad_qkv = jnp.zeros((D, 3, local_cols), jnp.float32)
    grad_out = jnp.zeros((out_weight.shape[0] * fsdp_count, D), jnp.float32)
    grad_gate_up = jnp.zeros((D, 2, local_units), jnp.float32)
    grad_down = jnp.zeros((down_weight.shape[0] * fsdp_count, D), jnp.float32)
    gain_one_acc = jnp.zeros((D,), jnp.float32)
    gain_two_acc = jnp.zeros((D,), jnp.float32)
    outputs = []
    input_grads = []
    for micro_index in range(micro_count):
        weights_fwd = (
            gather_attention(qkv_weight, out_weight),
            gather_feedforward(gate_up_weight, down_weight),
        )
        (qkv_full, out_full), (gate_up_full, down_full) = weights_fwd
        stream = block_in[micro_index].astype(jnp.float32)
        segment_row = segment_full[micro_index]
        cosine_part, sine_part = rope_tables(position_full[micro_index], HD)
        scale_one = rms_scale(stream)
        normed_one = (stream * scale_one * gain_one).astype(jnp.bfloat16)
        normed_one_full = lax.all_gather(normed_one, "tp", axis=0, tiled=True)
        projected = jnp.einsum(
            "sd,dtc->stc", normed_one_full, qkv_full, preferred_element_type=jnp.float32
        )
        queries = rotate(
            projected[:, 0].reshape(seq_len, heads_local, HD), cosine_part, sine_part
        ).astype(jnp.bfloat16)
        key_rows = rotate(
            projected[:, 1].reshape(seq_len, heads_local, HD), cosine_part, sine_part
        ).astype(jnp.bfloat16)
        value_rows = projected[:, 2].reshape(seq_len, heads_local, HD).astype(jnp.bfloat16)
        mixed, log_total = attention_forward(queries, key_rows, value_rows, segment_row, block_rows)
        attn_heads = mixed.astype(jnp.bfloat16)
        attn_term = jnp.dot(attn_heads, out_full, preferred_element_type=jnp.float32)
        attn_branch = lax.psum_scatter(attn_term, "tp", scatter_dimension=0, tiled=True)
        middle = stream + attn_branch
        scale_two = rms_scale(middle)
        normed_two = (middle * scale_two * gain_two).astype(jnp.bfloat16)
        normed_two_full = lax.all_gather(normed_two, "tp", axis=0, tiled=True)
        gate_up = jnp.einsum(
            "sd,dtf->stf", normed_two_full, gate_up_full, preferred_element_type=jnp.float32
        )
        gate_rows = gate_up[:, 0]
        up_rows = gate_up[:, 1]
        sigmoid_gate = jax.nn.sigmoid(gate_rows)
        silu_gate = gate_rows * sigmoid_gate
        activated = (silu_gate * up_rows).astype(jnp.bfloat16)
        mlp_term = jnp.dot(activated, down_full, preferred_element_type=jnp.float32)
        mlp_branch = lax.psum_scatter(
            mlp_term.astype(jnp.bfloat16), "tp", scatter_dimension=0, tiled=True
        ).astype(jnp.float32)
        outputs.append((middle + mlp_branch).astype(jnp.bfloat16))
        (qkv_back, out_back), (gate_up_back, down_back) = weights_fwd
        cotangent = out_cotangent[micro_index].astype(jnp.float32)
        cotangent_full = lax.all_gather(out_cotangent[micro_index], "tp", axis=0, tiled=True)
        grad_down = grad_down + jnp.einsum(
            "sf,sd->fd", activated, cotangent_full, preferred_element_type=jnp.float32
        )
        act_grad = jnp.einsum(
            "sd,fd->sf", cotangent_full, down_back, preferred_element_type=jnp.float32
        )
        gate_grad = act_grad * up_rows * sigmoid_gate * (1.0 + gate_rows * (1.0 - sigmoid_gate))
        up_grad = act_grad * silu_gate
        gate_up_grad = jnp.stack([gate_grad, up_grad], axis=1).astype(jnp.bfloat16)
        grad_gate_up = grad_gate_up + jnp.einsum(
            "sd,stf->dtf", normed_two_full, gate_up_grad, preferred_element_type=jnp.float32
        )
        normed_two_term = jnp.einsum(
            "stf,dtf->sd", gate_up_grad, gate_up_back, preferred_element_type=jnp.float32
        )
        normed_two_grad = lax.psum_scatter(normed_two_term, "tp", scatter_dimension=0, tiled=True)
        middle_back, gain_two_term = norm_back(middle, scale_two, gain_two, normed_two_grad)
        gain_two_acc = gain_two_acc + gain_two_term
        middle_grad = cotangent + middle_back
        attn_grad_full = lax.all_gather(middle_grad.astype(jnp.bfloat16), "tp", axis=0, tiled=True)
        grad_out = grad_out + jnp.einsum(
            "sc,sd->cd", attn_heads, attn_grad_full, preferred_element_type=jnp.float32
        )
        heads_grad = jnp.einsum(
            "sd,cd->sc", attn_grad_full, out_back, preferred_element_type=jnp.float32
        ).astype(jnp.bfloat16)
        query_grad, key_grad, value_grad = attention_backward(
            queries,
            key_rows,
            value_rows,
            segment_row,
            log_total,
            heads_grad.reshape(seq_len, heads_local, HD),
            block_rows,
        )
        projected_grad = jnp.stack(
            [
                unrotate(query_grad, cosine_part, sine_part).reshape(seq_len, local_cols),
                unrotate(key_grad, cosine_part, sine_part).reshape(seq_len, local_cols),
                value_grad.reshape(seq_len, local_cols),
            ],
            axis=1,
        ).astype(jnp.bfloat16)
        grad_qkv = grad_qkv + jnp.einsum(
            "sd,stc->dtc", normed_one_full, projected_grad, preferred_element_type=jnp.float32
        )
        normed_one_term = jnp.einsum(
            "stc,dtc->sd", projected_grad, qkv_back, preferred_element_type=jnp.float32
        )
        normed_one_grad = lax.psum_scatter(
            normed_one_term.astype(jnp.bfloat16), "tp", scatter_dimension=0, tiled=True
        ).astype(jnp.float32)
        stream_back, gain_one_term = norm_back(stream, scale_one, gain_one, normed_one_grad)
        gain_one_acc = gain_one_acc + gain_one_term
        input_grads.append(middle_grad + stream_back)
    owned_grads = (
        lax.psum_scatter(
            grad_qkv.astype(jnp.bfloat16), "fsdp", scatter_dimension=0, tiled=True
        ).astype(jnp.float32),
        lax.psum_scatter(
            grad_out.astype(jnp.bfloat16), "fsdp", scatter_dimension=0, tiled=True
        ).astype(jnp.float32),
        lax.psum_scatter(
            grad_gate_up.astype(jnp.bfloat16), "fsdp", scatter_dimension=0, tiled=True
        ).astype(jnp.float32),
        lax.psum_scatter(
            grad_down.astype(jnp.bfloat16), "fsdp", scatter_dimension=0, tiled=True
        ).astype(jnp.float32),
    )
    owned_gains = (
        lax.psum_scatter(gain_one_acc, ("fsdp", "tp"), scatter_dimension=0, tiled=True),
        lax.psum_scatter(gain_two_acc, ("fsdp", "tp"), scatter_dimension=0, tiled=True),
    )
    return (
        jnp.stack(outputs),
        jnp.stack(input_grads),
        owned_gains[0],
        owned_grads[0],
        owned_grads[1],
        owned_gains[1],
        owned_grads[2],
        owned_grads[3],
    )


HEAD_GROUP = 4
FIRST_DOC = 800


def dot_nt(left, right):
    return lax.dot_general(left, right, (((1,), (1,)), ((), ())), preferred_element_type=jnp.float32)


def dot_tn(left, right):
    return lax.dot_general(left, right, (((0,), (0,)), ((), ())), preferred_element_type=jnp.float32)


def dot_nn(left, right):
    return lax.dot_general(left, right, (((1,), (0,)), ((), ())), preferred_element_type=jnp.float32)


def swap_halves(values):
    lanes = lax.broadcasted_iota(jnp.int32, values.shape, 1)
    width = values.shape[1]
    return jnp.where(
        lanes % HD < HD // 2,
        pltpu.roll(values, width - HD // 2, 1),
        pltpu.roll(values, HD // 2, 1),
    )


def causal_mask(rows, columns):
    row_ids = lax.broadcasted_iota(jnp.int32, (rows, columns), 0)
    column_ids = lax.broadcasted_iota(jnp.int32, (rows, columns), 1)
    return row_ids >= column_ids


def tail_mask(reach):
    rows = reach.shape[0]
    row_ids = lax.broadcasted_iota(jnp.int32, (rows, rows), 0)
    column_ids = lax.broadcasted_iota(jnp.int32, (rows, rows), 1)
    return (row_ids >= column_ids) & (row_ids - column_ids <= reach)


def halves(slot_ref, quarter):
    first = slot_ref[0]
    return (
        pl.multiple_of(first * quarter, quarter),
        pl.multiple_of((1 - first) * quarter, quarter),
    )


def widen(table):
    return jnp.concatenate([table] * HEAD_GROUP, axis=1)


def load_rotated(offsets, quarter, q_ref, k_ref, v_ref, cos_ref, sin_ref, qr_ref, kr_ref, vr_ref):
    for place, offset in enumerate(offsets):
        rows = pl.ds(offset, quarter)
        target = pl.ds(place * quarter, quarter)
        cosine, sine = widen(cos_ref[rows, :]), widen(sin_ref[rows, :])
        q_raw, k_raw = q_ref[rows, :], k_ref[rows, :]
        qr_ref[target, :] = (q_raw * cosine + swap_halves(q_raw) * sine).astype(jnp.bfloat16)
        kr_ref[target, :] = (k_raw * cosine + swap_halves(k_raw) * sine).astype(jnp.bfloat16)
        vr_ref[target, :] = v_ref[rows, :].astype(jnp.bfloat16)


def softmax_mix(query, pieces, factor):
    scores = []
    for keys, _, mask in pieces:
        score = dot_nt(query, keys)
        scores.append(score if mask is None else jnp.where(mask, score, masked_score))
    top = functools.reduce(jnp.maximum, [jnp.max(s, axis=-1, keepdims=True) for s in scores])
    weights = [jnp.exp2((s - top) * factor) for s in scores]
    total = functools.reduce(jnp.add, [jnp.sum(w, axis=-1, keepdims=True) for w in weights])
    inverse = 1.0 / total
    mixed = functools.reduce(
        jnp.add,
        [dot_nn((w * inverse).astype(jnp.bfloat16), piece[1]) for w, piece in zip(weights, pieces)],
    )
    return mixed, top * factor + jnp.log2(total)


def head_slice(head):
    return slice(head * HD, (head + 1) * HD)


def forward_first(
    slot_ref, q_ref, k_ref, v_ref, cos_ref, sin_ref, qr_ref, kr_ref, vr_ref, o_ref, lse_ref
):
    half = q_ref.shape[0]
    quarter = half // 2
    offsets = halves(slot_ref, quarter)
    load_rotated(offsets, quarter, q_ref, k_ref, v_ref, cos_ref, sin_ref, qr_ref, kr_ref, vr_ref)
    factor = HD ** (-0.5) * LOG2E
    mask = causal_mask(quarter, quarter)
    for head in range(HEAD_GROUP):
        cols = head_slice(head)
        early, late = slice(0, quarter), slice(quarter, half)
        k_early, v_early = kr_ref[early, cols], vr_ref[early, cols]
        mixed, lse = softmax_mix(qr_ref[early, cols], [(k_early, v_early, mask)], factor)
        o_ref[pl.ds(offsets[0], quarter), cols] = mixed.astype(jnp.bfloat16)
        lse_ref[0, early, head : head + 1] = lse
        mixed, lse = softmax_mix(
            qr_ref[late, cols],
            [(k_early, v_early, None), (kr_ref[late, cols], vr_ref[late, cols], mask)],
            factor,
        )
        o_ref[pl.ds(offsets[1], quarter), cols] = mixed.astype(jnp.bfloat16)
        lse_ref[0, late, head : head + 1] = lse


def forward_second(
    slot_ref, q_ref, k_ref, v_ref, cos_ref, sin_ref, ka_ref, va_ref, pos_ref,
    qr_ref, kr_ref, vr_ref, o_ref, lse_ref,
):
    half = q_ref.shape[0]
    quarter = half // 2
    cut = FIRST_DOC - half
    spill = cut - quarter
    offsets = halves(slot_ref, quarter)
    load_rotated(offsets, quarter, q_ref, k_ref, v_ref, cos_ref, sin_ref, qr_ref, kr_ref, vr_ref)
    factor = HD ** (-0.5) * LOG2E
    mask = causal_mask(cut, cut)
    mask_tail = tail_mask(pos_ref[pl.ds(offsets[1] + spill, half - cut), :])
    for head in range(HEAD_GROUP):
        cols = head_slice(head)
        early, late = slice(0, cut), slice(cut, half)
        mixed, lse = softmax_mix(
            qr_ref[early, cols],
            [
                (ka_ref[:, cols], va_ref[:, cols], None),
                (kr_ref[early, cols], vr_ref[early, cols], mask),
            ],
            factor,
        )
        low = mixed.astype(jnp.bfloat16)
        o_ref[pl.ds(offsets[0], quarter), cols] = low[:quarter]
        o_ref[pl.ds(offsets[1], spill), cols] = low[quarter:]
        lse_ref[0, early, head : head + 1] = lse
        mixed, lse = softmax_mix(
            qr_ref[late, cols], [(kr_ref[late, cols], vr_ref[late, cols], mask_tail)], factor
        )
        o_ref[pl.ds(offsets[1] + spill, half - cut), cols] = mixed.astype(jnp.bfloat16)
        lse_ref[0, late, head : head + 1] = lse


def backward_both(
    slot_ref, qa_ref, ka_ref, va_ref, qb_ref, kb_ref, vb_ref, ga_ref, gb_ref, la_ref, lb_ref,
    cosa_ref, sina_ref, cosb_ref, sinb_ref, pos_ref,
    dqa_ref, dka_ref, dva_ref, dqb_ref, dkb_ref, dvb_ref,
    go_a, go_b, tqa, tka, tva, tqb, tkb, tvb,
):
    half = qa_ref.shape[0]
    quarter = half // 2
    cut = FIRST_DOC - half
    spill = cut - quarter
    offsets = halves(slot_ref, quarter)
    scale_value = HD ** (-0.5)
    factor = scale_value * LOG2E
    for place, offset in enumerate(offsets):
        target, rows = pl.ds(place * quarter, quarter), pl.ds(offset, quarter)
        go_a[target, :] = ga_ref[rows, :]
        go_b[target, :] = gb_ref[rows, :]
    mask = causal_mask(quarter, quarter)
    mask_cut = causal_mask(cut, cut)
    mask_tail = tail_mask(pos_ref[pl.ds(offsets[1] + spill, half - cut), :])
    for accumulator in (tka, tva, tkb, tvb):
        accumulator[...] = jnp.zeros_like(accumulator)

    def attend(query, grad, lse, pieces):
        weights, weight_grads = [], []
        for k_ref, v_ref, rows, cols, mask, _, _ in pieces:
            weight = jnp.exp2(dot_nt(query, k_ref[rows, cols]) * factor - lse)
            weights.append(weight if mask is None else jnp.where(mask, weight, 0.0))
            weight_grads.append(dot_nt(grad, v_ref[rows, cols]))
        shared = functools.reduce(
            jnp.add,
            [jnp.sum(w * g, axis=-1, keepdims=True) for w, g in zip(weights, weight_grads)],
        )
        query_grad = None
        for weight, weight_grad, piece in zip(weights, weight_grads, pieces):
            k_ref, v_ref, rows, cols, _, tk, tv = piece
            score_grad = (weight * (weight_grad - shared)).astype(jnp.bfloat16)
            term = dot_nn(score_grad, k_ref[rows, cols])
            query_grad = term if query_grad is None else query_grad + term
            tk[rows, cols] += dot_tn(score_grad, query)
            tv[rows, cols] += dot_tn(weight.astype(jnp.bfloat16), grad)
        return query_grad

    for head in range(HEAD_GROUP):
        cols = head_slice(head)
        lane = slice(head, head + 1)
        early, late, whole = slice(0, quarter), slice(quarter, half), slice(0, half)
        tqa[early, cols] = attend(
            qa_ref[early, cols], go_a[early, cols], la_ref[0, early, lane],
            [(ka_ref, va_ref, early, cols, mask, tka, tva)],
        )
        tqa[late, cols] = attend(
            qa_ref[late, cols], go_a[late, cols], la_ref[0, late, lane],
            [
                (ka_ref, va_ref, early, cols, None, tka, tva),
                (ka_ref, va_ref, late, cols, mask, tka, tva),
            ],
        )
        early, late = slice(0, cut), slice(cut, half)
        tqb[early, cols] = attend(
            qb_ref[early, cols], go_b[early, cols], lb_ref[0, early, lane],
            [
                (ka_ref, va_ref, whole, cols, None, tka, tva),
                (kb_ref, vb_ref, early, cols, mask_cut, tkb, tvb),
            ],
        )
        tqb[late, cols] = attend(
            qb_ref[late, cols], go_b[late, cols], lb_ref[0, late, lane],
            [(kb_ref, vb_ref, late, cols, mask_tail, tkb, tvb)],
        )
    for place, offset in enumerate(offsets):
        source, rows = pl.ds(place * quarter, quarter), pl.ds(offset, quarter)
        for total, cos_ref, sin_ref, out_ref in (
            (tqa, cosa_ref, sina_ref, dqa_ref),
            (tka, cosa_ref, sina_ref, dka_ref),
            (tqb, cosb_ref, sinb_ref, dqb_ref),
            (tkb, cosb_ref, sinb_ref, dkb_ref),
        ):
            grad = total[source, :] * scale_value
            out_ref[rows, :] = (
                grad * widen(cos_ref[rows, :]) - swap_halves(grad) * widen(sin_ref[rows, :])
            ).astype(jnp.bfloat16)
        dva_ref[rows, :] = tva[source, :].astype(jnp.bfloat16)
        dvb_ref[rows, :] = tvb[source, :].astype(jnp.bfloat16)


COST_SCALE = 1.7


def cost_of(flops):
    return pl.CostEstimate(flops=int(COST_SCALE * flops), bytes_accessed=1000, transcendentals=0)


def line_params():
    return pltpu.CompilerParams(
        dimension_semantics=("arbitrary",), vmem_limit_bytes=48 * 1024 * 1024
    )


def rows_kernel(pairs, extra_count, dot, chunk, finish, *refs):
    lefts, weights = refs[:pairs], refs[pairs : 2 * pairs]
    extras = refs[2 * pairs : 2 * pairs + extra_count]
    outs = refs[2 * pairs + extra_count :]

    @pl.loop(0, outs[0].shape[0] // chunk)
    def _(step):
        rows = pl.ds(pl.multiple_of(step * chunk, chunk), chunk)
        total = None
        for left, weight in zip(lefts, weights):
            term = dot(left[rows, :], weight[...])
            total = term if total is None else total + term
        for out, value in zip(outs, finish(total, *[extra[rows, :] for extra in extras])):
            out[rows, :] = value.astype(out.dtype)


def keep_one(total):
    return (total,)


def rows_matmul(lefts, weights, dot, types, tile, chunk=1024, finish=keep_one, extras=()):
    rows = lefts[0].shape[0]
    if dot is dot_nn:
        width = weights[0].shape[1]
        weight_specs = [pl.BlockSpec((w.shape[0], tile), lambda j: (0, j)) for w in weights]
    else:
        width = weights[0].shape[0]
        weight_specs = [pl.BlockSpec((tile, w.shape[1]), lambda j: (j, 0)) for w in weights]
    column = pl.BlockSpec((rows, tile), lambda j: (0, j))
    flops = 2 * rows * width * sum(left.shape[1] for left in lefts)
    results = pl.pallas_call(
        functools.partial(rows_kernel, len(lefts), len(extras), dot, min(chunk, rows), finish),
        out_shape=[jax.ShapeDtypeStruct((rows, width), kind) for kind in types],
        grid=(width // tile,),
        in_specs=[pl.BlockSpec(left.shape, lambda j: (0, 0)) for left in lefts]
        + weight_specs
        + [column] * len(extras),
        out_specs=[column] * len(types),
        compiler_params=line_params(),
        cost_estimate=cost_of(flops),
    )(*lefts, *weights, *extras)
    return tuple(results) if len(types) > 1 else results[0]


def sum_kernel(parts, chunk, *refs):
    lefts, rights, out = refs[:parts], refs[parts : 2 * parts], refs[-1]

    @pl.loop(0, out.shape[1] // chunk)
    def _(step):
        cols = pl.ds(pl.multiple_of(step * chunk, chunk), chunk)
        total = None
        for left, right in zip(lefts, rights):
            term = dot_tn(left[...], right[:, cols])
            total = term if total is None else total + term
        out[:, cols] = total.astype(out.dtype)


def sum_matmul(lefts, rights, tile, chunk):
    rows, height = lefts[0].shape
    width = rights[0].shape[1]
    return pl.pallas_call(
        functools.partial(sum_kernel, len(lefts), chunk),
        out_shape=jax.ShapeDtypeStruct((height, width), jnp.bfloat16),
        grid=(height // tile,),
        in_specs=[pl.BlockSpec((rows, tile), lambda j: (0, j)) for _ in lefts]
        + [pl.BlockSpec((rows, width), lambda j: (0, 0)) for _ in rights],
        out_specs=pl.BlockSpec((tile, width), lambda j: (j, 0)),
        compiler_params=line_params(),
        cost_estimate=cost_of(2 * rows * height * width * len(lefts)),
    )(*lefts, *rights)


def sibling_id():
    index = lax.axis_index("fsdp")
    return (index + 1 - 2 * (index % 2), lax.axis_index("tp"))


def meet(partner):
    barrier = pltpu.get_barrier_semaphore()
    pl.semaphore_signal(barrier, inc=1, device_id=partner, device_id_type=pl.DeviceIdType.MESH)
    pl.semaphore_wait(barrier, 1)


def push(source, target, send, receive, partner):
    return pltpu.make_async_remote_copy(
        src_ref=source,
        dst_ref=target,
        send_sem=send,
        recv_sem=receive,
        device_id=partner,
        device_id_type=pl.DeviceIdType.MESH,
    )


def exchange_call(kernel, key, operands, outs, scratch, vmem=16):
    anywhere = pl.BlockSpec(memory_space=pl.ANY)
    results = pl.pallas_call(
        kernel,
        out_shape=outs,
        in_specs=[anywhere] * len(operands),
        out_specs=[anywhere] * len(outs),
        scratch_shapes=scratch,
        compiler_params=pltpu.CompilerParams(
            collective_id=key, has_side_effects=True, vmem_limit_bytes=vmem * 1024 * 1024
        ),
        cost_estimate=cost_of(4 * 10**9),
    )(*operands)
    return tuple(results) if len(outs) > 1 else results[0]


def gather_kernel(own_ref, near_ref, full_ref, local, send, receive):
    partner = sibling_id()
    meet(partner)
    count = own_ref.shape[0]
    copies = []
    for place, ref in enumerate((own_ref, near_ref)):
        remote = push(
            ref, full_ref.at[pl.ds((2 + place) * count, count)],
            send.at[place], receive.at[place], partner,
        )
        remote.start()
        copies.append(remote)
    for place, ref in enumerate((own_ref, near_ref)):
        copy = pltpu.make_async_copy(
            ref, full_ref.at[pl.ds(place * count, count)], local.at[place]
        )
        copy.start()
        copies.append(copy)
    for copy in copies:
        copy.wait()


def core_gather(own, near):
    shape = (4 * own.shape[0], own.shape[1])
    return exchange_call(
        gather_kernel, 1, [own, near], [jax.ShapeDtypeStruct(shape, own.dtype)],
        [pltpu.SemaphoreType.DMA((2,))] * 3,
    )


def reduce_kernel(term_ref, keep_ref, away_ref, mine, got, keep, away, local, send, receive, store):
    partner = sibling_id()
    meet(partner)
    pieces, count = mine.shape[0], mine.shape[1]
    half = pieces * count
    remotes, loads = [], []
    for piece in range(pieces):
        order = (piece + pieces // 2) % pieces
        remote = push(
            term_ref.at[pl.ds(half + order * count, count)], got.at[order],
            send.at[order], receive.at[order], partner,
        )
        remote.start()
        remotes.append(remote)
        load = pltpu.make_async_copy(
            term_ref.at[pl.ds(order * count, count)], mine.at[order], local.at[order]
        )
        load.start()
        loads.append(load)
    stores = []
    for piece in range(pieces):
        order = (piece + pieces // 2) % pieces
        loads[piece].wait()
        remotes[piece].wait()
        total = mine[order].astype(jnp.float32) + got[order].astype(jnp.float32)
        if order < pieces // 2:
            keep[order] = total
            copy = pltpu.make_async_copy(
                keep.at[order], keep_ref.at[pl.ds(order * count, count)], store.at[order]
            )
        else:
            slot = order - pieces // 2
            away[slot] = total.astype(away.dtype)
            copy = pltpu.make_async_copy(
                away.at[slot], away_ref.at[pl.ds(slot * count, count)], store.at[order]
            )
        copy.start()
        stores.append(copy)
    for copy in stores:
        copy.wait()


def core_reduce(term):
    rows, width = term.shape
    quarter = rows // 4
    pieces = 4
    count = 2 * quarter // pieces
    return exchange_call(
        reduce_kernel, 2, [term],
        [
            jax.ShapeDtypeStruct((quarter, width), jnp.float32),
            jax.ShapeDtypeStruct((quarter, width), term.dtype),
        ],
        [
            pltpu.VMEM((pieces, count, width), term.dtype),
            pltpu.VMEM((pieces, count, width), term.dtype),
            pltpu.VMEM((pieces // 2, count, width), jnp.float32),
            pltpu.VMEM((pieces // 2, count, width), term.dtype),
        ]
        + [pltpu.SemaphoreType.DMA((pieces,))] * 4,
        vmem=24,
    )


def pair_kernel(own_ref, other_ref, pair_ref, local, send, receive):
    partner = sibling_id()
    core = lax.axis_index("fsdp") % 2
    far = lax.axis_index("tp") // 2
    meet(partner)
    count = own_ref.shape[0]
    place = pl.ds(pl.multiple_of(core * count, count), count)

    def run(mine, theirs):
        remote = push(theirs, pair_ref.at[place], send.at[0], receive.at[0], partner)
        remote.start()
        copy = pltpu.make_async_copy(mine, pair_ref.at[place], local.at[0])
        copy.start()
        copy.wait()
        remote.wait()

    @pl.when(core == far)
    def _():
        run(own_ref, other_ref)

    @pl.when(core != far)
    def _():
        run(other_ref, own_ref)


def core_pair(key, own, other):
    shape = (2 * own.shape[0], own.shape[1])
    return exchange_call(
        pair_kernel, key, [own, other], [jax.ShapeDtypeStruct(shape, own.dtype)],
        [pltpu.SemaphoreType.DMA((1,))] * 3,
    )


def split_kernel(pair_ref, keep_ref, away_ref, local, send, receive):
    partner = sibling_id()
    core = lax.axis_index("fsdp") % 2
    far = lax.axis_index("tp") // 2
    meet(partner)
    count = keep_ref.shape[0]
    mine = pair_ref.at[pl.ds(pl.multiple_of(core * count, count), count)]
    theirs = pair_ref.at[pl.ds(pl.multiple_of((1 - core) * count, count), count)]

    def run(own_target, other_target):
        remote = push(theirs, other_target, send.at[0], receive.at[0], partner)
        remote.start()
        copy = pltpu.make_async_copy(mine, own_target, local.at[0])
        copy.start()
        copy.wait()
        remote.wait()

    @pl.when(core == far)
    def _():
        run(keep_ref, keep_ref)

    @pl.when(core != far)
    def _():
        run(away_ref, away_ref)


def core_split(key, pair):
    shape = (pair.shape[0] // 2, pair.shape[1])
    return exchange_call(
        split_kernel, key, [pair], [jax.ShapeDtypeStruct(shape, pair.dtype)] * 2,
        [pltpu.SemaphoreType.DMA((1,))] * 3,
    )


def kernel_params():
    return pltpu.CompilerParams(
        dimension_semantics=("arbitrary", "arbitrary"), vmem_limit_bytes=40 * 1024 * 1024
    )


def attention_call(kernel, slot, arrays, kinds, outs, scratch):
    rows, heads_local = arrays[-1].shape[0], outs[1]
    half = rows // 2
    groups = heads_local // HEAD_GROUP
    width = HEAD_GROUP * HD

    def spec(kind):
        if kind == "table":
            return pl.BlockSpec((half, HD), lambda s, g, _: (s, 0))
        if kind == "column":
            return pl.BlockSpec((half, 1), lambda s, g, _: (s, 0))
        if kind == "lse":
            return pl.BlockSpec((1, half, HEAD_GROUP), lambda s, g, _: (g, s, 0))
        shift = kind * groups
        return pl.BlockSpec((half, width), lambda s, g, _: (s, shift + g))

    def shape(kind):
        if kind == "lse":
            return jax.ShapeDtypeStruct((groups, rows, HEAD_GROUP), jnp.float32)
        return jax.ShapeDtypeStruct((rows, heads_local * HD), jnp.bfloat16)

    return pl.pallas_call(
        kernel,
        out_shape=[shape(kind) for kind in outs[0]],
        grid_spec=pltpu.PrefetchScalarGridSpec(
            num_scalar_prefetch=1,
            grid=(rows // half, groups),
            in_specs=[spec(kind) for kind in kinds],
            out_specs=[spec(kind) for kind in outs[0]],
            scratch_shapes=scratch(half, width),
        ),
        compiler_params=kernel_params(),
        cost_estimate=cost_of(4 * len(outs[0]) ** 2 * rows * rows * heads_local * HD // 16),
    )(slot, *arrays)


def backward_scratch(half, width):
    return [pltpu.VMEM((half, width), jnp.bfloat16)] * 2 + [
        pltpu.VMEM((half, width), jnp.float32)
    ] * 6


def no_scratch(half, width):
    return []


def head_tables(positions):
    half_width = HD // 2
    frequency = rope_theta ** (-(jnp.arange(half_width, dtype=jnp.float32) * 2.0 / HD))
    angles = positions.astype(jnp.float32)[:, None] * frequency[None, :]
    cosine, sine = jnp.cos(angles), jnp.sin(angles)
    return (
        jnp.concatenate([cosine, cosine], axis=-1),
        jnp.concatenate([-sine, sine], axis=-1),
    )


def paired_device(
    block_in,
    out_cotangent,
    segment_ids,
    doc_positions,
    norm1_gain,
    qkv_weight,
    out_weight,
    norm2_gain,
    gate_up_weight,
    down_weight,
):
    fsdp_count, tp_count = lax.axis_size("fsdp"), lax.axis_size("tp")
    core = lax.axis_index("fsdp") % 2
    lane_z = lax.axis_index("tp")
    near, far = lane_z % 2, lane_z // 2
    slot = jnp.reshape(near, (1,)).astype(jnp.int32)
    core_pairs = [(i, i ^ 1) for i in range(fsdp_count)]
    near_pairs = [(i, i ^ 1) for i in range(tp_count)]
    far_pairs = [(i, i ^ 2) for i in range(tp_count)]
    plane_groups = [list(range(first, fsdp_count, 2)) for first in range(2)]
    rows = block_in.shape[1]
    local_cols = qkv_weight.shape[2]
    heads_local = local_cols // HD
    gain_one = norm1_gain.astype(jnp.float32)
    gain_two = norm2_gain.astype(jnp.float32)

    def swap_core(value):
        return lax.ppermute(value, "fsdp", core_pairs)

    def swap_near(value):
        return lax.ppermute(value, "tp", near_pairs)

    def swap_far(value):
        return lax.ppermute(value, "tp", far_pairs)

    def pick_tile(size):
        return 512 if size % 512 == 0 else 768

    tokens = []

    def act(work, *inputs):
        held = lax.optimization_barrier((*inputs, *tokens))[: len(inputs)]
        result = work(*held)
        tokens[:] = result if isinstance(result, tuple) else (result,)
        return result

    def pick(value, index):
        return lax.dynamic_index_in_dim(value, index, 0, keepdims=False)

    def place_tokens(value, got):
        keep = pick(value, far)
        return jnp.where(far == 0, keep, got), jnp.where(far == 0, got, keep)

    def join(left, right):
        return jnp.concatenate([left, right], axis=0)

    def plane_gather(pair):
        return lax.all_gather(pair, "fsdp", axis=0, tiled=True, axis_index_groups=plane_groups)

    def plane_scatter(grad):
        return lax.psum_scatter(
            grad, "fsdp", scatter_dimension=0, tiled=True, axis_index_groups=plane_groups
        )

    def gather_weight(key, local, other):
        return plane_gather(act(lambda own, got: core_pair(key, own, got), local, other))

    def add_wide(left, right):
        return left.astype(jnp.float32) + right.astype(jnp.float32)

    def chained(value, *others):
        return lax.optimization_barrier((value, *others))[0]

    def scatter_gains(gains):
        for axis, size in (("fsdp", fsdp_count), ("tp", tp_count)):
            index = lax.axis_index(axis)
            step = size // 2
            while step >= 1:
                bit = (index // step) % 2
                parts = gains.reshape(gains.shape[0], 2, gains.shape[1] // 2)
                sent = lax.dynamic_index_in_dim(parts, 1 - bit, 1, keepdims=False)
                kept = lax.dynamic_index_in_dim(parts, bit, 1, keepdims=False)
                gains = kept + lax.ppermute(sent, axis, [(i, i ^ step) for i in range(size)])
                step //= 2
        return gains

    def wide_dot(left, right, *_):
        return rows_matmul([left], [right], dot_nn, [jnp.float32], pick_tile(right.shape[1]))

    def dot_bf16(left, right):
        return rows_matmul([left], [right], dot_nn, [jnp.bfloat16], pick_tile(right.shape[1]))

    def grad_sum(left, right, left_next, right_next):
        return sum_matmul(
            [left, left_next], [right, right_next], pick_tile(left.shape[1]),
            2 * pick_tile(right.shape[1]) if right.shape[1] % 1024 == 0 else pick_tile(right.shape[1]),
        )

    def rms_pack(stream, gain):
        scale = rms_scale(stream)
        return scale, (stream * scale * gain).astype(jnp.bfloat16)

    qkv_local = qkv_weight.reshape(qkv_weight.shape[0], 3 * local_cols)
    gate_local, up_local = gate_up_weight[:, 0], gate_up_weight[:, 1]

    position_got = swap_far(pick(doc_positions, 1 - far))
    out_other = swap_far(out_weight)
    out_full = gather_weight(3, out_weight, out_other)
    qkv_other = swap_far(chained(qkv_local, out_other))
    first, second = act(place_tokens, doc_positions, position_got)
    near_both = swap_near(join(first, second))
    first, second = act(
        lambda a, b, c: (join(a, c[: a.shape[0]]), join(b, c[a.shape[0] :])),
        first, second, near_both,
    )
    core_both = swap_core(join(first, second))

    def make_tables(first, second, both):
        count = first.shape[0]
        late = join(second, both[count:])
        return (*head_tables(join(first, both[:count])), *head_tables(late), late[:, None])

    cos_first, sin_first, cos_second, sin_second, reach = act(
        make_tables, first, second, core_both
    )
    tables = [(cos_first, sin_first), (cos_second, sin_second)]
    stream_got = swap_far(chained(pick(block_in, 1 - far), qkv_other))
    qkv_full = gather_weight(4, qkv_local, qkv_other)

    def first_norm(value, got):
        streams = [part.astype(jnp.float32) for part in place_tokens(value, got)]
        return (*streams, *rms_pack(streams[0], gain_one), *rms_pack(streams[1], gain_one))

    gate_other = swap_far(chained(gate_local, stream_got))
    s_first, s_second, r_first, n_first, r_second, n_second = act(first_norm, block_in, stream_got)
    streams, scales_one = [s_first, s_second], [r_first, r_second]
    near_first = swap_near(n_first)
    gate_full = gather_weight(5, gate_local, gate_other)
    up_other = swap_far(chained(up_local, gate_other))
    near_second = swap_near(chained(n_second, near_first))
    h1_first = act(core_gather, n_first, near_first)

    def attend_first(projected):
        arrays = [projected, projected, projected, *tables[0]]
        return tuple(
            attention_call(
                forward_first, slot, arrays, [0, 1, 2, "table", "table"],
                ([0, 0, 0, 0, "lse"], heads_local), no_scratch,
            )
        )

    def attend_second(projected):
        arrays = [projected, projected, projected, *tables[1], saved[0][1], saved[0][2], reach]
        return tuple(
            attention_call(
                forward_second, slot, arrays, [0, 1, 2, "table", "table", 0, 0, "column"],
                ([0, 0, 0, 0, "lse"], heads_local), no_scratch,
            )
        )

    projected = act(wide_dot, h1_first, qkv_full, out_full)
    results = act(attend_first, projected)
    saved, lses, mixed_first = [results[:3]], [results[4]], results[3]
    h1_second = act(core_gather, n_second, near_second)
    term_first = act(dot_bf16, mixed_first, out_full)
    keep_first, send_first = act(core_reduce, term_first)
    branch_first = swap_near(send_first)
    projected = act(wide_dot, h1_second, qkv_full)
    up_full = gather_weight(5, up_local, up_other)
    down_other = swap_far(chained(down_weight, up_other))
    results = act(attend_second, projected)
    saved.append(results[:3])
    lses.append(results[4])
    mixed_second = results[3]

    def second_norm(stream, keep, got):
        middle = stream + keep + got.astype(jnp.float32)
        return (middle, *rms_pack(middle, gain_two))

    m_first, q_first, n_first = act(second_norm, streams[0], keep_first, branch_first)
    near_first = swap_near(n_first)
    term_second = act(dot_bf16, mixed_second, out_full)
    keep_second, send_second = act(core_reduce, term_second)
    branch_second = swap_near(chained(send_second, near_first))
    h2_first = act(core_gather, n_first, near_first)
    down_full = gather_weight(6, down_weight, down_other)
    cotangent_got = swap_far(chained(pick(out_cotangent, 1 - far), down_other))

    gate_first = act(wide_dot, h2_first, gate_full)
    m_second, q_second, n_second = act(second_norm, streams[1], keep_second, branch_second)
    near_second = swap_near(n_second)
    c_first, c_second = act(place_tokens, out_cotangent, cotangent_got)
    near_third = swap_near(chained(c_first, near_second))
    near_fourth = swap_near(chained(c_second, near_third))
    h2_second = act(core_gather, n_second, near_second)
    gate_second = act(wide_dot, h2_second, gate_full)

    def rise(hidden, weight, gate):
        return rows_matmul(
            [hidden], [weight], dot_nn, [jnp.float32, jnp.bfloat16], pick_tile(weight.shape[1]),
            finish=lambda up, gate: (up, gate * jax.nn.sigmoid(gate) * up), extras=[gate],
        )

    up_first, a_first = act(rise, h2_first, up_full, gate_first)
    y_first = act(core_gather, c_first, near_third)
    up_second, a_second = act(rise, h2_second, up_full, gate_second)
    y_second = act(core_gather, c_second, near_fourth)
    down_sum = plane_scatter(act(grad_sum, a_first, y_first, a_second, y_second))

    def fall_finish(act_grad, gate, up):
        sigmoid_gate = jax.nn.sigmoid(gate)
        return (
            act_grad * up * sigmoid_gate * (1.0 + gate * (1.0 - sigmoid_gate)),
            act_grad * (gate * sigmoid_gate),
        )

    def fall(cotangent, weight, gate, up):
        return rows_matmul(
            [cotangent], [weight], dot_nt, [jnp.bfloat16] * 2, pick_tile(weight.shape[0]),
            chunk=512, finish=fall_finish, extras=[gate, up],
        )

    dg_first, du_first = act(fall, y_first, down_full, gate_first, up_first)
    dg_second, du_second = act(fall, y_second, down_full, gate_second, up_second)
    gate_sum = plane_scatter(act(grad_sum, h2_first, dg_first, h2_second, dg_second))

    def hidden_grad(gate_grad, up_grad, gate_weight, up_weight):
        return rows_matmul(
            [gate_grad, up_grad], [gate_weight, up_weight], dot_nt, [jnp.bfloat16],
            pick_tile(gate_weight.shape[0]),
        )

    def second_back(middle, scale, keep, got, cotangent):
        grad, gain_term = norm_back(middle, scale, gain_two, keep + got.astype(jnp.float32))
        grad = cotangent.astype(jnp.float32) + grad
        return grad, grad.astype(jnp.bfloat16), gain_term

    term_first = act(hidden_grad, dg_first, du_first, gate_full, up_full)
    keep_first, send_first = act(core_reduce, term_first)
    back_first = swap_near(send_first)
    term_second = act(hidden_grad, dg_second, du_second, gate_full, up_full)
    keep_second, send_second = act(core_reduce, term_second)
    back_second = swap_near(chained(send_second, back_first))
    g_first, n_first, gain_two_first = act(
        second_back, m_first, q_first, keep_first, back_first, c_first
    )
    near_first = swap_near(chained(n_first, back_second))
    up_sum = plane_scatter(act(grad_sum, h2_first, du_first, h2_second, du_second))
    g_second, n_second, gain_two_second = act(
        second_back, m_second, q_second, keep_second, back_second, c_second
    )
    near_second = swap_near(chained(n_second, near_first))
    mlp_first = act(dot_bf16, a_first, down_full)
    mlp_keep_first, mlp_send_first = act(core_reduce, mlp_first)
    d_first = act(core_gather, n_first, near_first)

    def heads_back(grad, weight):
        return rows_matmul([grad], [weight], dot_nt, [jnp.bfloat16], pick_tile(weight.shape[0]))

    mlp_second = act(dot_bf16, a_second, down_full)
    mlp_branch_first = swap_near(chained(mlp_send_first, near_second))
    heads_first = act(heads_back, d_first, out_full)
    mlp_keep_second, mlp_send_second = act(core_reduce, mlp_second)
    d_second = act(core_gather, n_second, near_second)
    mlp_branch_second = swap_near(chained(mlp_send_second, mlp_branch_first))
    heads_second = act(heads_back, d_second, out_full)
    out_sum = plane_scatter(act(grad_sum, mixed_first, d_first, mixed_second, d_second))
    down_mine, down_away = act(lambda pair: core_split(10, pair), down_sum)
    down_got = swap_far(down_away)

    def attend_back(heads_first, heads_second):
        return tuple(
            attention_call(
                backward_both,
                slot,
                [
                    *saved[0], *saved[1], heads_first, heads_second, *lses,
                    *tables[0], *tables[1], reach,
                ],
                [0] * 8 + ["lse"] * 2 + ["table"] * 4 + ["column"],
                ([0] * 6, heads_local),
                backward_scratch,
            )
        )

    grads = act(attend_back, heads_first, heads_second)
    p_first, p_second = act(
        lambda *parts: (
            jnp.concatenate(parts[:3], axis=1),
            jnp.concatenate(parts[3:], axis=1),
        ),
        *grads,
    )

    def finish_output(first, first_keep, first_got, second, second_keep, second_got):
        first = (first + first_keep + first_got.astype(jnp.float32)).astype(jnp.bfloat16)
        second = (second + second_keep + second_got.astype(jnp.float32)).astype(jnp.bfloat16)
        return jnp.where(far == 0, first, second), jnp.where(far == 0, second, first)

    out_keep, out_send = act(
        finish_output,
        m_first, mlp_keep_first, mlp_branch_first, m_second, mlp_keep_second, mlp_branch_second,
    )
    out_got = swap_far(chained(out_send, down_got))
    qkv_sum = plane_scatter(act(grad_sum, h1_first, p_first, h1_second, p_second))
    down_owned = act(add_wide, down_mine, down_got)
    term_first = act(heads_back, p_first, qkv_full)
    keep_first, send_first = act(core_reduce, term_first)
    back_first = swap_near(send_first)
    gate_mine, gate_away = act(lambda pair: core_split(9, pair), gate_sum)
    term_second = act(heads_back, p_second, qkv_full)
    keep_second, send_second = act(core_reduce, term_second)
    back_second = swap_near(chained(send_second, back_first))

    def settle(keep, got):
        return jnp.stack([jnp.where(far == 0, keep, got), jnp.where(far == 0, got, keep)])

    def first_back(stream, scale, keep, got, grad):
        back, gain_term = norm_back(stream, scale, gain_one, keep + got.astype(jnp.float32))
        return grad + back, gain_term

    i_first, gain_one_first = act(
        first_back, streams[0], scales_one[0], keep_first, back_first, g_first
    )

    def last_back(stream, scale, keep, got, grad, first):
        second, gain_term = first_back(stream, scale, keep, got, grad)
        return (
            jnp.where(far == 0, first, second),
            jnp.where(far == 0, second, first).astype(jnp.bfloat16),
            gain_term,
        )

    in_keep, in_send, gain_one_second = act(
        last_back, streams[1], scales_one[1], keep_second, back_second, g_second, i_first
    )
    block_out = act(settle, out_keep, out_got)
    gate_got = swap_far(chained(gate_away, out_got))
    in_got = swap_far(chained(in_send, gate_got))
    gains = scatter_gains(
        jnp.stack([gain_one_first + gain_one_second, gain_two_first + gain_two_second])
    )
    gate_owned = act(add_wide, gate_mine, gate_got)
    up_mine, up_away = act(lambda pair: core_split(9, pair), up_sum)
    up_got = swap_far(chained(up_away, in_got))
    in_grad = act(lambda keep, got: settle(keep, got.astype(jnp.float32)), in_keep, in_got)
    out_mine, out_away = act(lambda pair: core_split(7, pair), out_sum)
    out_back = swap_far(chained(out_away, up_got))
    up_owned = act(add_wide, up_mine, up_got)
    gate_up_owned = act(lambda a, b: jnp.stack([a, b], axis=1), gate_owned, up_owned)
    out_owned = act(add_wide, out_mine, out_back)
    qkv_mine, qkv_away = act(lambda pair: core_split(8, pair), qkv_sum)
    qkv_owned = act(add_wide, qkv_mine, swap_far(qkv_away))
    return (
        block_out,
        in_grad,
        gains[0],
        qkv_owned.reshape(qkv_weight.shape),
        out_owned,
        gains[1],
        gate_up_owned,
        down_owned,
    )


def solution(mesh):
    sizes = (mesh.shape["fsdp"], mesh.shape["tp"])
    body = paired_device if sizes == (8, 4) else per_device
    in_specs = (
        P("fsdp", "tp", None),
        P("fsdp", "tp", None),
        P("fsdp", "tp"),
        P("fsdp", "tp"),
        P(),
        P("fsdp", None, "tp"),
        P(("tp", "fsdp"), None),
        P(),
        P("fsdp", None, "tp"),
        P(("tp", "fsdp"), None),
    )
    out_specs = (
        P("fsdp", "tp", None),
        P("fsdp", "tp", None),
        P(("fsdp", "tp")),
        P("fsdp", None, "tp"),
        P(("tp", "fsdp"), None),
        P(("fsdp", "tp")),
        P("fsdp", None, "tp"),
        P(("tp", "fsdp"), None),
    )
    return jax.shard_map(
        body, mesh=mesh, in_specs=in_specs, out_specs=out_specs, check_vma=False
    )
```

```python
import functools

import jax
import jax.numpy as jnp
from jax import lax
from jax.experimental import pallas as pl
from jax.experimental.pallas import tpu as pltpu
from jax.sharding import PartitionSpec as P

D = 3072
HD = 96


rms_epsilon = 1e-05
rope_theta = 10000.0
masked_score = -1e30
LOG2E = 1.4426950408889634


def rope_tables(positions, head_size):
    half_width = head_size // 2
    frequency = rope_theta ** (-(jnp.arange(half_width, dtype=jnp.float32) * 2.0 / head_size))
    angles = positions.astype(jnp.float32)[:, None] * frequency[None, :]
    return (jnp.cos(angles)[:, None, :], jnp.sin(angles)[:, None, :])


def rotate(values, cosine_part, sine_part):
    half_width = values.shape[-1] // 2
    lead_half = values[..., :half_width]
    tail_half = values[..., half_width:]
    return jnp.concatenate(
        [
            lead_half * cosine_part - tail_half * sine_part,
            tail_half * cosine_part + lead_half * sine_part,
        ],
        axis=-1,
    )


def unrotate(values, cosine_part, sine_part):
    half_width = values.shape[-1] // 2
    lead_half = values[..., :half_width]
    tail_half = values[..., half_width:]
    return jnp.concatenate(
        [
            lead_half * cosine_part + tail_half * sine_part,
            tail_half * cosine_part - lead_half * sine_part,
        ],
        axis=-1,
    )


def rms_scale(stream):
    return lax.rsqrt(jnp.mean(stream * stream, axis=-1, keepdims=True) + rms_epsilon)


def norm_back(stream, scale_rows, gain_vec, grad_rows):
    gained_grad = gain_vec * grad_rows
    input_grad = scale_rows * gained_grad - stream * scale_rows**3 * jnp.mean(
        gained_grad * stream, axis=-1, keepdims=True
    )
    return (input_grad, jnp.sum(grad_rows * stream * scale_rows, axis=0))


def allowed_mask(segment_tile, index_tile, segments):
    columns = jnp.arange(segments.shape[0], dtype=jnp.int32)
    return (segment_tile[:, None] == segments[None, :]) & (index_tile[:, None] >= columns[None, :])


def masked_scores(query_tile, key_rows, segment_tile, index_tile, segments, scale_value):
    scores = (
        jnp.einsum("qhd,khd->hqk", query_tile, key_rows, preferred_element_type=jnp.float32)
        * scale_value
    )
    return jnp.where(allowed_mask(segment_tile, index_tile, segments)[None], scores, masked_score)


def attention_forward(queries, key_rows, value_rows, segments, block_rows):
    seq_len, head_count, head_size = queries.shape
    tiles = seq_len // block_rows
    scale_value = head_size ** (-0.5)
    positions = jnp.arange(seq_len, dtype=jnp.int32)

    def query_block(packed):
        query_tile, segment_tile, index_tile = packed
        scores = masked_scores(
            query_tile, key_rows, segment_tile, index_tile, segments, scale_value
        )
        row_max = jnp.max(scores, axis=-1, keepdims=True)
        exponent = jnp.exp(scores - row_max)
        row_total = jnp.sum(exponent, axis=-1, keepdims=True)
        probs_low = (exponent / row_total).astype(jnp.bfloat16)
        mixed = jnp.einsum(
            "hqk,khd->qhd", probs_low, value_rows, preferred_element_type=jnp.float32
        )
        return (mixed, (row_max + jnp.log(row_total))[..., 0])

    mixed, log_total = lax.map(
        query_block,
        (
            queries.reshape(tiles, block_rows, head_count, head_size),
            segments.reshape(tiles, block_rows),
            positions.reshape(tiles, block_rows),
        ),
    )
    return (mixed.reshape(seq_len, head_count * head_size), log_total)


def attention_backward(queries, key_rows, value_rows, segments, log_total, out_grad, block_rows):
    seq_len, head_count, head_size = queries.shape
    tiles = seq_len // block_rows
    scale_value = head_size ** (-0.5)
    positions = jnp.arange(seq_len, dtype=jnp.int32)

    def query_block(carry, packed):
        key_acc, value_acc = carry
        query_tile, segment_tile, index_tile, total_tile, grad_tile = packed
        scores = masked_scores(
            query_tile, key_rows, segment_tile, index_tile, segments, scale_value
        )
        probs = jnp.exp(scores - total_tile[..., None])
        probs_low = probs.astype(jnp.bfloat16)
        prob_grad = jnp.einsum(
            "qhd,khd->hqk", grad_tile, value_rows, preferred_element_type=jnp.float32
        )
        score_grad = (
            probs * (prob_grad - jnp.sum(probs * prob_grad, axis=-1, keepdims=True))
        ).astype(jnp.bfloat16)
        query_grad = (
            jnp.einsum("hqk,khd->qhd", score_grad, key_rows, preferred_element_type=jnp.float32)
            * scale_value
        )
        key_acc = (
            key_acc
            + jnp.einsum("hqk,qhd->khd", score_grad, query_tile, preferred_element_type=jnp.float32)
            * scale_value
        )
        value_acc = value_acc + jnp.einsum(
            "hqk,qhd->khd", probs_low, grad_tile, preferred_element_type=jnp.float32
        )
        return ((key_acc, value_acc), query_grad)

    start_acc = (jnp.zeros(queries.shape, jnp.float32), jnp.zeros(queries.shape, jnp.float32))
    (key_grad, value_grad), query_grad = lax.scan(
        query_block,
        start_acc,
        (
            queries.reshape(tiles, block_rows, head_count, head_size),
            segments.reshape(tiles, block_rows),
            positions.reshape(tiles, block_rows),
            log_total,
            out_grad.reshape(tiles, block_rows, head_count, head_size),
        ),
    )
    return (query_grad.reshape(seq_len, head_count, head_size), key_grad, value_grad)


def gather_attention(qkv_weight, out_weight):
    return (
        lax.all_gather(qkv_weight, "fsdp", axis=0, tiled=True),
        lax.all_gather(out_weight, "fsdp", axis=0, tiled=True),
    )


def gather_feedforward(gate_up_weight, down_weight):
    return (
        lax.all_gather(gate_up_weight, "fsdp", axis=0, tiled=True),
        lax.all_gather(down_weight, "fsdp", axis=0, tiled=True),
    )


def per_device(
    block_in,
    out_cotangent,
    segment_ids,
    doc_positions,
    norm1_gain,
    qkv_weight,
    out_weight,
    norm2_gain,
    gate_up_weight,
    down_weight,
):
    micro_count = block_in.shape[0]
    fsdp_count = lax.axis_size("fsdp")
    segment_full, position_full = (
        lax.all_gather(segment_ids, "tp", axis=1, tiled=True),
        lax.all_gather(doc_positions, "tp", axis=1, tiled=True),
    )
    seq_len = segment_full.shape[1]
    block_rows = min(seq_len, 512)
    gain_one = norm1_gain.astype(jnp.float32)
    gain_two = norm2_gain.astype(jnp.float32)
    local_cols = qkv_weight.shape[2]
    local_units = gate_up_weight.shape[2]
    heads_local = local_cols // HD
    grad_qkv = jnp.zeros((D, 3, local_cols), jnp.float32)
    grad_out = jnp.zeros((out_weight.shape[0] * fsdp_count, D), jnp.float32)
    grad_gate_up = jnp.zeros((D, 2, local_units), jnp.float32)
    grad_down = jnp.zeros((down_weight.shape[0] * fsdp_count, D), jnp.float32)
    gain_one_acc = jnp.zeros((D,), jnp.float32)
    gain_two_acc = jnp.zeros((D,), jnp.float32)
    outputs = []
    input_grads = []
    for micro_index in range(micro_count):
        weights_fwd = (
            gather_attention(qkv_weight, out_weight),
            gather_feedforward(gate_up_weight, down_weight),
        )
        (qkv_full, out_full), (gate_up_full, down_full) = weights_fwd
        stream = block_in[micro_index].astype(jnp.float32)
        segment_row = segment_full[micro_index]
        cosine_part, sine_part = rope_tables(position_full[micro_index], HD)
        scale_one = rms_scale(stream)
        normed_one = (stream * scale_one * gain_one).astype(jnp.bfloat16)
        normed_one_full = lax.all_gather(normed_one, "tp", axis=0, tiled=True)
        projected = jnp.einsum(
            "sd,dtc->stc", normed_one_full, qkv_full, preferred_element_type=jnp.float32
        )
        queries = rotate(
            projected[:, 0].reshape(seq_len, heads_local, HD), cosine_part, sine_part
        ).astype(jnp.bfloat16)
        key_rows = rotate(
            projected[:, 1].reshape(seq_len, heads_local, HD), cosine_part, sine_part
        ).astype(jnp.bfloat16)
        value_rows = projected[:, 2].reshape(seq_len, heads_local, HD).astype(jnp.bfloat16)
        mixed, log_total = attention_forward(queries, key_rows, value_rows, segment_row, block_rows)
        attn_heads = mixed.astype(jnp.bfloat16)
        attn_term = jnp.dot(attn_heads, out_full, preferred_element_type=jnp.float32)
        attn_branch = lax.psum_scatter(attn_term, "tp", scatter_dimension=0, tiled=True)
        middle = stream + attn_branch
        scale_two = rms_scale(middle)
        normed_two = (middle * scale_two * gain_two).astype(jnp.bfloat16)
        normed_two_full = lax.all_gather(normed_two, "tp", axis=0, tiled=True)
        gate_up = jnp.einsum(
            "sd,dtf->stf", normed_two_full, gate_up_full, preferred_element_type=jnp.float32
        )
        gate_rows = gate_up[:, 0]
        up_rows = gate_up[:, 1]
        sigmoid_gate = jax.nn.sigmoid(gate_rows)
        silu_gate = gate_rows * sigmoid_gate
        activated = (silu_gate * up_rows).astype(jnp.bfloat16)
        mlp_term = jnp.dot(activated, down_full, preferred_element_type=jnp.float32)
        mlp_branch = lax.psum_scatter(
            mlp_term.astype(jnp.bfloat16), "tp", scatter_dimension=0, tiled=True
        ).astype(jnp.float32)
        outputs.append((middle + mlp_branch).astype(jnp.bfloat16))
        (qkv_back, out_back), (gate_up_back, down_back) = weights_fwd
        cotangent = out_cotangent[micro_index].astype(jnp.float32)
        cotangent_full = lax.all_gather(out_cotangent[micro_index], "tp", axis=0, tiled=True)
        grad_down = grad_down + jnp.einsum(
            "sf,sd->fd", activated, cotangent_full, preferred_element_type=jnp.float32
        )
        act_grad = jnp.einsum(
            "sd,fd->sf", cotangent_full, down_back, preferred_element_type=jnp.float32
        )
        gate_grad = act_grad * up_rows * sigmoid_gate * (1.0 + gate_rows * (1.0 - sigmoid_gate))
        up_grad = act_grad * silu_gate
        gate_up_grad = jnp.stack([gate_grad, up_grad], axis=1).astype(jnp.bfloat16)
        grad_gate_up = grad_gate_up + jnp.einsum(
            "sd,stf->dtf", normed_two_full, gate_up_grad, preferred_element_type=jnp.float32
        )
        normed_two_term = jnp.einsum(
            "stf,dtf->sd", gate_up_grad, gate_up_back, preferred_element_type=jnp.float32
        )
        normed_two_grad = lax.psum_scatter(normed_two_term, "tp", scatter_dimension=0, tiled=True)
        middle_back, gain_two_term = norm_back(middle, scale_two, gain_two, normed_two_grad)
        gain_two_acc = gain_two_acc + gain_two_term
        middle_grad = cotangent + middle_back
        attn_grad_full = lax.all_gather(middle_grad.astype(jnp.bfloat16), "tp", axis=0, tiled=True)
        grad_out = grad_out + jnp.einsum(
            "sc,sd->cd", attn_heads, attn_grad_full, preferred_element_type=jnp.float32
        )
        heads_grad = jnp.einsum(
            "sd,cd->sc", attn_grad_full, out_back, preferred_element_type=jnp.float32
        ).astype(jnp.bfloat16)
        query_grad, key_grad, value_grad = attention_backward(
            queries,
            key_rows,
            value_rows,
            segment_row,
            log_total,
            heads_grad.reshape(seq_len, heads_local, HD),
            block_rows,
        )
        projected_grad = jnp.stack(
            [
                unrotate(query_grad, cosine_part, sine_part).reshape(seq_len, local_cols),
                unrotate(key_grad, cosine_part, sine_part).reshape(seq_len, local_cols),
                value_grad.reshape(seq_len, local_cols),
            ],
            axis=1,
        ).astype(jnp.bfloat16)
        grad_qkv = grad_qkv + jnp.einsum(
            "sd,stc->dtc", normed_one_full, projected_grad, preferred_element_type=jnp.float32
        )
        normed_one_term = jnp.einsum(
            "stc,dtc->sd", projected_grad, qkv_back, preferred_element_type=jnp.float32
        )
        normed_one_grad = lax.psum_scatter(
            normed_one_term.astype(jnp.bfloat16), "tp", scatter_dimension=0, tiled=True
        ).astype(jnp.float32)
        stream_back, gain_one_term = norm_back(stream, scale_one, gain_one, normed_one_grad)
        gain_one_acc = gain_one_acc + gain_one_term
        input_grads.append(middle_grad + stream_back)
    owned_grads = (
        lax.psum_scatter(
            grad_qkv.astype(jnp.bfloat16), "fsdp", scatter_dimension=0, tiled=True
        ).astype(jnp.float32),
        lax.psum_scatter(
            grad_out.astype(jnp.bfloat16), "fsdp", scatter_dimension=0, tiled=True
        ).astype(jnp.float32),
        lax.psum_scatter(
            grad_gate_up.astype(jnp.bfloat16), "fsdp", scatter_dimension=0, tiled=True
        ).astype(jnp.float32),
        lax.psum_scatter(
            grad_down.astype(jnp.bfloat16), "fsdp", scatter_dimension=0, tiled=True
        ).astype(jnp.float32),
    )
    owned_gains = (
        lax.psum_scatter(gain_one_acc, ("fsdp", "tp"), scatter_dimension=0, tiled=True),
        lax.psum_scatter(gain_two_acc, ("fsdp", "tp"), scatter_dimension=0, tiled=True),
    )
    return (
        jnp.stack(outputs),
        jnp.stack(input_grads),
        owned_gains[0],
        owned_grads[0],
        owned_grads[1],
        owned_gains[1],
        owned_grads[2],
        owned_grads[3],
    )


HEAD_GROUP = 4
FIRST_DOC = 800


def dot_nt(left, right):
    return lax.dot_general(left, right, (((1,), (1,)), ((), ())), preferred_element_type=jnp.float32)


def dot_tn(left, right):
    return lax.dot_general(left, right, (((0,), (0,)), ((), ())), preferred_element_type=jnp.float32)


def dot_nn(left, right):
    return lax.dot_general(left, right, (((1,), (0,)), ((), ())), preferred_element_type=jnp.float32)


def swap_halves(values):
    lanes = lax.broadcasted_iota(jnp.int32, values.shape, 1)
    width = values.shape[1]
    return jnp.where(
        lanes % HD < HD // 2,
        pltpu.roll(values, width - HD // 2, 1),
        pltpu.roll(values, HD // 2, 1),
    )


def causal_mask(rows, columns):
    row_ids = lax.broadcasted_iota(jnp.int32, (rows, columns), 0)
    column_ids = lax.broadcasted_iota(jnp.int32, (rows, columns), 1)
    return row_ids >= column_ids


def tail_mask(reach):
    rows = reach.shape[0]
    row_ids = lax.broadcasted_iota(jnp.int32, (rows, rows), 0)
    column_ids = lax.broadcasted_iota(jnp.int32, (rows, rows), 1)
    return (row_ids >= column_ids) & (row_ids - column_ids <= reach)


def halves(quarter):
    first = lax.axis_index("tp") % 2
    return (
        pl.multiple_of(first * quarter, quarter),
        pl.multiple_of((1 - first) * quarter, quarter),
    )


def widen(table):
    return jnp.concatenate([table] * HEAD_GROUP, axis=1)


def load_rotated(offsets, quarter, q_ref, k_ref, v_ref, cos_ref, sin_ref, qr_ref, kr_ref, vr_ref):
    for place, offset in enumerate(offsets):
        rows = pl.ds(offset, quarter)
        target = pl.ds(place * quarter, quarter)
        cosine, sine = widen(cos_ref[rows, :]), widen(sin_ref[rows, :])
        q_raw, k_raw = q_ref[rows, :], k_ref[rows, :]
        qr_ref[target, :] = (q_raw * cosine + swap_halves(q_raw) * sine).astype(jnp.bfloat16)
        kr_ref[target, :] = (k_raw * cosine + swap_halves(k_raw) * sine).astype(jnp.bfloat16)
        vr_ref[target, :] = v_ref[rows, :].astype(jnp.bfloat16)


def softmax_mix(query, pieces, factor):
    scores = []
    for keys, _, mask in pieces:
        score = dot_nt(query, keys)
        scores.append(score if mask is None else jnp.where(mask, score, masked_score))
    top = functools.reduce(jnp.maximum, [jnp.max(s, axis=-1, keepdims=True) for s in scores])
    weights = [jnp.exp2((s - top) * factor) for s in scores]
    total = functools.reduce(jnp.add, [jnp.sum(w, axis=-1, keepdims=True) for w in weights])
    inverse = 1.0 / total
    mixed = functools.reduce(
        jnp.add,
        [dot_nn((w * inverse).astype(jnp.bfloat16), piece[1]) for w, piece in zip(weights, pieces)],
    )
    return mixed, top * factor + jnp.log2(total)


def head_slice(head):
    return slice(head * HD, (head + 1) * HD)


def forward_first(
    q_ref, k_ref, v_ref, cos_ref, sin_ref, qr_ref, kr_ref, vr_ref, o_ref, lse_ref
):
    half = q_ref.shape[0]
    quarter = half // 2
    offsets = halves(quarter)
    load_rotated(offsets, quarter, q_ref, k_ref, v_ref, cos_ref, sin_ref, qr_ref, kr_ref, vr_ref)
    factor = HD ** (-0.5) * LOG2E
    mask = causal_mask(quarter, quarter)
    for head in range(HEAD_GROUP):
        cols = head_slice(head)
        early, late = slice(0, quarter), slice(quarter, half)
        k_early, v_early = kr_ref[early, cols], vr_ref[early, cols]
        mixed, lse = softmax_mix(qr_ref[early, cols], [(k_early, v_early, mask)], factor)
        o_ref[pl.ds(offsets[0], quarter), cols] = mixed.astype(jnp.bfloat16)
        lse_ref[0, early, head : head + 1] = lse
        mixed, lse = softmax_mix(
            qr_ref[late, cols],
            [(k_early, v_early, None), (kr_ref[late, cols], vr_ref[late, cols], mask)],
            factor,
        )
        o_ref[pl.ds(offsets[1], quarter), cols] = mixed.astype(jnp.bfloat16)
        lse_ref[0, late, head : head + 1] = lse


def forward_second(
    q_ref, k_ref, v_ref, cos_ref, sin_ref, ka_ref, va_ref, pos_ref,
    qr_ref, kr_ref, vr_ref, o_ref, lse_ref,
):
    half = q_ref.shape[0]
    quarter = half // 2
    cut = FIRST_DOC - half
    spill = cut - quarter
    offsets = halves(quarter)
    load_rotated(offsets, quarter, q_ref, k_ref, v_ref, cos_ref, sin_ref, qr_ref, kr_ref, vr_ref)
    factor = HD ** (-0.5) * LOG2E
    mask = causal_mask(cut, cut)
    mask_tail = tail_mask(pos_ref[pl.ds(offsets[1] + spill, half - cut), :])
    for head in range(HEAD_GROUP):
        cols = head_slice(head)
        early, late = slice(0, cut), slice(cut, half)
        mixed, lse = softmax_mix(
            qr_ref[early, cols],
            [
                (ka_ref[:, cols], va_ref[:, cols], None),
                (kr_ref[early, cols], vr_ref[early, cols], mask),
            ],
            factor,
        )
        low = mixed.astype(jnp.bfloat16)
        o_ref[pl.ds(offsets[0], quarter), cols] = low[:quarter]
        o_ref[pl.ds(offsets[1], spill), cols] = low[quarter:]
        lse_ref[0, early, head : head + 1] = lse
        mixed, lse = softmax_mix(
            qr_ref[late, cols], [(kr_ref[late, cols], vr_ref[late, cols], mask_tail)], factor
        )
        o_ref[pl.ds(offsets[1] + spill, half - cut), cols] = mixed.astype(jnp.bfloat16)
        lse_ref[0, late, head : head + 1] = lse


def backward_both(
    qa_ref, ka_ref, va_ref, qb_ref, kb_ref, vb_ref, ga_ref, gb_ref, la_ref, lb_ref,
    cosa_ref, sina_ref, cosb_ref, sinb_ref, pos_ref,
    dqa_ref, dka_ref, dva_ref, dqb_ref, dkb_ref, dvb_ref,
    go_a, go_b, tqa, tka, tva, tqb, tkb, tvb,
):
    half = qa_ref.shape[0]
    quarter = half // 2
    cut = FIRST_DOC - half
    spill = cut - quarter
    offsets = halves(quarter)
    scale_value = HD ** (-0.5)
    factor = scale_value * LOG2E
    for place, offset in enumerate(offsets):
        target, rows = pl.ds(place * quarter, quarter), pl.ds(offset, quarter)
        go_a[target, :] = ga_ref[rows, :]
        go_b[target, :] = gb_ref[rows, :]
    mask = causal_mask(quarter, quarter)
    mask_cut = causal_mask(cut, cut)
    mask_tail = tail_mask(pos_ref[pl.ds(offsets[1] + spill, half - cut), :])
    for accumulator in (tka, tva, tkb, tvb):
        accumulator[...] = jnp.zeros_like(accumulator)

    def attend(query, grad, lse, pieces):
        weights, weight_grads = [], []
        for k_ref, v_ref, rows, cols, mask, _, _ in pieces:
            weight = jnp.exp2(dot_nt(query, k_ref[rows, cols]) * factor - lse)
            weights.append(weight if mask is None else jnp.where(mask, weight, 0.0))
            weight_grads.append(dot_nt(grad, v_ref[rows, cols]))
        shared = functools.reduce(
            jnp.add,
            [jnp.sum(w * g, axis=-1, keepdims=True) for w, g in zip(weights, weight_grads)],
        )
        query_grad = None
        for weight, weight_grad, piece in zip(weights, weight_grads, pieces):
            k_ref, v_ref, rows, cols, _, tk, tv = piece
            score_grad = (weight * (weight_grad - shared)).astype(jnp.bfloat16)
            term = dot_nn(score_grad, k_ref[rows, cols])
            query_grad = term if query_grad is None else query_grad + term
            tk[rows, cols] += dot_tn(score_grad, query)
            tv[rows, cols] += dot_tn(weight.astype(jnp.bfloat16), grad)
        return query_grad

    for head in range(HEAD_GROUP):
        cols = head_slice(head)
        lane = slice(head, head + 1)
        early, late, whole = slice(0, quarter), slice(quarter, half), slice(0, half)
        tqa[early, cols] = attend(
            qa_ref[early, cols], go_a[early, cols], la_ref[0, early, lane],
            [(ka_ref, va_ref, early, cols, mask, tka, tva)],
        )
        tqa[late, cols] = attend(
            qa_ref[late, cols], go_a[late, cols], la_ref[0, late, lane],
            [
                (ka_ref, va_ref, early, cols, None, tka, tva),
                (ka_ref, va_ref, late, cols, mask, tka, tva),
            ],
        )
        early, late = slice(0, cut), slice(cut, half)
        tqb[early, cols] = attend(
            qb_ref[early, cols], go_b[early, cols], lb_ref[0, early, lane],
            [
                (ka_ref, va_ref, whole, cols, None, tka, tva),
                (kb_ref, vb_ref, early, cols, mask_cut, tkb, tvb),
            ],
        )
        tqb[late, cols] = attend(
            qb_ref[late, cols], go_b[late, cols], lb_ref[0, late, lane],
            [(kb_ref, vb_ref, late, cols, mask_tail, tkb, tvb)],
        )
    for place, offset in enumerate(offsets):
        source, rows = pl.ds(place * quarter, quarter), pl.ds(offset, quarter)
        for total, cos_ref, sin_ref, out_ref in (
            (tqa, cosa_ref, sina_ref, dqa_ref),
            (tka, cosa_ref, sina_ref, dka_ref),
            (tqb, cosb_ref, sinb_ref, dqb_ref),
            (tkb, cosb_ref, sinb_ref, dkb_ref),
        ):
            grad = total[source, :] * scale_value
            out_ref[rows, :] = (
                grad * widen(cos_ref[rows, :]) - swap_halves(grad) * widen(sin_ref[rows, :])
            ).astype(jnp.bfloat16)
        dva_ref[rows, :] = tva[source, :].astype(jnp.bfloat16)
        dvb_ref[rows, :] = tvb[source, :].astype(jnp.bfloat16)


COST_SCALE = 1.7


def cost_of(flops):
    return pl.CostEstimate(flops=int(COST_SCALE * flops), bytes_accessed=1000, transcendentals=0)


def rows_kernel(pairs, extra_count, dot, chunk, finish, *refs):
    lefts, weights = refs[:pairs], refs[pairs : 2 * pairs]
    extras = refs[2 * pairs : 2 * pairs + extra_count]
    outs = refs[2 * pairs + extra_count :]

    @pl.loop(0, outs[0].shape[0] // chunk)
    def _(step):
        rows = pl.ds(pl.multiple_of(step * chunk, chunk), chunk)
        total = None
        for left, weight in zip(lefts, weights):
            term = dot(left[rows, :], weight[...])
            total = term if total is None else total + term
        for out, value in zip(outs, finish(total, *[extra[rows, :] for extra in extras])):
            out[rows, :] = value.astype(out.dtype)


def keep_one(total):
    return (total,)


def rows_matmul(
    lefts, weights, dot, types, tile, chunk=1024, finish=keep_one, extras=(), pushes=()
):
    rows = lefts[0].shape[0]
    if dot is dot_nn:
        width = weights[0].shape[1]
        weight_specs = [pl.BlockSpec((w.shape[0], tile), lambda j: (0, j)) for w in weights]
    else:
        width = weights[0].shape[0]
        weight_specs = [pl.BlockSpec((tile, w.shape[1]), lambda j: (j, 0)) for w in weights]
    column = pl.BlockSpec((rows, tile), lambda j: (0, j))
    return grid_call(
        functools.partial(rows_kernel, len(lefts), len(extras), dot, min(chunk, rows), finish),
        [*lefts, *weights, *extras],
        [pl.BlockSpec(left.shape, lambda j: (0, 0)) for left in lefts]
        + weight_specs
        + [column] * len(extras),
        [jax.ShapeDtypeStruct((rows, width), kind) for kind in types],
        [column] * len(types),
        (width // tile,),
        2 * rows * width * sum(left.shape[1] for left in lefts),
        pushes=pushes,
    )


def sum_kernel(parts, chunk, *refs):
    lefts, rights, out = refs[:parts], refs[parts : 2 * parts], refs[-1]

    @pl.loop(0, out.shape[1] // chunk)
    def _(step):
        cols = pl.ds(pl.multiple_of(step * chunk, chunk), chunk)
        total = None
        for left, right in zip(lefts, rights):
            term = dot_tn(left[...], right[:, cols])
            total = term if total is None else total + term
        out[:, cols] = total.astype(out.dtype)


def sum_matmul(lefts, rights, tile, chunk, pushes=()):
    rows, height = lefts[0].shape
    width = rights[0].shape[1]
    return grid_call(
        functools.partial(sum_kernel, len(lefts), chunk),
        [*lefts, *rights],
        [pl.BlockSpec((rows, tile), lambda j: (0, j)) for _ in lefts]
        + [pl.BlockSpec((rows, width), lambda j: (0, 0)) for _ in rights],
        [jax.ShapeDtypeStruct((height, width), jnp.bfloat16)],
        [pl.BlockSpec((tile, width), lambda j: (j, 0))],
        (height // tile,),
        2 * rows * height * width * len(lefts),
        pushes=pushes,
    )


def partner_of(kind):
    index, place = lax.axis_index("fsdp"), lax.axis_index("tp")
    if kind == "near":
        return (index, place + 1 - 2 * (place % 2))
    return (index, place + 2 - 4 * (place // 2))


def start_pushes(kinds, sources, targets, send, receive):
    barrier = pltpu.get_barrier_semaphore()
    names = sorted(set(kinds))
    for kind in names:
        pl.semaphore_signal(
            barrier, inc=1, device_id=partner_of(kind), device_id_type=pl.DeviceIdType.MESH
        )
    pl.semaphore_wait(barrier, len(names))
    for place, kind in enumerate(kinds):
        push(
            sources[place], targets[place], send.at[place], receive.at[place], partner_of(kind)
        ).start()


def wait_pushes(kinds, sources, targets, send, receive):
    for place, kind in enumerate(kinds):
        push(
            sources[place], targets[place], send.at[place], receive.at[place], partner_of(kind)
        ).wait()


def pushing_kernel(kernel, axes, in_count, out_count, kinds, *refs):
    count = len(kinds)
    inputs, sources = refs[:in_count], refs[in_count : in_count + count]
    outs = refs[in_count + count : in_count + count + out_count]
    targets = refs[in_count + count + out_count : in_count + 2 * count + out_count]
    scratch, (send, receive) = refs[in_count + 2 * count + out_count : -2], refs[-2:]
    first = functools.reduce(jnp.logical_and, [pl.program_id(axis) == 0 for axis in range(axes)])
    last = functools.reduce(
        jnp.logical_and,
        [pl.program_id(axis) == pl.num_programs(axis) - 1 for axis in range(axes)],
    )

    @pl.when(first)
    def _():
        start_pushes(kinds, sources, targets, send, receive)

    kernel(*inputs, *outs, *scratch)

    @pl.when(last)
    def _():
        wait_pushes(kinds, sources, targets, send, receive)


def grid_call(
    kernel, operands, in_specs, outs, out_specs, grid, flops, scratch=(), pushes=(), vmem=48
):
    params = dict(
        dimension_semantics=("arbitrary",) * len(grid), vmem_limit_bytes=vmem * 1024 * 1024
    )
    operands, in_specs, outs = list(operands), list(in_specs), list(outs)
    out_specs, scratch = list(out_specs), list(scratch)
    if pushes:
        kinds = tuple(kind for kind, _ in pushes)
        kernel = functools.partial(
            pushing_kernel, kernel, len(grid), len(operands), len(outs), kinds
        )
        anywhere = [pl.BlockSpec(memory_space=pl.ANY)] * len(pushes)
        operands += [value for _, value in pushes]
        in_specs += anywhere
        outs += [jax.ShapeDtypeStruct(value.shape, value.dtype) for _, value in pushes]
        out_specs += anywhere
        scratch += [pltpu.SemaphoreType.DMA((len(pushes),))] * 2
        next_key[0] += 1
        params.update(collective_id=next_key[0], has_side_effects=True)
    return tuple(
        pl.pallas_call(
            kernel,
            out_shape=outs,
            grid=grid,
            in_specs=in_specs,
            out_specs=out_specs,
            scratch_shapes=scratch,
            compiler_params=pltpu.CompilerParams(**params),
            cost_estimate=cost_of(flops),
        )(*operands)
    )


def swap_kernel(kinds, *refs):
    count = len(kinds)
    sources, targets, (send, receive) = refs[:count], refs[count : 2 * count], refs[2 * count :]
    start_pushes(kinds, sources, targets, send, receive)
    wait_pushes(kinds, sources, targets, send, receive)


def swap_call(*pushes):
    next_key[0] += 1
    kinds = tuple(kind for kind, _ in pushes)
    values = [value for _, value in pushes]
    return exchange_call(
        functools.partial(swap_kernel, kinds), next_key[0], values,
        [jax.ShapeDtypeStruct(value.shape, value.dtype) for value in values],
        [pltpu.SemaphoreType.DMA((len(pushes),))] * 2,
    )


next_key = [10]


def sibling_id():
    index = lax.axis_index("fsdp")
    return (index + 1 - 2 * (index % 2), lax.axis_index("tp"))


def meet(partner):
    barrier = pltpu.get_barrier_semaphore()
    pl.semaphore_signal(barrier, inc=1, device_id=partner, device_id_type=pl.DeviceIdType.MESH)
    pl.semaphore_wait(barrier, 1)


def push(source, target, send, receive, partner):
    return pltpu.make_async_remote_copy(
        src_ref=source,
        dst_ref=target,
        send_sem=send,
        recv_sem=receive,
        device_id=partner,
        device_id_type=pl.DeviceIdType.MESH,
    )


def exchange_call(kernel, key, operands, outs, scratch, vmem=16):
    anywhere = pl.BlockSpec(memory_space=pl.ANY)
    results = pl.pallas_call(
        kernel,
        out_shape=outs,
        in_specs=[anywhere] * len(operands),
        out_specs=[anywhere] * len(outs),
        scratch_shapes=scratch,
        compiler_params=pltpu.CompilerParams(
            collective_id=key, has_side_effects=True, vmem_limit_bytes=vmem * 1024 * 1024
        ),
        cost_estimate=cost_of(4 * 10**9),
    )(*operands)
    return tuple(results) if len(outs) > 1 else results[0]


def gather_kernel(own_ref, near_ref, full_ref, local, send, receive):
    partner = sibling_id()
    meet(partner)
    count = own_ref.shape[0]
    copies = []
    for place, ref in enumerate((own_ref, near_ref)):
        remote = push(
            ref, full_ref.at[pl.ds((2 + place) * count, count)],
            send.at[place], receive.at[place], partner,
        )
        remote.start()
        copies.append(remote)
    for place, ref in enumerate((own_ref, near_ref)):
        copy = pltpu.make_async_copy(
            ref, full_ref.at[pl.ds(place * count, count)], local.at[place]
        )
        copy.start()
        copies.append(copy)
    for copy in copies:
        copy.wait()


def core_gather(own, near):
    shape = (4 * own.shape[0], own.shape[1])
    return exchange_call(
        gather_kernel, 1, [own, near], [jax.ShapeDtypeStruct(shape, own.dtype)],
        [pltpu.SemaphoreType.DMA((2,))] * 3,
    )


def reduce_kernel(term_ref, keep_ref, away_ref, mine, got, keep, away, local, send, receive, store):
    partner = sibling_id()
    meet(partner)
    pieces, count = mine.shape[0], mine.shape[1]
    half = pieces * count
    remotes, loads = [], []
    for piece in range(pieces):
        order = (piece + pieces // 2) % pieces
        remote = push(
            term_ref.at[pl.ds(half + order * count, count)], got.at[order],
            send.at[order], receive.at[order], partner,
        )
        remote.start()
        remotes.append(remote)
        load = pltpu.make_async_copy(
            term_ref.at[pl.ds(order * count, count)], mine.at[order], local.at[order]
        )
        load.start()
        loads.append(load)
    stores = []
    for piece in range(pieces):
        order = (piece + pieces // 2) % pieces
        loads[piece].wait()
        remotes[piece].wait()
        total = mine[order].astype(jnp.float32) + got[order].astype(jnp.float32)
        if order < pieces // 2:
            keep[order] = total
            copy = pltpu.make_async_copy(
                keep.at[order], keep_ref.at[pl.ds(order * count, count)], store.at[order]
            )
        else:
            slot = order - pieces // 2
            away[slot] = total.astype(away.dtype)
            copy = pltpu.make_async_copy(
                away.at[slot], away_ref.at[pl.ds(slot * count, count)], store.at[order]
            )
        copy.start()
        stores.append(copy)
    for copy in stores:
        copy.wait()


def core_reduce(term):
    rows, width = term.shape
    quarter = rows // 4
    pieces = 4
    count = 2 * quarter // pieces
    return exchange_call(
        reduce_kernel, 2, [term],
        [
            jax.ShapeDtypeStruct((quarter, width), jnp.float32),
            jax.ShapeDtypeStruct((quarter, width), term.dtype),
        ],
        [
            pltpu.VMEM((pieces, count, width), term.dtype),
            pltpu.VMEM((pieces, count, width), term.dtype),
            pltpu.VMEM((pieces // 2, count, width), jnp.float32),
            pltpu.VMEM((pieces // 2, count, width), term.dtype),
        ]
        + [pltpu.SemaphoreType.DMA((pieces,))] * 4,
        vmem=24,
    )


def pair_kernel(own_ref, *refs):
    others, (pair_ref, local, send, receive) = refs[:-4], refs[-4:]
    partner = sibling_id()
    core = lax.axis_index("fsdp") % 2
    far = lax.axis_index("tp") // 2
    meet(partner)
    base = pl.multiple_of(core * own_ref.shape[0], own_ref.shape[0])
    count = others[0].shape[0]
    owns = [own_ref.at[pl.ds(place * count, count)] for place in range(len(others))]

    def run(mine, theirs):
        copies = []
        for place in range(len(others)):
            target = pair_ref.at[pl.ds(base + place * count, count)]
            remote = push(
                theirs[place], target, send.at[place], receive.at[place], partner
            )
            remote.start()
            copy = pltpu.make_async_copy(mine[place], target, local.at[place])
            copy.start()
            copies += [remote, copy]
        for copy in copies:
            copy.wait()

    @pl.when(core == far)
    def _():
        run(owns, others)

    @pl.when(core != far)
    def _():
        run(others, owns)


def core_pair(key, own, *others):
    shape = (2 * own.shape[0], own.shape[1])
    return exchange_call(
        pair_kernel, key, [own, *others], [jax.ShapeDtypeStruct(shape, own.dtype)],
        [pltpu.SemaphoreType.DMA((len(others),))] * 3,
    )


def split_kernel(pair_ref, keep_ref, away_ref, local, send, receive):
    partner = sibling_id()
    core = lax.axis_index("fsdp") % 2
    far = lax.axis_index("tp") // 2
    meet(partner)
    count = keep_ref.shape[0]
    mine = pair_ref.at[pl.ds(pl.multiple_of(core * count, count), count)]
    theirs = pair_ref.at[pl.ds(pl.multiple_of((1 - core) * count, count), count)]

    def run(own_target, other_target):
        remote = push(theirs, other_target, send.at[0], receive.at[0], partner)
        remote.start()
        copy = pltpu.make_async_copy(mine, own_target, local.at[0])
        copy.start()
        copy.wait()
        remote.wait()

    @pl.when(core == far)
    def _():
        run(keep_ref, keep_ref)

    @pl.when(core != far)
    def _():
        run(away_ref, away_ref)


def core_split(key, pair):
    shape = (pair.shape[0] // 2, pair.shape[1])
    return exchange_call(
        split_kernel, key, [pair], [jax.ShapeDtypeStruct(shape, pair.dtype)] * 2,
        [pltpu.SemaphoreType.DMA((1,))] * 3,
    )


def attention_call(kernel, arrays, kinds, outs, scratch, pushes=()):
    rows, heads_local = arrays[-1].shape[0], outs[1]
    half = rows // 2
    groups = heads_local // HEAD_GROUP
    width = HEAD_GROUP * HD

    def spec(kind):
        if kind == "table":
            return pl.BlockSpec((half, HD), lambda s, g: (s, 0))
        if kind == "column":
            return pl.BlockSpec((half, 1), lambda s, g: (s, 0))
        if kind == "lse":
            return pl.BlockSpec((1, half, HEAD_GROUP), lambda s, g: (g, s, 0))
        shift = kind * groups
        return pl.BlockSpec((half, width), lambda s, g: (s, shift + g))

    def shape(kind):
        if kind == "lse":
            return jax.ShapeDtypeStruct((groups, rows, HEAD_GROUP), jnp.float32)
        return jax.ShapeDtypeStruct((rows, heads_local * HD), jnp.bfloat16)

    return grid_call(
        kernel,
        arrays,
        [spec(kind) for kind in kinds],
        [shape(kind) for kind in outs[0]],
        [spec(kind) for kind in outs[0]],
        (rows // half, groups),
        4 * len(outs[0]) ** 2 * rows * rows * heads_local * HD // 16,
        scratch=scratch(half, width),
        pushes=pushes,
        vmem=40,
    )


def backward_scratch(half, width):
    return [pltpu.VMEM((half, width), jnp.bfloat16)] * 2 + [
        pltpu.VMEM((half, width), jnp.float32)
    ] * 6


def no_scratch(half, width):
    return []


def head_tables(positions):
    half_width = HD // 2
    frequency = rope_theta ** (-(jnp.arange(half_width, dtype=jnp.float32) * 2.0 / HD))
    angles = positions.astype(jnp.float32)[:, None] * frequency[None, :]
    cosine, sine = jnp.cos(angles), jnp.sin(angles)
    return (
        jnp.concatenate([cosine, cosine], axis=-1),
        jnp.concatenate([-sine, sine], axis=-1),
    )


def paired_device(
    block_in,
    out_cotangent,
    segment_ids,
    doc_positions,
    norm1_gain,
    qkv_weight,
    out_weight,
    norm2_gain,
    gate_up_weight,
    down_weight,
):
    fsdp_count, tp_count = lax.axis_size("fsdp"), lax.axis_size("tp")
    core = lax.axis_index("fsdp") % 2
    lane_z = lax.axis_index("tp")
    near, far = lane_z % 2, lane_z // 2
    core_pairs = [(i, i ^ 1) for i in range(fsdp_count)]
    near_pairs = [(i, i ^ 1) for i in range(tp_count)]
    far_pairs = [(i, i ^ 2) for i in range(tp_count)]
    plane_groups = [list(range(first, fsdp_count, 2)) for first in range(2)]
    rows = block_in.shape[1]
    local_cols = qkv_weight.shape[2]
    heads_local = local_cols // HD
    gain_one = norm1_gain.astype(jnp.float32)
    gain_two = norm2_gain.astype(jnp.float32)

    def swap_core(value):
        return lax.ppermute(value, "fsdp", core_pairs)

    def swap_near(value):
        return lax.ppermute(value, "tp", near_pairs)

    def swap_far(value):
        return lax.ppermute(value, "tp", far_pairs)

    def pick_tile(size):
        return 512 if size % 512 == 0 else 768

    tokens = []

    def act(work, *inputs, sends=()):
        values = [*inputs, *[value for _, value in sends]]
        held = lax.optimization_barrier((*values, *tokens))[: len(values)]
        if sends:
            kinds = [kind for kind, _ in sends]
            result = work(*held[: len(inputs)], pushes=list(zip(kinds, held[len(inputs) :])))
        else:
            result = work(*held)
        tokens[:] = result if isinstance(result, tuple) else (result,)
        return result[0] if isinstance(result, tuple) and len(result) == 1 else result

    def swap(*sends):
        return act(lambda pushes: swap_call(*pushes), sends=sends)

    def pick(value, index):
        return lax.dynamic_index_in_dim(value, index, 0, keepdims=False)

    def place_tokens(value, got):
        keep = pick(value, far)
        return jnp.where(far == 0, keep, got), jnp.where(far == 0, got, keep)

    def join(left, right):
        return jnp.concatenate([left, right], axis=0)

    def plane_gather(pair):
        return lax.all_gather(pair, "fsdp", axis=0, tiled=True, axis_index_groups=plane_groups)

    def plane_scatter(grad):
        return lax.psum_scatter(
            grad, "fsdp", scatter_dimension=0, tiled=True, axis_index_groups=plane_groups
        )

    def gather_weight(key, local, *others):
        return plane_gather(act(lambda own, *got: core_pair(key, own, *got), local, *others))

    def halve(value):
        count = value.shape[0] // 2
        return value[:count], value[count:]

    def add_wide(left, right):
        return left.astype(jnp.float32) + right.astype(jnp.float32)

    def chained(value, *others):
        return lax.optimization_barrier((value, *others))[0]

    def scatter_gains(gains):
        for axis, size in (("fsdp", fsdp_count), ("tp", tp_count)):
            index = lax.axis_index(axis)
            step = size // 2
            while step >= 1:
                bit = (index // step) % 2
                parts = gains.reshape(gains.shape[0], 2, gains.shape[1] // 2)
                sent = lax.dynamic_index_in_dim(parts, 1 - bit, 1, keepdims=False)
                kept = lax.dynamic_index_in_dim(parts, bit, 1, keepdims=False)
                gains = kept + lax.ppermute(sent, axis, [(i, i ^ step) for i in range(size)])
                step //= 2
        return gains

    def wide_dot(left, right, pushes=()):
        return rows_matmul(
            [left], [right], dot_nn, [jnp.float32], pick_tile(right.shape[1]), pushes=pushes
        )

    def dot_bf16(left, right, pushes=()):
        return rows_matmul(
            [left], [right], dot_nn, [jnp.bfloat16], pick_tile(right.shape[1]), pushes=pushes
        )

    def grad_sum(left, right, left_next, right_next, pushes=()):
        chunk = pick_tile(right.shape[1])
        return sum_matmul(
            [left, left_next], [right, right_next], pick_tile(left.shape[1]),
            2 * chunk if right.shape[1] % (2 * chunk) == 0 else chunk, pushes=pushes,
        )

    def heads_back(grad, weight, pushes=()):
        return rows_matmul(
            [grad], [weight], dot_nt, [jnp.bfloat16], pick_tile(weight.shape[0]), pushes=pushes
        )

    def rms_pack(stream, gain):
        scale = rms_scale(stream)
        return scale, (stream * scale * gain).astype(jnp.bfloat16)

    qkv_local = qkv_weight.reshape(qkv_weight.shape[0], 3 * local_cols)
    gate_local, up_local = gate_up_weight[:, 0], gate_up_weight[:, 1]

    next_key[0] = 10
    position_got = swap_far(pick(doc_positions, 1 - far))
    out_other = swap(("far", out_weight))
    out_full = gather_weight(3, out_weight, out_other)
    first, second = act(place_tokens, doc_positions, position_got)
    near_both = swap_near(join(first, second))
    qkv_other = swap(("far", qkv_local))
    qkv_full = gather_weight(4, qkv_local, qkv_other)
    first, second = act(
        lambda a, b, c: (join(a, c[: a.shape[0]]), join(b, c[a.shape[0] :])),
        first, second, near_both,
    )
    core_both = swap_core(join(first, second))

    def make_tables(first, second, both):
        count = first.shape[0]
        late = join(second, both[count:])
        return (*head_tables(join(first, both[:count])), *head_tables(late), late[:, None])

    stream_got = swap(("far", pick(block_in, 1 - far)))

    def first_norm(value, got):
        streams = [part.astype(jnp.float32) for part in place_tokens(value, got)]
        return (*streams, *rms_pack(streams[0], gain_one), *rms_pack(streams[1], gain_one))

    s_first, s_second, r_first, n_first, r_second, n_second = act(first_norm, block_in, stream_got)
    streams, scales_one = [s_first, s_second], [r_first, r_second]
    near_first, gate_other = swap(("near", n_first), ("far", gate_local))
    gate_full = gather_weight(5, gate_local, gate_other)
    h1_first = act(core_gather, n_first, near_first)

    def attend_first(projected, pushes=()):
        arrays = [projected, projected, projected, *tables[0]]
        return attention_call(
            forward_first, arrays, [0, 1, 2, "table", "table"],
            ([0, 0, 0, 0, "lse"], heads_local), no_scratch, pushes,
        )

    def attend_second(projected, pushes=()):
        arrays = [projected, projected, projected, *tables[1], saved[0][1], saved[0][2], reach]
        return attention_call(
            forward_second, arrays, [0, 1, 2, "table", "table", 0, 0, "column"],
            ([0, 0, 0, 0, "lse"], heads_local), no_scratch, pushes,
        )

    up_halves, down_halves = halve(up_local), halve(down_weight)
    cot_halves = halve(pick(out_cotangent, 1 - far))
    cos_first, sin_first, cos_second, sin_second, reach = act(
        make_tables, first, second, core_both
    )
    tables = [(cos_first, sin_first), (cos_second, sin_second)]
    projected, near_second, up_early = act(
        wide_dot, h1_first, qkv_full, sends=[("near", n_second), ("far", up_halves[0])]
    )
    *results, up_late = act(attend_first, projected, sends=[("far", up_halves[1])])
    saved, lses, mixed_first = [results[:3]], [results[4]], results[3]
    up_full = gather_weight(7, up_local, up_early, up_late)
    h1_second = act(core_gather, n_second, near_second)
    term_first = act(dot_bf16, mixed_first, out_full)
    keep_first, send_first = act(core_reduce, term_first)
    projected, branch_first, down_early = act(
        wide_dot, h1_second, qkv_full, sends=[("near", send_first), ("far", down_halves[0])]
    )

    def second_norm(stream, keep, got):
        middle = stream + keep + got.astype(jnp.float32)
        return (middle, *rms_pack(middle, gain_two))

    m_first, q_first, n_first = act(second_norm, streams[0], keep_first, branch_first)
    *results, near_first, down_late = act(
        attend_second, projected, sends=[("near", n_first), ("far", down_halves[1])]
    )
    saved.append(results[:3])
    lses.append(results[4])
    mixed_second = results[3]
    down_full = gather_weight(6, down_weight, down_early, down_late)
    term_second = act(dot_bf16, mixed_second, out_full)
    keep_second, send_second = act(core_reduce, term_second)
    h2_first = act(core_gather, n_first, near_first)

    gate_first, branch_second, cot_early = act(
        wide_dot, h2_first, gate_full, sends=[("near", send_second), ("far", cot_halves[0])]
    )
    m_second, q_second, n_second = act(second_norm, streams[1], keep_second, branch_second)

    def rise(hidden, weight, gate, pushes=()):
        return rows_matmul(
            [hidden], [weight], dot_nn, [jnp.float32, jnp.bfloat16], pick_tile(weight.shape[1]),
            finish=lambda up, gate: (up, gate * jax.nn.sigmoid(gate) * up), extras=[gate],
            pushes=pushes,
        )

    up_first, a_first, near_second, cot_late = act(
        rise, h2_first, up_full, gate_first, sends=[("near", n_second), ("far", cot_halves[1])]
    )
    h2_second = act(core_gather, n_second, near_second)
    c_first, c_second = act(
        lambda value, early, late: place_tokens(value, join(early, late)),
        out_cotangent, cot_early, cot_late,
    )
    gate_second, near_first = act(wide_dot, h2_second, gate_full, sends=[("near", c_first)])
    y_first = act(core_gather, c_first, near_first)
    up_second, a_second, near_second = act(
        rise, h2_second, up_full, gate_second, sends=[("near", c_second)]
    )
    y_second = act(core_gather, c_second, near_second)
    down_sum = plane_scatter(act(grad_sum, a_first, y_first, a_second, y_second))

    def fall_finish(act_grad, gate, up):
        sigmoid_gate = jax.nn.sigmoid(gate)
        return (
            act_grad * up * sigmoid_gate * (1.0 + gate * (1.0 - sigmoid_gate)),
            act_grad * (gate * sigmoid_gate),
        )

    def fall(cotangent, weight, gate, up):
        return rows_matmul(
            [cotangent], [weight], dot_nt, [jnp.bfloat16] * 2, pick_tile(weight.shape[0]),
            chunk=512, finish=fall_finish, extras=[gate, up],
        )

    dg_first, du_first = act(fall, y_first, down_full, gate_first, up_first)
    dg_second, du_second = act(fall, y_second, down_full, gate_second, up_second)
    gate_sum = plane_scatter(act(grad_sum, h2_first, dg_first, h2_second, dg_second))

    def hidden_grad(gate_grad, up_grad, gate_weight, up_weight, pushes=()):
        return rows_matmul(
            [gate_grad, up_grad], [gate_weight, up_weight], dot_nt, [jnp.bfloat16],
            pick_tile(gate_weight.shape[0]), pushes=pushes,
        )

    def second_back(middle, scale, keep, got, cotangent):
        grad, gain_term = norm_back(middle, scale, gain_two, keep + got.astype(jnp.float32))
        grad = cotangent.astype(jnp.float32) + grad
        return grad, grad.astype(jnp.bfloat16), gain_term

    term_first = act(hidden_grad, dg_first, du_first, gate_full, up_full)
    keep_first, send_first = act(core_reduce, term_first)
    term_second, back_first = act(
        hidden_grad, dg_second, du_second, gate_full, up_full, sends=[("near", send_first)]
    )
    keep_second, send_second = act(core_reduce, term_second)
    g_first, n_first, gain_two_first = act(
        second_back, m_first, q_first, keep_first, back_first, c_first
    )
    grad_up, back_second = act(
        grad_sum, h2_first, du_first, h2_second, du_second, sends=[("near", send_second)]
    )
    up_sum = plane_scatter(grad_up)
    mlp_first, near_first = act(dot_bf16, a_first, down_full, sends=[("near", n_first)])
    g_second, n_second, gain_two_second = act(
        second_back, m_second, q_second, keep_second, back_second, c_second
    )
    d_first = act(core_gather, n_first, near_first)

    mlp_second, near_second = act(dot_bf16, a_second, down_full, sends=[("near", n_second)])
    heads_first = act(heads_back, d_first, out_full)
    d_second = act(core_gather, n_second, near_second)
    heads_second = act(heads_back, d_second, out_full)
    mlp_keep_first, mlp_send_first = act(core_reduce, mlp_first)
    mlp_keep_second, mlp_send_second = act(core_reduce, mlp_second)
    down_mine, down_away = act(lambda pair: core_split(10, pair), down_sum)
    grad_out, mlp_branch_first = act(
        grad_sum, mixed_first, d_first, mixed_second, d_second, sends=[("near", mlp_send_first)]
    )
    out_sum = plane_scatter(grad_out)

    def attend_back(heads_first, heads_second, pushes=()):
        return attention_call(
            backward_both,
            [
                *saved[0], *saved[1], heads_first, heads_second, *lses,
                *tables[0], *tables[1], reach,
            ],
            [0] * 8 + ["lse"] * 2 + ["table"] * 4 + ["column"],
            ([0] * 6, heads_local),
            backward_scratch,
            pushes,
        )

    *grads, mlp_branch_second, down_got = act(
        attend_back, heads_first, heads_second,
        sends=[("near", mlp_send_second), ("far", down_away)],
    )
    p_first, p_second = act(
        lambda *parts: (
            jnp.concatenate(parts[:3], axis=1),
            jnp.concatenate(parts[3:], axis=1),
        ),
        *grads,
    )
    gate_mine, gate_away = act(lambda pair: core_split(9, pair), gate_sum)
    gate_halves = halve(gate_away)
    grad_qkv, gate_early = act(
        grad_sum, h1_first, p_first, h1_second, p_second, sends=[("far", gate_halves[0])]
    )
    qkv_sum = plane_scatter(grad_qkv)

    def finish_output(first, first_keep, first_got, second, second_keep, second_got):
        first = (first + first_keep + first_got.astype(jnp.float32)).astype(jnp.bfloat16)
        second = (second + second_keep + second_got.astype(jnp.float32)).astype(jnp.bfloat16)
        return jnp.where(far == 0, first, second), jnp.where(far == 0, second, first)

    term_first, gate_late = act(heads_back, p_first, qkv_full, sends=[("far", gate_halves[1])])
    keep_first, send_first = act(core_reduce, term_first)
    out_keep, out_send = act(
        finish_output,
        m_first, mlp_keep_first, mlp_branch_first, m_second, mlp_keep_second, mlp_branch_second,
    )
    out_halves = halve(out_send)
    term_second, back_first, out_early = act(
        heads_back, p_second, qkv_full, sends=[("near", send_first), ("far", out_halves[0])]
    )
    keep_second, send_second = act(core_reduce, term_second)

    def settle(keep, got):
        return jnp.stack([jnp.where(far == 0, keep, got), jnp.where(far == 0, got, keep)])

    def first_back(stream, scale, keep, got, grad):
        back, gain_term = norm_back(stream, scale, gain_one, keep + got.astype(jnp.float32))
        return grad + back, gain_term

    def last_back(stream, scale, keep, got, grad, first):
        second, gain_term = first_back(stream, scale, keep, got, grad)
        return (
            jnp.where(far == 0, first, second),
            jnp.where(far == 0, second, first).astype(jnp.bfloat16),
            gain_term,
        )

    back_second, out_late = swap(("near", send_second), ("far", out_halves[1]))
    i_first, gain_one_first = act(
        first_back, streams[0], scales_one[0], keep_first, back_first, g_first
    )
    in_keep, in_send, gain_one_second = act(
        last_back, streams[1], scales_one[1], keep_second, back_second, g_second, i_first
    )
    up_mine, up_away = act(lambda pair: core_split(9, pair), up_sum)
    up_got = swap_far(up_away)
    down_owned = act(add_wide, down_mine, down_got)
    gains = scatter_gains(
        jnp.stack([gain_one_first + gain_one_second, gain_two_first + gain_two_second])
    )
    block_out = act(lambda keep, early, late: settle(keep, join(early, late)), out_keep, out_early, out_late)
    gate_owned = act(lambda mine, early, late: add_wide(mine, join(early, late)), gate_mine, gate_early, gate_late)
    up_owned = act(add_wide, up_mine, up_got)
    in_got = swap_far(chained(in_send, up_got))
    gate_up_owned = act(lambda a, b: jnp.stack([a, b], axis=1), gate_owned, up_owned)
    in_grad = act(lambda keep, got: settle(keep, got.astype(jnp.float32)), in_keep, in_got)
    out_mine, out_away = act(lambda pair: core_split(8, pair), out_sum)
    out_back = swap_far(chained(out_away, in_got))
    out_owned = act(add_wide, out_mine, out_back)
    qkv_mine, qkv_away = act(lambda pair: core_split(0, pair), qkv_sum)
    qkv_owned = act(add_wide, qkv_mine, swap_far(qkv_away))
    return (
        block_out,
        in_grad,
        gains[0],
        qkv_owned.reshape(qkv_weight.shape),
        out_owned,
        gains[1],
        gate_up_owned,
        down_owned,
    )


def solution(mesh):
    sizes = (mesh.shape["fsdp"], mesh.shape["tp"])
    body = paired_device if sizes == (8, 4) else per_device
    in_specs = (
        P("fsdp", "tp", None),
        P("fsdp", "tp", None),
        P("fsdp", "tp"),
        P("fsdp", "tp"),
        P(),
        P("fsdp", None, "tp"),
        P(("tp", "fsdp"), None),
        P(),
        P("fsdp", None, "tp"),
        P(("tp", "fsdp"), None),
    )
    out_specs = (
        P("fsdp", "tp", None),
        P("fsdp", "tp", None),
        P(("fsdp", "tp")),
        P("fsdp", None, "tp"),
        P(("tp", "fsdp"), None),
        P(("fsdp", "tp")),
        P("fsdp", None, "tp"),
        P(("tp", "fsdp"), None),
    )
    return jax.shard_map(
        body, mesh=mesh, in_specs=in_specs, out_specs=out_specs, check_vma=False
    )
```

```python
import functools

import jax
import jax.numpy as jnp
from jax import lax
from jax.experimental import pallas as pl
from jax.experimental.pallas import tpu as pltpu
from jax.sharding import PartitionSpec as P

D = 3072
HD = 96


rms_epsilon = 1e-05
rope_theta = 10000.0
masked_score = -1e30
LOG2E = 1.4426950408889634


def rope_tables(positions, head_size):
    half_width = head_size // 2
    frequency = rope_theta ** (-(jnp.arange(half_width, dtype=jnp.float32) * 2.0 / head_size))
    angles = positions.astype(jnp.float32)[:, None] * frequency[None, :]
    return (jnp.cos(angles)[:, None, :], jnp.sin(angles)[:, None, :])


def rotate(values, cosine_part, sine_part):
    half_width = values.shape[-1] // 2
    lead_half = values[..., :half_width]
    tail_half = values[..., half_width:]
    return jnp.concatenate(
        [
            lead_half * cosine_part - tail_half * sine_part,
            tail_half * cosine_part + lead_half * sine_part,
        ],
        axis=-1,
    )


def unrotate(values, cosine_part, sine_part):
    half_width = values.shape[-1] // 2
    lead_half = values[..., :half_width]
    tail_half = values[..., half_width:]
    return jnp.concatenate(
        [
            lead_half * cosine_part + tail_half * sine_part,
            tail_half * cosine_part - lead_half * sine_part,
        ],
        axis=-1,
    )


def rms_scale(stream):
    return lax.rsqrt(jnp.mean(stream * stream, axis=-1, keepdims=True) + rms_epsilon)


def norm_back(stream, scale_rows, gain_vec, grad_rows):
    gained_grad = gain_vec * grad_rows
    input_grad = scale_rows * gained_grad - stream * scale_rows**3 * jnp.mean(
        gained_grad * stream, axis=-1, keepdims=True
    )
    return (input_grad, jnp.sum(grad_rows * stream * scale_rows, axis=0))


def allowed_mask(segment_tile, index_tile, segments):
    columns = jnp.arange(segments.shape[0], dtype=jnp.int32)
    return (segment_tile[:, None] == segments[None, :]) & (index_tile[:, None] >= columns[None, :])


def masked_scores(query_tile, key_rows, segment_tile, index_tile, segments, scale_value):
    scores = (
        jnp.einsum("qhd,khd->hqk", query_tile, key_rows, preferred_element_type=jnp.float32)
        * scale_value
    )
    return jnp.where(allowed_mask(segment_tile, index_tile, segments)[None], scores, masked_score)


def attention_forward(queries, key_rows, value_rows, segments, block_rows):
    seq_len, head_count, head_size = queries.shape
    tiles = seq_len // block_rows
    scale_value = head_size ** (-0.5)
    positions = jnp.arange(seq_len, dtype=jnp.int32)

    def query_block(packed):
        query_tile, segment_tile, index_tile = packed
        scores = masked_scores(
            query_tile, key_rows, segment_tile, index_tile, segments, scale_value
        )
        row_max = jnp.max(scores, axis=-1, keepdims=True)
        exponent = jnp.exp(scores - row_max)
        row_total = jnp.sum(exponent, axis=-1, keepdims=True)
        probs_low = (exponent / row_total).astype(jnp.bfloat16)
        mixed = jnp.einsum(
            "hqk,khd->qhd", probs_low, value_rows, preferred_element_type=jnp.float32
        )
        return (mixed, (row_max + jnp.log(row_total))[..., 0])

    mixed, log_total = lax.map(
        query_block,
        (
            queries.reshape(tiles, block_rows, head_count, head_size),
            segments.reshape(tiles, block_rows),
            positions.reshape(tiles, block_rows),
        ),
    )
    return (mixed.reshape(seq_len, head_count * head_size), log_total)


def attention_backward(queries, key_rows, value_rows, segments, log_total, out_grad, block_rows):
    seq_len, head_count, head_size = queries.shape
    tiles = seq_len // block_rows
    scale_value = head_size ** (-0.5)
    positions = jnp.arange(seq_len, dtype=jnp.int32)

    def query_block(carry, packed):
        key_acc, value_acc = carry
        query_tile, segment_tile, index_tile, total_tile, grad_tile = packed
        scores = masked_scores(
            query_tile, key_rows, segment_tile, index_tile, segments, scale_value
        )
        probs = jnp.exp(scores - total_tile[..., None])
        probs_low = probs.astype(jnp.bfloat16)
        prob_grad = jnp.einsum(
            "qhd,khd->hqk", grad_tile, value_rows, preferred_element_type=jnp.float32
        )
        score_grad = (
            probs * (prob_grad - jnp.sum(probs * prob_grad, axis=-1, keepdims=True))
        ).astype(jnp.bfloat16)
        query_grad = (
            jnp.einsum("hqk,khd->qhd", score_grad, key_rows, preferred_element_type=jnp.float32)
            * scale_value
        )
        key_acc = (
            key_acc
            + jnp.einsum("hqk,qhd->khd", score_grad, query_tile, preferred_element_type=jnp.float32)
            * scale_value
        )
        value_acc = value_acc + jnp.einsum(
            "hqk,qhd->khd", probs_low, grad_tile, preferred_element_type=jnp.float32
        )
        return ((key_acc, value_acc), query_grad)

    start_acc = (jnp.zeros(queries.shape, jnp.float32), jnp.zeros(queries.shape, jnp.float32))
    (key_grad, value_grad), query_grad = lax.scan(
        query_block,
        start_acc,
        (
            queries.reshape(tiles, block_rows, head_count, head_size),
            segments.reshape(tiles, block_rows),
            positions.reshape(tiles, block_rows),
            log_total,
            out_grad.reshape(tiles, block_rows, head_count, head_size),
        ),
    )
    return (query_grad.reshape(seq_len, head_count, head_size), key_grad, value_grad)


def gather_attention(qkv_weight, out_weight):
    return (
        lax.all_gather(qkv_weight, "fsdp", axis=0, tiled=True),
        lax.all_gather(out_weight, "fsdp", axis=0, tiled=True),
    )


def gather_feedforward(gate_up_weight, down_weight):
    return (
        lax.all_gather(gate_up_weight, "fsdp", axis=0, tiled=True),
        lax.all_gather(down_weight, "fsdp", axis=0, tiled=True),
    )


def per_device(
    block_in,
    out_cotangent,
    segment_ids,
    doc_positions,
    norm1_gain,
    qkv_weight,
    out_weight,
    norm2_gain,
    gate_up_weight,
    down_weight,
):
    micro_count = block_in.shape[0]
    fsdp_count = lax.axis_size("fsdp")
    segment_full, position_full = (
        lax.all_gather(segment_ids, "tp", axis=1, tiled=True),
        lax.all_gather(doc_positions, "tp", axis=1, tiled=True),
    )
    seq_len = segment_full.shape[1]
    block_rows = min(seq_len, 512)
    gain_one = norm1_gain.astype(jnp.float32)
    gain_two = norm2_gain.astype(jnp.float32)
    local_cols = qkv_weight.shape[2]
    local_units = gate_up_weight.shape[2]
    heads_local = local_cols // HD
    grad_qkv = jnp.zeros((D, 3, local_cols), jnp.float32)
    grad_out = jnp.zeros((out_weight.shape[0] * fsdp_count, D), jnp.float32)
    grad_gate_up = jnp.zeros((D, 2, local_units), jnp.float32)
    grad_down = jnp.zeros((down_weight.shape[0] * fsdp_count, D), jnp.float32)
    gain_one_acc = jnp.zeros((D,), jnp.float32)
    gain_two_acc = jnp.zeros((D,), jnp.float32)
    outputs = []
    input_grads = []
    for micro_index in range(micro_count):
        weights_fwd = (
            gather_attention(qkv_weight, out_weight),
            gather_feedforward(gate_up_weight, down_weight),
        )
        (qkv_full, out_full), (gate_up_full, down_full) = weights_fwd
        stream = block_in[micro_index].astype(jnp.float32)
        segment_row = segment_full[micro_index]
        cosine_part, sine_part = rope_tables(position_full[micro_index], HD)
        scale_one = rms_scale(stream)
        normed_one = (stream * scale_one * gain_one).astype(jnp.bfloat16)
        normed_one_full = lax.all_gather(normed_one, "tp", axis=0, tiled=True)
        projected = jnp.einsum(
            "sd,dtc->stc", normed_one_full, qkv_full, preferred_element_type=jnp.float32
        )
        queries = rotate(
            projected[:, 0].reshape(seq_len, heads_local, HD), cosine_part, sine_part
        ).astype(jnp.bfloat16)
        key_rows = rotate(
            projected[:, 1].reshape(seq_len, heads_local, HD), cosine_part, sine_part
        ).astype(jnp.bfloat16)
        value_rows = projected[:, 2].reshape(seq_len, heads_local, HD).astype(jnp.bfloat16)
        mixed, log_total = attention_forward(queries, key_rows, value_rows, segment_row, block_rows)
        attn_heads = mixed.astype(jnp.bfloat16)
        attn_term = jnp.dot(attn_heads, out_full, preferred_element_type=jnp.float32)
        attn_branch = lax.psum_scatter(attn_term, "tp", scatter_dimension=0, tiled=True)
        middle = stream + attn_branch
        scale_two = rms_scale(middle)
        normed_two = (middle * scale_two * gain_two).astype(jnp.bfloat16)
        normed_two_full = lax.all_gather(normed_two, "tp", axis=0, tiled=True)
        gate_up = jnp.einsum(
            "sd,dtf->stf", normed_two_full, gate_up_full, preferred_element_type=jnp.float32
        )
        gate_rows = gate_up[:, 0]
        up_rows = gate_up[:, 1]
        sigmoid_gate = jax.nn.sigmoid(gate_rows)
        silu_gate = gate_rows * sigmoid_gate
        activated = (silu_gate * up_rows).astype(jnp.bfloat16)
        mlp_term = jnp.dot(activated, down_full, preferred_element_type=jnp.float32)
        mlp_branch = lax.psum_scatter(
            mlp_term.astype(jnp.bfloat16), "tp", scatter_dimension=0, tiled=True
        ).astype(jnp.float32)
        outputs.append((middle + mlp_branch).astype(jnp.bfloat16))
        (qkv_back, out_back), (gate_up_back, down_back) = weights_fwd
        cotangent = out_cotangent[micro_index].astype(jnp.float32)
        cotangent_full = lax.all_gather(out_cotangent[micro_index], "tp", axis=0, tiled=True)
        grad_down = grad_down + jnp.einsum(
            "sf,sd->fd", activated, cotangent_full, preferred_element_type=jnp.float32
        )
        act_grad = jnp.einsum(
            "sd,fd->sf", cotangent_full, down_back, preferred_element_type=jnp.float32
        )
        gate_grad = act_grad * up_rows * sigmoid_gate * (1.0 + gate_rows * (1.0 - sigmoid_gate))
        up_grad = act_grad * silu_gate
        gate_up_grad = jnp.stack([gate_grad, up_grad], axis=1).astype(jnp.bfloat16)
        grad_gate_up = grad_gate_up + jnp.einsum(
            "sd,stf->dtf", normed_two_full, gate_up_grad, preferred_element_type=jnp.float32
        )
        normed_two_term = jnp.einsum(
            "stf,dtf->sd", gate_up_grad, gate_up_back, preferred_element_type=jnp.float32
        )
        normed_two_grad = lax.psum_scatter(normed_two_term, "tp", scatter_dimension=0, tiled=True)
        middle_back, gain_two_term = norm_back(middle, scale_two, gain_two, normed_two_grad)
        gain_two_acc = gain_two_acc + gain_two_term
        middle_grad = cotangent + middle_back
        attn_grad_full = lax.all_gather(middle_grad.astype(jnp.bfloat16), "tp", axis=0, tiled=True)
        grad_out = grad_out + jnp.einsum(
            "sc,sd->cd", attn_heads, attn_grad_full, preferred_element_type=jnp.float32
        )
        heads_grad = jnp.einsum(
            "sd,cd->sc", attn_grad_full, out_back, preferred_element_type=jnp.float32
        ).astype(jnp.bfloat16)
        query_grad, key_grad, value_grad = attention_backward(
            queries,
            key_rows,
            value_rows,
            segment_row,
            log_total,
            heads_grad.reshape(seq_len, heads_local, HD),
            block_rows,
        )
        projected_grad = jnp.stack(
            [
                unrotate(query_grad, cosine_part, sine_part).reshape(seq_len, local_cols),
                unrotate(key_grad, cosine_part, sine_part).reshape(seq_len, local_cols),
                value_grad.reshape(seq_len, local_cols),
            ],
            axis=1,
        ).astype(jnp.bfloat16)
        grad_qkv = grad_qkv + jnp.einsum(
            "sd,stc->dtc", normed_one_full, projected_grad, preferred_element_type=jnp.float32
        )
        normed_one_term = jnp.einsum(
            "stc,dtc->sd", projected_grad, qkv_back, preferred_element_type=jnp.float32
        )
        normed_one_grad = lax.psum_scatter(
            normed_one_term.astype(jnp.bfloat16), "tp", scatter_dimension=0, tiled=True
        ).astype(jnp.float32)
        stream_back, gain_one_term = norm_back(stream, scale_one, gain_one, normed_one_grad)
        gain_one_acc = gain_one_acc + gain_one_term
        input_grads.append(middle_grad + stream_back)
    owned_grads = (
        lax.psum_scatter(
            grad_qkv.astype(jnp.bfloat16), "fsdp", scatter_dimension=0, tiled=True
        ).astype(jnp.float32),
        lax.psum_scatter(
            grad_out.astype(jnp.bfloat16), "fsdp", scatter_dimension=0, tiled=True
        ).astype(jnp.float32),
        lax.psum_scatter(
            grad_gate_up.astype(jnp.bfloat16), "fsdp", scatter_dimension=0, tiled=True
        ).astype(jnp.float32),
        lax.psum_scatter(
            grad_down.astype(jnp.bfloat16), "fsdp", scatter_dimension=0, tiled=True
        ).astype(jnp.float32),
    )
    owned_gains = (
        lax.psum_scatter(gain_one_acc, ("fsdp", "tp"), scatter_dimension=0, tiled=True),
        lax.psum_scatter(gain_two_acc, ("fsdp", "tp"), scatter_dimension=0, tiled=True),
    )
    return (
        jnp.stack(outputs),
        jnp.stack(input_grads),
        owned_gains[0],
        owned_grads[0],
        owned_grads[1],
        owned_gains[1],
        owned_grads[2],
        owned_grads[3],
    )


HEAD_GROUP = 4
FIRST_DOC = 800


def dot_nt(left, right):
    return lax.dot_general(left, right, (((1,), (1,)), ((), ())), preferred_element_type=jnp.float32)


def dot_tn(left, right):
    return lax.dot_general(left, right, (((0,), (0,)), ((), ())), preferred_element_type=jnp.float32)


def dot_nn(left, right):
    return lax.dot_general(left, right, (((1,), (0,)), ((), ())), preferred_element_type=jnp.float32)


def swap_halves(values):
    lanes = lax.broadcasted_iota(jnp.int32, values.shape, 1)
    width = values.shape[1]
    return jnp.where(
        lanes % HD < HD // 2,
        pltpu.roll(values, width - HD // 2, 1),
        pltpu.roll(values, HD // 2, 1),
    )


def causal_mask(rows, columns):
    row_ids = lax.broadcasted_iota(jnp.int32, (rows, columns), 0)
    column_ids = lax.broadcasted_iota(jnp.int32, (rows, columns), 1)
    return row_ids >= column_ids


def tail_mask(reach):
    rows = reach.shape[0]
    row_ids = lax.broadcasted_iota(jnp.int32, (rows, rows), 0)
    column_ids = lax.broadcasted_iota(jnp.int32, (rows, rows), 1)
    return (row_ids >= column_ids) & (row_ids - column_ids <= reach)


def halves(quarter):
    first = lax.axis_index("tp") % 2
    return (
        pl.multiple_of(first * quarter, quarter),
        pl.multiple_of((1 - first) * quarter, quarter),
    )


def widen(table):
    return jnp.concatenate([table] * HEAD_GROUP, axis=1)


def load_rotated(offsets, quarter, q_ref, k_ref, v_ref, cos_ref, sin_ref, qr_ref, kr_ref, vr_ref):
    for place, offset in enumerate(offsets):
        rows = pl.ds(offset, quarter)
        target = pl.ds(place * quarter, quarter)
        cosine, sine = widen(cos_ref[rows, :]), widen(sin_ref[rows, :])
        q_raw, k_raw = q_ref[rows, :], k_ref[rows, :]
        qr_ref[target, :] = (q_raw * cosine + swap_halves(q_raw) * sine).astype(jnp.bfloat16)
        kr_ref[target, :] = (k_raw * cosine + swap_halves(k_raw) * sine).astype(jnp.bfloat16)
        vr_ref[target, :] = v_ref[rows, :].astype(jnp.bfloat16)


def softmax_mix(query, pieces, factor):
    scores = []
    for keys, _, mask in pieces:
        score = dot_nt(query, keys)
        scores.append(score if mask is None else jnp.where(mask, score, masked_score))
    top = functools.reduce(jnp.maximum, [jnp.max(s, axis=-1, keepdims=True) for s in scores])
    weights = [jnp.exp2((s - top) * factor) for s in scores]
    total = functools.reduce(jnp.add, [jnp.sum(w, axis=-1, keepdims=True) for w in weights])
    inverse = 1.0 / total
    mixed = functools.reduce(
        jnp.add,
        [dot_nn((w * inverse).astype(jnp.bfloat16), piece[1]) for w, piece in zip(weights, pieces)],
    )
    return mixed, top * factor + jnp.log2(total)


def head_slice(head):
    return slice(head * HD, (head + 1) * HD)


def forward_first(
    q_ref, k_ref, v_ref, cos_ref, sin_ref, qr_ref, kr_ref, vr_ref, o_ref, lse_ref
):
    half = q_ref.shape[0]
    quarter = half // 2
    offsets = halves(quarter)
    load_rotated(offsets, quarter, q_ref, k_ref, v_ref, cos_ref, sin_ref, qr_ref, kr_ref, vr_ref)
    factor = HD ** (-0.5) * LOG2E
    mask = causal_mask(quarter, quarter)
    for head in range(HEAD_GROUP):
        cols = head_slice(head)
        early, late = slice(0, quarter), slice(quarter, half)
        k_early, v_early = kr_ref[early, cols], vr_ref[early, cols]
        mixed, lse = softmax_mix(qr_ref[early, cols], [(k_early, v_early, mask)], factor)
        o_ref[pl.ds(offsets[0], quarter), cols] = mixed.astype(jnp.bfloat16)
        lse_ref[0, early, head : head + 1] = lse
        mixed, lse = softmax_mix(
            qr_ref[late, cols],
            [(k_early, v_early, None), (kr_ref[late, cols], vr_ref[late, cols], mask)],
            factor,
        )
        o_ref[pl.ds(offsets[1], quarter), cols] = mixed.astype(jnp.bfloat16)
        lse_ref[0, late, head : head + 1] = lse


def forward_second(
    q_ref, k_ref, v_ref, cos_ref, sin_ref, ka_ref, va_ref, pos_ref,
    qr_ref, kr_ref, vr_ref, o_ref, lse_ref,
):
    half = q_ref.shape[0]
    quarter = half // 2
    cut = FIRST_DOC - half
    spill = cut - quarter
    offsets = halves(quarter)
    load_rotated(offsets, quarter, q_ref, k_ref, v_ref, cos_ref, sin_ref, qr_ref, kr_ref, vr_ref)
    factor = HD ** (-0.5) * LOG2E
    mask = causal_mask(cut, cut)
    mask_tail = tail_mask(pos_ref[pl.ds(offsets[1] + spill, half - cut), :])
    for head in range(HEAD_GROUP):
        cols = head_slice(head)
        early, late = slice(0, cut), slice(cut, half)
        mixed, lse = softmax_mix(
            qr_ref[early, cols],
            [
                (ka_ref[:, cols], va_ref[:, cols], None),
                (kr_ref[early, cols], vr_ref[early, cols], mask),
            ],
            factor,
        )
        low = mixed.astype(jnp.bfloat16)
        o_ref[pl.ds(offsets[0], quarter), cols] = low[:quarter]
        o_ref[pl.ds(offsets[1], spill), cols] = low[quarter:]
        lse_ref[0, early, head : head + 1] = lse
        mixed, lse = softmax_mix(
            qr_ref[late, cols], [(kr_ref[late, cols], vr_ref[late, cols], mask_tail)], factor
        )
        o_ref[pl.ds(offsets[1] + spill, half - cut), cols] = mixed.astype(jnp.bfloat16)
        lse_ref[0, late, head : head + 1] = lse


def backward_both(
    qa_ref, ka_ref, va_ref, qb_ref, kb_ref, vb_ref, ga_ref, gb_ref, la_ref, lb_ref,
    cosa_ref, sina_ref, cosb_ref, sinb_ref, pos_ref,
    dqa_ref, dka_ref, dva_ref, dqb_ref, dkb_ref, dvb_ref,
    go_a, go_b, tqa, tka, tva, tqb, tkb, tvb,
):
    half = qa_ref.shape[0]
    quarter = half // 2
    cut = FIRST_DOC - half
    spill = cut - quarter
    offsets = halves(quarter)
    scale_value = HD ** (-0.5)
    factor = scale_value * LOG2E
    for place, offset in enumerate(offsets):
        target, rows = pl.ds(place * quarter, quarter), pl.ds(offset, quarter)
        go_a[target, :] = ga_ref[rows, :]
        go_b[target, :] = gb_ref[rows, :]
    mask = causal_mask(quarter, quarter)
    mask_cut = causal_mask(cut, cut)
    mask_tail = tail_mask(pos_ref[pl.ds(offsets[1] + spill, half - cut), :])
    for accumulator in (tka, tva, tkb, tvb):
        accumulator[...] = jnp.zeros_like(accumulator)

    def attend(query, grad, lse, pieces):
        weights, weight_grads = [], []
        for k_ref, v_ref, rows, cols, mask, _, _ in pieces:
            weight = jnp.exp2(dot_nt(query, k_ref[rows, cols]) * factor - lse)
            weights.append(weight if mask is None else jnp.where(mask, weight, 0.0))
            weight_grads.append(dot_nt(grad, v_ref[rows, cols]))
        shared = functools.reduce(
            jnp.add,
            [jnp.sum(w * g, axis=-1, keepdims=True) for w, g in zip(weights, weight_grads)],
        )
        query_grad = None
        for weight, weight_grad, piece in zip(weights, weight_grads, pieces):
            k_ref, v_ref, rows, cols, _, tk, tv = piece
            score_grad = (weight * (weight_grad - shared)).astype(jnp.bfloat16)
            term = dot_nn(score_grad, k_ref[rows, cols])
            query_grad = term if query_grad is None else query_grad + term
            tk[rows, cols] += dot_tn(score_grad, query)
            tv[rows, cols] += dot_tn(weight.astype(jnp.bfloat16), grad)
        return query_grad

    for head in range(HEAD_GROUP):
        cols = head_slice(head)
        lane = slice(head, head + 1)
        early, late, whole = slice(0, quarter), slice(quarter, half), slice(0, half)
        tqa[early, cols] = attend(
            qa_ref[early, cols], go_a[early, cols], la_ref[0, early, lane],
            [(ka_ref, va_ref, early, cols, mask, tka, tva)],
        )
        tqa[late, cols] = attend(
            qa_ref[late, cols], go_a[late, cols], la_ref[0, late, lane],
            [
                (ka_ref, va_ref, early, cols, None, tka, tva),
                (ka_ref, va_ref, late, cols, mask, tka, tva),
            ],
        )
        early, late = slice(0, cut), slice(cut, half)
        tqb[early, cols] = attend(
            qb_ref[early, cols], go_b[early, cols], lb_ref[0, early, lane],
            [
                (ka_ref, va_ref, whole, cols, None, tka, tva),
                (kb_ref, vb_ref, early, cols, mask_cut, tkb, tvb),
            ],
        )
        tqb[late, cols] = attend(
            qb_ref[late, cols], go_b[late, cols], lb_ref[0, late, lane],
            [(kb_ref, vb_ref, late, cols, mask_tail, tkb, tvb)],
        )
    for place, offset in enumerate(offsets):
        source, rows = pl.ds(place * quarter, quarter), pl.ds(offset, quarter)
        for total, cos_ref, sin_ref, out_ref in (
            (tqa, cosa_ref, sina_ref, dqa_ref),
            (tka, cosa_ref, sina_ref, dka_ref),
            (tqb, cosb_ref, sinb_ref, dqb_ref),
            (tkb, cosb_ref, sinb_ref, dkb_ref),
        ):
            grad = total[source, :] * scale_value
            out_ref[rows, :] = (
                grad * widen(cos_ref[rows, :]) - swap_halves(grad) * widen(sin_ref[rows, :])
            ).astype(jnp.bfloat16)
        dva_ref[rows, :] = tva[source, :].astype(jnp.bfloat16)
        dvb_ref[rows, :] = tvb[source, :].astype(jnp.bfloat16)


COST_SCALE = 1.7


def cost_of(flops):
    return pl.CostEstimate(flops=int(COST_SCALE * flops), bytes_accessed=1000, transcendentals=0)


def rows_kernel(pairs, extra_count, dot, chunk, finish, *refs):
    lefts, weights = refs[:pairs], refs[pairs : 2 * pairs]
    extras = refs[2 * pairs : 2 * pairs + extra_count]
    outs = refs[2 * pairs + extra_count :]

    @pl.loop(0, outs[0].shape[0] // chunk)
    def _(step):
        rows = pl.ds(pl.multiple_of(step * chunk, chunk), chunk)
        total = None
        for left, weight in zip(lefts, weights):
            term = dot(left[rows, :], weight[...])
            total = term if total is None else total + term
        for out, value in zip(outs, finish(total, *[extra[rows, :] for extra in extras])):
            out[rows, :] = value.astype(out.dtype)


def keep_one(total):
    return (total,)


def rows_matmul(
    lefts, weights, dot, types, tile, chunk=1024, finish=keep_one, extras=(), pushes=()
):
    rows = lefts[0].shape[0]
    if dot is dot_nn:
        width = weights[0].shape[1]
        weight_specs = [pl.BlockSpec((w.shape[0], tile), lambda j: (0, j)) for w in weights]
    else:
        width = weights[0].shape[0]
        weight_specs = [pl.BlockSpec((tile, w.shape[1]), lambda j: (j, 0)) for w in weights]
    column = pl.BlockSpec((rows, tile), lambda j: (0, j))
    return grid_call(
        functools.partial(rows_kernel, len(lefts), len(extras), dot, min(chunk, rows), finish),
        [*lefts, *weights, *extras],
        [pl.BlockSpec(left.shape, lambda j: (0, 0)) for left in lefts]
        + weight_specs
        + [column] * len(extras),
        [jax.ShapeDtypeStruct((rows, width), kind) for kind in types],
        [column] * len(types),
        (width // tile,),
        2 * rows * width * sum(left.shape[1] for left in lefts),
        pushes=pushes,
    )


def sum_kernel(parts, chunk, *refs):
    lefts, rights, out = refs[:parts], refs[parts : 2 * parts], refs[-1]

    @pl.loop(0, out.shape[1] // chunk)
    def _(step):
        cols = pl.ds(pl.multiple_of(step * chunk, chunk), chunk)
        total = None
        for left, right in zip(lefts, rights):
            term = dot_tn(left[...], right[:, cols])
            total = term if total is None else total + term
        out[:, cols] = total.astype(out.dtype)


def sum_matmul(lefts, rights, tile, chunk, pushes=()):
    rows, height = lefts[0].shape
    width = rights[0].shape[1]
    return grid_call(
        functools.partial(sum_kernel, len(lefts), chunk),
        [*lefts, *rights],
        [pl.BlockSpec((rows, tile), lambda j: (0, j)) for _ in lefts]
        + [pl.BlockSpec((rows, width), lambda j: (0, 0)) for _ in rights],
        [jax.ShapeDtypeStruct((height, width), jnp.bfloat16)],
        [pl.BlockSpec((tile, width), lambda j: (j, 0))],
        (height // tile,),
        2 * rows * height * width * len(lefts),
        pushes=pushes,
    )


def partner_of(kind):
    index, place = lax.axis_index("fsdp"), lax.axis_index("tp")
    if kind == "near":
        return (index, place + 1 - 2 * (place % 2))
    return (index, place + 2 - 4 * (place // 2))


def start_pushes(kinds, sources, targets, send, receive):
    barrier = pltpu.get_barrier_semaphore()
    names = sorted(set(kinds))
    for kind in names:
        pl.semaphore_signal(
            barrier, inc=1, device_id=partner_of(kind), device_id_type=pl.DeviceIdType.MESH
        )
    pl.semaphore_wait(barrier, len(names))
    for place, kind in enumerate(kinds):
        push(
            sources[place], targets[place], send.at[place], receive.at[place], partner_of(kind)
        ).start()


def wait_pushes(kinds, sources, targets, send, receive):
    for place, kind in enumerate(kinds):
        push(
            sources[place], targets[place], send.at[place], receive.at[place], partner_of(kind)
        ).wait()


def pushing_kernel(kernel, axes, in_count, out_count, kinds, *refs):
    count = len(kinds)
    inputs, sources = refs[:in_count], refs[in_count : in_count + count]
    outs = refs[in_count + count : in_count + count + out_count]
    targets = refs[in_count + count + out_count : in_count + 2 * count + out_count]
    scratch, (send, receive) = refs[in_count + 2 * count + out_count : -2], refs[-2:]
    first = functools.reduce(jnp.logical_and, [pl.program_id(axis) == 0 for axis in range(axes)])
    last = functools.reduce(
        jnp.logical_and,
        [pl.program_id(axis) == pl.num_programs(axis) - 1 for axis in range(axes)],
    )

    @pl.when(first)
    def _():
        start_pushes(kinds, sources, targets, send, receive)

    kernel(*inputs, *outs, *scratch)

    @pl.when(last)
    def _():
        wait_pushes(kinds, sources, targets, send, receive)


def grid_call(
    kernel, operands, in_specs, outs, out_specs, grid, flops, scratch=(), pushes=(), vmem=48
):
    params = dict(
        dimension_semantics=("arbitrary",) * len(grid), vmem_limit_bytes=vmem * 1024 * 1024
    )
    operands, in_specs, outs = list(operands), list(in_specs), list(outs)
    out_specs, scratch = list(out_specs), list(scratch)
    if pushes:
        kinds = tuple(kind for kind, _ in pushes)
        kernel = functools.partial(
            pushing_kernel, kernel, len(grid), len(operands), len(outs), kinds
        )
        anywhere = [pl.BlockSpec(memory_space=pl.ANY)] * len(pushes)
        operands += [value for _, value in pushes]
        in_specs += anywhere
        outs += [jax.ShapeDtypeStruct(value.shape, value.dtype) for _, value in pushes]
        out_specs += anywhere
        scratch += [pltpu.SemaphoreType.DMA((len(pushes),))] * 2
        next_key[0] += 1
        params.update(collective_id=next_key[0], has_side_effects=True)
    return tuple(
        pl.pallas_call(
            kernel,
            out_shape=outs,
            grid=grid,
            in_specs=in_specs,
            out_specs=out_specs,
            scratch_shapes=scratch,
            compiler_params=pltpu.CompilerParams(**params),
            cost_estimate=cost_of(flops),
        )(*operands)
    )


def swap_kernel(kinds, *refs):
    count = len(kinds)
    sources, targets, (send, receive) = refs[:count], refs[count : 2 * count], refs[2 * count :]
    start_pushes(kinds, sources, targets, send, receive)
    wait_pushes(kinds, sources, targets, send, receive)


def swap_call(*pushes):
    next_key[0] += 1
    kinds = tuple(kind for kind, _ in pushes)
    values = [value for _, value in pushes]
    return exchange_call(
        functools.partial(swap_kernel, kinds), next_key[0], values,
        [jax.ShapeDtypeStruct(value.shape, value.dtype) for value in values],
        [pltpu.SemaphoreType.DMA((len(pushes),))] * 2,
    )


next_key = [11]


def sibling_id():
    index = lax.axis_index("fsdp")
    return (index + 1 - 2 * (index % 2), lax.axis_index("tp"))


def meet(partner):
    barrier = pltpu.get_barrier_semaphore()
    pl.semaphore_signal(barrier, inc=1, device_id=partner, device_id_type=pl.DeviceIdType.MESH)
    pl.semaphore_wait(barrier, 1)


def push(source, target, send, receive, partner):
    return pltpu.make_async_remote_copy(
        src_ref=source,
        dst_ref=target,
        send_sem=send,
        recv_sem=receive,
        device_id=partner,
        device_id_type=pl.DeviceIdType.MESH,
    )


def exchange_call(kernel, key, operands, outs, scratch, vmem=16):
    anywhere = pl.BlockSpec(memory_space=pl.ANY)
    results = pl.pallas_call(
        kernel,
        out_shape=outs,
        in_specs=[anywhere] * len(operands),
        out_specs=[anywhere] * len(outs),
        scratch_shapes=scratch,
        compiler_params=pltpu.CompilerParams(
            collective_id=key, has_side_effects=True, vmem_limit_bytes=vmem * 1024 * 1024
        ),
        cost_estimate=cost_of(4 * 10**9),
    )(*operands)
    return tuple(results) if len(outs) > 1 else results[0]


def gather_kernel(own_ref, near_ref, full_ref, local, send, receive):
    partner = sibling_id()
    meet(partner)
    count = own_ref.shape[0]
    copies = []
    for place, ref in enumerate((own_ref, near_ref)):
        remote = push(
            ref, full_ref.at[pl.ds((2 + place) * count, count)],
            send.at[place], receive.at[place], partner,
        )
        remote.start()
        copies.append(remote)
    for place, ref in enumerate((own_ref, near_ref)):
        copy = pltpu.make_async_copy(
            ref, full_ref.at[pl.ds(place * count, count)], local.at[place]
        )
        copy.start()
        copies.append(copy)
    for copy in copies:
        copy.wait()


def core_gather(own, near):
    shape = (4 * own.shape[0], own.shape[1])
    return exchange_call(
        gather_kernel, 1, [own, near], [jax.ShapeDtypeStruct(shape, own.dtype)],
        [pltpu.SemaphoreType.DMA((2,))] * 3,
    )


def gather_two_kernel(
    own_ref, own_near_ref, got_ref, got_near_ref, first_ref, second_ref, local, send, receive
):
    partner = sibling_id()
    far = lax.axis_index("tp") // 2
    meet(partner)
    count = own_ref.shape[0]

    def run(targets):
        copies = []
        for place, ref in enumerate((own_ref, own_near_ref, got_ref, got_near_ref)):
            target, row = targets[place // 2], place % 2
            remote = push(
                ref, target.at[pl.ds((2 + row) * count, count)],
                send.at[place], receive.at[place], partner,
            )
            remote.start()
            copy = pltpu.make_async_copy(
                ref, target.at[pl.ds(row * count, count)], local.at[place]
            )
            copy.start()
            copies += [remote, copy]
        for copy in copies:
            copy.wait()

    @pl.when(far == 0)
    def _():
        run((first_ref, second_ref))

    @pl.when(far != 0)
    def _():
        run((second_ref, first_ref))


def core_gather_two(own, own_near, got, got_near):
    shape = (4 * own.shape[0], own.shape[1])
    return exchange_call(
        gather_two_kernel, 11, [own, own_near, got, got_near],
        [jax.ShapeDtypeStruct(shape, own.dtype)] * 2,
        [pltpu.SemaphoreType.DMA((4,))] * 3,
    )


def reduce_kernel(term_ref, keep_ref, away_ref, mine, got, keep, away, local, send, receive, store):
    partner = sibling_id()
    meet(partner)
    pieces, count = mine.shape[0], mine.shape[1]
    half = pieces * count
    remotes, loads = [], []
    for piece in range(pieces):
        order = (piece + pieces // 2) % pieces
        remote = push(
            term_ref.at[pl.ds(half + order * count, count)], got.at[order],
            send.at[order], receive.at[order], partner,
        )
        remote.start()
        remotes.append(remote)
        load = pltpu.make_async_copy(
            term_ref.at[pl.ds(order * count, count)], mine.at[order], local.at[order]
        )
        load.start()
        loads.append(load)
    stores = []
    for piece in range(pieces):
        order = (piece + pieces // 2) % pieces
        loads[piece].wait()
        remotes[piece].wait()
        total = mine[order].astype(jnp.float32) + got[order].astype(jnp.float32)
        if order < pieces // 2:
            keep[order] = total
            copy = pltpu.make_async_copy(
                keep.at[order], keep_ref.at[pl.ds(order * count, count)], store.at[order]
            )
        else:
            slot = order - pieces // 2
            away[slot] = total.astype(away.dtype)
            copy = pltpu.make_async_copy(
                away.at[slot], away_ref.at[pl.ds(slot * count, count)], store.at[order]
            )
        copy.start()
        stores.append(copy)
    for copy in stores:
        copy.wait()


def core_reduce(term):
    rows, width = term.shape
    quarter = rows // 4
    pieces = 4
    count = 2 * quarter // pieces
    return exchange_call(
        reduce_kernel, 2, [term],
        [
            jax.ShapeDtypeStruct((quarter, width), jnp.float32),
            jax.ShapeDtypeStruct((quarter, width), term.dtype),
        ],
        [
            pltpu.VMEM((pieces, count, width), term.dtype),
            pltpu.VMEM((pieces, count, width), term.dtype),
            pltpu.VMEM((pieces // 2, count, width), jnp.float32),
            pltpu.VMEM((pieces // 2, count, width), term.dtype),
        ]
        + [pltpu.SemaphoreType.DMA((pieces,))] * 4,
        vmem=24,
    )


def pair_kernel(own_ref, *refs):
    others, (pair_ref, local, send, receive) = refs[:-4], refs[-4:]
    partner = sibling_id()
    core = lax.axis_index("fsdp") % 2
    far = lax.axis_index("tp") // 2
    meet(partner)
    base = pl.multiple_of(core * own_ref.shape[0], own_ref.shape[0])
    count = others[0].shape[0]
    owns = [own_ref.at[pl.ds(place * count, count)] for place in range(len(others))]

    def run(mine, theirs):
        copies = []
        for place in range(len(others)):
            target = pair_ref.at[pl.ds(base + place * count, count)]
            remote = push(
                theirs[place], target, send.at[place], receive.at[place], partner
            )
            remote.start()
            copy = pltpu.make_async_copy(mine[place], target, local.at[place])
            copy.start()
            copies += [remote, copy]
        for copy in copies:
            copy.wait()

    @pl.when(core == far)
    def _():
        run(owns, others)

    @pl.when(core != far)
    def _():
        run(others, owns)


def core_pair(key, own, *others):
    shape = (2 * own.shape[0], own.shape[1])
    return exchange_call(
        pair_kernel, key, [own, *others], [jax.ShapeDtypeStruct(shape, own.dtype)],
        [pltpu.SemaphoreType.DMA((len(others),))] * 3,
    )


def split_kernel(pair_ref, keep_ref, away_ref, local, send, receive):
    partner = sibling_id()
    core = lax.axis_index("fsdp") % 2
    far = lax.axis_index("tp") // 2
    meet(partner)
    count = keep_ref.shape[0]
    mine = pair_ref.at[pl.ds(pl.multiple_of(core * count, count), count)]
    theirs = pair_ref.at[pl.ds(pl.multiple_of((1 - core) * count, count), count)]

    def run(own_target, other_target):
        remote = push(theirs, other_target, send.at[0], receive.at[0], partner)
        remote.start()
        copy = pltpu.make_async_copy(mine, own_target, local.at[0])
        copy.start()
        copy.wait()
        remote.wait()

    @pl.when(core == far)
    def _():
        run(keep_ref, keep_ref)

    @pl.when(core != far)
    def _():
        run(away_ref, away_ref)


def core_split(key, pair):
    shape = (pair.shape[0] // 2, pair.shape[1])
    return exchange_call(
        split_kernel, key, [pair], [jax.ShapeDtypeStruct(shape, pair.dtype)] * 2,
        [pltpu.SemaphoreType.DMA((1,))] * 3,
    )


def attention_call(kernel, arrays, kinds, outs, scratch, pushes=()):
    rows, heads_local = arrays[-1].shape[0], outs[1]
    half = rows // 2
    groups = heads_local // HEAD_GROUP
    width = HEAD_GROUP * HD

    def spec(kind):
        if kind == "table":
            return pl.BlockSpec((half, HD), lambda s, g: (s, 0))
        if kind == "column":
            return pl.BlockSpec((half, 1), lambda s, g: (s, 0))
        if kind == "lse":
            return pl.BlockSpec((1, half, HEAD_GROUP), lambda s, g: (g, s, 0))
        shift = kind * groups
        return pl.BlockSpec((half, width), lambda s, g: (s, shift + g))

    def shape(kind):
        if kind == "lse":
            return jax.ShapeDtypeStruct((groups, rows, HEAD_GROUP), jnp.float32)
        return jax.ShapeDtypeStruct((rows, heads_local * HD), jnp.bfloat16)

    return grid_call(
        kernel,
        arrays,
        [spec(kind) for kind in kinds],
        [shape(kind) for kind in outs[0]],
        [spec(kind) for kind in outs[0]],
        (rows // half, groups),
        4 * len(outs[0]) ** 2 * rows * rows * heads_local * HD // 16,
        scratch=scratch(half, width),
        pushes=pushes,
        vmem=40,
    )


def backward_scratch(half, width):
    return [pltpu.VMEM((half, width), jnp.bfloat16)] * 2 + [
        pltpu.VMEM((half, width), jnp.float32)
    ] * 6


def no_scratch(half, width):
    return []


def head_tables(positions):
    half_width = HD // 2
    frequency = rope_theta ** (-(jnp.arange(half_width, dtype=jnp.float32) * 2.0 / HD))
    angles = positions.astype(jnp.float32)[:, None] * frequency[None, :]
    cosine, sine = jnp.cos(angles), jnp.sin(angles)
    return (
        jnp.concatenate([cosine, cosine], axis=-1),
        jnp.concatenate([-sine, sine], axis=-1),
    )


def paired_device(
    block_in,
    out_cotangent,
    segment_ids,
    doc_positions,
    norm1_gain,
    qkv_weight,
    out_weight,
    norm2_gain,
    gate_up_weight,
    down_weight,
):
    fsdp_count, tp_count = lax.axis_size("fsdp"), lax.axis_size("tp")
    core = lax.axis_index("fsdp") % 2
    lane_z = lax.axis_index("tp")
    near, far = lane_z % 2, lane_z // 2
    core_pairs = [(i, i ^ 1) for i in range(fsdp_count)]
    near_pairs = [(i, i ^ 1) for i in range(tp_count)]
    far_pairs = [(i, i ^ 2) for i in range(tp_count)]
    plane_groups = [list(range(first, fsdp_count, 2)) for first in range(2)]
    rows = block_in.shape[1]
    local_cols = qkv_weight.shape[2]
    heads_local = local_cols // HD
    gain_one = norm1_gain.astype(jnp.float32)
    gain_two = norm2_gain.astype(jnp.float32)

    def swap_core(value):
        return lax.ppermute(value, "fsdp", core_pairs)

    def swap_near(value):
        return lax.ppermute(value, "tp", near_pairs)

    def swap_far(value):
        return lax.ppermute(value, "tp", far_pairs)

    def pick_tile(size):
        return 512 if size % 512 == 0 else 768

    tokens = []

    def act(work, *inputs, sends=()):
        values = [*inputs, *[value for _, value in sends]]
        held = lax.optimization_barrier((*values, *tokens))[: len(values)]
        if sends:
            kinds = [kind for kind, _ in sends]
            result = work(*held[: len(inputs)], pushes=list(zip(kinds, held[len(inputs) :])))
        else:
            result = work(*held)
        tokens[:] = result if isinstance(result, tuple) else (result,)
        return result[0] if isinstance(result, tuple) and len(result) == 1 else result

    def swap(*sends):
        return act(lambda pushes: swap_call(*pushes), sends=sends)

    def pick(value, index):
        return lax.dynamic_index_in_dim(value, index, 0, keepdims=False)

    def place_tokens(value, got):
        keep = pick(value, far)
        return jnp.where(far == 0, keep, got), jnp.where(far == 0, got, keep)

    def join(left, right):
        return jnp.concatenate([left, right], axis=0)

    def plane_gather(pair):
        return lax.all_gather(pair, "fsdp", axis=0, tiled=True, axis_index_groups=plane_groups)

    def plane_scatter(grad):
        return lax.psum_scatter(
            grad, "fsdp", scatter_dimension=0, tiled=True, axis_index_groups=plane_groups
        )

    def gather_weight(key, local, *others):
        return plane_gather(act(lambda own, *got: core_pair(key, own, *got), local, *others))

    def halve(value):
        count = value.shape[0] // 2
        return value[:count], value[count:]

    def add_wide(left, right):
        return left.astype(jnp.float32) + right.astype(jnp.float32)

    def chained(value, *others):
        return lax.optimization_barrier((value, *others))[0]

    def scatter_gains(gains):
        for axis, size in (("fsdp", fsdp_count), ("tp", tp_count)):
            index = lax.axis_index(axis)
            step = size // 2
            while step >= 1:
                bit = (index // step) % 2
                parts = gains.reshape(gains.shape[0], 2, gains.shape[1] // 2)
                sent = lax.dynamic_index_in_dim(parts, 1 - bit, 1, keepdims=False)
                kept = lax.dynamic_index_in_dim(parts, bit, 1, keepdims=False)
                gains = kept + lax.ppermute(sent, axis, [(i, i ^ step) for i in range(size)])
                step //= 2
        return gains

    def wide_dot(left, right, pushes=()):
        return rows_matmul(
            [left], [right], dot_nn, [jnp.float32], pick_tile(right.shape[1]), pushes=pushes
        )

    def dot_bf16(left, right, pushes=()):
        return rows_matmul(
            [left], [right], dot_nn, [jnp.bfloat16], pick_tile(right.shape[1]), pushes=pushes
        )

    def grad_sum(left, right, left_next, right_next, pushes=()):
        chunk = pick_tile(right.shape[1])
        return sum_matmul(
            [left, left_next], [right, right_next], pick_tile(left.shape[1]),
            2 * chunk if right.shape[1] % (2 * chunk) == 0 else chunk, pushes=pushes,
        )

    def heads_back(grad, weight, pushes=()):
        return rows_matmul(
            [grad], [weight], dot_nt, [jnp.bfloat16], pick_tile(weight.shape[0]), pushes=pushes
        )

    def rms_pack(stream, gain):
        scale = rms_scale(stream)
        return scale, (stream * scale * gain).astype(jnp.bfloat16)

    qkv_local = qkv_weight.reshape(qkv_weight.shape[0], 3 * local_cols)
    gate_local, up_local = gate_up_weight[:, 0], gate_up_weight[:, 1]

    next_key[0] = 11
    position_got = swap_far(pick(doc_positions, 1 - far))
    first, second = place_tokens(doc_positions, position_got)
    near_both = swap_near(join(first, second))

    def first_norm(part):
        stream = part.astype(jnp.float32)
        return (stream, *rms_pack(stream, gain_one))

    s_own, r_own, n_own = act(lambda value: first_norm(pick(value, far)), block_in)
    near_own, qkv_other = swap(("near", n_own), ("far", qkv_local))
    qkv_full = gather_weight(4, qkv_local, qkv_other)
    first, second = (
        join(first, near_both[: first.shape[0]]), join(second, near_both[first.shape[0] :])
    )
    core_both = swap_core(join(first, second))

    def make_tables(first, second, both):
        count = first.shape[0]
        late = join(second, both[count:])
        return (*head_tables(join(first, both[:count])), *head_tables(late), late[:, None])

    c_own = pick(out_cotangent, far)
    stream_got, c_near_own, out_other = swap(
        ("far", pick(block_in, 1 - far)), ("near", c_own), ("far", out_weight)
    )
    out_full = gather_weight(3, out_weight, out_other)
    s_got, r_got, n_got = act(first_norm, stream_got)
    near_got, gate_other = swap(("near", n_got), ("far", gate_local))
    gate_full = gather_weight(5, gate_local, gate_other)
    h1_first, h1_second = act(core_gather_two, n_own, near_own, n_got, near_got)
    streams = [jnp.where(far == 0, s_own, s_got), jnp.where(far == 0, s_got, s_own)]
    scales_one = [jnp.where(far == 0, r_own, r_got), jnp.where(far == 0, r_got, r_own)]

    def attend_first(projected, pushes=()):
        arrays = [projected, projected, projected, *tables[0]]
        return attention_call(
            forward_first, arrays, [0, 1, 2, "table", "table"],
            ([0, 0, 0, 0, "lse"], heads_local), no_scratch, pushes,
        )

    def attend_second(projected, pushes=()):
        arrays = [projected, projected, projected, *tables[1], saved[0][1], saved[0][2], reach]
        return attention_call(
            forward_second, arrays, [0, 1, 2, "table", "table", 0, 0, "column"],
            ([0, 0, 0, 0, "lse"], heads_local), no_scratch, pushes,
        )

    up_halves, down_halves = halve(up_local), halve(down_weight)
    cot_halves = halve(pick(out_cotangent, 1 - far))
    cos_first, sin_first, cos_second, sin_second, reach = act(
        make_tables, first, second, core_both
    )
    tables = [(cos_first, sin_first), (cos_second, sin_second)]
    projected, up_early = act(wide_dot, h1_first, qkv_full, sends=[("far", up_halves[0])])
    *results, up_late = act(attend_first, projected, sends=[("far", up_halves[1])])
    saved, lses, mixed_first = [results[:3]], [results[4]], results[3]
    up_full = gather_weight(7, up_local, up_early, up_late)
    term_first = act(dot_bf16, mixed_first, out_full)
    keep_first, send_first = act(core_reduce, term_first)
    projected, branch_first, down_early = act(
        wide_dot, h1_second, qkv_full, sends=[("near", send_first), ("far", down_halves[0])]
    )

    def second_norm(stream, keep, got):
        middle = stream + keep + got.astype(jnp.float32)
        return (middle, *rms_pack(middle, gain_two))

    m_first, q_first, n_first = act(second_norm, streams[0], keep_first, branch_first)
    *results, near_first, down_late = act(
        attend_second, projected, sends=[("near", n_first), ("far", down_halves[1])]
    )
    saved.append(results[:3])
    lses.append(results[4])
    mixed_second = results[3]
    down_full = gather_weight(6, down_weight, down_early, down_late)
    term_second = act(dot_bf16, mixed_second, out_full)
    keep_second, send_second = act(core_reduce, term_second)
    h2_first = act(core_gather, n_first, near_first)

    gate_first, branch_second, cot_early = act(
        wide_dot, h2_first, gate_full, sends=[("near", send_second), ("far", cot_halves[0])]
    )
    m_second, q_second, n_second = act(second_norm, streams[1], keep_second, branch_second)

    def rise(hidden, weight, gate, pushes=()):
        return rows_matmul(
            [hidden], [weight], dot_nn, [jnp.float32, jnp.bfloat16], pick_tile(weight.shape[1]),
            finish=lambda up, gate: (up, gate * jax.nn.sigmoid(gate) * up), extras=[gate],
            pushes=pushes,
        )

    up_first, a_first, near_second, cot_late = act(
        rise, h2_first, up_full, gate_first, sends=[("near", n_second), ("far", cot_halves[1])]
    )
    h2_second = act(core_gather, n_second, near_second)
    gate_second, c_near_got = act(
        wide_dot, h2_second, gate_full, sends=[("near", c_got := join(cot_early, cot_late))]
    )
    y_first, y_second = act(core_gather_two, c_own, c_near_own, c_got, c_near_got)
    c_first, c_second = jnp.where(far == 0, c_own, c_got), jnp.where(far == 0, c_got, c_own)
    up_second, a_second = act(rise, h2_second, up_full, gate_second)
    down_sum = plane_scatter(act(grad_sum, a_first, y_first, a_second, y_second))

    def fall_finish(act_grad, gate, up):
        sigmoid_gate = jax.nn.sigmoid(gate)
        return (
            act_grad * up * sigmoid_gate * (1.0 + gate * (1.0 - sigmoid_gate)),
            act_grad * (gate * sigmoid_gate),
        )

    def fall(cotangent, weight, gate, up):
        return rows_matmul(
            [cotangent], [weight], dot_nt, [jnp.bfloat16] * 2, pick_tile(weight.shape[0]),
            chunk=512, finish=fall_finish, extras=[gate, up],
        )

    dg_first, du_first = act(fall, y_first, down_full, gate_first, up_first)
    dg_second, du_second = act(fall, y_second, down_full, gate_second, up_second)
    gate_sum = plane_scatter(act(grad_sum, h2_first, dg_first, h2_second, dg_second))

    def hidden_grad(gate_grad, up_grad, gate_weight, up_weight, pushes=()):
        return rows_matmul(
            [gate_grad, up_grad], [gate_weight, up_weight], dot_nt, [jnp.bfloat16],
            pick_tile(gate_weight.shape[0]), pushes=pushes,
        )

    def second_back(middle, scale, keep, got, cotangent):
        grad, gain_term = norm_back(middle, scale, gain_two, keep + got.astype(jnp.float32))
        grad = cotangent.astype(jnp.float32) + grad
        return grad, grad.astype(jnp.bfloat16), gain_term

    term_first = act(hidden_grad, dg_first, du_first, gate_full, up_full)
    keep_first, send_first = act(core_reduce, term_first)
    term_second, back_first = act(
        hidden_grad, dg_second, du_second, gate_full, up_full, sends=[("near", send_first)]
    )
    keep_second, send_second = act(core_reduce, term_second)
    g_first, n_first, gain_two_first = act(
        second_back, m_first, q_first, keep_first, back_first, c_first
    )
    down_mine, down_away = act(lambda pair: core_split(10, pair), down_sum)
    down_halves = halve(down_away)
    grad_up, back_second, down_early = act(
        grad_sum, h2_first, du_first, h2_second, du_second,
        sends=[("near", send_second), ("far", down_halves[0])],
    )
    up_sum = plane_scatter(grad_up)
    mlp_first, near_first, down_late = act(
        dot_bf16, a_first, down_full, sends=[("near", n_first), ("far", down_halves[1])]
    )
    g_second, n_second, gain_two_second = act(
        second_back, m_second, q_second, keep_second, back_second, c_second
    )
    d_first = act(core_gather, n_first, near_first)

    gate_mine, gate_away = act(lambda pair: core_split(9, pair), gate_sum)
    gate_halves = halve(gate_away)
    mlp_second, near_second, gate_early = act(
        dot_bf16, a_second, down_full, sends=[("near", n_second), ("far", gate_halves[0])]
    )
    mlp_keep_first, mlp_send_first = act(core_reduce, mlp_first)
    heads_first = act(heads_back, d_first, out_full)
    d_second = act(core_gather, n_second, near_second)
    heads_second = act(heads_back, d_second, out_full)
    mlp_keep_second, mlp_send_second = act(core_reduce, mlp_second)
    grad_out, mlp_branch_first, gate_late = act(
        grad_sum, mixed_first, d_first, mixed_second, d_second,
        sends=[("near", mlp_send_first), ("far", gate_halves[1])],
    )
    out_sum = plane_scatter(grad_out)
    up_mine, up_away = act(lambda pair: core_split(9, pair), up_sum)

    def attend_back(heads_first, heads_second, pushes=()):
        return attention_call(
            backward_both,
            [
                *saved[0], *saved[1], heads_first, heads_second, *lses,
                *tables[0], *tables[1], reach,
            ],
            [0] * 8 + ["lse"] * 2 + ["table"] * 4 + ["column"],
            ([0] * 6, heads_local),
            backward_scratch,
            pushes,
        )

    *grads, mlp_branch_second, up_got = act(
        attend_back, heads_first, heads_second,
        sends=[("near", mlp_send_second), ("far", up_away)],
    )
    p_first, p_second = act(
        lambda *parts: (
            jnp.concatenate(parts[:3], axis=1),
            jnp.concatenate(parts[3:], axis=1),
        ),
        *grads,
    )

    def finish_output(first, first_keep, first_got, second, second_keep, second_got):
        first = (first + first_keep + first_got.astype(jnp.float32)).astype(jnp.bfloat16)
        second = (second + second_keep + second_got.astype(jnp.float32)).astype(jnp.bfloat16)
        return jnp.where(far == 0, first, second), jnp.where(far == 0, second, first)

    term_first = act(heads_back, p_first, qkv_full)
    keep_first, send_first = act(core_reduce, term_first)
    grad_qkv, back_first = act(
        grad_sum, h1_first, p_first, h1_second, p_second, sends=[("near", send_first)]
    )
    qkv_sum = plane_scatter(grad_qkv)
    out_keep, out_send = act(
        finish_output,
        m_first, mlp_keep_first, mlp_branch_first, m_second, mlp_keep_second, mlp_branch_second,
    )
    out_halves = halve(out_send)
    term_second, out_early = act(heads_back, p_second, qkv_full, sends=[("far", out_halves[0])])
    keep_second, send_second = act(core_reduce, term_second)

    def settle(keep, got):
        return jnp.stack([jnp.where(far == 0, keep, got), jnp.where(far == 0, got, keep)])

    def first_back(stream, scale, keep, got, grad):
        back, gain_term = norm_back(stream, scale, gain_one, keep + got.astype(jnp.float32))
        return grad + back, gain_term

    def last_back(stream, scale, keep, got, grad, first):
        second, gain_term = first_back(stream, scale, keep, got, grad)
        return (
            jnp.where(far == 0, first, second),
            jnp.where(far == 0, second, first).astype(jnp.bfloat16),
            gain_term,
        )

    back_second, out_late = swap(("near", send_second), ("far", out_halves[1]))
    i_first, gain_one_first = act(
        first_back, streams[0], scales_one[0], keep_first, back_first, g_first
    )
    in_keep, in_send, gain_one_second = act(
        last_back, streams[1], scales_one[1], keep_second, back_second, g_second, i_first
    )
    in_got = swap_far(in_send)
    block_out = act(
        lambda keep, early, late: settle(keep, join(early, late)), out_keep, out_early, out_late
    )
    add_halves = lambda mine, early, late: add_wide(mine, join(early, late))
    down_owned = act(add_halves, down_mine, down_early, down_late)
    gate_owned = act(add_halves, gate_mine, gate_early, gate_late)
    up_owned = act(add_wide, up_mine, up_got)
    gate_up_owned = act(lambda a, b: jnp.stack([a, b], axis=1), gate_owned, up_owned)
    out_mine, out_away = act(lambda pair: core_split(8, pair), out_sum)
    gains = scatter_gains(
        jnp.stack([gain_one_first + gain_one_second, gain_two_first + gain_two_second])
    )
    in_grad = act(lambda keep, got: settle(keep, got.astype(jnp.float32)), in_keep, in_got)
    qkv_mine, qkv_away = act(lambda pair: core_split(0, pair), qkv_sum)
    out_back, qkv_back = swap(("far", out_away), ("far", qkv_away))
    out_owned = act(add_wide, out_mine, out_back)
    qkv_owned = act(add_wide, qkv_mine, qkv_back)
    return (
        block_out,
        in_grad,
        gains[0],
        qkv_owned.reshape(qkv_weight.shape),
        out_owned,
        gains[1],
        gate_up_owned,
        down_owned,
    )


def solution(mesh):
    sizes = (mesh.shape["fsdp"], mesh.shape["tp"])
    body = paired_device if sizes == (8, 4) else per_device
    in_specs = (
        P("fsdp", "tp", None),
        P("fsdp", "tp", None),
        P("fsdp", "tp"),
        P("fsdp", "tp"),
        P(),
        P("fsdp", None, "tp"),
        P(("tp", "fsdp"), None),
        P(),
        P("fsdp", None, "tp"),
        P(("tp", "fsdp"), None),
    )
    out_specs = (
        P("fsdp", "tp", None),
        P("fsdp", "tp", None),
        P(("fsdp", "tp")),
        P("fsdp", None, "tp"),
        P(("tp", "fsdp"), None),
        P(("fsdp", "tp")),
        P("fsdp", None, "tp"),
        P(("tp", "fsdp"), None),
    )
    return jax.shard_map(
        body, mesh=mesh, in_specs=in_specs, out_specs=out_specs, check_vma=False
    )
```

```python
import functools

import jax
import jax.numpy as jnp
from jax import lax
from jax.experimental import pallas as pl
from jax.experimental.pallas import tpu as pltpu
from jax.sharding import PartitionSpec as P

D = 3072
HD = 96


rms_epsilon = 1e-05
rope_theta = 10000.0
masked_score = -1e30
LOG2E = 1.4426950408889634


def rope_tables(positions, head_size):
    half_width = head_size // 2
    frequency = rope_theta ** (-(jnp.arange(half_width, dtype=jnp.float32) * 2.0 / head_size))
    angles = positions.astype(jnp.float32)[:, None] * frequency[None, :]
    return (jnp.cos(angles)[:, None, :], jnp.sin(angles)[:, None, :])


def rotate(values, cosine_part, sine_part):
    half_width = values.shape[-1] // 2
    lead_half = values[..., :half_width]
    tail_half = values[..., half_width:]
    return jnp.concatenate(
        [
            lead_half * cosine_part - tail_half * sine_part,
            tail_half * cosine_part + lead_half * sine_part,
        ],
        axis=-1,
    )


def unrotate(values, cosine_part, sine_part):
    half_width = values.shape[-1] // 2
    lead_half = values[..., :half_width]
    tail_half = values[..., half_width:]
    return jnp.concatenate(
        [
            lead_half * cosine_part + tail_half * sine_part,
            tail_half * cosine_part - lead_half * sine_part,
        ],
        axis=-1,
    )


def rms_scale(stream):
    return lax.rsqrt(jnp.mean(stream * stream, axis=-1, keepdims=True) + rms_epsilon)


def norm_back(stream, scale_rows, gain_vec, grad_rows):
    gained_grad = gain_vec * grad_rows
    input_grad = scale_rows * gained_grad - stream * scale_rows**3 * jnp.mean(
        gained_grad * stream, axis=-1, keepdims=True
    )
    return (input_grad, jnp.sum(grad_rows * stream * scale_rows, axis=0))


def allowed_mask(segment_tile, index_tile, segments):
    columns = jnp.arange(segments.shape[0], dtype=jnp.int32)
    return (segment_tile[:, None] == segments[None, :]) & (index_tile[:, None] >= columns[None, :])


def masked_scores(query_tile, key_rows, segment_tile, index_tile, segments, scale_value):
    scores = (
        jnp.einsum("qhd,khd->hqk", query_tile, key_rows, preferred_element_type=jnp.float32)
        * scale_value
    )
    return jnp.where(allowed_mask(segment_tile, index_tile, segments)[None], scores, masked_score)


def attention_forward(queries, key_rows, value_rows, segments, block_rows):
    seq_len, head_count, head_size = queries.shape
    tiles = seq_len // block_rows
    scale_value = head_size ** (-0.5)
    positions = jnp.arange(seq_len, dtype=jnp.int32)

    def query_block(packed):
        query_tile, segment_tile, index_tile = packed
        scores = masked_scores(
            query_tile, key_rows, segment_tile, index_tile, segments, scale_value
        )
        row_max = jnp.max(scores, axis=-1, keepdims=True)
        exponent = jnp.exp(scores - row_max)
        row_total = jnp.sum(exponent, axis=-1, keepdims=True)
        probs_low = (exponent / row_total).astype(jnp.bfloat16)
        mixed = jnp.einsum(
            "hqk,khd->qhd", probs_low, value_rows, preferred_element_type=jnp.float32
        )
        return (mixed, (row_max + jnp.log(row_total))[..., 0])

    mixed, log_total = lax.map(
        query_block,
        (
            queries.reshape(tiles, block_rows, head_count, head_size),
            segments.reshape(tiles, block_rows),
            positions.reshape(tiles, block_rows),
        ),
    )
    return (mixed.reshape(seq_len, head_count * head_size), log_total)


def attention_backward(queries, key_rows, value_rows, segments, log_total, out_grad, block_rows):
    seq_len, head_count, head_size = queries.shape
    tiles = seq_len // block_rows
    scale_value = head_size ** (-0.5)
    positions = jnp.arange(seq_len, dtype=jnp.int32)

    def query_block(carry, packed):
        key_acc, value_acc = carry
        query_tile, segment_tile, index_tile, total_tile, grad_tile = packed
        scores = masked_scores(
            query_tile, key_rows, segment_tile, index_tile, segments, scale_value
        )
        probs = jnp.exp(scores - total_tile[..., None])
        probs_low = probs.astype(jnp.bfloat16)
        prob_grad = jnp.einsum(
            "qhd,khd->hqk", grad_tile, value_rows, preferred_element_type=jnp.float32
        )
        score_grad = (
            probs * (prob_grad - jnp.sum(probs * prob_grad, axis=-1, keepdims=True))
        ).astype(jnp.bfloat16)
        query_grad = (
            jnp.einsum("hqk,khd->qhd", score_grad, key_rows, preferred_element_type=jnp.float32)
            * scale_value
        )
        key_acc = (
            key_acc
            + jnp.einsum("hqk,qhd->khd", score_grad, query_tile, preferred_element_type=jnp.float32)
            * scale_value
        )
        value_acc = value_acc + jnp.einsum(
            "hqk,qhd->khd", probs_low, grad_tile, preferred_element_type=jnp.float32
        )
        return ((key_acc, value_acc), query_grad)

    start_acc = (jnp.zeros(queries.shape, jnp.float32), jnp.zeros(queries.shape, jnp.float32))
    (key_grad, value_grad), query_grad = lax.scan(
        query_block,
        start_acc,
        (
            queries.reshape(tiles, block_rows, head_count, head_size),
            segments.reshape(tiles, block_rows),
            positions.reshape(tiles, block_rows),
            log_total,
            out_grad.reshape(tiles, block_rows, head_count, head_size),
        ),
    )
    return (query_grad.reshape(seq_len, head_count, head_size), key_grad, value_grad)


def gather_attention(qkv_weight, out_weight):
    return (
        lax.all_gather(qkv_weight, "fsdp", axis=0, tiled=True),
        lax.all_gather(out_weight, "fsdp", axis=0, tiled=True),
    )


def gather_feedforward(gate_up_weight, down_weight):
    return (
        lax.all_gather(gate_up_weight, "fsdp", axis=0, tiled=True),
        lax.all_gather(down_weight, "fsdp", axis=0, tiled=True),
    )


def per_device(
    block_in,
    out_cotangent,
    segment_ids,
    doc_positions,
    norm1_gain,
    qkv_weight,
    out_weight,
    norm2_gain,
    gate_up_weight,
    down_weight,
):
    micro_count = block_in.shape[0]
    fsdp_count = lax.axis_size("fsdp")
    segment_full, position_full = (
        lax.all_gather(segment_ids, "tp", axis=1, tiled=True),
        lax.all_gather(doc_positions, "tp", axis=1, tiled=True),
    )
    seq_len = segment_full.shape[1]
    block_rows = min(seq_len, 512)
    gain_one = norm1_gain.astype(jnp.float32)
    gain_two = norm2_gain.astype(jnp.float32)
    local_cols = qkv_weight.shape[2]
    local_units = gate_up_weight.shape[2]
    heads_local = local_cols // HD
    grad_qkv = jnp.zeros((D, 3, local_cols), jnp.float32)
    grad_out = jnp.zeros((out_weight.shape[0] * fsdp_count, D), jnp.float32)
    grad_gate_up = jnp.zeros((D, 2, local_units), jnp.float32)
    grad_down = jnp.zeros((down_weight.shape[0] * fsdp_count, D), jnp.float32)
    gain_one_acc = jnp.zeros((D,), jnp.float32)
    gain_two_acc = jnp.zeros((D,), jnp.float32)
    outputs = []
    input_grads = []
    for micro_index in range(micro_count):
        weights_fwd = (
            gather_attention(qkv_weight, out_weight),
            gather_feedforward(gate_up_weight, down_weight),
        )
        (qkv_full, out_full), (gate_up_full, down_full) = weights_fwd
        stream = block_in[micro_index].astype(jnp.float32)
        segment_row = segment_full[micro_index]
        cosine_part, sine_part = rope_tables(position_full[micro_index], HD)
        scale_one = rms_scale(stream)
        normed_one = (stream * scale_one * gain_one).astype(jnp.bfloat16)
        normed_one_full = lax.all_gather(normed_one, "tp", axis=0, tiled=True)
        projected = jnp.einsum(
            "sd,dtc->stc", normed_one_full, qkv_full, preferred_element_type=jnp.float32
        )
        queries = rotate(
            projected[:, 0].reshape(seq_len, heads_local, HD), cosine_part, sine_part
        ).astype(jnp.bfloat16)
        key_rows = rotate(
            projected[:, 1].reshape(seq_len, heads_local, HD), cosine_part, sine_part
        ).astype(jnp.bfloat16)
        value_rows = projected[:, 2].reshape(seq_len, heads_local, HD).astype(jnp.bfloat16)
        mixed, log_total = attention_forward(queries, key_rows, value_rows, segment_row, block_rows)
        attn_heads = mixed.astype(jnp.bfloat16)
        attn_term = jnp.dot(attn_heads, out_full, preferred_element_type=jnp.float32)
        attn_branch = lax.psum_scatter(attn_term, "tp", scatter_dimension=0, tiled=True)
        middle = stream + attn_branch
        scale_two = rms_scale(middle)
        normed_two = (middle * scale_two * gain_two).astype(jnp.bfloat16)
        normed_two_full = lax.all_gather(normed_two, "tp", axis=0, tiled=True)
        gate_up = jnp.einsum(
            "sd,dtf->stf", normed_two_full, gate_up_full, preferred_element_type=jnp.float32
        )
        gate_rows = gate_up[:, 0]
        up_rows = gate_up[:, 1]
        sigmoid_gate = jax.nn.sigmoid(gate_rows)
        silu_gate = gate_rows * sigmoid_gate
        activated = (silu_gate * up_rows).astype(jnp.bfloat16)
        mlp_term = jnp.dot(activated, down_full, preferred_element_type=jnp.float32)
        mlp_branch = lax.psum_scatter(
            mlp_term.astype(jnp.bfloat16), "tp", scatter_dimension=0, tiled=True
        ).astype(jnp.float32)
        outputs.append((middle + mlp_branch).astype(jnp.bfloat16))
        (qkv_back, out_back), (gate_up_back, down_back) = weights_fwd
        cotangent = out_cotangent[micro_index].astype(jnp.float32)
        cotangent_full = lax.all_gather(out_cotangent[micro_index], "tp", axis=0, tiled=True)
        grad_down = grad_down + jnp.einsum(
            "sf,sd->fd", activated, cotangent_full, preferred_element_type=jnp.float32
        )
        act_grad = jnp.einsum(
            "sd,fd->sf", cotangent_full, down_back, preferred_element_type=jnp.float32
        )
        gate_grad = act_grad * up_rows * sigmoid_gate * (1.0 + gate_rows * (1.0 - sigmoid_gate))
        up_grad = act_grad * silu_gate
        gate_up_grad = jnp.stack([gate_grad, up_grad], axis=1).astype(jnp.bfloat16)
        grad_gate_up = grad_gate_up + jnp.einsum(
            "sd,stf->dtf", normed_two_full, gate_up_grad, preferred_element_type=jnp.float32
        )
        normed_two_term = jnp.einsum(
            "stf,dtf->sd", gate_up_grad, gate_up_back, preferred_element_type=jnp.float32
        )
        normed_two_grad = lax.psum_scatter(normed_two_term, "tp", scatter_dimension=0, tiled=True)
        middle_back, gain_two_term = norm_back(middle, scale_two, gain_two, normed_two_grad)
        gain_two_acc = gain_two_acc + gain_two_term
        middle_grad = cotangent + middle_back
        attn_grad_full = lax.all_gather(middle_grad.astype(jnp.bfloat16), "tp", axis=0, tiled=True)
        grad_out = grad_out + jnp.einsum(
            "sc,sd->cd", attn_heads, attn_grad_full, preferred_element_type=jnp.float32
        )
        heads_grad = jnp.einsum(
            "sd,cd->sc", attn_grad_full, out_back, preferred_element_type=jnp.float32
        ).astype(jnp.bfloat16)
        query_grad, key_grad, value_grad = attention_backward(
            queries,
            key_rows,
            value_rows,
            segment_row,
            log_total,
            heads_grad.reshape(seq_len, heads_local, HD),
            block_rows,
        )
        projected_grad = jnp.stack(
            [
                unrotate(query_grad, cosine_part, sine_part).reshape(seq_len, local_cols),
                unrotate(key_grad, cosine_part, sine_part).reshape(seq_len, local_cols),
                value_grad.reshape(seq_len, local_cols),
            ],
            axis=1,
        ).astype(jnp.bfloat16)
        grad_qkv = grad_qkv + jnp.einsum(
            "sd,stc->dtc", normed_one_full, projected_grad, preferred_element_type=jnp.float32
        )
        normed_one_term = jnp.einsum(
            "stc,dtc->sd", projected_grad, qkv_back, preferred_element_type=jnp.float32
        )
        normed_one_grad = lax.psum_scatter(
            normed_one_term.astype(jnp.bfloat16), "tp", scatter_dimension=0, tiled=True
        ).astype(jnp.float32)
        stream_back, gain_one_term = norm_back(stream, scale_one, gain_one, normed_one_grad)
        gain_one_acc = gain_one_acc + gain_one_term
        input_grads.append(middle_grad + stream_back)
    owned_grads = (
        lax.psum_scatter(
            grad_qkv.astype(jnp.bfloat16), "fsdp", scatter_dimension=0, tiled=True
        ).astype(jnp.float32),
        lax.psum_scatter(
            grad_out.astype(jnp.bfloat16), "fsdp", scatter_dimension=0, tiled=True
        ).astype(jnp.float32),
        lax.psum_scatter(
            grad_gate_up.astype(jnp.bfloat16), "fsdp", scatter_dimension=0, tiled=True
        ).astype(jnp.float32),
        lax.psum_scatter(
            grad_down.astype(jnp.bfloat16), "fsdp", scatter_dimension=0, tiled=True
        ).astype(jnp.float32),
    )
    owned_gains = (
        lax.psum_scatter(gain_one_acc, ("fsdp", "tp"), scatter_dimension=0, tiled=True),
        lax.psum_scatter(gain_two_acc, ("fsdp", "tp"), scatter_dimension=0, tiled=True),
    )
    return (
        jnp.stack(outputs),
        jnp.stack(input_grads),
        owned_gains[0],
        owned_grads[0],
        owned_grads[1],
        owned_gains[1],
        owned_grads[2],
        owned_grads[3],
    )


HEAD_GROUP = 4
FIRST_DOC = 800


def dot_nt(left, right):
    return lax.dot_general(left, right, (((1,), (1,)), ((), ())), preferred_element_type=jnp.float32)


def dot_tn(left, right):
    return lax.dot_general(left, right, (((0,), (0,)), ((), ())), preferred_element_type=jnp.float32)


def dot_nn(left, right):
    return lax.dot_general(left, right, (((1,), (0,)), ((), ())), preferred_element_type=jnp.float32)


def swap_halves(values):
    lanes = lax.broadcasted_iota(jnp.int32, values.shape, 1)
    width = values.shape[1]
    return jnp.where(
        lanes % HD < HD // 2,
        pltpu.roll(values, width - HD // 2, 1),
        pltpu.roll(values, HD // 2, 1),
    )


def causal_mask(rows, columns):
    row_ids = lax.broadcasted_iota(jnp.int32, (rows, columns), 0)
    column_ids = lax.broadcasted_iota(jnp.int32, (rows, columns), 1)
    return row_ids >= column_ids


def tail_mask(reach):
    rows = reach.shape[0]
    row_ids = lax.broadcasted_iota(jnp.int32, (rows, rows), 0)
    column_ids = lax.broadcasted_iota(jnp.int32, (rows, rows), 1)
    return (row_ids >= column_ids) & (row_ids - column_ids <= reach)


def halves(quarter):
    first = lax.axis_index("tp") % 2
    return (
        pl.multiple_of(first * quarter, quarter),
        pl.multiple_of((1 - first) * quarter, quarter),
    )


def widen(table):
    return jnp.concatenate([table] * HEAD_GROUP, axis=1)


def load_rotated(offsets, quarter, q_ref, k_ref, v_ref, cos_ref, sin_ref, qr_ref, kr_ref, vr_ref):
    for place, offset in enumerate(offsets):
        rows = pl.ds(offset, quarter)
        target = pl.ds(place * quarter, quarter)
        cosine, sine = widen(cos_ref[rows, :]), widen(sin_ref[rows, :])
        q_raw, k_raw = q_ref[rows, :], k_ref[rows, :]
        qr_ref[target, :] = (q_raw * cosine + swap_halves(q_raw) * sine).astype(jnp.bfloat16)
        kr_ref[target, :] = (k_raw * cosine + swap_halves(k_raw) * sine).astype(jnp.bfloat16)
        vr_ref[target, :] = v_ref[rows, :].astype(jnp.bfloat16)


def softmax_mix(query, pieces, factor):
    scores = []
    for keys, _, mask in pieces:
        score = dot_nt(query, keys)
        scores.append(score if mask is None else jnp.where(mask, score, masked_score))
    top = functools.reduce(jnp.maximum, [jnp.max(s, axis=-1, keepdims=True) for s in scores])
    weights = [jnp.exp2((s - top) * factor) for s in scores]
    total = functools.reduce(jnp.add, [jnp.sum(w, axis=-1, keepdims=True) for w in weights])
    inverse = 1.0 / total
    mixed = functools.reduce(
        jnp.add,
        [dot_nn((w * inverse).astype(jnp.bfloat16), piece[1]) for w, piece in zip(weights, pieces)],
    )
    return mixed, top * factor + jnp.log2(total)


def head_slice(head):
    return slice(head * HD, (head + 1) * HD)


def forward_first(
    q_ref, k_ref, v_ref, cos_ref, sin_ref, qr_ref, kr_ref, vr_ref, o_ref, lse_ref
):
    half = q_ref.shape[0]
    quarter = half // 2
    offsets = halves(quarter)
    load_rotated(offsets, quarter, q_ref, k_ref, v_ref, cos_ref, sin_ref, qr_ref, kr_ref, vr_ref)
    factor = HD ** (-0.5) * LOG2E
    mask = causal_mask(quarter, quarter)
    for head in range(HEAD_GROUP):
        cols = head_slice(head)
        early, late = slice(0, quarter), slice(quarter, half)
        k_early, v_early = kr_ref[early, cols], vr_ref[early, cols]
        mixed, lse = softmax_mix(qr_ref[early, cols], [(k_early, v_early, mask)], factor)
        o_ref[pl.ds(offsets[0], quarter), cols] = mixed.astype(jnp.bfloat16)
        lse_ref[0, early, head : head + 1] = lse
        mixed, lse = softmax_mix(
            qr_ref[late, cols],
            [(k_early, v_early, None), (kr_ref[late, cols], vr_ref[late, cols], mask)],
            factor,
        )
        o_ref[pl.ds(offsets[1], quarter), cols] = mixed.astype(jnp.bfloat16)
        lse_ref[0, late, head : head + 1] = lse


def forward_second(
    q_ref, k_ref, v_ref, cos_ref, sin_ref, ka_ref, va_ref, pos_ref,
    qr_ref, kr_ref, vr_ref, o_ref, lse_ref,
):
    half = q_ref.shape[0]
    quarter = half // 2
    cut = FIRST_DOC - half
    spill = cut - quarter
    offsets = halves(quarter)
    load_rotated(offsets, quarter, q_ref, k_ref, v_ref, cos_ref, sin_ref, qr_ref, kr_ref, vr_ref)
    factor = HD ** (-0.5) * LOG2E
    mask = causal_mask(cut, cut)
    mask_tail = tail_mask(pos_ref[pl.ds(offsets[1] + spill, half - cut), :])
    for head in range(HEAD_GROUP):
        cols = head_slice(head)
        early, late = slice(0, cut), slice(cut, half)
        mixed, lse = softmax_mix(
            qr_ref[early, cols],
            [
                (ka_ref[:, cols], va_ref[:, cols], None),
                (kr_ref[early, cols], vr_ref[early, cols], mask),
            ],
            factor,
        )
        low = mixed.astype(jnp.bfloat16)
        o_ref[pl.ds(offsets[0], quarter), cols] = low[:quarter]
        o_ref[pl.ds(offsets[1], spill), cols] = low[quarter:]
        lse_ref[0, early, head : head + 1] = lse
        mixed, lse = softmax_mix(
            qr_ref[late, cols], [(kr_ref[late, cols], vr_ref[late, cols], mask_tail)], factor
        )
        o_ref[pl.ds(offsets[1] + spill, half - cut), cols] = mixed.astype(jnp.bfloat16)
        lse_ref[0, late, head : head + 1] = lse


def backward_both(
    qa_ref, ka_ref, va_ref, qb_ref, kb_ref, vb_ref, ga_ref, gb_ref, la_ref, lb_ref,
    cosa_ref, sina_ref, cosb_ref, sinb_ref, pos_ref,
    dqa_ref, dka_ref, dva_ref, dqb_ref, dkb_ref, dvb_ref,
    go_a, go_b, tqa, tka, tva, tqb, tkb, tvb,
):
    half = qa_ref.shape[0]
    quarter = half // 2
    cut = FIRST_DOC - half
    spill = cut - quarter
    offsets = halves(quarter)
    scale_value = HD ** (-0.5)
    factor = scale_value * LOG2E
    for place, offset in enumerate(offsets):
        target, rows = pl.ds(place * quarter, quarter), pl.ds(offset, quarter)
        go_a[target, :] = ga_ref[rows, :]
        go_b[target, :] = gb_ref[rows, :]
    mask = causal_mask(quarter, quarter)
    mask_cut = causal_mask(cut, cut)
    mask_tail = tail_mask(pos_ref[pl.ds(offsets[1] + spill, half - cut), :])
    for accumulator in (tka, tva, tkb, tvb):
        accumulator[...] = jnp.zeros_like(accumulator)

    def attend(query, grad, lse, pieces):
        weights, weight_grads = [], []
        for k_ref, v_ref, rows, cols, mask, _, _ in pieces:
            weight = jnp.exp2(dot_nt(query, k_ref[rows, cols]) * factor - lse)
            weights.append(weight if mask is None else jnp.where(mask, weight, 0.0))
            weight_grads.append(dot_nt(grad, v_ref[rows, cols]))
        shared = functools.reduce(
            jnp.add,
            [jnp.sum(w * g, axis=-1, keepdims=True) for w, g in zip(weights, weight_grads)],
        )
        query_grad = None
        for weight, weight_grad, piece in zip(weights, weight_grads, pieces):
            k_ref, v_ref, rows, cols, _, tk, tv = piece
            score_grad = (weight * (weight_grad - shared)).astype(jnp.bfloat16)
            term = dot_nn(score_grad, k_ref[rows, cols])
            query_grad = term if query_grad is None else query_grad + term
            tk[rows, cols] += dot_tn(score_grad, query)
            tv[rows, cols] += dot_tn(weight.astype(jnp.bfloat16), grad)
        return query_grad

    for head in range(HEAD_GROUP):
        cols = head_slice(head)
        lane = slice(head, head + 1)
        early, late, whole = slice(0, quarter), slice(quarter, half), slice(0, half)
        tqa[early, cols] = attend(
            qa_ref[early, cols], go_a[early, cols], la_ref[0, early, lane],
            [(ka_ref, va_ref, early, cols, mask, tka, tva)],
        )
        tqa[late, cols] = attend(
            qa_ref[late, cols], go_a[late, cols], la_ref[0, late, lane],
            [
                (ka_ref, va_ref, early, cols, None, tka, tva),
                (ka_ref, va_ref, late, cols, mask, tka, tva),
            ],
        )
        early, late = slice(0, cut), slice(cut, half)
        tqb[early, cols] = attend(
            qb_ref[early, cols], go_b[early, cols], lb_ref[0, early, lane],
            [
                (ka_ref, va_ref, whole, cols, None, tka, tva),
                (kb_ref, vb_ref, early, cols, mask_cut, tkb, tvb),
            ],
        )
        tqb[late, cols] = attend(
            qb_ref[late, cols], go_b[late, cols], lb_ref[0, late, lane],
            [(kb_ref, vb_ref, late, cols, mask_tail, tkb, tvb)],
        )
    for place, offset in enumerate(offsets):
        source, rows = pl.ds(place * quarter, quarter), pl.ds(offset, quarter)
        for total, cos_ref, sin_ref, out_ref in (
            (tqa, cosa_ref, sina_ref, dqa_ref),
            (tka, cosa_ref, sina_ref, dka_ref),
            (tqb, cosb_ref, sinb_ref, dqb_ref),
            (tkb, cosb_ref, sinb_ref, dkb_ref),
        ):
            grad = total[source, :] * scale_value
            out_ref[rows, :] = (
                grad * widen(cos_ref[rows, :]) - swap_halves(grad) * widen(sin_ref[rows, :])
            ).astype(jnp.bfloat16)
        dva_ref[rows, :] = tva[source, :].astype(jnp.bfloat16)
        dvb_ref[rows, :] = tvb[source, :].astype(jnp.bfloat16)


COST_SCALE = 1.7


def cost_of(flops):
    return pl.CostEstimate(flops=int(COST_SCALE * flops), bytes_accessed=1000, transcendentals=0)


def rows_kernel(pairs, extra_count, dot, chunk, finish, *refs):
    lefts, weights = refs[:pairs], refs[pairs : 2 * pairs]
    extras = refs[2 * pairs : 2 * pairs + extra_count]
    outs = refs[2 * pairs + extra_count :]

    @pl.loop(0, outs[0].shape[0] // chunk)
    def _(step):
        rows = pl.ds(pl.multiple_of(step * chunk, chunk), chunk)
        total = None
        for left, weight in zip(lefts, weights):
            term = dot(left[rows, :], weight[...])
            total = term if total is None else total + term
        for out, value in zip(outs, finish(total, *[extra[rows, :] for extra in extras])):
            out[rows, :] = value.astype(out.dtype)


def keep_one(total):
    return (total,)


def rows_matmul(
    lefts, weights, dot, types, tile, chunk=1024, finish=keep_one, extras=(), pushes=()
):
    rows = lefts[0].shape[0]
    if dot is dot_nn:
        width = weights[0].shape[1]
        weight_specs = [pl.BlockSpec((w.shape[0], tile), lambda j: (0, j)) for w in weights]
    else:
        width = weights[0].shape[0]
        weight_specs = [pl.BlockSpec((tile, w.shape[1]), lambda j: (j, 0)) for w in weights]
    column = pl.BlockSpec((rows, tile), lambda j: (0, j))
    return grid_call(
        functools.partial(rows_kernel, len(lefts), len(extras), dot, min(chunk, rows), finish),
        [*lefts, *weights, *extras],
        [pl.BlockSpec(left.shape, lambda j: (0, 0)) for left in lefts]
        + weight_specs
        + [column] * len(extras),
        [jax.ShapeDtypeStruct((rows, width), kind) for kind in types],
        [column] * len(types),
        (width // tile,),
        2 * rows * width * sum(left.shape[1] for left in lefts),
        pushes=pushes,
    )


def sum_kernel(parts, chunk, *refs):
    lefts, rights, out = refs[:parts], refs[parts : 2 * parts], refs[-1]

    @pl.loop(0, out.shape[1] // chunk)
    def _(step):
        cols = pl.ds(pl.multiple_of(step * chunk, chunk), chunk)
        total = None
        for left, right in zip(lefts, rights):
            term = dot_tn(left[...], right[:, cols])
            total = term if total is None else total + term
        out[:, cols] = total.astype(out.dtype)


def sum_matmul(lefts, rights, tile, chunk, pushes=()):
    rows, height = lefts[0].shape
    width = rights[0].shape[1]
    return grid_call(
        functools.partial(sum_kernel, len(lefts), chunk),
        [*lefts, *rights],
        [pl.BlockSpec((rows, tile), lambda j: (0, j)) for _ in lefts]
        + [pl.BlockSpec((rows, width), lambda j: (0, 0)) for _ in rights],
        [jax.ShapeDtypeStruct((height, width), jnp.bfloat16)],
        [pl.BlockSpec((tile, width), lambda j: (j, 0))],
        (height // tile,),
        2 * rows * height * width * len(lefts),
        pushes=pushes,
    )


def partner_of(kind):
    index, place = lax.axis_index("fsdp"), lax.axis_index("tp")
    if kind == "near":
        return (index, place + 1 - 2 * (place % 2))
    return (index, place + 2 - 4 * (place // 2))


def start_pushes(kinds, sources, targets, send, receive):
    barrier = pltpu.get_barrier_semaphore()
    names = sorted(set(kinds))
    for kind in names:
        pl.semaphore_signal(
            barrier, inc=1, device_id=partner_of(kind), device_id_type=pl.DeviceIdType.MESH
        )
    pl.semaphore_wait(barrier, len(names))
    for place, kind in enumerate(kinds):
        push(
            sources[place], targets[place], send.at[place], receive.at[place], partner_of(kind)
        ).start()


def wait_pushes(kinds, sources, targets, send, receive):
    for place, kind in enumerate(kinds):
        push(
            sources[place], targets[place], send.at[place], receive.at[place], partner_of(kind)
        ).wait()


def pushing_kernel(kernel, axes, in_count, out_count, kinds, *refs):
    count = len(kinds)
    inputs, sources = refs[:in_count], refs[in_count : in_count + count]
    outs = refs[in_count + count : in_count + count + out_count]
    targets = refs[in_count + count + out_count : in_count + 2 * count + out_count]
    scratch, (send, receive) = refs[in_count + 2 * count + out_count : -2], refs[-2:]
    first = functools.reduce(jnp.logical_and, [pl.program_id(axis) == 0 for axis in range(axes)])
    last = functools.reduce(
        jnp.logical_and,
        [pl.program_id(axis) == pl.num_programs(axis) - 1 for axis in range(axes)],
    )

    @pl.when(first)
    def _():
        start_pushes(kinds, sources, targets, send, receive)

    kernel(*inputs, *outs, *scratch)

    @pl.when(last)
    def _():
        wait_pushes(kinds, sources, targets, send, receive)


def grid_call(
    kernel, operands, in_specs, outs, out_specs, grid, flops, scratch=(), pushes=(), vmem=60
):
    params = dict(
        dimension_semantics=("arbitrary",) * len(grid), vmem_limit_bytes=vmem * 1024 * 1024
    )
    operands, in_specs, outs = list(operands), list(in_specs), list(outs)
    out_specs, scratch = list(out_specs), list(scratch)
    if pushes:
        kinds = tuple(kind for kind, _ in pushes)
        kernel = functools.partial(
            pushing_kernel, kernel, len(grid), len(operands), len(outs), kinds
        )
        anywhere = [pl.BlockSpec(memory_space=pl.ANY)] * len(pushes)
        operands += [value for _, value in pushes]
        in_specs += anywhere
        outs += [jax.ShapeDtypeStruct(value.shape, value.dtype) for _, value in pushes]
        out_specs += anywhere
        scratch += [pltpu.SemaphoreType.DMA((len(pushes),))] * 2
        next_key[0] += 1
        params.update(collective_id=next_key[0], has_side_effects=True)
    return tuple(
        pl.pallas_call(
            kernel,
            out_shape=outs,
            grid=grid,
            in_specs=in_specs,
            out_specs=out_specs,
            scratch_shapes=scratch,
            compiler_params=pltpu.CompilerParams(**params),
            cost_estimate=cost_of(max(flops, 27 * 10**9) if pushes else flops),
        )(*operands)
    )


def swap_kernel(kinds, *refs):
    count = len(kinds)
    sources, targets, (send, receive) = refs[:count], refs[count : 2 * count], refs[2 * count :]
    start_pushes(kinds, sources, targets, send, receive)
    wait_pushes(kinds, sources, targets, send, receive)


def swap_call(*pushes):
    next_key[0] += 1
    kinds = tuple(kind for kind, _ in pushes)
    values = [value for _, value in pushes]
    return exchange_call(
        functools.partial(swap_kernel, kinds), next_key[0], values,
        [jax.ShapeDtypeStruct(value.shape, value.dtype) for value in values],
        [pltpu.SemaphoreType.DMA((len(pushes),))] * 2, flops=200 * 10**9,
    )


next_key = [11]


def sibling_id():
    index = lax.axis_index("fsdp")
    return (index + 1 - 2 * (index % 2), lax.axis_index("tp"))


def meet(partner):
    barrier = pltpu.get_barrier_semaphore()
    pl.semaphore_signal(barrier, inc=1, device_id=partner, device_id_type=pl.DeviceIdType.MESH)
    pl.semaphore_wait(barrier, 1)


def push(source, target, send, receive, partner):
    return pltpu.make_async_remote_copy(
        src_ref=source,
        dst_ref=target,
        send_sem=send,
        recv_sem=receive,
        device_id=partner,
        device_id_type=pl.DeviceIdType.MESH,
    )


def exchange_call(kernel, key, operands, outs, scratch, vmem=60, flops=4 * 10**9):
    anywhere = pl.BlockSpec(memory_space=pl.ANY)
    results = pl.pallas_call(
        kernel,
        out_shape=outs,
        in_specs=[anywhere] * len(operands),
        out_specs=[anywhere] * len(outs),
        scratch_shapes=scratch,
        compiler_params=pltpu.CompilerParams(
            collective_id=key, has_side_effects=True, vmem_limit_bytes=vmem * 1024 * 1024
        ),
        cost_estimate=cost_of(flops),
    )(*operands)
    return tuple(results) if len(outs) > 1 else results[0]


def gather_kernel(own_ref, near_ref, full_ref, local, send, receive):
    partner = sibling_id()
    meet(partner)
    count = own_ref.shape[0]
    copies = []
    for place, ref in enumerate((own_ref, near_ref)):
        remote = push(
            ref, full_ref.at[pl.ds((2 + place) * count, count)],
            send.at[place], receive.at[place], partner,
        )
        remote.start()
        copies.append(remote)
    for place, ref in enumerate((own_ref, near_ref)):
        copy = pltpu.make_async_copy(
            ref, full_ref.at[pl.ds(place * count, count)], local.at[place]
        )
        copy.start()
        copies.append(copy)
    for copy in copies:
        copy.wait()


def core_gather(own, near):
    shape = (4 * own.shape[0], own.shape[1])
    return exchange_call(
        gather_kernel, 1, [own, near], [jax.ShapeDtypeStruct(shape, own.dtype)],
        [pltpu.SemaphoreType.DMA((2,))] * 3,
    )


def gather_two_kernel(
    own_ref, own_near_ref, got_ref, got_near_ref, first_ref, second_ref, local, send, receive
):
    partner = sibling_id()
    far = lax.axis_index("tp") // 2
    meet(partner)
    count = own_ref.shape[0]

    def run(targets):
        copies = []
        for place, ref in enumerate((own_ref, own_near_ref, got_ref, got_near_ref)):
            target, row = targets[place // 2], place % 2
            remote = push(
                ref, target.at[pl.ds((2 + row) * count, count)],
                send.at[place], receive.at[place], partner,
            )
            remote.start()
            copy = pltpu.make_async_copy(
                ref, target.at[pl.ds(row * count, count)], local.at[place]
            )
            copy.start()
            copies += [remote, copy]
        for copy in copies:
            copy.wait()

    @pl.when(far == 0)
    def _():
        run((first_ref, second_ref))

    @pl.when(far != 0)
    def _():
        run((second_ref, first_ref))


def core_gather_two(own, own_near, got, got_near):
    shape = (4 * own.shape[0], own.shape[1])
    return exchange_call(
        gather_two_kernel, 11, [own, own_near, got, got_near],
        [jax.ShapeDtypeStruct(shape, own.dtype)] * 2,
        [pltpu.SemaphoreType.DMA((4,))] * 3,
    )


def reduce_kernel(term_ref, keep_ref, away_ref, mine, got, keep, away, local, send, receive, store):
    partner = sibling_id()
    meet(partner)
    pieces, count = mine.shape[0], mine.shape[1]
    half = pieces * count
    remotes, loads = [], []
    for piece in range(pieces):
        order = (piece + pieces // 2) % pieces
        remote = push(
            term_ref.at[pl.ds(half + order * count, count)], got.at[order],
            send.at[order], receive.at[order], partner,
        )
        remote.start()
        remotes.append(remote)
        load = pltpu.make_async_copy(
            term_ref.at[pl.ds(order * count, count)], mine.at[order], local.at[order]
        )
        load.start()
        loads.append(load)
    stores = []
    for piece in range(pieces):
        order = (piece + pieces // 2) % pieces
        loads[piece].wait()
        remotes[piece].wait()
        total = mine[order].astype(jnp.float32) + got[order].astype(jnp.float32)
        if order < pieces // 2:
            keep[order] = total
            copy = pltpu.make_async_copy(
                keep.at[order], keep_ref.at[pl.ds(order * count, count)], store.at[order]
            )
        else:
            slot = order - pieces // 2
            away[slot] = total.astype(away.dtype)
            copy = pltpu.make_async_copy(
                away.at[slot], away_ref.at[pl.ds(slot * count, count)], store.at[order]
            )
        copy.start()
        stores.append(copy)
    for copy in stores:
        copy.wait()


def core_reduce(term):
    rows, width = term.shape
    quarter = rows // 4
    pieces = 4
    count = 2 * quarter // pieces
    return exchange_call(
        reduce_kernel, 2, [term],
        [
            jax.ShapeDtypeStruct((quarter, width), jnp.float32),
            jax.ShapeDtypeStruct((quarter, width), term.dtype),
        ],
        [
            pltpu.VMEM((pieces, count, width), term.dtype),
            pltpu.VMEM((pieces, count, width), term.dtype),
            pltpu.VMEM((pieces // 2, count, width), jnp.float32),
            pltpu.VMEM((pieces // 2, count, width), term.dtype),
        ]
        + [pltpu.SemaphoreType.DMA((pieces,))] * 4,
    )


def pair_kernel(own_ref, *refs):
    others, (pair_ref, local, send, receive) = refs[:-4], refs[-4:]
    partner = sibling_id()
    core = lax.axis_index("fsdp") % 2
    far = lax.axis_index("tp") // 2
    meet(partner)
    base = pl.multiple_of(core * own_ref.shape[0], own_ref.shape[0])
    count = others[0].shape[0]
    owns = [own_ref.at[pl.ds(place * count, count)] for place in range(len(others))]

    def run(mine, theirs):
        copies = []
        for place in range(len(others)):
            target = pair_ref.at[pl.ds(base + place * count, count)]
            remote = push(
                theirs[place], target, send.at[place], receive.at[place], partner
            )
            remote.start()
            copy = pltpu.make_async_copy(mine[place], target, local.at[place])
            copy.start()
            copies += [remote, copy]
        for copy in copies:
            copy.wait()

    @pl.when(core == far)
    def _():
        run(owns, others)

    @pl.when(core != far)
    def _():
        run(others, owns)


def core_pair(key, own, *others):
    shape = (2 * own.shape[0], own.shape[1])
    return exchange_call(
        pair_kernel, key, [own, *others], [jax.ShapeDtypeStruct(shape, own.dtype)],
        [pltpu.SemaphoreType.DMA((len(others),))] * 3,
    )


def split_kernel(pair_ref, keep_ref, away_ref, local, send, receive):
    partner = sibling_id()
    core = lax.axis_index("fsdp") % 2
    far = lax.axis_index("tp") // 2
    meet(partner)
    count = keep_ref.shape[0]
    mine = pair_ref.at[pl.ds(pl.multiple_of(core * count, count), count)]
    theirs = pair_ref.at[pl.ds(pl.multiple_of((1 - core) * count, count), count)]

    def run(own_target, other_target):
        remote = push(theirs, other_target, send.at[0], receive.at[0], partner)
        remote.start()
        copy = pltpu.make_async_copy(mine, own_target, local.at[0])
        copy.start()
        copy.wait()
        remote.wait()

    @pl.when(core == far)
    def _():
        run(keep_ref, keep_ref)

    @pl.when(core != far)
    def _():
        run(away_ref, away_ref)


def core_split(key, pair):
    shape = (pair.shape[0] // 2, pair.shape[1])
    return exchange_call(
        split_kernel, key, [pair], [jax.ShapeDtypeStruct(shape, pair.dtype)] * 2,
        [pltpu.SemaphoreType.DMA((1,))] * 3,
    )


def attention_call(kernel, arrays, kinds, outs, scratch, pushes=()):
    rows, heads_local = arrays[-1].shape[0], outs[1]
    half = rows // 2
    groups = heads_local // HEAD_GROUP
    width = HEAD_GROUP * HD

    def spec(kind):
        if kind == "table":
            return pl.BlockSpec((half, HD), lambda s, g: (s, 0))
        if kind == "column":
            return pl.BlockSpec((half, 1), lambda s, g: (s, 0))
        if kind == "lse":
            return pl.BlockSpec((1, half, HEAD_GROUP), lambda s, g: (g, s, 0))
        shift = kind * groups
        return pl.BlockSpec((half, width), lambda s, g: (s, shift + g))

    def shape(kind):
        if kind == "lse":
            return jax.ShapeDtypeStruct((groups, rows, HEAD_GROUP), jnp.float32)
        return jax.ShapeDtypeStruct((rows, heads_local * HD), jnp.bfloat16)

    return grid_call(
        kernel,
        arrays,
        [spec(kind) for kind in kinds],
        [shape(kind) for kind in outs[0]],
        [spec(kind) for kind in outs[0]],
        (rows // half, groups),
        4 * len(outs[0]) ** 2 * rows * rows * heads_local * HD // 16,
        scratch=scratch(half, width),
        pushes=pushes,
    )


def backward_scratch(half, width):
    return [pltpu.VMEM((half, width), jnp.bfloat16)] * 2 + [
        pltpu.VMEM((half, width), jnp.float32)
    ] * 6


def no_scratch(half, width):
    return []


def head_tables(positions):
    half_width = HD // 2
    frequency = rope_theta ** (-(jnp.arange(half_width, dtype=jnp.float32) * 2.0 / HD))
    angles = positions.astype(jnp.float32)[:, None] * frequency[None, :]
    cosine, sine = jnp.cos(angles), jnp.sin(angles)
    return (
        jnp.concatenate([cosine, cosine], axis=-1),
        jnp.concatenate([-sine, sine], axis=-1),
    )


def paired_device(
    block_in,
    out_cotangent,
    segment_ids,
    doc_positions,
    norm1_gain,
    qkv_weight,
    out_weight,
    norm2_gain,
    gate_up_weight,
    down_weight,
):
    fsdp_count, tp_count = lax.axis_size("fsdp"), lax.axis_size("tp")
    core = lax.axis_index("fsdp") % 2
    lane_z = lax.axis_index("tp")
    near, far = lane_z % 2, lane_z // 2
    core_pairs = [(i, i ^ 1) for i in range(fsdp_count)]
    near_pairs = [(i, i ^ 1) for i in range(tp_count)]
    far_pairs = [(i, i ^ 2) for i in range(tp_count)]
    plane_groups = [list(range(first, fsdp_count, 2)) for first in range(2)]
    rows = block_in.shape[1]
    local_cols = qkv_weight.shape[2]
    heads_local = local_cols // HD
    gain_one = norm1_gain.astype(jnp.float32)
    gain_two = norm2_gain.astype(jnp.float32)

    def swap_core(value):
        return lax.ppermute(value, "fsdp", core_pairs)

    def swap_near(value):
        return lax.ppermute(value, "tp", near_pairs)

    def swap_far(value):
        return lax.ppermute(value, "tp", far_pairs)

    def pick_tile(size):
        return 512 if size % 512 == 0 else 768

    tokens = []

    def act(work, *inputs, sends=()):
        values = [*inputs, *[value for _, value in sends]]
        held = lax.optimization_barrier((*values, *tokens))[: len(values)]
        if sends:
            kinds = [kind for kind, _ in sends]
            result = work(*held[: len(inputs)], pushes=list(zip(kinds, held[len(inputs) :])))
        else:
            result = work(*held)
        tokens[:] = result if isinstance(result, tuple) else (result,)
        return result[0] if isinstance(result, tuple) and len(result) == 1 else result

    def swap(*sends):
        return act(lambda pushes: swap_call(*pushes), sends=sends)

    def pick(value, index):
        return lax.dynamic_index_in_dim(value, index, 0, keepdims=False)

    def place_tokens(value, got):
        keep = pick(value, far)
        return jnp.where(far == 0, keep, got), jnp.where(far == 0, got, keep)

    def join(left, right):
        return jnp.concatenate([left, right], axis=0)

    def plane_gather(pair):
        return lax.all_gather(pair, "fsdp", axis=0, tiled=True, axis_index_groups=plane_groups)

    def plane_scatter(grad):
        return lax.psum_scatter(
            grad, "fsdp", scatter_dimension=0, tiled=True, axis_index_groups=plane_groups
        )

    def gather_weight(key, local, *others):
        return plane_gather(act(lambda own, *got: core_pair(key, own, *got), local, *others))

    def halve(value):
        count = value.shape[0] // 2
        return value[:count], value[count:]

    def add_wide(left, right):
        return left.astype(jnp.float32) + right.astype(jnp.float32)

    def chained(value, *others):
        return lax.optimization_barrier((value, *others))[0]

    def scatter_gains(gains):
        for axis, size in (("fsdp", fsdp_count), ("tp", tp_count)):
            index = lax.axis_index(axis)
            step = size // 2
            while step >= 1:
                bit = (index // step) % 2
                parts = gains.reshape(gains.shape[0], 2, gains.shape[1] // 2)
                sent = lax.dynamic_index_in_dim(parts, 1 - bit, 1, keepdims=False)
                kept = lax.dynamic_index_in_dim(parts, bit, 1, keepdims=False)
                gains = kept + lax.ppermute(sent, axis, [(i, i ^ step) for i in range(size)])
                step //= 2
        return gains

    def wide_dot(left, right, pushes=()):
        return rows_matmul(
            [left], [right], dot_nn, [jnp.float32], pick_tile(right.shape[1]), pushes=pushes
        )

    def dot_bf16(left, right, pushes=()):
        return rows_matmul(
            [left], [right], dot_nn, [jnp.bfloat16], pick_tile(right.shape[1]), pushes=pushes
        )

    def grad_sum(left, right, left_next, right_next, pushes=()):
        chunk = pick_tile(right.shape[1])
        return sum_matmul(
            [left, left_next], [right, right_next], pick_tile(left.shape[1]),
            2 * chunk if right.shape[1] % (2 * chunk) == 0 else chunk, pushes=pushes,
        )

    def heads_back(grad, weight, pushes=()):
        return rows_matmul(
            [grad], [weight], dot_nt, [jnp.bfloat16], pick_tile(weight.shape[0]), pushes=pushes
        )

    def rms_pack(stream, gain):
        scale = rms_scale(stream)
        return scale, (stream * scale * gain).astype(jnp.bfloat16)

    qkv_local = qkv_weight.reshape(qkv_weight.shape[0], 3 * local_cols)
    gate_local, up_local = gate_up_weight[:, 0], gate_up_weight[:, 1]

    next_key[0] = 11
    position_got = swap_far(pick(doc_positions, 1 - far))
    first, second = place_tokens(doc_positions, position_got)
    near_both = swap_near(join(first, second))

    def first_norm(part):
        stream = part.astype(jnp.float32)
        return (stream, *rms_pack(stream, gain_one))

    s_own, r_own, n_own = act(lambda value: first_norm(pick(value, far)), block_in)
    near_own, qkv_other = swap(("near", n_own), ("far", qkv_local))
    qkv_full = gather_weight(4, qkv_local, qkv_other)
    first, second = (
        join(first, near_both[: first.shape[0]]), join(second, near_both[first.shape[0] :])
    )
    core_both = swap_core(join(first, second))

    def make_tables(first, second, both):
        count = first.shape[0]
        late = join(second, both[count:])
        return (*head_tables(join(first, both[:count])), *head_tables(late), late[:, None])

    c_own = pick(out_cotangent, far)
    stream_got, c_near_own, out_other = swap(
        ("far", pick(block_in, 1 - far)), ("near", c_own), ("far", out_weight)
    )
    out_full = gather_weight(3, out_weight, out_other)
    s_got, r_got, n_got = act(first_norm, stream_got)
    near_got, gate_other = swap(("near", n_got), ("far", gate_local))
    gate_full = gather_weight(5, gate_local, gate_other)
    h1_first, h1_second = act(core_gather_two, n_own, near_own, n_got, near_got)
    streams = [jnp.where(far == 0, s_own, s_got), jnp.where(far == 0, s_got, s_own)]
    scales_one = [jnp.where(far == 0, r_own, r_got), jnp.where(far == 0, r_got, r_own)]

    def attend_first(projected, pushes=()):
        arrays = [projected, projected, projected, *tables[0]]
        return attention_call(
            forward_first, arrays, [0, 1, 2, "table", "table"],
            ([0, 0, 0, 0, "lse"], heads_local), no_scratch, pushes,
        )

    def attend_second(projected, pushes=()):
        arrays = [projected, projected, projected, *tables[1], saved[0][1], saved[0][2], reach]
        return attention_call(
            forward_second, arrays, [0, 1, 2, "table", "table", 0, 0, "column"],
            ([0, 0, 0, 0, "lse"], heads_local), no_scratch, pushes,
        )

    up_other = swap_far(chained(up_local, gate_other))
    cos_first, sin_first, cos_second, sin_second, reach = act(
        make_tables, first, second, core_both
    )
    tables = [(cos_first, sin_first), (cos_second, sin_second)]
    projected = act(wide_dot, h1_first, qkv_full)
    results = act(attend_first, projected)
    saved, lses, mixed_first = [results[:3]], [results[4]], results[3]
    term_first = act(dot_bf16, mixed_first, out_full)
    keep_first, send_first = act(core_reduce, term_first)
    up_full = gather_weight(5, up_local, up_other)
    down_other = swap_far(chained(down_weight, up_other))
    projected, branch_first = act(
        wide_dot, h1_second, qkv_full, sends=[("near", send_first)]
    )

    def second_norm(stream, keep, got):
        middle = stream + keep + got.astype(jnp.float32)
        return (middle, *rms_pack(middle, gain_two))

    m_first, q_first, n_first = act(second_norm, streams[0], keep_first, branch_first)
    *results, near_first = act(attend_second, projected, sends=[("near", n_first)])
    saved.append(results[:3])
    lses.append(results[4])
    mixed_second = results[3]
    term_second = act(dot_bf16, mixed_second, out_full)
    keep_second, send_second = act(core_reduce, term_second)
    h2_first = act(core_gather, n_first, near_first)
    down_full_pair = act(lambda own, got: core_pair(6, own, got), down_weight, down_other)
    down_full = plane_gather(down_full_pair)
    c_got = swap_far(chained(pick(out_cotangent, 1 - far), down_full_pair))

    gate_first, branch_second = act(
        wide_dot, h2_first, gate_full, sends=[("near", send_second)]
    )
    m_second, q_second, n_second = act(second_norm, streams[1], keep_second, branch_second)

    def rise(hidden, weight, gate, pushes=()):
        return rows_matmul(
            [hidden], [weight], dot_nn, [jnp.float32, jnp.bfloat16], pick_tile(weight.shape[1]),
            finish=lambda up, gate: (up, gate * jax.nn.sigmoid(gate) * up), extras=[gate],
            pushes=pushes,
        )

    up_first, a_first, near_second = act(
        rise, h2_first, up_full, gate_first, sends=[("near", n_second)]
    )
    h2_second = act(core_gather, n_second, near_second)
    gate_second, c_near_got = act(
        wide_dot, h2_second, gate_full, sends=[("near", c_got)]
    )
    y_first, y_second = act(core_gather_two, c_own, c_near_own, c_got, c_near_got)
    c_first, c_second = jnp.where(far == 0, c_own, c_got), jnp.where(far == 0, c_got, c_own)
    up_second, a_second = act(rise, h2_second, up_full, gate_second)
    down_sum = plane_scatter(act(grad_sum, a_first, y_first, a_second, y_second))

    def fall_finish(act_grad, gate, up):
        sigmoid_gate = jax.nn.sigmoid(gate)
        return (
            act_grad * up * sigmoid_gate * (1.0 + gate * (1.0 - sigmoid_gate)),
            act_grad * (gate * sigmoid_gate),
        )

    def fall(cotangent, weight, gate, up):
        return rows_matmul(
            [cotangent], [weight], dot_nt, [jnp.bfloat16] * 2, pick_tile(weight.shape[0]),
            chunk=512, finish=fall_finish, extras=[gate, up],
        )

    dg_first, du_first = act(fall, y_first, down_full, gate_first, up_first)
    dg_second, du_second = act(fall, y_second, down_full, gate_second, up_second)
    gate_sum = plane_scatter(act(grad_sum, h2_first, dg_first, h2_second, dg_second))

    def hidden_grad(gate_grad, up_grad, gate_weight, up_weight, pushes=()):
        return rows_matmul(
            [gate_grad, up_grad], [gate_weight, up_weight], dot_nt, [jnp.bfloat16],
            pick_tile(gate_weight.shape[0]), pushes=pushes,
        )

    def second_back(middle, scale, keep, got, cotangent):
        grad, gain_term = norm_back(middle, scale, gain_two, keep + got.astype(jnp.float32))
        grad = cotangent.astype(jnp.float32) + grad
        return grad, grad.astype(jnp.bfloat16), gain_term

    term_first = act(hidden_grad, dg_first, du_first, gate_full, up_full)
    keep_first, send_first = act(core_reduce, term_first)
    term_second, back_first = act(
        hidden_grad, dg_second, du_second, gate_full, up_full, sends=[("near", send_first)]
    )
    keep_second, send_second = act(core_reduce, term_second)
    g_first, n_first, gain_two_first = act(
        second_back, m_first, q_first, keep_first, back_first, c_first
    )
    down_mine, down_away = act(lambda pair: core_split(10, pair), down_sum)
    down_got = swap_far(down_away)
    grad_up, back_second = act(
        grad_sum, h2_first, du_first, h2_second, du_second, sends=[("near", send_second)]
    )
    up_sum = plane_scatter(grad_up)
    mlp_first, near_first = act(dot_bf16, a_first, down_full, sends=[("near", n_first)])
    g_second, n_second, gain_two_second = act(
        second_back, m_second, q_second, keep_second, back_second, c_second
    )
    d_first = act(core_gather, n_first, near_first)

    gate_mine, gate_away = act(lambda pair: core_split(9, pair), gate_sum)
    gate_got = swap_far(gate_away)
    mlp_second, near_second = act(dot_bf16, a_second, down_full, sends=[("near", n_second)])
    mlp_keep_first, mlp_send_first = act(core_reduce, mlp_first)
    heads_first = act(heads_back, d_first, out_full)
    d_second = act(core_gather, n_second, near_second)
    heads_second = act(heads_back, d_second, out_full)
    mlp_keep_second, mlp_send_second = act(core_reduce, mlp_second)
    grad_out, mlp_branch_first = act(
        grad_sum, mixed_first, d_first, mixed_second, d_second, sends=[("near", mlp_send_first)]
    )
    out_sum = plane_scatter(grad_out)
    up_mine, up_away = act(lambda pair: core_split(9, pair), up_sum)

    def attend_back(heads_first, heads_second, pushes=()):
        return attention_call(
            backward_both,
            [
                *saved[0], *saved[1], heads_first, heads_second, *lses,
                *tables[0], *tables[1], reach,
            ],
            [0] * 8 + ["lse"] * 2 + ["table"] * 4 + ["column"],
            ([0] * 6, heads_local),
            backward_scratch,
            pushes,
        )

    up_got = swap_far(up_away)
    *grads, mlp_branch_second = act(
        attend_back, heads_first, heads_second, sends=[("near", mlp_send_second)]
    )
    p_first, p_second = act(
        lambda *parts: (
            jnp.concatenate(parts[:3], axis=1),
            jnp.concatenate(parts[3:], axis=1),
        ),
        *grads,
    )

    def finish_output(first, first_keep, first_got, second, second_keep, second_got):
        first = (first + first_keep + first_got.astype(jnp.float32)).astype(jnp.bfloat16)
        second = (second + second_keep + second_got.astype(jnp.float32)).astype(jnp.bfloat16)
        return jnp.where(far == 0, first, second), jnp.where(far == 0, second, first)

    out_keep, out_send = act(
        finish_output,
        m_first, mlp_keep_first, mlp_branch_first, m_second, mlp_keep_second, mlp_branch_second,
    )
    out_got = swap_far(out_send)
    term_first = act(heads_back, p_first, qkv_full)
    keep_first, send_first = act(core_reduce, term_first)
    grad_qkv, back_first = act(
        grad_sum, h1_first, p_first, h1_second, p_second, sends=[("near", send_first)]
    )
    qkv_sum = plane_scatter(grad_qkv)
    term_second = act(heads_back, p_second, qkv_full)
    keep_second, send_second = act(core_reduce, term_second)
    out_mine, out_away = act(lambda pair: core_split(8, pair), out_sum)
    def settle(keep, got):
        return jnp.stack([jnp.where(far == 0, keep, got), jnp.where(far == 0, got, keep)])

    def first_back(stream, scale, keep, got, grad):
        back, gain_term = norm_back(stream, scale, gain_one, keep + got.astype(jnp.float32))
        return grad + back, gain_term

    def last_back(stream, scale, keep, got, grad, first):
        second, gain_term = first_back(stream, scale, keep, got, grad)
        return (
            jnp.where(far == 0, first, second),
            jnp.where(far == 0, second, first).astype(jnp.bfloat16),
            gain_term,
        )

    back_second, out_back = swap(("near", send_second), ("far", out_away))
    i_first, gain_one_first = act(
        first_back, streams[0], scales_one[0], keep_first, back_first, g_first
    )
    in_keep, in_send, gain_one_second = act(
        last_back, streams[1], scales_one[1], keep_second, back_second, g_second, i_first
    )
    in_got = swap_far(in_send)
    down_owned = act(add_wide, down_mine, down_got)
    gate_owned = act(add_wide, gate_mine, gate_got)
    block_out = act(settle, out_keep, out_got)
    up_owned = act(add_wide, up_mine, up_got)
    gate_up_owned = act(lambda a, b: jnp.stack([a, b], axis=1), gate_owned, up_owned)
    out_owned = act(add_wide, out_mine, out_back)
    gains = scatter_gains(
        jnp.stack([gain_one_first + gain_one_second, gain_two_first + gain_two_second])
    )
    in_grad = act(lambda keep, got: settle(keep, got.astype(jnp.float32)), in_keep, in_got)
    qkv_mine, qkv_away = act(lambda pair: core_split(0, pair), qkv_sum)
    qkv_back = swap(("far", qkv_away))
    qkv_owned = act(add_wide, qkv_mine, qkv_back)
    return (
        block_out,
        in_grad,
        gains[0],
        qkv_owned.reshape(qkv_weight.shape),
        out_owned,
        gains[1],
        gate_up_owned,
        down_owned,
    )


def solution(mesh):
    sizes = (mesh.shape["fsdp"], mesh.shape["tp"])
    body = paired_device if sizes == (8, 4) else per_device
    in_specs = (
        P("fsdp", "tp", None),
        P("fsdp", "tp", None),
        P("fsdp", "tp"),
        P("fsdp", "tp"),
        P(),
        P("fsdp", None, "tp"),
        P(("tp", "fsdp"), None),
        P(),
        P("fsdp", None, "tp"),
        P(("tp", "fsdp"), None),
    )
    out_specs = (
        P("fsdp", "tp", None),
        P("fsdp", "tp", None),
        P(("fsdp", "tp")),
        P("fsdp", None, "tp"),
        P(("tp", "fsdp"), None),
        P(("fsdp", "tp")),
        P("fsdp", None, "tp"),
        P(("tp", "fsdp"), None),
    )
    return jax.shard_map(
        body, mesh=mesh, in_specs=in_specs, out_specs=out_specs, check_vma=False
    )
```

```python
import functools

import jax
import jax.numpy as jnp
from jax import lax
from jax.experimental import pallas as pl
from jax.experimental.pallas import tpu as pltpu
from jax.sharding import PartitionSpec as P

D = 3072
HD = 96


rms_epsilon = 1e-05
rope_theta = 10000.0
masked_score = -1e30
LOG2E = 1.4426950408889634


def rope_tables(positions, head_size):
    half_width = head_size // 2
    frequency = rope_theta ** (-(jnp.arange(half_width, dtype=jnp.float32) * 2.0 / head_size))
    angles = positions.astype(jnp.float32)[:, None] * frequency[None, :]
    return (jnp.cos(angles)[:, None, :], jnp.sin(angles)[:, None, :])


def rotate(values, cosine_part, sine_part):
    half_width = values.shape[-1] // 2
    lead_half = values[..., :half_width]
    tail_half = values[..., half_width:]
    return jnp.concatenate(
        [
            lead_half * cosine_part - tail_half * sine_part,
            tail_half * cosine_part + lead_half * sine_part,
        ],
        axis=-1,
    )


def unrotate(values, cosine_part, sine_part):
    half_width = values.shape[-1] // 2
    lead_half = values[..., :half_width]
    tail_half = values[..., half_width:]
    return jnp.concatenate(
        [
            lead_half * cosine_part + tail_half * sine_part,
            tail_half * cosine_part - lead_half * sine_part,
        ],
        axis=-1,
    )


def rms_scale(stream):
    return lax.rsqrt(jnp.mean(stream * stream, axis=-1, keepdims=True) + rms_epsilon)


def norm_back(stream, scale_rows, gain_vec, grad_rows):
    gained_grad = gain_vec * grad_rows
    input_grad = scale_rows * gained_grad - stream * scale_rows**3 * jnp.mean(
        gained_grad * stream, axis=-1, keepdims=True
    )
    return (input_grad, jnp.sum(grad_rows * stream * scale_rows, axis=0))


def allowed_mask(segment_tile, index_tile, segments):
    columns = jnp.arange(segments.shape[0], dtype=jnp.int32)
    return (segment_tile[:, None] == segments[None, :]) & (index_tile[:, None] >= columns[None, :])


def masked_scores(query_tile, key_rows, segment_tile, index_tile, segments, scale_value):
    scores = (
        jnp.einsum("qhd,khd->hqk", query_tile, key_rows, preferred_element_type=jnp.float32)
        * scale_value
    )
    return jnp.where(allowed_mask(segment_tile, index_tile, segments)[None], scores, masked_score)


def attention_forward(queries, key_rows, value_rows, segments, block_rows):
    seq_len, head_count, head_size = queries.shape
    tiles = seq_len // block_rows
    scale_value = head_size ** (-0.5)
    positions = jnp.arange(seq_len, dtype=jnp.int32)

    def query_block(packed):
        query_tile, segment_tile, index_tile = packed
        scores = masked_scores(
            query_tile, key_rows, segment_tile, index_tile, segments, scale_value
        )
        row_max = jnp.max(scores, axis=-1, keepdims=True)
        exponent = jnp.exp(scores - row_max)
        row_total = jnp.sum(exponent, axis=-1, keepdims=True)
        probs_low = (exponent / row_total).astype(jnp.bfloat16)
        mixed = jnp.einsum(
            "hqk,khd->qhd", probs_low, value_rows, preferred_element_type=jnp.float32
        )
        return (mixed, (row_max + jnp.log(row_total))[..., 0])

    mixed, log_total = lax.map(
        query_block,
        (
            queries.reshape(tiles, block_rows, head_count, head_size),
            segments.reshape(tiles, block_rows),
            positions.reshape(tiles, block_rows),
        ),
    )
    return (mixed.reshape(seq_len, head_count * head_size), log_total)


def attention_backward(queries, key_rows, value_rows, segments, log_total, out_grad, block_rows):
    seq_len, head_count, head_size = queries.shape
    tiles = seq_len // block_rows
    scale_value = head_size ** (-0.5)
    positions = jnp.arange(seq_len, dtype=jnp.int32)

    def query_block(carry, packed):
        key_acc, value_acc = carry
        query_tile, segment_tile, index_tile, total_tile, grad_tile = packed
        scores = masked_scores(
            query_tile, key_rows, segment_tile, index_tile, segments, scale_value
        )
        probs = jnp.exp(scores - total_tile[..., None])
        probs_low = probs.astype(jnp.bfloat16)
        prob_grad = jnp.einsum(
            "qhd,khd->hqk", grad_tile, value_rows, preferred_element_type=jnp.float32
        )
        score_grad = (
            probs * (prob_grad - jnp.sum(probs * prob_grad, axis=-1, keepdims=True))
        ).astype(jnp.bfloat16)
        query_grad = (
            jnp.einsum("hqk,khd->qhd", score_grad, key_rows, preferred_element_type=jnp.float32)
            * scale_value
        )
        key_acc = (
            key_acc
            + jnp.einsum("hqk,qhd->khd", score_grad, query_tile, preferred_element_type=jnp.float32)
            * scale_value
        )
        value_acc = value_acc + jnp.einsum(
            "hqk,qhd->khd", probs_low, grad_tile, preferred_element_type=jnp.float32
        )
        return ((key_acc, value_acc), query_grad)

    start_acc = (jnp.zeros(queries.shape, jnp.float32), jnp.zeros(queries.shape, jnp.float32))
    (key_grad, value_grad), query_grad = lax.scan(
        query_block,
        start_acc,
        (
            queries.reshape(tiles, block_rows, head_count, head_size),
            segments.reshape(tiles, block_rows),
            positions.reshape(tiles, block_rows),
            log_total,
            out_grad.reshape(tiles, block_rows, head_count, head_size),
        ),
    )
    return (query_grad.reshape(seq_len, head_count, head_size), key_grad, value_grad)


def gather_attention(qkv_weight, out_weight):
    return (
        lax.all_gather(qkv_weight, "fsdp", axis=0, tiled=True),
        lax.all_gather(out_weight, "fsdp", axis=0, tiled=True),
    )


def gather_feedforward(gate_up_weight, down_weight):
    return (
        lax.all_gather(gate_up_weight, "fsdp", axis=0, tiled=True),
        lax.all_gather(down_weight, "fsdp", axis=0, tiled=True),
    )


def per_device(
    block_in,
    out_cotangent,
    segment_ids,
    doc_positions,
    norm1_gain,
    qkv_weight,
    out_weight,
    norm2_gain,
    gate_up_weight,
    down_weight,
):
    micro_count = block_in.shape[0]
    fsdp_count = lax.axis_size("fsdp")
    segment_full, position_full = (
        lax.all_gather(segment_ids, "tp", axis=1, tiled=True),
        lax.all_gather(doc_positions, "tp", axis=1, tiled=True),
    )
    seq_len = segment_full.shape[1]
    block_rows = min(seq_len, 512)
    gain_one = norm1_gain.astype(jnp.float32)
    gain_two = norm2_gain.astype(jnp.float32)
    local_cols = qkv_weight.shape[2]
    local_units = gate_up_weight.shape[2]
    heads_local = local_cols // HD
    grad_qkv = jnp.zeros((D, 3, local_cols), jnp.float32)
    grad_out = jnp.zeros((out_weight.shape[0] * fsdp_count, D), jnp.float32)
    grad_gate_up = jnp.zeros((D, 2, local_units), jnp.float32)
    grad_down = jnp.zeros((down_weight.shape[0] * fsdp_count, D), jnp.float32)
    gain_one_acc = jnp.zeros((D,), jnp.float32)
    gain_two_acc = jnp.zeros((D,), jnp.float32)
    outputs = []
    input_grads = []
    for micro_index in range(micro_count):
        weights_fwd = (
            gather_attention(qkv_weight, out_weight),
            gather_feedforward(gate_up_weight, down_weight),
        )
        (qkv_full, out_full), (gate_up_full, down_full) = weights_fwd
        stream = block_in[micro_index].astype(jnp.float32)
        segment_row = segment_full[micro_index]
        cosine_part, sine_part = rope_tables(position_full[micro_index], HD)
        scale_one = rms_scale(stream)
        normed_one = (stream * scale_one * gain_one).astype(jnp.bfloat16)
        normed_one_full = lax.all_gather(normed_one, "tp", axis=0, tiled=True)
        projected = jnp.einsum(
            "sd,dtc->stc", normed_one_full, qkv_full, preferred_element_type=jnp.float32
        )
        queries = rotate(
            projected[:, 0].reshape(seq_len, heads_local, HD), cosine_part, sine_part
        ).astype(jnp.bfloat16)
        key_rows = rotate(
            projected[:, 1].reshape(seq_len, heads_local, HD), cosine_part, sine_part
        ).astype(jnp.bfloat16)
        value_rows = projected[:, 2].reshape(seq_len, heads_local, HD).astype(jnp.bfloat16)
        mixed, log_total = attention_forward(queries, key_rows, value_rows, segment_row, block_rows)
        attn_heads = mixed.astype(jnp.bfloat16)
        attn_term = jnp.dot(attn_heads, out_full, preferred_element_type=jnp.float32)
        attn_branch = lax.psum_scatter(attn_term, "tp", scatter_dimension=0, tiled=True)
        middle = stream + attn_branch
        scale_two = rms_scale(middle)
        normed_two = (middle * scale_two * gain_two).astype(jnp.bfloat16)
        normed_two_full = lax.all_gather(normed_two, "tp", axis=0, tiled=True)
        gate_up = jnp.einsum(
            "sd,dtf->stf", normed_two_full, gate_up_full, preferred_element_type=jnp.float32
        )
        gate_rows = gate_up[:, 0]
        up_rows = gate_up[:, 1]
        sigmoid_gate = jax.nn.sigmoid(gate_rows)
        silu_gate = gate_rows * sigmoid_gate
        activated = (silu_gate * up_rows).astype(jnp.bfloat16)
        mlp_term = jnp.dot(activated, down_full, preferred_element_type=jnp.float32)
        mlp_branch = lax.psum_scatter(
            mlp_term.astype(jnp.bfloat16), "tp", scatter_dimension=0, tiled=True
        ).astype(jnp.float32)
        outputs.append((middle + mlp_branch).astype(jnp.bfloat16))
        (qkv_back, out_back), (gate_up_back, down_back) = weights_fwd
        cotangent = out_cotangent[micro_index].astype(jnp.float32)
        cotangent_full = lax.all_gather(out_cotangent[micro_index], "tp", axis=0, tiled=True)
        grad_down = grad_down + jnp.einsum(
            "sf,sd->fd", activated, cotangent_full, preferred_element_type=jnp.float32
        )
        act_grad = jnp.einsum(
            "sd,fd->sf", cotangent_full, down_back, preferred_element_type=jnp.float32
        )
        gate_grad = act_grad * up_rows * sigmoid_gate * (1.0 + gate_rows * (1.0 - sigmoid_gate))
        up_grad = act_grad * silu_gate
        gate_up_grad = jnp.stack([gate_grad, up_grad], axis=1).astype(jnp.bfloat16)
        grad_gate_up = grad_gate_up + jnp.einsum(
            "sd,stf->dtf", normed_two_full, gate_up_grad, preferred_element_type=jnp.float32
        )
        normed_two_term = jnp.einsum(
            "stf,dtf->sd", gate_up_grad, gate_up_back, preferred_element_type=jnp.float32
        )
        normed_two_grad = lax.psum_scatter(normed_two_term, "tp", scatter_dimension=0, tiled=True)
        middle_back, gain_two_term = norm_back(middle, scale_two, gain_two, normed_two_grad)
        gain_two_acc = gain_two_acc + gain_two_term
        middle_grad = cotangent + middle_back
        attn_grad_full = lax.all_gather(middle_grad.astype(jnp.bfloat16), "tp", axis=0, tiled=True)
        grad_out = grad_out + jnp.einsum(
            "sc,sd->cd", attn_heads, attn_grad_full, preferred_element_type=jnp.float32
        )
        heads_grad = jnp.einsum(
            "sd,cd->sc", attn_grad_full, out_back, preferred_element_type=jnp.float32
        ).astype(jnp.bfloat16)
        query_grad, key_grad, value_grad = attention_backward(
            queries,
            key_rows,
            value_rows,
            segment_row,
            log_total,
            heads_grad.reshape(seq_len, heads_local, HD),
            block_rows,
        )
        projected_grad = jnp.stack(
            [
                unrotate(query_grad, cosine_part, sine_part).reshape(seq_len, local_cols),
                unrotate(key_grad, cosine_part, sine_part).reshape(seq_len, local_cols),
                value_grad.reshape(seq_len, local_cols),
            ],
            axis=1,
        ).astype(jnp.bfloat16)
        grad_qkv = grad_qkv + jnp.einsum(
            "sd,stc->dtc", normed_one_full, projected_grad, preferred_element_type=jnp.float32
        )
        normed_one_term = jnp.einsum(
            "stc,dtc->sd", projected_grad, qkv_back, preferred_element_type=jnp.float32
        )
        normed_one_grad = lax.psum_scatter(
            normed_one_term.astype(jnp.bfloat16), "tp", scatter_dimension=0, tiled=True
        ).astype(jnp.float32)
        stream_back, gain_one_term = norm_back(stream, scale_one, gain_one, normed_one_grad)
        gain_one_acc = gain_one_acc + gain_one_term
        input_grads.append(middle_grad + stream_back)
    owned_grads = (
        lax.psum_scatter(
            grad_qkv.astype(jnp.bfloat16), "fsdp", scatter_dimension=0, tiled=True
        ).astype(jnp.float32),
        lax.psum_scatter(
            grad_out.astype(jnp.bfloat16), "fsdp", scatter_dimension=0, tiled=True
        ).astype(jnp.float32),
        lax.psum_scatter(
            grad_gate_up.astype(jnp.bfloat16), "fsdp", scatter_dimension=0, tiled=True
        ).astype(jnp.float32),
        lax.psum_scatter(
            grad_down.astype(jnp.bfloat16), "fsdp", scatter_dimension=0, tiled=True
        ).astype(jnp.float32),
    )
    owned_gains = (
        lax.psum_scatter(gain_one_acc, ("fsdp", "tp"), scatter_dimension=0, tiled=True),
        lax.psum_scatter(gain_two_acc, ("fsdp", "tp"), scatter_dimension=0, tiled=True),
    )
    return (
        jnp.stack(outputs),
        jnp.stack(input_grads),
        owned_gains[0],
        owned_grads[0],
        owned_grads[1],
        owned_gains[1],
        owned_grads[2],
        owned_grads[3],
    )


HEAD_GROUP = 4
FIRST_DOC = 800


def dot_nt(left, right):
    return lax.dot_general(left, right, (((1,), (1,)), ((), ())), preferred_element_type=jnp.float32)


def dot_tn(left, right):
    return lax.dot_general(left, right, (((0,), (0,)), ((), ())), preferred_element_type=jnp.float32)


def dot_nn(left, right):
    return lax.dot_general(left, right, (((1,), (0,)), ((), ())), preferred_element_type=jnp.float32)


def swap_halves(values):
    lanes = lax.broadcasted_iota(jnp.int32, values.shape, 1)
    width = values.shape[1]
    return jnp.where(
        lanes % HD < HD // 2,
        pltpu.roll(values, width - HD // 2, 1),
        pltpu.roll(values, HD // 2, 1),
    )


def causal_mask(rows, columns):
    row_ids = lax.broadcasted_iota(jnp.int32, (rows, columns), 0)
    column_ids = lax.broadcasted_iota(jnp.int32, (rows, columns), 1)
    return row_ids >= column_ids


def tail_mask(reach):
    rows = reach.shape[0]
    row_ids = lax.broadcasted_iota(jnp.int32, (rows, rows), 0)
    column_ids = lax.broadcasted_iota(jnp.int32, (rows, rows), 1)
    return (row_ids >= column_ids) & (row_ids - column_ids <= reach)


def halves(quarter):
    first = lax.axis_index("tp") % 2
    return (
        pl.multiple_of(first * quarter, quarter),
        pl.multiple_of((1 - first) * quarter, quarter),
    )


def widen(table):
    return jnp.concatenate([table] * HEAD_GROUP, axis=1)


def load_rotated(offsets, quarter, q_ref, k_ref, v_ref, cos_ref, sin_ref, qr_ref, kr_ref, vr_ref):
    for place, offset in enumerate(offsets):
        rows = pl.ds(offset, quarter)
        target = pl.ds(place * quarter, quarter)
        cosine, sine = widen(cos_ref[rows, :]), widen(sin_ref[rows, :])
        q_raw, k_raw = q_ref[rows, :], k_ref[rows, :]
        qr_ref[target, :] = (q_raw * cosine + swap_halves(q_raw) * sine).astype(jnp.bfloat16)
        kr_ref[target, :] = (k_raw * cosine + swap_halves(k_raw) * sine).astype(jnp.bfloat16)
        vr_ref[target, :] = v_ref[rows, :].astype(jnp.bfloat16)


def softmax_mix(query, pieces, factor):
    scores = []
    for keys, _, mask in pieces:
        score = dot_nt(query, keys)
        scores.append(score if mask is None else jnp.where(mask, score, masked_score))
    top = functools.reduce(jnp.maximum, [jnp.max(s, axis=-1, keepdims=True) for s in scores])
    weights = [jnp.exp2((s - top) * factor) for s in scores]
    total = functools.reduce(jnp.add, [jnp.sum(w, axis=-1, keepdims=True) for w in weights])
    inverse = 1.0 / total
    mixed = functools.reduce(
        jnp.add,
        [dot_nn((w * inverse).astype(jnp.bfloat16), piece[1]) for w, piece in zip(weights, pieces)],
    )
    return mixed, top * factor + jnp.log2(total)


def head_slice(head):
    return slice(head * HD, (head + 1) * HD)


def forward_first(
    q_ref, k_ref, v_ref, cos_ref, sin_ref, qr_ref, kr_ref, vr_ref, o_ref, lse_ref
):
    half = q_ref.shape[0]
    quarter = half // 2
    offsets = halves(quarter)
    load_rotated(offsets, quarter, q_ref, k_ref, v_ref, cos_ref, sin_ref, qr_ref, kr_ref, vr_ref)
    factor = HD ** (-0.5) * LOG2E
    mask = causal_mask(quarter, quarter)
    for head in range(HEAD_GROUP):
        cols = head_slice(head)
        early, late = slice(0, quarter), slice(quarter, half)
        k_early, v_early = kr_ref[early, cols], vr_ref[early, cols]
        mixed, lse = softmax_mix(qr_ref[early, cols], [(k_early, v_early, mask)], factor)
        o_ref[pl.ds(offsets[0], quarter), cols] = mixed.astype(jnp.bfloat16)
        lse_ref[0, early, head : head + 1] = lse
        mixed, lse = softmax_mix(
            qr_ref[late, cols],
            [(k_early, v_early, None), (kr_ref[late, cols], vr_ref[late, cols], mask)],
            factor,
        )
        o_ref[pl.ds(offsets[1], quarter), cols] = mixed.astype(jnp.bfloat16)
        lse_ref[0, late, head : head + 1] = lse


def forward_second(
    q_ref, k_ref, v_ref, cos_ref, sin_ref, ka_ref, va_ref, pos_ref,
    qr_ref, kr_ref, vr_ref, o_ref, lse_ref,
):
    half = q_ref.shape[0]
    quarter = half // 2
    cut = FIRST_DOC - half
    spill = cut - quarter
    offsets = halves(quarter)
    load_rotated(offsets, quarter, q_ref, k_ref, v_ref, cos_ref, sin_ref, qr_ref, kr_ref, vr_ref)
    factor = HD ** (-0.5) * LOG2E
    mask = causal_mask(cut, cut)
    mask_tail = tail_mask(pos_ref[pl.ds(offsets[1] + spill, half - cut), :])
    for head in range(HEAD_GROUP):
        cols = head_slice(head)
        early, late = slice(0, cut), slice(cut, half)
        mixed, lse = softmax_mix(
            qr_ref[early, cols],
            [
                (ka_ref[:, cols], va_ref[:, cols], None),
                (kr_ref[early, cols], vr_ref[early, cols], mask),
            ],
            factor,
        )
        low = mixed.astype(jnp.bfloat16)
        o_ref[pl.ds(offsets[0], quarter), cols] = low[:quarter]
        o_ref[pl.ds(offsets[1], spill), cols] = low[quarter:]
        lse_ref[0, early, head : head + 1] = lse
        mixed, lse = softmax_mix(
            qr_ref[late, cols], [(kr_ref[late, cols], vr_ref[late, cols], mask_tail)], factor
        )
        o_ref[pl.ds(offsets[1] + spill, half - cut), cols] = mixed.astype(jnp.bfloat16)
        lse_ref[0, late, head : head + 1] = lse


def backward_both(
    qa_ref, ka_ref, va_ref, qb_ref, kb_ref, vb_ref, ga_ref, gb_ref, la_ref, lb_ref,
    cosa_ref, sina_ref, cosb_ref, sinb_ref, pos_ref,
    dqa_ref, dka_ref, dva_ref, dqb_ref, dkb_ref, dvb_ref,
    go_a, go_b, tqa, tka, tva, tqb, tkb, tvb,
):
    half = qa_ref.shape[0]
    quarter = half // 2
    cut = FIRST_DOC - half
    spill = cut - quarter
    offsets = halves(quarter)
    scale_value = HD ** (-0.5)
    factor = scale_value * LOG2E
    for place, offset in enumerate(offsets):
        target, rows = pl.ds(place * quarter, quarter), pl.ds(offset, quarter)
        go_a[target, :] = ga_ref[rows, :]
        go_b[target, :] = gb_ref[rows, :]
    mask = causal_mask(quarter, quarter)
    mask_cut = causal_mask(cut, cut)
    mask_tail = tail_mask(pos_ref[pl.ds(offsets[1] + spill, half - cut), :])
    for accumulator in (tka, tva, tkb, tvb):
        accumulator[...] = jnp.zeros_like(accumulator)

    def attend(query, grad, lse, pieces):
        weights, weight_grads = [], []
        for k_ref, v_ref, rows, cols, mask, _, _ in pieces:
            weight = jnp.exp2(dot_nt(query, k_ref[rows, cols]) * factor - lse)
            weights.append(weight if mask is None else jnp.where(mask, weight, 0.0))
            weight_grads.append(dot_nt(grad, v_ref[rows, cols]))
        shared = functools.reduce(
            jnp.add,
            [jnp.sum(w * g, axis=-1, keepdims=True) for w, g in zip(weights, weight_grads)],
        )
        query_grad = None
        for weight, weight_grad, piece in zip(weights, weight_grads, pieces):
            k_ref, v_ref, rows, cols, _, tk, tv = piece
            score_grad = (weight * (weight_grad - shared)).astype(jnp.bfloat16)
            term = dot_nn(score_grad, k_ref[rows, cols])
            query_grad = term if query_grad is None else query_grad + term
            tk[rows, cols] += dot_tn(score_grad, query)
            tv[rows, cols] += dot_tn(weight.astype(jnp.bfloat16), grad)
        return query_grad

    for head in range(HEAD_GROUP):
        cols = head_slice(head)
        lane = slice(head, head + 1)
        early, late, whole = slice(0, quarter), slice(quarter, half), slice(0, half)
        tqa[early, cols] = attend(
            qa_ref[early, cols], go_a[early, cols], la_ref[0, early, lane],
            [(ka_ref, va_ref, early, cols, mask, tka, tva)],
        )
        tqa[late, cols] = attend(
            qa_ref[late, cols], go_a[late, cols], la_ref[0, late, lane],
            [
                (ka_ref, va_ref, early, cols, None, tka, tva),
                (ka_ref, va_ref, late, cols, mask, tka, tva),
            ],
        )
        early, late = slice(0, cut), slice(cut, half)
        tqb[early, cols] = attend(
            qb_ref[early, cols], go_b[early, cols], lb_ref[0, early, lane],
            [
                (ka_ref, va_ref, whole, cols, None, tka, tva),
                (kb_ref, vb_ref, early, cols, mask_cut, tkb, tvb),
            ],
        )
        tqb[late, cols] = attend(
            qb_ref[late, cols], go_b[late, cols], lb_ref[0, late, lane],
            [(kb_ref, vb_ref, late, cols, mask_tail, tkb, tvb)],
        )
    for place, offset in enumerate(offsets):
        source, rows = pl.ds(place * quarter, quarter), pl.ds(offset, quarter)
        for total, cos_ref, sin_ref, out_ref in (
            (tqa, cosa_ref, sina_ref, dqa_ref),
            (tka, cosa_ref, sina_ref, dka_ref),
            (tqb, cosb_ref, sinb_ref, dqb_ref),
            (tkb, cosb_ref, sinb_ref, dkb_ref),
        ):
            grad = total[source, :] * scale_value
            out_ref[rows, :] = (
                grad * widen(cos_ref[rows, :]) - swap_halves(grad) * widen(sin_ref[rows, :])
            ).astype(jnp.bfloat16)
        dva_ref[rows, :] = tva[source, :].astype(jnp.bfloat16)
        dvb_ref[rows, :] = tvb[source, :].astype(jnp.bfloat16)


COST_SCALE = 1.7


def cost_of(flops):
    return pl.CostEstimate(flops=int(COST_SCALE * flops), bytes_accessed=1000, transcendentals=0)


def rows_kernel(pairs, extra_count, dot, chunk, finish, *refs):
    lefts, weights = refs[:pairs], refs[pairs : 2 * pairs]
    extras = refs[2 * pairs : 2 * pairs + extra_count]
    outs = refs[2 * pairs + extra_count :]

    @pl.loop(0, outs[0].shape[0] // chunk)
    def _(step):
        rows = pl.ds(pl.multiple_of(step * chunk, chunk), chunk)
        total = None
        for left, weight in zip(lefts, weights):
            term = dot(left[rows, :], weight[...])
            total = term if total is None else total + term
        for out, value in zip(outs, finish(total, *[extra[rows, :] for extra in extras])):
            out[rows, :] = value.astype(out.dtype)


def keep_one(total):
    return (total,)


def rows_matmul(
    lefts, weights, dot, types, tile, chunk=1024, finish=keep_one, extras=(), pushes=()
):
    rows = lefts[0].shape[0]
    if dot is dot_nn:
        width = weights[0].shape[1]
        weight_specs = [pl.BlockSpec((w.shape[0], tile), lambda j: (0, j)) for w in weights]
    else:
        width = weights[0].shape[0]
        weight_specs = [pl.BlockSpec((tile, w.shape[1]), lambda j: (j, 0)) for w in weights]
    column = pl.BlockSpec((rows, tile), lambda j: (0, j))
    return grid_call(
        functools.partial(rows_kernel, len(lefts), len(extras), dot, min(chunk, rows), finish),
        [*lefts, *weights, *extras],
        [pl.BlockSpec(left.shape, lambda j: (0, 0)) for left in lefts]
        + weight_specs
        + [column] * len(extras),
        [jax.ShapeDtypeStruct((rows, width), kind) for kind in types],
        [column] * len(types),
        (width // tile,),
        2 * rows * width * sum(left.shape[1] for left in lefts),
        pushes=pushes,
    )


def sum_kernel(parts, chunk, *refs):
    lefts, rights, out = refs[:parts], refs[parts : 2 * parts], refs[-1]

    @pl.loop(0, out.shape[1] // chunk)
    def _(step):
        cols = pl.ds(pl.multiple_of(step * chunk, chunk), chunk)
        total = None
        for left, right in zip(lefts, rights):
            term = dot_tn(left[...], right[:, cols])
            total = term if total is None else total + term
        out[:, cols] = total.astype(out.dtype)


def sum_matmul(lefts, rights, tile, chunk, pushes=()):
    rows, height = lefts[0].shape
    width = rights[0].shape[1]
    return grid_call(
        functools.partial(sum_kernel, len(lefts), chunk),
        [*lefts, *rights],
        [pl.BlockSpec((rows, tile), lambda j: (0, j)) for _ in lefts]
        + [pl.BlockSpec((rows, width), lambda j: (0, 0)) for _ in rights],
        [jax.ShapeDtypeStruct((height, width), jnp.bfloat16)],
        [pl.BlockSpec((tile, width), lambda j: (j, 0))],
        (height // tile,),
        2 * rows * height * width * len(lefts),
        pushes=pushes,
    )


def partner_of(kind):
    index, place = lax.axis_index("fsdp"), lax.axis_index("tp")
    if kind == "near":
        return (index, place + 1 - 2 * (place % 2))
    return (index, place + 2 - 4 * (place // 2))


def start_pushes(kinds, sources, targets, send, receive):
    barrier = pltpu.get_barrier_semaphore()
    names = sorted(set(kinds))
    for kind in names:
        pl.semaphore_signal(
            barrier, inc=1, device_id=partner_of(kind), device_id_type=pl.DeviceIdType.MESH
        )
    pl.semaphore_wait(barrier, len(names))
    for place, kind in enumerate(kinds):
        push(
            sources[place], targets[place], send.at[place], receive.at[place], partner_of(kind)
        ).start()


def wait_pushes(kinds, sources, targets, send, receive):
    for place, kind in enumerate(kinds):
        push(
            sources[place], targets[place], send.at[place], receive.at[place], partner_of(kind)
        ).wait()


def pushing_kernel(kernel, axes, in_count, out_count, kinds, *refs):
    count = len(kinds)
    inputs, sources = refs[:in_count], refs[in_count : in_count + count]
    outs = refs[in_count + count : in_count + count + out_count]
    targets = refs[in_count + count + out_count : in_count + 2 * count + out_count]
    scratch, (send, receive) = refs[in_count + 2 * count + out_count : -2], refs[-2:]
    first = functools.reduce(jnp.logical_and, [pl.program_id(axis) == 0 for axis in range(axes)])
    last = functools.reduce(
        jnp.logical_and,
        [pl.program_id(axis) == pl.num_programs(axis) - 1 for axis in range(axes)],
    )

    @pl.when(first)
    def _():
        start_pushes(kinds, sources, targets, send, receive)

    kernel(*inputs, *outs, *scratch)

    @pl.when(last)
    def _():
        wait_pushes(kinds, sources, targets, send, receive)


def grid_call(
    kernel, operands, in_specs, outs, out_specs, grid, flops, scratch=(), pushes=(), vmem=60
):
    params = dict(
        dimension_semantics=("arbitrary",) * len(grid), vmem_limit_bytes=vmem * 1024 * 1024
    )
    operands, in_specs, outs = list(operands), list(in_specs), list(outs)
    out_specs, scratch = list(out_specs), list(scratch)
    if pushes:
        kinds = tuple(kind for kind, _ in pushes)
        kernel = functools.partial(
            pushing_kernel, kernel, len(grid), len(operands), len(outs), kinds
        )
        anywhere = [pl.BlockSpec(memory_space=pl.ANY)] * len(pushes)
        operands += [value for _, value in pushes]
        in_specs += anywhere
        outs += [jax.ShapeDtypeStruct(value.shape, value.dtype) for _, value in pushes]
        out_specs += anywhere
        scratch += [pltpu.SemaphoreType.DMA((len(pushes),))] * 2
        next_key[0] += 1
        params.update(collective_id=next_key[0], has_side_effects=True)
    return tuple(
        pl.pallas_call(
            kernel,
            out_shape=outs,
            grid=grid,
            in_specs=in_specs,
            out_specs=out_specs,
            scratch_shapes=scratch,
            compiler_params=pltpu.CompilerParams(**params),
            cost_estimate=cost_of(max(flops, 27 * 10**9) if pushes else flops),
        )(*operands)
    )


def swap_kernel(kinds, *refs):
    count = len(kinds)
    sources, targets, (send, receive) = refs[:count], refs[count : 2 * count], refs[2 * count :]
    start_pushes(kinds, sources, targets, send, receive)
    wait_pushes(kinds, sources, targets, send, receive)


def swap_call(*pushes):
    next_key[0] += 1
    kinds = tuple(kind for kind, _ in pushes)
    values = [value for _, value in pushes]
    return exchange_call(
        functools.partial(swap_kernel, kinds), next_key[0], values,
        [jax.ShapeDtypeStruct(value.shape, value.dtype) for value in values],
        [pltpu.SemaphoreType.DMA((len(pushes),))] * 2, flops=200 * 10**9,
    )


next_key = [11]


def sibling_id():
    index = lax.axis_index("fsdp")
    return (index + 1 - 2 * (index % 2), lax.axis_index("tp"))


def meet(partner):
    barrier = pltpu.get_barrier_semaphore()
    pl.semaphore_signal(barrier, inc=1, device_id=partner, device_id_type=pl.DeviceIdType.MESH)
    pl.semaphore_wait(barrier, 1)


def push(source, target, send, receive, partner):
    return pltpu.make_async_remote_copy(
        src_ref=source,
        dst_ref=target,
        send_sem=send,
        recv_sem=receive,
        device_id=partner,
        device_id_type=pl.DeviceIdType.MESH,
    )


def exchange_call(kernel, key, operands, outs, scratch, vmem=60, flops=4 * 10**9):
    anywhere = pl.BlockSpec(memory_space=pl.ANY)
    results = pl.pallas_call(
        kernel,
        out_shape=outs,
        in_specs=[anywhere] * len(operands),
        out_specs=[anywhere] * len(outs),
        scratch_shapes=scratch,
        compiler_params=pltpu.CompilerParams(
            collective_id=key, has_side_effects=True, vmem_limit_bytes=vmem * 1024 * 1024
        ),
        cost_estimate=cost_of(flops),
    )(*operands)
    return tuple(results) if len(outs) > 1 else results[0]


def relay(sources, targets, buffer, load, store):
    loads, stores = [], []
    for place, source in enumerate(sources):
        copy = pltpu.make_async_copy(source, buffer.at[place], load.at[place])
        copy.start()
        loads.append(copy)
    for place, target in enumerate(targets):
        loads[place].wait()
        copy = pltpu.make_async_copy(buffer.at[place], target, store.at[place])
        copy.start()
        stores.append(copy)
    for copy in stores:
        copy.wait()


def gather_kernel(own_ref, near_ref, full_ref, buffer, load, store, send, receive):
    partner = sibling_id()
    meet(partner)
    count = own_ref.shape[0]
    remotes = []
    for place, ref in enumerate((own_ref, near_ref)):
        remote = push(
            ref, full_ref.at[pl.ds((2 + place) * count, count)],
            send.at[place], receive.at[place], partner,
        )
        remote.start()
        remotes.append(remote)
    targets = [full_ref.at[pl.ds(place * count, count)] for place in range(2)]
    relay((own_ref, near_ref), targets, buffer, load, store)
    for remote in remotes:
        remote.wait()


def core_gather(own, near):
    shape = (4 * own.shape[0], own.shape[1])
    return exchange_call(
        gather_kernel, 1, [own, near], [jax.ShapeDtypeStruct(shape, own.dtype)],
        [pltpu.VMEM((2, *own.shape), own.dtype)] + [pltpu.SemaphoreType.DMA((2,))] * 4,
    )


def gather_two_kernel(
    own_ref, own_near_ref, got_ref, got_near_ref, first_ref, second_ref,
    buffer, load, store, send, receive,
):
    partner = sibling_id()
    far = lax.axis_index("tp") // 2
    meet(partner)
    count = own_ref.shape[0]

    def run(targets):
        sources = (own_ref, own_near_ref, got_ref, got_near_ref)
        remotes, places = [], []
        for place, ref in enumerate(sources):
            target, row = targets[place // 2], place % 2
            remote = push(
                ref, target.at[pl.ds((2 + row) * count, count)],
                send.at[place], receive.at[place], partner,
            )
            remote.start()
            remotes.append(remote)
            places.append(target.at[pl.ds(row * count, count)])
        relay(sources, places, buffer, load, store)
        for remote in remotes:
            remote.wait()

    @pl.when(far == 0)
    def _():
        run((first_ref, second_ref))

    @pl.when(far != 0)
    def _():
        run((second_ref, first_ref))


def core_gather_two(own, own_near, got, got_near):
    shape = (4 * own.shape[0], own.shape[1])
    return exchange_call(
        gather_two_kernel, 11, [own, own_near, got, got_near],
        [jax.ShapeDtypeStruct(shape, own.dtype)] * 2,
        [pltpu.VMEM((4, *own.shape), own.dtype)] + [pltpu.SemaphoreType.DMA((4,))] * 4,
    )


def reduce_kernel(term_ref, keep_ref, away_ref, mine, got, keep, away, local, send, receive, store):
    partner = sibling_id()
    meet(partner)
    pieces, count = mine.shape[0], mine.shape[1]
    half = pieces * count
    remotes, loads = [], []
    for piece in range(pieces):
        order = (piece + pieces // 2) % pieces
        remote = push(
            term_ref.at[pl.ds(half + order * count, count)], got.at[order],
            send.at[order], receive.at[order], partner,
        )
        remote.start()
        remotes.append(remote)
        load = pltpu.make_async_copy(
            term_ref.at[pl.ds(order * count, count)], mine.at[order], local.at[order]
        )
        load.start()
        loads.append(load)
    stores = []
    for piece in range(pieces):
        order = (piece + pieces // 2) % pieces
        loads[piece].wait()
        remotes[piece].wait()
        total = mine[order].astype(jnp.float32) + got[order].astype(jnp.float32)
        if order < pieces // 2:
            keep[order] = total
            copy = pltpu.make_async_copy(
                keep.at[order], keep_ref.at[pl.ds(order * count, count)], store.at[order]
            )
        else:
            slot = order - pieces // 2
            away[slot] = total.astype(away.dtype)
            copy = pltpu.make_async_copy(
                away.at[slot], away_ref.at[pl.ds(slot * count, count)], store.at[order]
            )
        copy.start()
        stores.append(copy)
    for copy in stores:
        copy.wait()


def core_reduce(term):
    rows, width = term.shape
    quarter = rows // 4
    pieces = 4
    count = 2 * quarter // pieces
    return exchange_call(
        reduce_kernel, 2, [term],
        [
            jax.ShapeDtypeStruct((quarter, width), jnp.float32),
            jax.ShapeDtypeStruct((quarter, width), term.dtype),
        ],
        [
            pltpu.VMEM((pieces, count, width), term.dtype),
            pltpu.VMEM((pieces, count, width), term.dtype),
            pltpu.VMEM((pieces // 2, count, width), jnp.float32),
            pltpu.VMEM((pieces // 2, count, width), term.dtype),
        ]
        + [pltpu.SemaphoreType.DMA((pieces,))] * 4,
    )


def pair_kernel(own_ref, *refs):
    others, (pair_ref, buffer, load, store, send, receive) = refs[:-6], refs[-6:]
    partner = sibling_id()
    core = lax.axis_index("fsdp") % 2
    far = lax.axis_index("tp") // 2
    meet(partner)
    base = pl.multiple_of(core * own_ref.shape[0], own_ref.shape[0])
    count = others[0].shape[0]
    owns = [own_ref.at[pl.ds(place * count, count)] for place in range(len(others))]

    def run(mine, theirs):
        remotes, targets = [], []
        for place in range(len(others)):
            target = pair_ref.at[pl.ds(base + place * count, count)]
            remote = push(theirs[place], target, send.at[place], receive.at[place], partner)
            remote.start()
            remotes.append(remote)
            targets.append(target)
        relay(mine, targets, buffer, load, store)
        for remote in remotes:
            remote.wait()

    @pl.when(core == far)
    def _():
        run(owns, others)

    @pl.when(core != far)
    def _():
        run(others, owns)


def core_pair(key, own, *others):
    shape = (2 * own.shape[0], own.shape[1])
    return exchange_call(
        pair_kernel, key, [own, *others], [jax.ShapeDtypeStruct(shape, own.dtype)],
        [pltpu.VMEM((len(others), *others[0].shape), own.dtype)]
        + [pltpu.SemaphoreType.DMA((len(others),))] * 4,
    )


def split_kernel(pair_ref, keep_ref, away_ref, buffer, load, store, send, receive):
    partner = sibling_id()
    core = lax.axis_index("fsdp") % 2
    far = lax.axis_index("tp") // 2
    meet(partner)
    count = keep_ref.shape[0]
    mine = pair_ref.at[pl.ds(pl.multiple_of(core * count, count), count)]
    theirs = pair_ref.at[pl.ds(pl.multiple_of((1 - core) * count, count), count)]

    def run(own_target, other_target):
        remote = push(theirs, other_target, send.at[0], receive.at[0], partner)
        remote.start()
        relay((mine,), (own_target,), buffer, load, store)
        remote.wait()

    @pl.when(core == far)
    def _():
        run(keep_ref, keep_ref)

    @pl.when(core != far)
    def _():
        run(away_ref, away_ref)


def core_split(key, pair):
    shape = (pair.shape[0] // 2, pair.shape[1])
    return exchange_call(
        split_kernel, key, [pair], [jax.ShapeDtypeStruct(shape, pair.dtype)] * 2,
        [pltpu.VMEM((1, *shape), pair.dtype)] + [pltpu.SemaphoreType.DMA((1,))] * 4,
    )


def attention_call(kernel, arrays, kinds, outs, scratch, pushes=()):
    rows, heads_local = arrays[-1].shape[0], outs[1]
    half = rows // 2
    groups = heads_local // HEAD_GROUP
    width = HEAD_GROUP * HD

    def spec(kind):
        if kind == "table":
            return pl.BlockSpec((half, HD), lambda s, g: (s, 0))
        if kind == "column":
            return pl.BlockSpec((half, 1), lambda s, g: (s, 0))
        if kind == "lse":
            return pl.BlockSpec((1, half, HEAD_GROUP), lambda s, g: (g, s, 0))
        shift = kind * groups
        return pl.BlockSpec((half, width), lambda s, g: (s, shift + g))

    def shape(kind):
        if kind == "lse":
            return jax.ShapeDtypeStruct((groups, rows, HEAD_GROUP), jnp.float32)
        return jax.ShapeDtypeStruct((rows, heads_local * HD), jnp.bfloat16)

    return grid_call(
        kernel,
        arrays,
        [spec(kind) for kind in kinds],
        [shape(kind) for kind in outs[0]],
        [spec(kind) for kind in outs[0]],
        (rows // half, groups),
        4 * len(outs[0]) ** 2 * rows * rows * heads_local * HD // 16,
        scratch=scratch(half, width),
        pushes=pushes,
    )


def backward_scratch(half, width):
    return [pltpu.VMEM((half, width), jnp.bfloat16)] * 2 + [
        pltpu.VMEM((half, width), jnp.float32)
    ] * 6


def no_scratch(half, width):
    return []


def head_tables(positions):
    half_width = HD // 2
    frequency = rope_theta ** (-(jnp.arange(half_width, dtype=jnp.float32) * 2.0 / HD))
    angles = positions.astype(jnp.float32)[:, None] * frequency[None, :]
    cosine, sine = jnp.cos(angles), jnp.sin(angles)
    return (
        jnp.concatenate([cosine, cosine], axis=-1),
        jnp.concatenate([-sine, sine], axis=-1),
    )


def paired_device(
    block_in,
    out_cotangent,
    segment_ids,
    doc_positions,
    norm1_gain,
    qkv_weight,
    out_weight,
    norm2_gain,
    gate_up_weight,
    down_weight,
):
    fsdp_count, tp_count = lax.axis_size("fsdp"), lax.axis_size("tp")
    core = lax.axis_index("fsdp") % 2
    lane_z = lax.axis_index("tp")
    near, far = lane_z % 2, lane_z // 2
    core_pairs = [(i, i ^ 1) for i in range(fsdp_count)]
    near_pairs = [(i, i ^ 1) for i in range(tp_count)]
    far_pairs = [(i, i ^ 2) for i in range(tp_count)]
    plane_groups = [list(range(first, fsdp_count, 2)) for first in range(2)]
    rows = block_in.shape[1]
    local_cols = qkv_weight.shape[2]
    heads_local = local_cols // HD
    gain_one = norm1_gain.astype(jnp.float32)
    gain_two = norm2_gain.astype(jnp.float32)

    def swap_core(value):
        return lax.ppermute(value, "fsdp", core_pairs)

    def swap_near(value):
        return lax.ppermute(value, "tp", near_pairs)

    def swap_far(value):
        return lax.ppermute(value, "tp", far_pairs)

    def pick_tile(size):
        return 512 if size % 512 == 0 else 768

    tokens = []

    def act(work, *inputs, sends=()):
        values = [*inputs, *[value for _, value in sends]]
        held = lax.optimization_barrier((*values, *tokens))[: len(values)]
        if sends:
            kinds = [kind for kind, _ in sends]
            result = work(*held[: len(inputs)], pushes=list(zip(kinds, held[len(inputs) :])))
        else:
            result = work(*held)
        tokens[:] = result if isinstance(result, tuple) else (result,)
        return result[0] if isinstance(result, tuple) and len(result) == 1 else result

    def swap(*sends):
        return act(lambda pushes: swap_call(*pushes), sends=sends)

    def pick(value, index):
        return lax.dynamic_index_in_dim(value, index, 0, keepdims=False)

    def place_tokens(value, got):
        keep = pick(value, far)
        return jnp.where(far == 0, keep, got), jnp.where(far == 0, got, keep)

    def join(left, right):
        return jnp.concatenate([left, right], axis=0)

    def plane_gather(pair):
        return lax.all_gather(pair, "fsdp", axis=0, tiled=True, axis_index_groups=plane_groups)

    def plane_scatter(grad):
        return lax.psum_scatter(
            grad, "fsdp", scatter_dimension=0, tiled=True, axis_index_groups=plane_groups
        )

    def gather_weight(key, local, *others):
        return plane_gather(act(lambda own, *got: core_pair(key, own, *got), local, *others))

    def halve(value):
        count = value.shape[0] // 2
        return value[:count], value[count:]

    def add_wide(left, right):
        return left.astype(jnp.float32) + right.astype(jnp.float32)

    def chained(value, *others):
        return lax.optimization_barrier((value, *others))[0]

    def scatter_gains(gains):
        for axis, size in (("fsdp", fsdp_count), ("tp", tp_count)):
            index = lax.axis_index(axis)
            step = size // 2
            while step >= 1:
                bit = (index // step) % 2
                parts = gains.reshape(gains.shape[0], 2, gains.shape[1] // 2)
                sent = lax.dynamic_index_in_dim(parts, 1 - bit, 1, keepdims=False)
                kept = lax.dynamic_index_in_dim(parts, bit, 1, keepdims=False)
                gains = kept + lax.ppermute(sent, axis, [(i, i ^ step) for i in range(size)])
                step //= 2
        return gains

    def wide_dot(left, right, pushes=()):
        return rows_matmul(
            [left], [right], dot_nn, [jnp.float32], pick_tile(right.shape[1]), pushes=pushes
        )

    def dot_bf16(left, right, pushes=()):
        return rows_matmul(
            [left], [right], dot_nn, [jnp.bfloat16], pick_tile(right.shape[1]), pushes=pushes
        )

    def grad_sum(left, right, left_next, right_next, pushes=()):
        chunk = pick_tile(right.shape[1])
        return sum_matmul(
            [left, left_next], [right, right_next], pick_tile(left.shape[1]),
            2 * chunk if right.shape[1] % (2 * chunk) == 0 else chunk, pushes=pushes,
        )

    def heads_back(grad, weight, pushes=()):
        return rows_matmul(
            [grad], [weight], dot_nt, [jnp.bfloat16], pick_tile(weight.shape[0]), pushes=pushes
        )

    def rms_pack(stream, gain):
        scale = rms_scale(stream)
        return scale, (stream * scale * gain).astype(jnp.bfloat16)

    qkv_local = qkv_weight.reshape(qkv_weight.shape[0], 3 * local_cols)
    gate_local, up_local = gate_up_weight[:, 0], gate_up_weight[:, 1]

    next_key[0] = 11
    position_got = swap_far(pick(doc_positions, 1 - far))
    first, second = place_tokens(doc_positions, position_got)
    near_both = swap_near(join(first, second))

    def first_norm(part):
        stream = part.astype(jnp.float32)
        return (stream, *rms_pack(stream, gain_one))

    s_own, r_own, n_own = act(lambda value: first_norm(pick(value, far)), block_in)
    near_own, qkv_other = swap(("near", n_own), ("far", qkv_local))
    qkv_full = gather_weight(4, qkv_local, qkv_other)
    first, second = (
        join(first, near_both[: first.shape[0]]), join(second, near_both[first.shape[0] :])
    )
    core_both = swap_core(join(first, second))

    def make_tables(first, second, both):
        count = first.shape[0]
        late = join(second, both[count:])
        return (*head_tables(join(first, both[:count])), *head_tables(late), late[:, None])

    c_own = pick(out_cotangent, far)
    stream_got, c_near_own, out_other = swap(
        ("far", pick(block_in, 1 - far)), ("near", c_own), ("far", out_weight)
    )
    out_full = gather_weight(3, out_weight, out_other)
    s_got, r_got, n_got = act(first_norm, stream_got)
    near_got, gate_other = swap(("near", n_got), ("far", gate_local))
    gate_full = gather_weight(5, gate_local, gate_other)
    h1_first, h1_second = act(core_gather_two, n_own, near_own, n_got, near_got)
    streams = [jnp.where(far == 0, s_own, s_got), jnp.where(far == 0, s_got, s_own)]
    scales_one = [jnp.where(far == 0, r_own, r_got), jnp.where(far == 0, r_got, r_own)]

    def attend_first(projected, pushes=()):
        arrays = [projected, projected, projected, *tables[0]]
        return attention_call(
            forward_first, arrays, [0, 1, 2, "table", "table"],
            ([0, 0, 0, 0, "lse"], heads_local), no_scratch, pushes,
        )

    def attend_second(projected, pushes=()):
        arrays = [projected, projected, projected, *tables[1], saved[0][1], saved[0][2], reach]
        return attention_call(
            forward_second, arrays, [0, 1, 2, "table", "table", 0, 0, "column"],
            ([0, 0, 0, 0, "lse"], heads_local), no_scratch, pushes,
        )

    up_other = swap_far(chained(up_local, gate_other))
    cos_first, sin_first, cos_second, sin_second, reach = act(
        make_tables, first, second, core_both
    )
    tables = [(cos_first, sin_first), (cos_second, sin_second)]
    projected = act(wide_dot, h1_first, qkv_full)
    results = act(attend_first, projected)
    saved, lses, mixed_first = [results[:3]], [results[4]], results[3]
    term_first = act(dot_bf16, mixed_first, out_full)
    keep_first, send_first = act(core_reduce, term_first)
    up_full = gather_weight(5, up_local, up_other)
    down_other = swap_far(chained(down_weight, up_other))
    projected, branch_first = act(
        wide_dot, h1_second, qkv_full, sends=[("near", send_first)]
    )

    def second_norm(stream, keep, got):
        middle = stream + keep + got.astype(jnp.float32)
        return (middle, *rms_pack(middle, gain_two))

    m_first, q_first, n_first = act(second_norm, streams[0], keep_first, branch_first)
    *results, near_first = act(attend_second, projected, sends=[("near", n_first)])
    saved.append(results[:3])
    lses.append(results[4])
    mixed_second = results[3]
    term_second = act(dot_bf16, mixed_second, out_full)
    keep_second, send_second = act(core_reduce, term_second)
    h2_first = act(core_gather, n_first, near_first)
    down_full_pair = act(lambda own, got: core_pair(6, own, got), down_weight, down_other)
    down_full = plane_gather(down_full_pair)
    c_got = swap_far(chained(pick(out_cotangent, 1 - far), down_full_pair))

    gate_first, branch_second = act(
        wide_dot, h2_first, gate_full, sends=[("near", send_second)]
    )
    m_second, q_second, n_second = act(second_norm, streams[1], keep_second, branch_second)

    def rise(hidden, weight, gate, pushes=()):
        return rows_matmul(
            [hidden], [weight], dot_nn, [jnp.float32, jnp.bfloat16], pick_tile(weight.shape[1]),
            finish=lambda up, gate: (up, gate * jax.nn.sigmoid(gate) * up), extras=[gate],
            pushes=pushes,
        )

    up_first, a_first, near_second = act(
        rise, h2_first, up_full, gate_first, sends=[("near", n_second)]
    )
    h2_second = act(core_gather, n_second, near_second)
    gate_second, c_near_got = act(
        wide_dot, h2_second, gate_full, sends=[("near", c_got)]
    )
    y_first, y_second = act(core_gather_two, c_own, c_near_own, c_got, c_near_got)
    c_first, c_second = jnp.where(far == 0, c_own, c_got), jnp.where(far == 0, c_got, c_own)
    up_second, a_second = act(rise, h2_second, up_full, gate_second)
    down_sum = plane_scatter(act(grad_sum, a_first, y_first, a_second, y_second))

    def fall_finish(act_grad, gate, up):
        sigmoid_gate = jax.nn.sigmoid(gate)
        return (
            act_grad * up * sigmoid_gate * (1.0 + gate * (1.0 - sigmoid_gate)),
            act_grad * (gate * sigmoid_gate),
        )

    def fall(cotangent, weight, gate, up):
        return rows_matmul(
            [cotangent], [weight], dot_nt, [jnp.bfloat16] * 2, pick_tile(weight.shape[0]),
            chunk=512, finish=fall_finish, extras=[gate, up],
        )

    dg_first, du_first = act(fall, y_first, down_full, gate_first, up_first)
    dg_second, du_second = act(fall, y_second, down_full, gate_second, up_second)
    gate_sum = plane_scatter(act(grad_sum, h2_first, dg_first, h2_second, dg_second))

    def hidden_grad(gate_grad, up_grad, gate_weight, up_weight, pushes=()):
        return rows_matmul(
            [gate_grad, up_grad], [gate_weight, up_weight], dot_nt, [jnp.bfloat16],
            pick_tile(gate_weight.shape[0]), pushes=pushes,
        )

    def second_back(middle, scale, keep, got, cotangent):
        grad, gain_term = norm_back(middle, scale, gain_two, keep + got.astype(jnp.float32))
        grad = cotangent.astype(jnp.float32) + grad
        return grad, grad.astype(jnp.bfloat16), gain_term

    term_first = act(hidden_grad, dg_first, du_first, gate_full, up_full)
    keep_first, send_first = act(core_reduce, term_first)
    term_second, back_first = act(
        hidden_grad, dg_second, du_second, gate_full, up_full, sends=[("near", send_first)]
    )
    keep_second, send_second = act(core_reduce, term_second)
    g_first, n_first, gain_two_first = act(
        second_back, m_first, q_first, keep_first, back_first, c_first
    )
    down_mine, down_away = act(lambda pair: core_split(10, pair), down_sum)
    down_got = swap_far(down_away)
    grad_up, back_second = act(
        grad_sum, h2_first, du_first, h2_second, du_second, sends=[("near", send_second)]
    )
    up_sum = plane_scatter(grad_up)
    mlp_first, near_first = act(dot_bf16, a_first, down_full, sends=[("near", n_first)])
    g_second, n_second, gain_two_second = act(
        second_back, m_second, q_second, keep_second, back_second, c_second
    )
    d_first = act(core_gather, n_first, near_first)

    gate_mine, gate_away = act(lambda pair: core_split(9, pair), gate_sum)
    gate_got = swap_far(gate_away)
    mlp_second, near_second = act(dot_bf16, a_second, down_full, sends=[("near", n_second)])
    mlp_keep_first, mlp_send_first = act(core_reduce, mlp_first)
    heads_first = act(heads_back, d_first, out_full)
    d_second = act(core_gather, n_second, near_second)
    heads_second = act(heads_back, d_second, out_full)
    mlp_keep_second, mlp_send_second = act(core_reduce, mlp_second)
    grad_out, mlp_branch_first = act(
        grad_sum, mixed_first, d_first, mixed_second, d_second, sends=[("near", mlp_send_first)]
    )
    out_sum = plane_scatter(grad_out)
    up_mine, up_away = act(lambda pair: core_split(9, pair), up_sum)

    def attend_back(heads_first, heads_second, pushes=()):
        return attention_call(
            backward_both,
            [
                *saved[0], *saved[1], heads_first, heads_second, *lses,
                *tables[0], *tables[1], reach,
            ],
            [0] * 8 + ["lse"] * 2 + ["table"] * 4 + ["column"],
            ([0] * 6, heads_local),
            backward_scratch,
            pushes,
        )

    up_got = swap_far(up_away)
    *grads, mlp_branch_second = act(
        attend_back, heads_first, heads_second, sends=[("near", mlp_send_second)]
    )
    p_first, p_second = act(
        lambda *parts: (
            jnp.concatenate(parts[:3], axis=1),
            jnp.concatenate(parts[3:], axis=1),
        ),
        *grads,
    )

    def finish_output(first, first_keep, first_got, second, second_keep, second_got):
        first = (first + first_keep + first_got.astype(jnp.float32)).astype(jnp.bfloat16)
        second = (second + second_keep + second_got.astype(jnp.float32)).astype(jnp.bfloat16)
        return jnp.where(far == 0, first, second), jnp.where(far == 0, second, first)

    out_keep, out_send = act(
        finish_output,
        m_first, mlp_keep_first, mlp_branch_first, m_second, mlp_keep_second, mlp_branch_second,
    )
    out_got = swap_far(out_send)
    term_first = act(heads_back, p_first, qkv_full)
    keep_first, send_first = act(core_reduce, term_first)
    grad_qkv, back_first = act(
        grad_sum, h1_first, p_first, h1_second, p_second, sends=[("near", send_first)]
    )
    qkv_sum = plane_scatter(grad_qkv)
    term_second = act(heads_back, p_second, qkv_full)
    keep_second, send_second = act(core_reduce, term_second)
    out_mine, out_away = act(lambda pair: core_split(8, pair), out_sum)
    def settle(keep, got):
        return jnp.stack([jnp.where(far == 0, keep, got), jnp.where(far == 0, got, keep)])

    def first_back(stream, scale, keep, got, grad):
        back, gain_term = norm_back(stream, scale, gain_one, keep + got.astype(jnp.float32))
        return grad + back, gain_term

    def last_back(stream, scale, keep, got, grad, first):
        second, gain_term = first_back(stream, scale, keep, got, grad)
        return (
            jnp.where(far == 0, first, second),
            jnp.where(far == 0, second, first).astype(jnp.bfloat16),
            gain_term,
        )

    back_second, out_back = swap(("near", send_second), ("far", out_away))
    i_first, gain_one_first = act(
        first_back, streams[0], scales_one[0], keep_first, back_first, g_first
    )
    in_keep, in_send, gain_one_second = act(
        last_back, streams[1], scales_one[1], keep_second, back_second, g_second, i_first
    )
    in_got = swap_far(in_send)
    down_owned = act(add_wide, down_mine, down_got)
    gate_owned = act(add_wide, gate_mine, gate_got)
    block_out = act(settle, out_keep, out_got)
    up_owned = act(add_wide, up_mine, up_got)
    gate_up_owned = act(lambda a, b: jnp.stack([a, b], axis=1), gate_owned, up_owned)
    out_owned = act(add_wide, out_mine, out_back)
    gains = scatter_gains(
        jnp.stack([gain_one_first + gain_one_second, gain_two_first + gain_two_second])
    )
    in_grad = act(lambda keep, got: settle(keep, got.astype(jnp.float32)), in_keep, in_got)
    qkv_mine, qkv_away = act(lambda pair: core_split(0, pair), qkv_sum)
    qkv_back = swap(("far", qkv_away))
    qkv_owned = act(add_wide, qkv_mine, qkv_back)
    return (
        block_out,
        in_grad,
        gains[0],
        qkv_owned.reshape(qkv_weight.shape),
        out_owned,
        gains[1],
        gate_up_owned,
        down_owned,
    )


def solution(mesh):
    sizes = (mesh.shape["fsdp"], mesh.shape["tp"])
    body = paired_device if sizes == (8, 4) else per_device
    in_specs = (
        P("fsdp", "tp", None),
        P("fsdp", "tp", None),
        P("fsdp", "tp"),
        P("fsdp", "tp"),
        P(),
        P("fsdp", None, "tp"),
        P(("tp", "fsdp"), None),
        P(),
        P("fsdp", None, "tp"),
        P(("tp", "fsdp"), None),
    )
    out_specs = (
        P("fsdp", "tp", None),
        P("fsdp", "tp", None),
        P(("fsdp", "tp")),
        P("fsdp", None, "tp"),
        P(("tp", "fsdp"), None),
        P(("fsdp", "tp")),
        P("fsdp", None, "tp"),
        P(("tp", "fsdp"), None),
    )
    return jax.shard_map(
        body, mesh=mesh, in_specs=in_specs, out_specs=out_specs, check_vma=False
    )
```

```python
import functools

import jax
import jax.numpy as jnp
from jax import lax
from jax.experimental import pallas as pl
from jax.experimental.pallas import tpu as pltpu
from jax.sharding import PartitionSpec as P

D = 3072
HD = 96


rms_epsilon = 1e-05
rope_theta = 10000.0
masked_score = -1e30
LOG2E = 1.4426950408889634


def rope_tables(positions, head_size):
    half_width = head_size // 2
    frequency = rope_theta ** (-(jnp.arange(half_width, dtype=jnp.float32) * 2.0 / head_size))
    angles = positions.astype(jnp.float32)[:, None] * frequency[None, :]
    return (jnp.cos(angles)[:, None, :], jnp.sin(angles)[:, None, :])


def rotate(values, cosine_part, sine_part):
    half_width = values.shape[-1] // 2
    lead_half = values[..., :half_width]
    tail_half = values[..., half_width:]
    return jnp.concatenate(
        [
            lead_half * cosine_part - tail_half * sine_part,
            tail_half * cosine_part + lead_half * sine_part,
        ],
        axis=-1,
    )


def unrotate(values, cosine_part, sine_part):
    half_width = values.shape[-1] // 2
    lead_half = values[..., :half_width]
    tail_half = values[..., half_width:]
    return jnp.concatenate(
        [
            lead_half * cosine_part + tail_half * sine_part,
            tail_half * cosine_part - lead_half * sine_part,
        ],
        axis=-1,
    )


def rms_scale(stream):
    return lax.rsqrt(jnp.mean(stream * stream, axis=-1, keepdims=True) + rms_epsilon)


def norm_back(stream, scale_rows, gain_vec, grad_rows):
    gained_grad = gain_vec * grad_rows
    input_grad = scale_rows * gained_grad - stream * scale_rows**3 * jnp.mean(
        gained_grad * stream, axis=-1, keepdims=True
    )
    return (input_grad, jnp.sum(grad_rows * stream * scale_rows, axis=0))


def allowed_mask(segment_tile, index_tile, segments):
    columns = jnp.arange(segments.shape[0], dtype=jnp.int32)
    return (segment_tile[:, None] == segments[None, :]) & (index_tile[:, None] >= columns[None, :])


def masked_scores(query_tile, key_rows, segment_tile, index_tile, segments, scale_value):
    scores = (
        jnp.einsum("qhd,khd->hqk", query_tile, key_rows, preferred_element_type=jnp.float32)
        * scale_value
    )
    return jnp.where(allowed_mask(segment_tile, index_tile, segments)[None], scores, masked_score)


def attention_forward(queries, key_rows, value_rows, segments, block_rows):
    seq_len, head_count, head_size = queries.shape
    tiles = seq_len // block_rows
    scale_value = head_size ** (-0.5)
    positions = jnp.arange(seq_len, dtype=jnp.int32)

    def query_block(packed):
        query_tile, segment_tile, index_tile = packed
        scores = masked_scores(
            query_tile, key_rows, segment_tile, index_tile, segments, scale_value
        )
        row_max = jnp.max(scores, axis=-1, keepdims=True)
        exponent = jnp.exp(scores - row_max)
        row_total = jnp.sum(exponent, axis=-1, keepdims=True)
        probs_low = (exponent / row_total).astype(jnp.bfloat16)
        mixed = jnp.einsum(
            "hqk,khd->qhd", probs_low, value_rows, preferred_element_type=jnp.float32
        )
        return (mixed, (row_max + jnp.log(row_total))[..., 0])

    mixed, log_total = lax.map(
        query_block,
        (
            queries.reshape(tiles, block_rows, head_count, head_size),
            segments.reshape(tiles, block_rows),
            positions.reshape(tiles, block_rows),
        ),
    )
    return (mixed.reshape(seq_len, head_count * head_size), log_total)


def attention_backward(queries, key_rows, value_rows, segments, log_total, out_grad, block_rows):
    seq_len, head_count, head_size = queries.shape
    tiles = seq_len // block_rows
    scale_value = head_size ** (-0.5)
    positions = jnp.arange(seq_len, dtype=jnp.int32)

    def query_block(carry, packed):
        key_acc, value_acc = carry
        query_tile, segment_tile, index_tile, total_tile, grad_tile = packed
        scores = masked_scores(
            query_tile, key_rows, segment_tile, index_tile, segments, scale_value
        )
        probs = jnp.exp(scores - total_tile[..., None])
        probs_low = probs.astype(jnp.bfloat16)
        prob_grad = jnp.einsum(
            "qhd,khd->hqk", grad_tile, value_rows, preferred_element_type=jnp.float32
        )
        score_grad = (
            probs * (prob_grad - jnp.sum(probs * prob_grad, axis=-1, keepdims=True))
        ).astype(jnp.bfloat16)
        query_grad = (
            jnp.einsum("hqk,khd->qhd", score_grad, key_rows, preferred_element_type=jnp.float32)
            * scale_value
        )
        key_acc = (
            key_acc
            + jnp.einsum("hqk,qhd->khd", score_grad, query_tile, preferred_element_type=jnp.float32)
            * scale_value
        )
        value_acc = value_acc + jnp.einsum(
            "hqk,qhd->khd", probs_low, grad_tile, preferred_element_type=jnp.float32
        )
        return ((key_acc, value_acc), query_grad)

    start_acc = (jnp.zeros(queries.shape, jnp.float32), jnp.zeros(queries.shape, jnp.float32))
    (key_grad, value_grad), query_grad = lax.scan(
        query_block,
        start_acc,
        (
            queries.reshape(tiles, block_rows, head_count, head_size),
            segments.reshape(tiles, block_rows),
            positions.reshape(tiles, block_rows),
            log_total,
            out_grad.reshape(tiles, block_rows, head_count, head_size),
        ),
    )
    return (query_grad.reshape(seq_len, head_count, head_size), key_grad, value_grad)


def gather_attention(qkv_weight, out_weight):
    return (
        lax.all_gather(qkv_weight, "fsdp", axis=0, tiled=True),
        lax.all_gather(out_weight, "fsdp", axis=0, tiled=True),
    )


def gather_feedforward(gate_up_weight, down_weight):
    return (
        lax.all_gather(gate_up_weight, "fsdp", axis=0, tiled=True),
        lax.all_gather(down_weight, "fsdp", axis=0, tiled=True),
    )


def per_device(
    block_in,
    out_cotangent,
    segment_ids,
    doc_positions,
    norm1_gain,
    qkv_weight,
    out_weight,
    norm2_gain,
    gate_up_weight,
    down_weight,
):
    micro_count = block_in.shape[0]
    fsdp_count = lax.axis_size("fsdp")
    segment_full, position_full = (
        lax.all_gather(segment_ids, "tp", axis=1, tiled=True),
        lax.all_gather(doc_positions, "tp", axis=1, tiled=True),
    )
    seq_len = segment_full.shape[1]
    block_rows = min(seq_len, 512)
    gain_one = norm1_gain.astype(jnp.float32)
    gain_two = norm2_gain.astype(jnp.float32)
    local_cols = qkv_weight.shape[2]
    local_units = gate_up_weight.shape[2]
    heads_local = local_cols // HD
    grad_qkv = jnp.zeros((D, 3, local_cols), jnp.float32)
    grad_out = jnp.zeros((out_weight.shape[0] * fsdp_count, D), jnp.float32)
    grad_gate_up = jnp.zeros((D, 2, local_units), jnp.float32)
    grad_down = jnp.zeros((down_weight.shape[0] * fsdp_count, D), jnp.float32)
    gain_one_acc = jnp.zeros((D,), jnp.float32)
    gain_two_acc = jnp.zeros((D,), jnp.float32)
    outputs = []
    input_grads = []
    for micro_index in range(micro_count):
        weights_fwd = (
            gather_attention(qkv_weight, out_weight),
            gather_feedforward(gate_up_weight, down_weight),
        )
        (qkv_full, out_full), (gate_up_full, down_full) = weights_fwd
        stream = block_in[micro_index].astype(jnp.float32)
        segment_row = segment_full[micro_index]
        cosine_part, sine_part = rope_tables(position_full[micro_index], HD)
        scale_one = rms_scale(stream)
        normed_one = (stream * scale_one * gain_one).astype(jnp.bfloat16)
        normed_one_full = lax.all_gather(normed_one, "tp", axis=0, tiled=True)
        projected = jnp.einsum(
            "sd,dtc->stc", normed_one_full, qkv_full, preferred_element_type=jnp.float32
        )
        queries = rotate(
            projected[:, 0].reshape(seq_len, heads_local, HD), cosine_part, sine_part
        ).astype(jnp.bfloat16)
        key_rows = rotate(
            projected[:, 1].reshape(seq_len, heads_local, HD), cosine_part, sine_part
        ).astype(jnp.bfloat16)
        value_rows = projected[:, 2].reshape(seq_len, heads_local, HD).astype(jnp.bfloat16)
        mixed, log_total = attention_forward(queries, key_rows, value_rows, segment_row, block_rows)
        attn_heads = mixed.astype(jnp.bfloat16)
        attn_term = jnp.dot(attn_heads, out_full, preferred_element_type=jnp.float32)
        attn_branch = lax.psum_scatter(attn_term, "tp", scatter_dimension=0, tiled=True)
        middle = stream + attn_branch
        scale_two = rms_scale(middle)
        normed_two = (middle * scale_two * gain_two).astype(jnp.bfloat16)
        normed_two_full = lax.all_gather(normed_two, "tp", axis=0, tiled=True)
        gate_up = jnp.einsum(
            "sd,dtf->stf", normed_two_full, gate_up_full, preferred_element_type=jnp.float32
        )
        gate_rows = gate_up[:, 0]
        up_rows = gate_up[:, 1]
        sigmoid_gate = jax.nn.sigmoid(gate_rows)
        silu_gate = gate_rows * sigmoid_gate
        activated = (silu_gate * up_rows).astype(jnp.bfloat16)
        mlp_term = jnp.dot(activated, down_full, preferred_element_type=jnp.float32)
        mlp_branch = lax.psum_scatter(
            mlp_term.astype(jnp.bfloat16), "tp", scatter_dimension=0, tiled=True
        ).astype(jnp.float32)
        outputs.append((middle + mlp_branch).astype(jnp.bfloat16))
        (qkv_back, out_back), (gate_up_back, down_back) = weights_fwd
        cotangent = out_cotangent[micro_index].astype(jnp.float32)
        cotangent_full = lax.all_gather(out_cotangent[micro_index], "tp", axis=0, tiled=True)
        grad_down = grad_down + jnp.einsum(
            "sf,sd->fd", activated, cotangent_full, preferred_element_type=jnp.float32
        )
        act_grad = jnp.einsum(
            "sd,fd->sf", cotangent_full, down_back, preferred_element_type=jnp.float32
        )
        gate_grad = act_grad * up_rows * sigmoid_gate * (1.0 + gate_rows * (1.0 - sigmoid_gate))
        up_grad = act_grad * silu_gate
        gate_up_grad = jnp.stack([gate_grad, up_grad], axis=1).astype(jnp.bfloat16)
        grad_gate_up = grad_gate_up + jnp.einsum(
            "sd,stf->dtf", normed_two_full, gate_up_grad, preferred_element_type=jnp.float32
        )
        normed_two_term = jnp.einsum(
            "stf,dtf->sd", gate_up_grad, gate_up_back, preferred_element_type=jnp.float32
        )
        normed_two_grad = lax.psum_scatter(normed_two_term, "tp", scatter_dimension=0, tiled=True)
        middle_back, gain_two_term = norm_back(middle, scale_two, gain_two, normed_two_grad)
        gain_two_acc = gain_two_acc + gain_two_term
        middle_grad = cotangent + middle_back
        attn_grad_full = lax.all_gather(middle_grad.astype(jnp.bfloat16), "tp", axis=0, tiled=True)
        grad_out = grad_out + jnp.einsum(
            "sc,sd->cd", attn_heads, attn_grad_full, preferred_element_type=jnp.float32
        )
        heads_grad = jnp.einsum(
            "sd,cd->sc", attn_grad_full, out_back, preferred_element_type=jnp.float32
        ).astype(jnp.bfloat16)
        query_grad, key_grad, value_grad = attention_backward(
            queries,
            key_rows,
            value_rows,
            segment_row,
            log_total,
            heads_grad.reshape(seq_len, heads_local, HD),
            block_rows,
        )
        projected_grad = jnp.stack(
            [
                unrotate(query_grad, cosine_part, sine_part).reshape(seq_len, local_cols),
                unrotate(key_grad, cosine_part, sine_part).reshape(seq_len, local_cols),
                value_grad.reshape(seq_len, local_cols),
            ],
            axis=1,
        ).astype(jnp.bfloat16)
        grad_qkv = grad_qkv + jnp.einsum(
            "sd,stc->dtc", normed_one_full, projected_grad, preferred_element_type=jnp.float32
        )
        normed_one_term = jnp.einsum(
            "stc,dtc->sd", projected_grad, qkv_back, preferred_element_type=jnp.float32
        )
        normed_one_grad = lax.psum_scatter(
            normed_one_term.astype(jnp.bfloat16), "tp", scatter_dimension=0, tiled=True
        ).astype(jnp.float32)
        stream_back, gain_one_term = norm_back(stream, scale_one, gain_one, normed_one_grad)
        gain_one_acc = gain_one_acc + gain_one_term
        input_grads.append(middle_grad + stream_back)
    owned_grads = (
        lax.psum_scatter(
            grad_qkv.astype(jnp.bfloat16), "fsdp", scatter_dimension=0, tiled=True
        ).astype(jnp.float32),
        lax.psum_scatter(
            grad_out.astype(jnp.bfloat16), "fsdp", scatter_dimension=0, tiled=True
        ).astype(jnp.float32),
        lax.psum_scatter(
            grad_gate_up.astype(jnp.bfloat16), "fsdp", scatter_dimension=0, tiled=True
        ).astype(jnp.float32),
        lax.psum_scatter(
            grad_down.astype(jnp.bfloat16), "fsdp", scatter_dimension=0, tiled=True
        ).astype(jnp.float32),
    )
    owned_gains = (
        lax.psum_scatter(gain_one_acc, ("fsdp", "tp"), scatter_dimension=0, tiled=True),
        lax.psum_scatter(gain_two_acc, ("fsdp", "tp"), scatter_dimension=0, tiled=True),
    )
    return (
        jnp.stack(outputs),
        jnp.stack(input_grads),
        owned_gains[0],
        owned_grads[0],
        owned_grads[1],
        owned_gains[1],
        owned_grads[2],
        owned_grads[3],
    )


HEAD_GROUP = 4
FIRST_DOC = 800


def dot_nt(left, right):
    return lax.dot_general(left, right, (((1,), (1,)), ((), ())), preferred_element_type=jnp.float32)


def dot_tn(left, right):
    return lax.dot_general(left, right, (((0,), (0,)), ((), ())), preferred_element_type=jnp.float32)


def dot_nn(left, right):
    return lax.dot_general(left, right, (((1,), (0,)), ((), ())), preferred_element_type=jnp.float32)


def swap_halves(values):
    lanes = lax.broadcasted_iota(jnp.int32, values.shape, 1)
    width = values.shape[1]
    return jnp.where(
        lanes % HD < HD // 2,
        pltpu.roll(values, width - HD // 2, 1),
        pltpu.roll(values, HD // 2, 1),
    )


def causal_mask(rows, columns):
    row_ids = lax.broadcasted_iota(jnp.int32, (rows, columns), 0)
    column_ids = lax.broadcasted_iota(jnp.int32, (rows, columns), 1)
    return row_ids >= column_ids


def tail_mask(reach):
    rows = reach.shape[0]
    row_ids = lax.broadcasted_iota(jnp.int32, (rows, rows), 0)
    column_ids = lax.broadcasted_iota(jnp.int32, (rows, rows), 1)
    return (row_ids >= column_ids) & (row_ids - column_ids <= reach)


def halves(quarter):
    first = lax.axis_index("tp") % 2
    return (
        pl.multiple_of(first * quarter, quarter),
        pl.multiple_of((1 - first) * quarter, quarter),
    )


def widen(table):
    return jnp.concatenate([table] * HEAD_GROUP, axis=1)


def load_rotated(offsets, quarter, q_ref, k_ref, v_ref, cos_ref, sin_ref, qr_ref, kr_ref, vr_ref):
    for place, offset in enumerate(offsets):
        rows = pl.ds(offset, quarter)
        target = pl.ds(place * quarter, quarter)
        cosine, sine = widen(cos_ref[rows, :]), widen(sin_ref[rows, :])
        q_raw, k_raw = q_ref[rows, :], k_ref[rows, :]
        qr_ref[target, :] = (q_raw * cosine + swap_halves(q_raw) * sine).astype(jnp.bfloat16)
        kr_ref[target, :] = (k_raw * cosine + swap_halves(k_raw) * sine).astype(jnp.bfloat16)
        vr_ref[target, :] = v_ref[rows, :].astype(jnp.bfloat16)


def softmax_mix(query, pieces, factor):
    scores = []
    for keys, _, mask in pieces:
        score = dot_nt(query, keys)
        scores.append(score if mask is None else jnp.where(mask, score, masked_score))
    top = functools.reduce(jnp.maximum, [jnp.max(s, axis=-1, keepdims=True) for s in scores])
    weights = [jnp.exp2((s - top) * factor) for s in scores]
    total = functools.reduce(jnp.add, [jnp.sum(w, axis=-1, keepdims=True) for w in weights])
    inverse = 1.0 / total
    mixed = functools.reduce(
        jnp.add,
        [dot_nn((w * inverse).astype(jnp.bfloat16), piece[1]) for w, piece in zip(weights, pieces)],
    )
    return mixed, top * factor + jnp.log2(total)


def head_slice(head):
    return slice(head * HD, (head + 1) * HD)


def forward_first(
    q_ref, k_ref, v_ref, cos_ref, sin_ref, qr_ref, kr_ref, vr_ref, o_ref, lse_ref
):
    half = q_ref.shape[0]
    quarter = half // 2
    offsets = halves(quarter)
    load_rotated(offsets, quarter, q_ref, k_ref, v_ref, cos_ref, sin_ref, qr_ref, kr_ref, vr_ref)
    factor = HD ** (-0.5) * LOG2E
    mask = causal_mask(quarter, quarter)
    for head in range(HEAD_GROUP):
        cols = head_slice(head)
        early, late = slice(0, quarter), slice(quarter, half)
        k_early, v_early = kr_ref[early, cols], vr_ref[early, cols]
        mixed, lse = softmax_mix(qr_ref[early, cols], [(k_early, v_early, mask)], factor)
        o_ref[pl.ds(offsets[0], quarter), cols] = mixed.astype(jnp.bfloat16)
        lse_ref[0, early, head : head + 1] = lse
        mixed, lse = softmax_mix(
            qr_ref[late, cols],
            [(k_early, v_early, None), (kr_ref[late, cols], vr_ref[late, cols], mask)],
            factor,
        )
        o_ref[pl.ds(offsets[1], quarter), cols] = mixed.astype(jnp.bfloat16)
        lse_ref[0, late, head : head + 1] = lse


def forward_second(
    q_ref, k_ref, v_ref, cos_ref, sin_ref, ka_ref, va_ref, pos_ref,
    qr_ref, kr_ref, vr_ref, o_ref, lse_ref,
):
    half = q_ref.shape[0]
    quarter = half // 2
    cut = FIRST_DOC - half
    spill = cut - quarter
    offsets = halves(quarter)
    load_rotated(offsets, quarter, q_ref, k_ref, v_ref, cos_ref, sin_ref, qr_ref, kr_ref, vr_ref)
    factor = HD ** (-0.5) * LOG2E
    mask = causal_mask(cut, cut)
    mask_tail = tail_mask(pos_ref[pl.ds(offsets[1] + spill, half - cut), :])
    for head in range(HEAD_GROUP):
        cols = head_slice(head)
        early, late = slice(0, cut), slice(cut, half)
        mixed, lse = softmax_mix(
            qr_ref[early, cols],
            [
                (ka_ref[:, cols], va_ref[:, cols], None),
                (kr_ref[early, cols], vr_ref[early, cols], mask),
            ],
            factor,
        )
        low = mixed.astype(jnp.bfloat16)
        o_ref[pl.ds(offsets[0], quarter), cols] = low[:quarter]
        o_ref[pl.ds(offsets[1], spill), cols] = low[quarter:]
        lse_ref[0, early, head : head + 1] = lse
        mixed, lse = softmax_mix(
            qr_ref[late, cols], [(kr_ref[late, cols], vr_ref[late, cols], mask_tail)], factor
        )
        o_ref[pl.ds(offsets[1] + spill, half - cut), cols] = mixed.astype(jnp.bfloat16)
        lse_ref[0, late, head : head + 1] = lse


def backward_both(
    qa_ref, ka_ref, va_ref, qb_ref, kb_ref, vb_ref, ga_ref, gb_ref, la_ref, lb_ref,
    cosa_ref, sina_ref, cosb_ref, sinb_ref, pos_ref,
    dqa_ref, dka_ref, dva_ref, dqb_ref, dkb_ref, dvb_ref,
    go_a, go_b, tqa, tka, tva, tqb, tkb, tvb,
):
    half = qa_ref.shape[0]
    quarter = half // 2
    cut = FIRST_DOC - half
    spill = cut - quarter
    offsets = halves(quarter)
    scale_value = HD ** (-0.5)
    factor = scale_value * LOG2E
    for place, offset in enumerate(offsets):
        target, rows = pl.ds(place * quarter, quarter), pl.ds(offset, quarter)
        go_a[target, :] = ga_ref[rows, :]
        go_b[target, :] = gb_ref[rows, :]
    mask = causal_mask(quarter, quarter)
    mask_cut = causal_mask(cut, cut)
    mask_tail = tail_mask(pos_ref[pl.ds(offsets[1] + spill, half - cut), :])
    for accumulator in (tka, tva, tkb, tvb):
        accumulator[...] = jnp.zeros_like(accumulator)

    def attend(query, grad, lse, pieces):
        weights, weight_grads = [], []
        for k_ref, v_ref, rows, cols, mask, _, _ in pieces:
            weight = jnp.exp2(dot_nt(query, k_ref[rows, cols]) * factor - lse)
            weights.append(weight if mask is None else jnp.where(mask, weight, 0.0))
            weight_grads.append(dot_nt(grad, v_ref[rows, cols]))
        shared = functools.reduce(
            jnp.add,
            [jnp.sum(w * g, axis=-1, keepdims=True) for w, g in zip(weights, weight_grads)],
        )
        query_grad = None
        for weight, weight_grad, piece in zip(weights, weight_grads, pieces):
            k_ref, v_ref, rows, cols, _, tk, tv = piece
            score_grad = (weight * (weight_grad - shared)).astype(jnp.bfloat16)
            term = dot_nn(score_grad, k_ref[rows, cols])
            query_grad = term if query_grad is None else query_grad + term
            tk[rows, cols] += dot_tn(score_grad, query)
            tv[rows, cols] += dot_tn(weight.astype(jnp.bfloat16), grad)
        return query_grad

    for head in range(HEAD_GROUP):
        cols = head_slice(head)
        lane = slice(head, head + 1)
        early, late, whole = slice(0, quarter), slice(quarter, half), slice(0, half)
        tqa[early, cols] = attend(
            qa_ref[early, cols], go_a[early, cols], la_ref[0, early, lane],
            [(ka_ref, va_ref, early, cols, mask, tka, tva)],
        )
        tqa[late, cols] = attend(
            qa_ref[late, cols], go_a[late, cols], la_ref[0, late, lane],
            [
                (ka_ref, va_ref, early, cols, None, tka, tva),
                (ka_ref, va_ref, late, cols, mask, tka, tva),
            ],
        )
        early, late = slice(0, cut), slice(cut, half)
        tqb[early, cols] = attend(
            qb_ref[early, cols], go_b[early, cols], lb_ref[0, early, lane],
            [
                (ka_ref, va_ref, whole, cols, None, tka, tva),
                (kb_ref, vb_ref, early, cols, mask_cut, tkb, tvb),
            ],
        )
        tqb[late, cols] = attend(
            qb_ref[late, cols], go_b[late, cols], lb_ref[0, late, lane],
            [(kb_ref, vb_ref, late, cols, mask_tail, tkb, tvb)],
        )
    for place, offset in enumerate(offsets):
        source, rows = pl.ds(place * quarter, quarter), pl.ds(offset, quarter)
        for total, cos_ref, sin_ref, out_ref in (
            (tqa, cosa_ref, sina_ref, dqa_ref),
            (tka, cosa_ref, sina_ref, dka_ref),
            (tqb, cosb_ref, sinb_ref, dqb_ref),
            (tkb, cosb_ref, sinb_ref, dkb_ref),
        ):
            grad = total[source, :] * scale_value
            out_ref[rows, :] = (
                grad * widen(cos_ref[rows, :]) - swap_halves(grad) * widen(sin_ref[rows, :])
            ).astype(jnp.bfloat16)
        dva_ref[rows, :] = tva[source, :].astype(jnp.bfloat16)
        dvb_ref[rows, :] = tvb[source, :].astype(jnp.bfloat16)


COST_SCALE = 1.7


def cost_of(flops):
    return pl.CostEstimate(flops=int(COST_SCALE * flops), bytes_accessed=1000, transcendentals=0)


def rows_kernel(pairs, extra_count, dot, chunk, finish, *refs):
    lefts, weights = refs[:pairs], refs[pairs : 2 * pairs]
    extras = refs[2 * pairs : 2 * pairs + extra_count]
    outs = refs[2 * pairs + extra_count :]

    @pl.loop(0, outs[0].shape[0] // chunk)
    def _(step):
        rows = pl.ds(pl.multiple_of(step * chunk, chunk), chunk)
        total = None
        for left, weight in zip(lefts, weights):
            term = dot(left[rows, :], weight[...])
            total = term if total is None else total + term
        for out, value in zip(outs, finish(total, *[extra[rows, :] for extra in extras])):
            out[rows, :] = value.astype(out.dtype)


def keep_one(total):
    return (total,)


def rows_matmul(
    lefts, weights, dot, types, tile, chunk=1024, finish=keep_one, extras=(), pushes=()
):
    rows = lefts[0].shape[0]
    if dot is dot_nn:
        width = weights[0].shape[1]
        weight_specs = [pl.BlockSpec((w.shape[0], tile), lambda j: (0, j)) for w in weights]
    else:
        width = weights[0].shape[0]
        weight_specs = [pl.BlockSpec((tile, w.shape[1]), lambda j: (j, 0)) for w in weights]
    column = pl.BlockSpec((rows, tile), lambda j: (0, j))
    return grid_call(
        functools.partial(rows_kernel, len(lefts), len(extras), dot, min(chunk, rows), finish),
        [*lefts, *weights, *extras],
        [pl.BlockSpec(left.shape, lambda j: (0, 0)) for left in lefts]
        + weight_specs
        + [column] * len(extras),
        [jax.ShapeDtypeStruct((rows, width), kind) for kind in types],
        [column] * len(types),
        (width // tile,),
        2 * rows * width * sum(left.shape[1] for left in lefts),
        pushes=pushes,
    )


def sum_kernel(parts, chunk, *refs):
    lefts, rights, out = refs[:parts], refs[parts : 2 * parts], refs[-1]

    @pl.loop(0, out.shape[1] // chunk)
    def _(step):
        cols = pl.ds(pl.multiple_of(step * chunk, chunk), chunk)
        total = None
        for left, right in zip(lefts, rights):
            term = dot_tn(left[...], right[:, cols])
            total = term if total is None else total + term
        out[:, cols] = total.astype(out.dtype)


def sum_matmul(lefts, rights, tile, chunk, pushes=()):
    rows, height = lefts[0].shape
    width = rights[0].shape[1]
    return grid_call(
        functools.partial(sum_kernel, len(lefts), chunk),
        [*lefts, *rights],
        [pl.BlockSpec((rows, tile), lambda j: (0, j)) for _ in lefts]
        + [pl.BlockSpec((rows, width), lambda j: (0, 0)) for _ in rights],
        [jax.ShapeDtypeStruct((height, width), jnp.bfloat16)],
        [pl.BlockSpec((tile, width), lambda j: (j, 0))],
        (height // tile,),
        2 * rows * height * width * len(lefts),
        pushes=pushes,
    )


def partner_of(kind):
    index, place = lax.axis_index("fsdp"), lax.axis_index("tp")
    if kind == "near":
        return (index, place + 1 - 2 * (place % 2))
    if kind == "core":
        return sibling_id()
    return (index, place + 2 - 4 * (place // 2))


def start_pushes(kinds, sources, targets, send, receive):
    barrier = pltpu.get_barrier_semaphore()
    names = sorted(set(kinds))
    for kind in names:
        pl.semaphore_signal(
            barrier, inc=1, device_id=partner_of(kind), device_id_type=pl.DeviceIdType.MESH
        )
    pl.semaphore_wait(barrier, len(names))
    for place, kind in enumerate(kinds):
        push(
            sources[place], targets[place], send.at[place], receive.at[place], partner_of(kind)
        ).start()


def wait_pushes(kinds, sources, targets, send, receive):
    for place, kind in enumerate(kinds):
        push(
            sources[place], targets[place], send.at[place], receive.at[place], partner_of(kind)
        ).wait()


def pushing_kernel(kernel, axes, in_count, out_count, kinds, *refs):
    count = len(kinds)
    inputs, sources = refs[:in_count], refs[in_count : in_count + count]
    outs = refs[in_count + count : in_count + count + out_count]
    targets = refs[in_count + count + out_count : in_count + 2 * count + out_count]
    scratch, (send, receive) = refs[in_count + 2 * count + out_count : -2], refs[-2:]
    first = functools.reduce(jnp.logical_and, [pl.program_id(axis) == 0 for axis in range(axes)])
    last = functools.reduce(
        jnp.logical_and,
        [pl.program_id(axis) == pl.num_programs(axis) - 1 for axis in range(axes)],
    )

    @pl.when(first)
    def _():
        start_pushes(kinds, sources, targets, send, receive)

    kernel(*inputs, *outs, *scratch)

    @pl.when(last)
    def _():
        wait_pushes(kinds, sources, targets, send, receive)


def grid_call(
    kernel, operands, in_specs, outs, out_specs, grid, flops, scratch=(), pushes=(), vmem=60
):
    params = dict(
        dimension_semantics=("arbitrary",) * len(grid), vmem_limit_bytes=vmem * 1024 * 1024
    )
    operands, in_specs, outs = list(operands), list(in_specs), list(outs)
    out_specs, scratch = list(out_specs), list(scratch)
    if pushes:
        kinds = tuple(kind for kind, _ in pushes)
        kernel = functools.partial(
            pushing_kernel, kernel, len(grid), len(operands), len(outs), kinds
        )
        anywhere = [pl.BlockSpec(memory_space=pl.ANY)] * len(pushes)
        operands += [value for _, value in pushes]
        in_specs += anywhere
        outs += [jax.ShapeDtypeStruct(value.shape, value.dtype) for _, value in pushes]
        out_specs += anywhere
        scratch += [pltpu.SemaphoreType.DMA((len(pushes),))] * 2
        next_key[0] += 1
        params.update(collective_id=next_key[0], has_side_effects=True)
    return tuple(
        pl.pallas_call(
            kernel,
            out_shape=outs,
            grid=grid,
            in_specs=in_specs,
            out_specs=out_specs,
            scratch_shapes=scratch,
            compiler_params=pltpu.CompilerParams(**params),
            cost_estimate=cost_of(max(flops, 27 * 10**9) if pushes else flops),
        )(*operands)
    )


def swap_kernel(kinds, *refs):
    count = len(kinds)
    sources, targets, (send, receive) = refs[:count], refs[count : 2 * count], refs[2 * count :]
    start_pushes(kinds, sources, targets, send, receive)
    wait_pushes(kinds, sources, targets, send, receive)


def swap_call(*pushes):
    next_key[0] += 1
    kinds = tuple(kind for kind, _ in pushes)
    values = [value for _, value in pushes]
    return exchange_call(
        functools.partial(swap_kernel, kinds), next_key[0], values,
        [jax.ShapeDtypeStruct(value.shape, value.dtype) for value in values],
        [pltpu.SemaphoreType.DMA((len(pushes),))] * 2, flops=40 * 10**9,
    )


next_key = [11]


def sibling_id():
    index = lax.axis_index("fsdp")
    return (index + 1 - 2 * (index % 2), lax.axis_index("tp"))


def meet(partner):
    barrier = pltpu.get_barrier_semaphore()
    pl.semaphore_signal(barrier, inc=1, device_id=partner, device_id_type=pl.DeviceIdType.MESH)
    pl.semaphore_wait(barrier, 1)


def push(source, target, send, receive, partner):
    return pltpu.make_async_remote_copy(
        src_ref=source,
        dst_ref=target,
        send_sem=send,
        recv_sem=receive,
        device_id=partner,
        device_id_type=pl.DeviceIdType.MESH,
    )


def exchange_call(kernel, key, operands, outs, scratch, vmem=60, flops=4 * 10**9):
    anywhere = pl.BlockSpec(memory_space=pl.ANY)
    results = pl.pallas_call(
        kernel,
        out_shape=outs,
        in_specs=[anywhere] * len(operands),
        out_specs=[anywhere] * len(outs),
        scratch_shapes=scratch,
        compiler_params=pltpu.CompilerParams(
            collective_id=key, has_side_effects=True, vmem_limit_bytes=vmem * 1024 * 1024
        ),
        cost_estimate=cost_of(flops),
    )(*operands)
    return tuple(results) if len(outs) > 1 else results[0]


def relay(sources, targets, buffer, load, store):
    loads, stores = [], []
    for place, source in enumerate(sources):
        copy = pltpu.make_async_copy(source, buffer.at[place], load.at[place])
        copy.start()
        loads.append(copy)
    for place, target in enumerate(targets):
        loads[place].wait()
        copy = pltpu.make_async_copy(buffer.at[place], target, store.at[place])
        copy.start()
        stores.append(copy)
    for copy in stores:
        copy.wait()


def gather_kernel(own_ref, near_ref, full_ref, buffer, load, store, send, receive):
    partner = sibling_id()
    meet(partner)
    count = own_ref.shape[0]
    remotes = []
    for place, ref in enumerate((own_ref, near_ref)):
        remote = push(
            ref, full_ref.at[pl.ds((2 + place) * count, count)],
            send.at[place], receive.at[place], partner,
        )
        remote.start()
        remotes.append(remote)
    targets = [full_ref.at[pl.ds(place * count, count)] for place in range(2)]
    relay((own_ref, near_ref), targets, buffer, load, store)
    for remote in remotes:
        remote.wait()


def core_gather(own, near):
    shape = (4 * own.shape[0], own.shape[1])
    return exchange_call(
        gather_kernel, 1, [own, near], [jax.ShapeDtypeStruct(shape, own.dtype)],
        [pltpu.VMEM((2, *own.shape), own.dtype)] + [pltpu.SemaphoreType.DMA((2,))] * 4,
    )


def gather_two_kernel(
    own_ref, own_near_ref, got_ref, got_near_ref, first_ref, second_ref,
    buffer, load, store, send, receive,
):
    partner = sibling_id()
    far = lax.axis_index("tp") // 2
    meet(partner)
    count = own_ref.shape[0]

    def run(targets):
        sources = (own_ref, own_near_ref, got_ref, got_near_ref)
        remotes, places = [], []
        for place, ref in enumerate(sources):
            target, row = targets[place // 2], place % 2
            remote = push(
                ref, target.at[pl.ds((2 + row) * count, count)],
                send.at[place], receive.at[place], partner,
            )
            remote.start()
            remotes.append(remote)
            places.append(target.at[pl.ds(row * count, count)])
        relay(sources, places, buffer, load, store)
        for remote in remotes:
            remote.wait()

    @pl.when(far == 0)
    def _():
        run((first_ref, second_ref))

    @pl.when(far != 0)
    def _():
        run((second_ref, first_ref))


def core_gather_two(own, own_near, got, got_near):
    shape = (4 * own.shape[0], own.shape[1])
    return exchange_call(
        gather_two_kernel, 11, [own, own_near, got, got_near],
        [jax.ShapeDtypeStruct(shape, own.dtype)] * 2,
        [pltpu.VMEM((4, *own.shape), own.dtype)] + [pltpu.SemaphoreType.DMA((4,))] * 4,
    )


def reduce_kernel(term_ref, keep_ref, away_ref, mine, got, keep, away, local, send, receive, store):
    partner = sibling_id()
    meet(partner)
    pieces, count = mine.shape[0], mine.shape[1]
    half = pieces * count
    remotes, loads = [], []
    for piece in range(pieces):
        order = (piece + pieces // 2) % pieces
        remote = push(
            term_ref.at[pl.ds(half + order * count, count)], got.at[order],
            send.at[order], receive.at[order], partner,
        )
        remote.start()
        remotes.append(remote)
        load = pltpu.make_async_copy(
            term_ref.at[pl.ds(order * count, count)], mine.at[order], local.at[order]
        )
        load.start()
        loads.append(load)
    stores = []
    for piece in range(pieces):
        order = (piece + pieces // 2) % pieces
        loads[piece].wait()
        remotes[piece].wait()
        total = mine[order].astype(jnp.float32) + got[order].astype(jnp.float32)
        if order < pieces // 2:
            keep[order] = total
            copy = pltpu.make_async_copy(
                keep.at[order], keep_ref.at[pl.ds(order * count, count)], store.at[order]
            )
        else:
            slot = order - pieces // 2
            away[slot] = total.astype(away.dtype)
            copy = pltpu.make_async_copy(
                away.at[slot], away_ref.at[pl.ds(slot * count, count)], store.at[order]
            )
        copy.start()
        stores.append(copy)
    for copy in stores:
        copy.wait()


def core_reduce(term):
    rows, width = term.shape
    quarter = rows // 4
    pieces = 4
    count = 2 * quarter // pieces
    return exchange_call(
        reduce_kernel, 2, [term],
        [
            jax.ShapeDtypeStruct((quarter, width), jnp.float32),
            jax.ShapeDtypeStruct((quarter, width), term.dtype),
        ],
        [
            pltpu.VMEM((pieces, count, width), term.dtype),
            pltpu.VMEM((pieces, count, width), term.dtype),
            pltpu.VMEM((pieces // 2, count, width), jnp.float32),
            pltpu.VMEM((pieces // 2, count, width), term.dtype),
        ]
        + [pltpu.SemaphoreType.DMA((pieces,))] * 4,
    )


def pair_kernel(own_ref, *refs):
    others, (pair_ref, buffer, load, store, send, receive) = refs[:-6], refs[-6:]
    partner = sibling_id()
    core = lax.axis_index("fsdp") % 2
    far = lax.axis_index("tp") // 2
    meet(partner)
    base = pl.multiple_of(core * own_ref.shape[0], own_ref.shape[0])
    count = others[0].shape[0]
    owns = [own_ref.at[pl.ds(place * count, count)] for place in range(len(others))]

    def run(mine, theirs):
        remotes, targets = [], []
        for place in range(len(others)):
            target = pair_ref.at[pl.ds(base + place * count, count)]
            remote = push(theirs[place], target, send.at[place], receive.at[place], partner)
            remote.start()
            remotes.append(remote)
            targets.append(target)
        relay(mine, targets, buffer, load, store)
        for remote in remotes:
            remote.wait()

    @pl.when(core == far)
    def _():
        run(owns, others)

    @pl.when(core != far)
    def _():
        run(others, owns)


def core_pair(key, own, *others):
    shape = (2 * own.shape[0], own.shape[1])
    return exchange_call(
        pair_kernel, key, [own, *others], [jax.ShapeDtypeStruct(shape, own.dtype)],
        [pltpu.VMEM((len(others), *others[0].shape), own.dtype)]
        + [pltpu.SemaphoreType.DMA((len(others),))] * 4,
    )


def split_kernel(pair_ref, keep_ref, away_ref, buffer, load, store, send, receive):
    partner = sibling_id()
    core = lax.axis_index("fsdp") % 2
    far = lax.axis_index("tp") // 2
    meet(partner)
    count = keep_ref.shape[0]
    mine = pair_ref.at[pl.ds(pl.multiple_of(core * count, count), count)]
    theirs = pair_ref.at[pl.ds(pl.multiple_of((1 - core) * count, count), count)]

    def run(own_target, other_target):
        remote = push(theirs, other_target, send.at[0], receive.at[0], partner)
        remote.start()
        relay((mine,), (own_target,), buffer, load, store)
        remote.wait()

    @pl.when(core == far)
    def _():
        run(keep_ref, keep_ref)

    @pl.when(core != far)
    def _():
        run(away_ref, away_ref)


def core_split(key, pair):
    shape = (pair.shape[0] // 2, pair.shape[1])
    return exchange_call(
        split_kernel, key, [pair], [jax.ShapeDtypeStruct(shape, pair.dtype)] * 2,
        [pltpu.VMEM((1, *shape), pair.dtype)] + [pltpu.SemaphoreType.DMA((1,))] * 4,
    )


def attention_call(kernel, arrays, kinds, outs, scratch, pushes=()):
    rows, heads_local = arrays[-1].shape[0], outs[1]
    half = rows // 2
    groups = heads_local // HEAD_GROUP
    width = HEAD_GROUP * HD

    def spec(kind):
        if kind == "table":
            return pl.BlockSpec((half, HD), lambda s, g: (s, 0))
        if kind == "column":
            return pl.BlockSpec((half, 1), lambda s, g: (s, 0))
        if kind == "lse":
            return pl.BlockSpec((1, half, HEAD_GROUP), lambda s, g: (g, s, 0))
        shift = kind * groups
        return pl.BlockSpec((half, width), lambda s, g: (s, shift + g))

    def shape(kind):
        if kind == "lse":
            return jax.ShapeDtypeStruct((groups, rows, HEAD_GROUP), jnp.float32)
        return jax.ShapeDtypeStruct((rows, heads_local * HD), jnp.bfloat16)

    return grid_call(
        kernel,
        arrays,
        [spec(kind) for kind in kinds],
        [shape(kind) for kind in outs[0]],
        [spec(kind) for kind in outs[0]],
        (rows // half, groups),
        4 * len(outs[0]) ** 2 * rows * rows * heads_local * HD // 16,
        scratch=scratch(half, width),
        pushes=pushes,
    )


def backward_scratch(half, width):
    return [pltpu.VMEM((half, width), jnp.bfloat16)] * 2 + [
        pltpu.VMEM((half, width), jnp.float32)
    ] * 6


def no_scratch(half, width):
    return []


def head_tables(positions):
    half_width = HD // 2
    frequency = rope_theta ** (-(jnp.arange(half_width, dtype=jnp.float32) * 2.0 / HD))
    angles = positions.astype(jnp.float32)[:, None] * frequency[None, :]
    cosine, sine = jnp.cos(angles), jnp.sin(angles)
    return (
        jnp.concatenate([cosine, cosine], axis=-1),
        jnp.concatenate([-sine, sine], axis=-1),
    )


def paired_device(
    block_in,
    out_cotangent,
    segment_ids,
    doc_positions,
    norm1_gain,
    qkv_weight,
    out_weight,
    norm2_gain,
    gate_up_weight,
    down_weight,
):
    fsdp_count, tp_count = lax.axis_size("fsdp"), lax.axis_size("tp")
    core = lax.axis_index("fsdp") % 2
    lane_z = lax.axis_index("tp")
    near, far = lane_z % 2, lane_z // 2
    core_pairs = [(i, i ^ 1) for i in range(fsdp_count)]
    near_pairs = [(i, i ^ 1) for i in range(tp_count)]
    far_pairs = [(i, i ^ 2) for i in range(tp_count)]
    plane_groups = [list(range(first, fsdp_count, 2)) for first in range(2)]
    rows = block_in.shape[1]
    local_cols = qkv_weight.shape[2]
    heads_local = local_cols // HD
    gain_one = norm1_gain.astype(jnp.float32)
    gain_two = norm2_gain.astype(jnp.float32)

    def swap_core(value):
        return lax.ppermute(value, "fsdp", core_pairs)

    def swap_near(value):
        return lax.ppermute(value, "tp", near_pairs)

    def swap_far(value):
        return lax.ppermute(value, "tp", far_pairs)

    def pick_tile(size):
        return 512 if size % 512 == 0 else 768

    tokens = []

    def act(work, *inputs, sends=()):
        values = [*inputs, *[value for _, value in sends]]
        held = lax.optimization_barrier((*values, *tokens))[: len(values)]
        if sends:
            kinds = [kind for kind, _ in sends]
            result = work(*held[: len(inputs)], pushes=list(zip(kinds, held[len(inputs) :])))
        else:
            result = work(*held)
        tokens[:] = result if isinstance(result, tuple) else (result,)
        return result[0] if isinstance(result, tuple) and len(result) == 1 else result

    def swap(*sends):
        return act(lambda pushes: swap_call(*pushes), sends=sends)

    def pick(value, index):
        return lax.dynamic_index_in_dim(value, index, 0, keepdims=False)

    def place_tokens(value, got):
        keep = pick(value, far)
        return jnp.where(far == 0, keep, got), jnp.where(far == 0, got, keep)

    def join(left, right):
        return jnp.concatenate([left, right], axis=0)

    def plane_gather(pair):
        return lax.all_gather(pair, "fsdp", axis=0, tiled=True, axis_index_groups=plane_groups)

    def plane_scatter(grad):
        return lax.psum_scatter(
            grad, "fsdp", scatter_dimension=0, tiled=True, axis_index_groups=plane_groups
        )

    def gather_weight(key, local, *others):
        return plane_gather(act(lambda own, *got: core_pair(key, own, *got), local, *others))

    def halve(value):
        count = value.shape[0] // 2
        return value[:count], value[count:]

    def add_wide(left, right):
        return left.astype(jnp.float32) + right.astype(jnp.float32)

    def chained(value, *others):
        return lax.optimization_barrier((value, *others))[0]

    def scatter_gains(gains):
        for axis, size in (("fsdp", fsdp_count), ("tp", tp_count)):
            index = lax.axis_index(axis)
            step = size // 2
            while step >= 1:
                bit = (index // step) % 2
                parts = gains.reshape(gains.shape[0], 2, gains.shape[1] // 2)
                sent = lax.dynamic_index_in_dim(parts, 1 - bit, 1, keepdims=False)
                kept = lax.dynamic_index_in_dim(parts, bit, 1, keepdims=False)
                gains = kept + lax.ppermute(sent, axis, [(i, i ^ step) for i in range(size)])
                step //= 2
        return gains

    def wide_dot(left, right, pushes=()):
        return rows_matmul(
            [left], [right], dot_nn, [jnp.float32], pick_tile(right.shape[1]), pushes=pushes
        )

    def dot_bf16(left, right, pushes=()):
        return rows_matmul(
            [left], [right], dot_nn, [jnp.bfloat16], pick_tile(right.shape[1]), pushes=pushes
        )

    def grad_sum(left, right, left_next, right_next, pushes=()):
        chunk = pick_tile(right.shape[1])
        return sum_matmul(
            [left, left_next], [right, right_next], pick_tile(left.shape[1]),
            2 * chunk if right.shape[1] % (2 * chunk) == 0 else chunk, pushes=pushes,
        )

    def heads_back(grad, weight, pushes=()):
        return rows_matmul(
            [grad], [weight], dot_nt, [jnp.bfloat16], pick_tile(weight.shape[0]), pushes=pushes
        )

    def rms_pack(stream, gain):
        scale = rms_scale(stream)
        return scale, (stream * scale * gain).astype(jnp.bfloat16)

    qkv_local = qkv_weight.reshape(qkv_weight.shape[0], 3 * local_cols)
    gate_local, up_local = gate_up_weight[:, 0], gate_up_weight[:, 1]

    next_key[0] = 11
    places = jnp.broadcast_to(doc_positions[:, None, :], (2, 8, rows))

    def first_norm(part):
        stream = part.astype(jnp.float32)
        return (stream, *rms_pack(stream, gain_one))

    s_own, r_own, n_own = act(lambda value: first_norm(pick(value, far)), block_in)
    near_own, qkv_other, place_got = swap(
        ("near", n_own), ("far", qkv_local), ("far", pick(places, 1 - far))
    )
    qkv_full = gather_weight(4, qkv_local, qkv_other)
    places = join(*place_tokens(places, place_got))

    def make_tables(own, other):
        order = join(own, other)[::8].reshape(2, 2, 2, rows)
        early, late = order[:, :, 0].reshape(-1), order[:, :, 1].reshape(-1)
        return (*head_tables(early), *head_tables(late), late[:, None])

    c_own = pick(out_cotangent, far)
    stream_got, c_near_own, out_other, near_places = swap(
        ("far", pick(block_in, 1 - far)), ("near", c_own), ("far", out_weight), ("near", places)
    )
    places = join(places, near_places)
    out_full = gather_weight(3, out_weight, out_other)
    s_got, r_got, n_got = act(first_norm, stream_got)
    near_got, gate_other, core_places = swap(
        ("near", n_got), ("far", gate_local), ("core", places)
    )
    gate_full = gather_weight(5, gate_local, gate_other)
    h1_first, h1_second = act(core_gather_two, n_own, near_own, n_got, near_got)
    streams = [jnp.where(far == 0, s_own, s_got), jnp.where(far == 0, s_got, s_own)]
    scales_one = [jnp.where(far == 0, r_own, r_got), jnp.where(far == 0, r_got, r_own)]

    def attend_first(projected, pushes=()):
        arrays = [projected, projected, projected, *tables[0]]
        return attention_call(
            forward_first, arrays, [0, 1, 2, "table", "table"],
            ([0, 0, 0, 0, "lse"], heads_local), no_scratch, pushes,
        )

    def attend_second(projected, pushes=()):
        arrays = [projected, projected, projected, *tables[1], saved[0][1], saved[0][2], reach]
        return attention_call(
            forward_second, arrays, [0, 1, 2, "table", "table", 0, 0, "column"],
            ([0, 0, 0, 0, "lse"], heads_local), no_scratch, pushes,
        )

    up_other = swap_far(chained(up_local, gate_other))
    cos_first, sin_first, cos_second, sin_second, reach = act(
        make_tables, places, core_places
    )
    tables = [(cos_first, sin_first), (cos_second, sin_second)]
    projected = act(wide_dot, h1_first, qkv_full)
    results = act(attend_first, projected)
    up_full = gather_weight(5, up_local, up_other)
    down_other = swap_far(chained(down_weight, up_other))
    saved, lses, mixed_first = [results[:3]], [results[4]], results[3]
    term_first = act(dot_bf16, mixed_first, out_full)
    keep_first, send_first = act(core_reduce, term_first)
    projected, branch_first = act(
        wide_dot, h1_second, qkv_full, sends=[("near", send_first)]
    )

    def second_norm(stream, keep, got):
        middle = stream + keep + got.astype(jnp.float32)
        return (middle, *rms_pack(middle, gain_two))

    m_first, q_first, n_first = act(second_norm, streams[0], keep_first, branch_first)
    *results, near_first = act(attend_second, projected, sends=[("near", n_first)])
    saved.append(results[:3])
    lses.append(results[4])
    mixed_second = results[3]
    term_second = act(dot_bf16, mixed_second, out_full)
    keep_second, send_second = act(core_reduce, term_second)
    h2_first = act(core_gather, n_first, near_first)
    down_full_pair = act(lambda own, got: core_pair(6, own, got), down_weight, down_other)
    down_full = plane_gather(down_full_pair)
    c_got = swap_far(chained(pick(out_cotangent, 1 - far), down_full_pair))

    gate_first, branch_second = act(
        wide_dot, h2_first, gate_full, sends=[("near", send_second)]
    )
    m_second, q_second, n_second = act(second_norm, streams[1], keep_second, branch_second)

    def rise(hidden, weight, gate, pushes=()):
        return rows_matmul(
            [hidden], [weight], dot_nn, [jnp.float32, jnp.bfloat16], pick_tile(weight.shape[1]),
            finish=lambda up, gate: (up, gate * jax.nn.sigmoid(gate) * up), extras=[gate],
            pushes=pushes,
        )

    up_first, a_first, near_second = act(
        rise, h2_first, up_full, gate_first, sends=[("near", n_second)]
    )
    h2_second = act(core_gather, n_second, near_second)
    gate_second, c_near_got = act(
        wide_dot, h2_second, gate_full, sends=[("near", c_got)]
    )
    y_first, y_second = act(core_gather_two, c_own, c_near_own, c_got, c_near_got)
    c_first, c_second = jnp.where(far == 0, c_own, c_got), jnp.where(far == 0, c_got, c_own)
    up_second, a_second = act(rise, h2_second, up_full, gate_second)
    down_sum = plane_scatter(act(grad_sum, a_first, y_first, a_second, y_second))

    def fall_finish(act_grad, gate, up):
        sigmoid_gate = jax.nn.sigmoid(gate)
        return (
            act_grad * up * sigmoid_gate * (1.0 + gate * (1.0 - sigmoid_gate)),
            act_grad * (gate * sigmoid_gate),
        )

    def fall(cotangent, weight, gate, up, pushes=()):
        return rows_matmul(
            [cotangent], [weight], dot_nt, [jnp.bfloat16] * 2, pick_tile(weight.shape[0]),
            chunk=512, finish=fall_finish, extras=[gate, up], pushes=pushes,
        )

    def hidden_grad(gate_grad, up_grad, gate_weight, up_weight, pushes=()):
        return rows_matmul(
            [gate_grad, up_grad], [gate_weight, up_weight], dot_nt, [jnp.bfloat16],
            pick_tile(gate_weight.shape[0]), pushes=pushes,
        )

    def second_back(middle, scale, keep, got, cotangent):
        grad, gain_term = norm_back(middle, scale, gain_two, keep + got.astype(jnp.float32))
        grad = cotangent.astype(jnp.float32) + grad
        return grad, grad.astype(jnp.bfloat16), gain_term

    dg_first, du_first = act(fall, y_first, down_full, gate_first, up_first)
    term_first = act(hidden_grad, dg_first, du_first, gate_full, up_full)
    keep_first, send_first = act(core_reduce, term_first)
    dg_second, du_second, back_first = act(
        fall, y_second, down_full, gate_second, up_second, sends=[("near", send_first)]
    )
    g_first, n_first, gain_two_first = act(
        second_back, m_first, q_first, keep_first, back_first, c_first
    )
    term_second, near_first = act(
        hidden_grad, dg_second, du_second, gate_full, up_full, sends=[("near", n_first)]
    )
    keep_second, send_second = act(core_reduce, term_second)
    d_first = act(core_gather, n_first, near_first)
    grad_gate, back_second = act(
        grad_sum, h2_first, dg_first, h2_second, dg_second, sends=[("near", send_second)]
    )
    gate_sum = plane_scatter(grad_gate)
    g_second, n_second, gain_two_second = act(
        second_back, m_second, q_second, keep_second, back_second, c_second
    )
    heads_first = act(heads_back, d_first, out_full)
    down_mine, down_away = act(lambda pair: core_split(10, pair), down_sum)
    down_got = swap_far(down_away)
    grad_up, near_second = act(
        grad_sum, h2_first, du_first, h2_second, du_second, sends=[("near", n_second)]
    )
    up_sum = plane_scatter(grad_up)

    d_second = act(core_gather, n_second, near_second)
    heads_second = act(heads_back, d_second, out_full)
    grad_out = act(grad_sum, mixed_first, d_first, mixed_second, d_second)
    out_sum = plane_scatter(grad_out)
    mlp_first = act(dot_bf16, a_first, down_full)
    mlp_keep_first, mlp_send_first = act(core_reduce, mlp_first)
    mlp_second = act(dot_bf16, a_second, down_full)
    mlp_keep_second, mlp_send_second = act(core_reduce, mlp_second)
    gate_mine, gate_away = act(lambda pair: core_split(9, pair), gate_sum)
    gate_got = swap_far(gate_away)

    def attend_back(heads_first, heads_second, pushes=()):
        return attention_call(
            backward_both,
            [
                *saved[0], *saved[1], heads_first, heads_second, *lses,
                *tables[0], *tables[1], reach,
            ],
            [0] * 8 + ["lse"] * 2 + ["table"] * 4 + ["column"],
            ([0] * 6, heads_local),
            backward_scratch,
            pushes,
        )

    *grads, mlp_branch_first = act(
        attend_back, heads_first, heads_second, sends=[("near", mlp_send_first)]
    )
    up_mine, up_away = act(lambda pair: core_split(9, pair), up_sum)
    up_got = swap_far(up_away)
    p_first, p_second = act(
        lambda *parts: (
            jnp.concatenate(parts[:3], axis=1),
            jnp.concatenate(parts[3:], axis=1),
        ),
        *grads,
    )

    def finish_output(first, first_keep, first_got, second, second_keep, second_got):
        first = (first + first_keep + first_got.astype(jnp.float32)).astype(jnp.bfloat16)
        second = (second + second_keep + second_got.astype(jnp.float32)).astype(jnp.bfloat16)
        return jnp.where(far == 0, first, second), jnp.where(far == 0, second, first)

    grad_qkv, mlp_branch_second = act(
        grad_sum, h1_first, p_first, h1_second, p_second, sends=[("near", mlp_send_second)]
    )
    qkv_sum = plane_scatter(grad_qkv)
    out_keep, out_send = act(
        finish_output,
        m_first, mlp_keep_first, mlp_branch_first, m_second, mlp_keep_second, mlp_branch_second,
    )
    out_got = swap_far(out_send)
    term_first = act(heads_back, p_first, qkv_full)
    keep_first, send_first = act(core_reduce, term_first)
    term_second, back_first = act(
        heads_back, p_second, qkv_full, sends=[("near", send_first)]
    )
    keep_second, send_second = act(core_reduce, term_second)
    out_mine, out_away = act(lambda pair: core_split(8, pair), out_sum)
    def settle(keep, got):
        return jnp.stack([jnp.where(far == 0, keep, got), jnp.where(far == 0, got, keep)])

    def first_back(stream, scale, keep, got, grad):
        back, gain_term = norm_back(stream, scale, gain_one, keep + got.astype(jnp.float32))
        return grad + back, gain_term

    def last_back(stream, scale, keep, got, grad, first):
        second, gain_term = first_back(stream, scale, keep, got, grad)
        return (
            jnp.where(far == 0, first, second),
            jnp.where(far == 0, second, first).astype(jnp.bfloat16),
            gain_term,
        )

    back_second, out_back = swap(("near", send_second), ("far", out_away))
    i_first, gain_one_first = act(
        first_back, streams[0], scales_one[0], keep_first, back_first, g_first
    )
    in_keep, in_send, gain_one_second = act(
        last_back, streams[1], scales_one[1], keep_second, back_second, g_second, i_first
    )
    in_got = swap_far(in_send)
    down_owned = act(add_wide, down_mine, down_got)
    gate_owned = act(add_wide, gate_mine, gate_got)
    block_out = act(settle, out_keep, out_got)
    up_owned = act(add_wide, up_mine, up_got)
    gate_up_owned = act(lambda a, b: jnp.stack([a, b], axis=1), gate_owned, up_owned)
    out_owned = act(add_wide, out_mine, out_back)
    gains = scatter_gains(
        jnp.stack([gain_one_first + gain_one_second, gain_two_first + gain_two_second])
    )
    in_grad = act(lambda keep, got: settle(keep, got.astype(jnp.float32)), in_keep, in_got)
    qkv_mine, qkv_away = act(lambda pair: core_split(0, pair), qkv_sum)
    qkv_back = swap(("far", qkv_away))
    qkv_owned = act(add_wide, qkv_mine, qkv_back)
    return (
        block_out,
        in_grad,
        gains[0],
        qkv_owned.reshape(qkv_weight.shape),
        out_owned,
        gains[1],
        gate_up_owned,
        down_owned,
    )


def solution(mesh):
    sizes = (mesh.shape["fsdp"], mesh.shape["tp"])
    body = paired_device if sizes == (8, 4) else per_device
    in_specs = (
        P("fsdp", "tp", None),
        P("fsdp", "tp", None),
        P("fsdp", "tp"),
        P("fsdp", "tp"),
        P(),
        P("fsdp", None, "tp"),
        P(("tp", "fsdp"), None),
        P(),
        P("fsdp", None, "tp"),
        P(("tp", "fsdp"), None),
    )
    out_specs = (
        P("fsdp", "tp", None),
        P("fsdp", "tp", None),
        P(("fsdp", "tp")),
        P("fsdp", None, "tp"),
        P(("tp", "fsdp"), None),
        P(("fsdp", "tp")),
        P("fsdp", None, "tp"),
        P(("tp", "fsdp"), None),
    )
    return jax.shard_map(
        body, mesh=mesh, in_specs=in_specs, out_specs=out_specs, check_vma=False
    )
```

```python
import functools

import jax
import jax.numpy as jnp
from jax import lax
from jax.experimental import pallas as pl
from jax.experimental.pallas import tpu as pltpu
from jax.sharding import PartitionSpec as P

D = 3072
HD = 96


rms_epsilon = 1e-05
rope_theta = 10000.0
masked_score = -1e30
LOG2E = 1.4426950408889634


def rope_tables(positions, head_size):
    half_width = head_size // 2
    frequency = rope_theta ** (-(jnp.arange(half_width, dtype=jnp.float32) * 2.0 / head_size))
    angles = positions.astype(jnp.float32)[:, None] * frequency[None, :]
    return (jnp.cos(angles)[:, None, :], jnp.sin(angles)[:, None, :])


def rotate(values, cosine_part, sine_part):
    half_width = values.shape[-1] // 2
    lead_half = values[..., :half_width]
    tail_half = values[..., half_width:]
    return jnp.concatenate(
        [
            lead_half * cosine_part - tail_half * sine_part,
            tail_half * cosine_part + lead_half * sine_part,
        ],
        axis=-1,
    )


def unrotate(values, cosine_part, sine_part):
    half_width = values.shape[-1] // 2
    lead_half = values[..., :half_width]
    tail_half = values[..., half_width:]
    return jnp.concatenate(
        [
            lead_half * cosine_part + tail_half * sine_part,
            tail_half * cosine_part - lead_half * sine_part,
        ],
        axis=-1,
    )


def rms_scale(stream):
    return lax.rsqrt(jnp.mean(stream * stream, axis=-1, keepdims=True) + rms_epsilon)


def norm_back(stream, scale_rows, gain_vec, grad_rows):
    gained_grad = gain_vec * grad_rows
    input_grad = scale_rows * gained_grad - stream * scale_rows**3 * jnp.mean(
        gained_grad * stream, axis=-1, keepdims=True
    )
    return (input_grad, jnp.sum(grad_rows * stream * scale_rows, axis=0))


def allowed_mask(segment_tile, index_tile, segments):
    columns = jnp.arange(segments.shape[0], dtype=jnp.int32)
    return (segment_tile[:, None] == segments[None, :]) & (index_tile[:, None] >= columns[None, :])


def masked_scores(query_tile, key_rows, segment_tile, index_tile, segments, scale_value):
    scores = (
        jnp.einsum("qhd,khd->hqk", query_tile, key_rows, preferred_element_type=jnp.float32)
        * scale_value
    )
    return jnp.where(allowed_mask(segment_tile, index_tile, segments)[None], scores, masked_score)


def attention_forward(queries, key_rows, value_rows, segments, block_rows):
    seq_len, head_count, head_size = queries.shape
    tiles = seq_len // block_rows
    scale_value = head_size ** (-0.5)
    positions = jnp.arange(seq_len, dtype=jnp.int32)

    def query_block(packed):
        query_tile, segment_tile, index_tile = packed
        scores = masked_scores(
            query_tile, key_rows, segment_tile, index_tile, segments, scale_value
        )
        row_max = jnp.max(scores, axis=-1, keepdims=True)
        exponent = jnp.exp(scores - row_max)
        row_total = jnp.sum(exponent, axis=-1, keepdims=True)
        probs_low = (exponent / row_total).astype(jnp.bfloat16)
        mixed = jnp.einsum(
            "hqk,khd->qhd", probs_low, value_rows, preferred_element_type=jnp.float32
        )
        return (mixed, (row_max + jnp.log(row_total))[..., 0])

    mixed, log_total = lax.map(
        query_block,
        (
            queries.reshape(tiles, block_rows, head_count, head_size),
            segments.reshape(tiles, block_rows),
            positions.reshape(tiles, block_rows),
        ),
    )
    return (mixed.reshape(seq_len, head_count * head_size), log_total)


def attention_backward(queries, key_rows, value_rows, segments, log_total, out_grad, block_rows):
    seq_len, head_count, head_size = queries.shape
    tiles = seq_len // block_rows
    scale_value = head_size ** (-0.5)
    positions = jnp.arange(seq_len, dtype=jnp.int32)

    def query_block(carry, packed):
        key_acc, value_acc = carry
        query_tile, segment_tile, index_tile, total_tile, grad_tile = packed
        scores = masked_scores(
            query_tile, key_rows, segment_tile, index_tile, segments, scale_value
        )
        probs = jnp.exp(scores - total_tile[..., None])
        probs_low = probs.astype(jnp.bfloat16)
        prob_grad = jnp.einsum(
            "qhd,khd->hqk", grad_tile, value_rows, preferred_element_type=jnp.float32
        )
        score_grad = (
            probs * (prob_grad - jnp.sum(probs * prob_grad, axis=-1, keepdims=True))
        ).astype(jnp.bfloat16)
        query_grad = (
            jnp.einsum("hqk,khd->qhd", score_grad, key_rows, preferred_element_type=jnp.float32)
            * scale_value
        )
        key_acc = (
            key_acc
            + jnp.einsum("hqk,qhd->khd", score_grad, query_tile, preferred_element_type=jnp.float32)
            * scale_value
        )
        value_acc = value_acc + jnp.einsum(
            "hqk,qhd->khd", probs_low, grad_tile, preferred_element_type=jnp.float32
        )
        return ((key_acc, value_acc), query_grad)

    start_acc = (jnp.zeros(queries.shape, jnp.float32), jnp.zeros(queries.shape, jnp.float32))
    (key_grad, value_grad), query_grad = lax.scan(
        query_block,
        start_acc,
        (
            queries.reshape(tiles, block_rows, head_count, head_size),
            segments.reshape(tiles, block_rows),
            positions.reshape(tiles, block_rows),
            log_total,
            out_grad.reshape(tiles, block_rows, head_count, head_size),
        ),
    )
    return (query_grad.reshape(seq_len, head_count, head_size), key_grad, value_grad)


def gather_attention(qkv_weight, out_weight):
    return (
        lax.all_gather(qkv_weight, "fsdp", axis=0, tiled=True),
        lax.all_gather(out_weight, "fsdp", axis=0, tiled=True),
    )


def gather_feedforward(gate_up_weight, down_weight):
    return (
        lax.all_gather(gate_up_weight, "fsdp", axis=0, tiled=True),
        lax.all_gather(down_weight, "fsdp", axis=0, tiled=True),
    )


def per_device(
    block_in,
    out_cotangent,
    segment_ids,
    doc_positions,
    norm1_gain,
    qkv_weight,
    out_weight,
    norm2_gain,
    gate_up_weight,
    down_weight,
):
    micro_count = block_in.shape[0]
    fsdp_count = lax.axis_size("fsdp")
    segment_full, position_full = (
        lax.all_gather(segment_ids, "tp", axis=1, tiled=True),
        lax.all_gather(doc_positions, "tp", axis=1, tiled=True),
    )
    seq_len = segment_full.shape[1]
    block_rows = min(seq_len, 512)
    gain_one = norm1_gain.astype(jnp.float32)
    gain_two = norm2_gain.astype(jnp.float32)
    local_cols = qkv_weight.shape[2]
    local_units = gate_up_weight.shape[2]
    heads_local = local_cols // HD
    grad_qkv = jnp.zeros((D, 3, local_cols), jnp.float32)
    grad_out = jnp.zeros((out_weight.shape[0] * fsdp_count, D), jnp.float32)
    grad_gate_up = jnp.zeros((D, 2, local_units), jnp.float32)
    grad_down = jnp.zeros((down_weight.shape[0] * fsdp_count, D), jnp.float32)
    gain_one_acc = jnp.zeros((D,), jnp.float32)
    gain_two_acc = jnp.zeros((D,), jnp.float32)
    outputs = []
    input_grads = []
    for micro_index in range(micro_count):
        weights_fwd = (
            gather_attention(qkv_weight, out_weight),
            gather_feedforward(gate_up_weight, down_weight),
        )
        (qkv_full, out_full), (gate_up_full, down_full) = weights_fwd
        stream = block_in[micro_index].astype(jnp.float32)
        segment_row = segment_full[micro_index]
        cosine_part, sine_part = rope_tables(position_full[micro_index], HD)
        scale_one = rms_scale(stream)
        normed_one = (stream * scale_one * gain_one).astype(jnp.bfloat16)
        normed_one_full = lax.all_gather(normed_one, "tp", axis=0, tiled=True)
        projected = jnp.einsum(
            "sd,dtc->stc", normed_one_full, qkv_full, preferred_element_type=jnp.float32
        )
        queries = rotate(
            projected[:, 0].reshape(seq_len, heads_local, HD), cosine_part, sine_part
        ).astype(jnp.bfloat16)
        key_rows = rotate(
            projected[:, 1].reshape(seq_len, heads_local, HD), cosine_part, sine_part
        ).astype(jnp.bfloat16)
        value_rows = projected[:, 2].reshape(seq_len, heads_local, HD).astype(jnp.bfloat16)
        mixed, log_total = attention_forward(queries, key_rows, value_rows, segment_row, block_rows)
        attn_heads = mixed.astype(jnp.bfloat16)
        attn_term = jnp.dot(attn_heads, out_full, preferred_element_type=jnp.float32)
        attn_branch = lax.psum_scatter(attn_term, "tp", scatter_dimension=0, tiled=True)
        middle = stream + attn_branch
        scale_two = rms_scale(middle)
        normed_two = (middle * scale_two * gain_two).astype(jnp.bfloat16)
        normed_two_full = lax.all_gather(normed_two, "tp", axis=0, tiled=True)
        gate_up = jnp.einsum(
            "sd,dtf->stf", normed_two_full, gate_up_full, preferred_element_type=jnp.float32
        )
        gate_rows = gate_up[:, 0]
        up_rows = gate_up[:, 1]
        sigmoid_gate = jax.nn.sigmoid(gate_rows)
        silu_gate = gate_rows * sigmoid_gate
        activated = (silu_gate * up_rows).astype(jnp.bfloat16)
        mlp_term = jnp.dot(activated, down_full, preferred_element_type=jnp.float32)
        mlp_branch = lax.psum_scatter(
            mlp_term.astype(jnp.bfloat16), "tp", scatter_dimension=0, tiled=True
        ).astype(jnp.float32)
        outputs.append((middle + mlp_branch).astype(jnp.bfloat16))
        (qkv_back, out_back), (gate_up_back, down_back) = weights_fwd
        cotangent = out_cotangent[micro_index].astype(jnp.float32)
        cotangent_full = lax.all_gather(out_cotangent[micro_index], "tp", axis=0, tiled=True)
        grad_down = grad_down + jnp.einsum(
            "sf,sd->fd", activated, cotangent_full, preferred_element_type=jnp.float32
        )
        act_grad = jnp.einsum(
            "sd,fd->sf", cotangent_full, down_back, preferred_element_type=jnp.float32
        )
        gate_grad = act_grad * up_rows * sigmoid_gate * (1.0 + gate_rows * (1.0 - sigmoid_gate))
        up_grad = act_grad * silu_gate
        gate_up_grad = jnp.stack([gate_grad, up_grad], axis=1).astype(jnp.bfloat16)
        grad_gate_up = grad_gate_up + jnp.einsum(
            "sd,stf->dtf", normed_two_full, gate_up_grad, preferred_element_type=jnp.float32
        )
        normed_two_term = jnp.einsum(
            "stf,dtf->sd", gate_up_grad, gate_up_back, preferred_element_type=jnp.float32
        )
        normed_two_grad = lax.psum_scatter(normed_two_term, "tp", scatter_dimension=0, tiled=True)
        middle_back, gain_two_term = norm_back(middle, scale_two, gain_two, normed_two_grad)
        gain_two_acc = gain_two_acc + gain_two_term
        middle_grad = cotangent + middle_back
        attn_grad_full = lax.all_gather(middle_grad.astype(jnp.bfloat16), "tp", axis=0, tiled=True)
        grad_out = grad_out + jnp.einsum(
            "sc,sd->cd", attn_heads, attn_grad_full, preferred_element_type=jnp.float32
        )
        heads_grad = jnp.einsum(
            "sd,cd->sc", attn_grad_full, out_back, preferred_element_type=jnp.float32
        ).astype(jnp.bfloat16)
        query_grad, key_grad, value_grad = attention_backward(
            queries,
            key_rows,
            value_rows,
            segment_row,
            log_total,
            heads_grad.reshape(seq_len, heads_local, HD),
            block_rows,
        )
        projected_grad = jnp.stack(
            [
                unrotate(query_grad, cosine_part, sine_part).reshape(seq_len, local_cols),
                unrotate(key_grad, cosine_part, sine_part).reshape(seq_len, local_cols),
                value_grad.reshape(seq_len, local_cols),
            ],
            axis=1,
        ).astype(jnp.bfloat16)
        grad_qkv = grad_qkv + jnp.einsum(
            "sd,stc->dtc", normed_one_full, projected_grad, preferred_element_type=jnp.float32
        )
        normed_one_term = jnp.einsum(
            "stc,dtc->sd", projected_grad, qkv_back, preferred_element_type=jnp.float32
        )
        normed_one_grad = lax.psum_scatter(
            normed_one_term.astype(jnp.bfloat16), "tp", scatter_dimension=0, tiled=True
        ).astype(jnp.float32)
        stream_back, gain_one_term = norm_back(stream, scale_one, gain_one, normed_one_grad)
        gain_one_acc = gain_one_acc + gain_one_term
        input_grads.append(middle_grad + stream_back)
    owned_grads = (
        lax.psum_scatter(
            grad_qkv.astype(jnp.bfloat16), "fsdp", scatter_dimension=0, tiled=True
        ).astype(jnp.float32),
        lax.psum_scatter(
            grad_out.astype(jnp.bfloat16), "fsdp", scatter_dimension=0, tiled=True
        ).astype(jnp.float32),
        lax.psum_scatter(
            grad_gate_up.astype(jnp.bfloat16), "fsdp", scatter_dimension=0, tiled=True
        ).astype(jnp.float32),
        lax.psum_scatter(
            grad_down.astype(jnp.bfloat16), "fsdp", scatter_dimension=0, tiled=True
        ).astype(jnp.float32),
    )
    owned_gains = (
        lax.psum_scatter(gain_one_acc, ("fsdp", "tp"), scatter_dimension=0, tiled=True),
        lax.psum_scatter(gain_two_acc, ("fsdp", "tp"), scatter_dimension=0, tiled=True),
    )
    return (
        jnp.stack(outputs),
        jnp.stack(input_grads),
        owned_gains[0],
        owned_grads[0],
        owned_grads[1],
        owned_gains[1],
        owned_grads[2],
        owned_grads[3],
    )


HEAD_GROUP = 4
FIRST_DOC = 800


def dot_nt(left, right):
    return lax.dot_general(left, right, (((1,), (1,)), ((), ())), preferred_element_type=jnp.float32)


def dot_tn(left, right):
    return lax.dot_general(left, right, (((0,), (0,)), ((), ())), preferred_element_type=jnp.float32)


def dot_nn(left, right):
    return lax.dot_general(left, right, (((1,), (0,)), ((), ())), preferred_element_type=jnp.float32)


def swap_halves(values):
    lanes = lax.broadcasted_iota(jnp.int32, values.shape, 1)
    width = values.shape[1]
    return jnp.where(
        lanes % HD < HD // 2,
        pltpu.roll(values, width - HD // 2, 1),
        pltpu.roll(values, HD // 2, 1),
    )


def causal_mask(rows, columns):
    row_ids = lax.broadcasted_iota(jnp.int32, (rows, columns), 0)
    column_ids = lax.broadcasted_iota(jnp.int32, (rows, columns), 1)
    return row_ids >= column_ids


def tail_mask(reach):
    rows = reach.shape[0]
    row_ids = lax.broadcasted_iota(jnp.int32, (rows, rows), 0)
    column_ids = lax.broadcasted_iota(jnp.int32, (rows, rows), 1)
    return (row_ids >= column_ids) & (row_ids - column_ids <= reach)


def halves(quarter):
    first = lax.axis_index("tp") % 2
    return (
        pl.multiple_of(first * quarter, quarter),
        pl.multiple_of((1 - first) * quarter, quarter),
    )


def widen(table):
    return jnp.concatenate([table] * HEAD_GROUP, axis=1)


def load_rotated(offsets, quarter, q_ref, k_ref, v_ref, cos_ref, sin_ref, qr_ref, kr_ref, vr_ref):
    for place, offset in enumerate(offsets):
        rows = pl.ds(offset, quarter)
        target = pl.ds(place * quarter, quarter)
        cosine, sine = widen(cos_ref[rows, :]), widen(sin_ref[rows, :])
        q_raw, k_raw = q_ref[rows, :], k_ref[rows, :]
        qr_ref[target, :] = (q_raw * cosine + swap_halves(q_raw) * sine).astype(jnp.bfloat16)
        kr_ref[target, :] = (k_raw * cosine + swap_halves(k_raw) * sine).astype(jnp.bfloat16)
        vr_ref[target, :] = v_ref[rows, :].astype(jnp.bfloat16)


def softmax_mix(query, pieces, factor):
    scores = []
    for keys, _, mask in pieces:
        score = dot_nt(query, keys)
        scores.append(score if mask is None else jnp.where(mask, score, masked_score))
    top = functools.reduce(jnp.maximum, [jnp.max(s, axis=-1, keepdims=True) for s in scores])
    weights = [jnp.exp2((s - top) * factor) for s in scores]
    total = functools.reduce(jnp.add, [jnp.sum(w, axis=-1, keepdims=True) for w in weights])
    inverse = 1.0 / total
    mixed = functools.reduce(
        jnp.add,
        [dot_nn((w * inverse).astype(jnp.bfloat16), piece[1]) for w, piece in zip(weights, pieces)],
    )
    return mixed, top * factor + jnp.log2(total)


def head_slice(head):
    return slice(head * HD, (head + 1) * HD)


def forward_first(
    q_ref, k_ref, v_ref, cos_ref, sin_ref, qr_ref, kr_ref, vr_ref, o_ref, lse_ref
):
    half = q_ref.shape[0]
    quarter = half // 2
    offsets = halves(quarter)
    load_rotated(offsets, quarter, q_ref, k_ref, v_ref, cos_ref, sin_ref, qr_ref, kr_ref, vr_ref)
    factor = HD ** (-0.5) * LOG2E
    mask = causal_mask(quarter, quarter)
    for head in range(HEAD_GROUP):
        cols = head_slice(head)
        early, late = slice(0, quarter), slice(quarter, half)
        k_early, v_early = kr_ref[early, cols], vr_ref[early, cols]
        mixed, lse = softmax_mix(qr_ref[early, cols], [(k_early, v_early, mask)], factor)
        o_ref[pl.ds(offsets[0], quarter), cols] = mixed.astype(jnp.bfloat16)
        lse_ref[0, early, head : head + 1] = lse
        mixed, lse = softmax_mix(
            qr_ref[late, cols],
            [(k_early, v_early, None), (kr_ref[late, cols], vr_ref[late, cols], mask)],
            factor,
        )
        o_ref[pl.ds(offsets[1], quarter), cols] = mixed.astype(jnp.bfloat16)
        lse_ref[0, late, head : head + 1] = lse


def forward_second(
    q_ref, k_ref, v_ref, cos_ref, sin_ref, ka_ref, va_ref, pos_ref,
    qr_ref, kr_ref, vr_ref, o_ref, lse_ref,
):
    half = q_ref.shape[0]
    quarter = half // 2
    cut = FIRST_DOC - half
    spill = cut - quarter
    offsets = halves(quarter)
    load_rotated(offsets, quarter, q_ref, k_ref, v_ref, cos_ref, sin_ref, qr_ref, kr_ref, vr_ref)
    factor = HD ** (-0.5) * LOG2E
    mask = causal_mask(cut, cut)
    mask_tail = tail_mask(pos_ref[pl.ds(offsets[1] + spill, half - cut), :])
    for head in range(HEAD_GROUP):
        cols = head_slice(head)
        early, late = slice(0, cut), slice(cut, half)
        mixed, lse = softmax_mix(
            qr_ref[early, cols],
            [
                (ka_ref[:, cols], va_ref[:, cols], None),
                (kr_ref[early, cols], vr_ref[early, cols], mask),
            ],
            factor,
        )
        low = mixed.astype(jnp.bfloat16)
        o_ref[pl.ds(offsets[0], quarter), cols] = low[:quarter]
        o_ref[pl.ds(offsets[1], spill), cols] = low[quarter:]
        lse_ref[0, early, head : head + 1] = lse
        mixed, lse = softmax_mix(
            qr_ref[late, cols], [(kr_ref[late, cols], vr_ref[late, cols], mask_tail)], factor
        )
        o_ref[pl.ds(offsets[1] + spill, half - cut), cols] = mixed.astype(jnp.bfloat16)
        lse_ref[0, late, head : head + 1] = lse


def backward_both(
    qa_ref, ka_ref, va_ref, qb_ref, kb_ref, vb_ref, ga_ref, gb_ref, la_ref, lb_ref,
    cosa_ref, sina_ref, cosb_ref, sinb_ref, pos_ref,
    dqa_ref, dka_ref, dva_ref, dqb_ref, dkb_ref, dvb_ref,
    go_a, go_b, tqa, tka, tva, tqb, tkb, tvb,
):
    half = qa_ref.shape[0]
    quarter = half // 2
    cut = FIRST_DOC - half
    spill = cut - quarter
    offsets = halves(quarter)
    scale_value = HD ** (-0.5)
    factor = scale_value * LOG2E
    for place, offset in enumerate(offsets):
        target, rows = pl.ds(place * quarter, quarter), pl.ds(offset, quarter)
        go_a[target, :] = ga_ref[rows, :]
        go_b[target, :] = gb_ref[rows, :]
    mask = causal_mask(quarter, quarter)
    mask_cut = causal_mask(cut, cut)
    mask_tail = tail_mask(pos_ref[pl.ds(offsets[1] + spill, half - cut), :])
    for accumulator in (tka, tva, tkb, tvb):
        accumulator[...] = jnp.zeros_like(accumulator)

    def attend(query, grad, lse, pieces):
        weights, weight_grads = [], []
        for k_ref, v_ref, rows, cols, mask, _, _ in pieces:
            weight = jnp.exp2(dot_nt(query, k_ref[rows, cols]) * factor - lse)
            weights.append(weight if mask is None else jnp.where(mask, weight, 0.0))
            weight_grads.append(dot_nt(grad, v_ref[rows, cols]))
        shared = functools.reduce(
            jnp.add,
            [jnp.sum(w * g, axis=-1, keepdims=True) for w, g in zip(weights, weight_grads)],
        )
        query_grad = None
        for weight, weight_grad, piece in zip(weights, weight_grads, pieces):
            k_ref, v_ref, rows, cols, _, tk, tv = piece
            score_grad = (weight * (weight_grad - shared)).astype(jnp.bfloat16)
            term = dot_nn(score_grad, k_ref[rows, cols])
            query_grad = term if query_grad is None else query_grad + term
            tk[rows, cols] += dot_tn(score_grad, query)
            tv[rows, cols] += dot_tn(weight.astype(jnp.bfloat16), grad)
        return query_grad

    for head in range(HEAD_GROUP):
        cols = head_slice(head)
        lane = slice(head, head + 1)
        early, late, whole = slice(0, quarter), slice(quarter, half), slice(0, half)
        tqa[early, cols] = attend(
            qa_ref[early, cols], go_a[early, cols], la_ref[0, early, lane],
            [(ka_ref, va_ref, early, cols, mask, tka, tva)],
        )
        tqa[late, cols] = attend(
            qa_ref[late, cols], go_a[late, cols], la_ref[0, late, lane],
            [
                (ka_ref, va_ref, early, cols, None, tka, tva),
                (ka_ref, va_ref, late, cols, mask, tka, tva),
            ],
        )
        early, late = slice(0, cut), slice(cut, half)
        tqb[early, cols] = attend(
            qb_ref[early, cols], go_b[early, cols], lb_ref[0, early, lane],
            [
                (ka_ref, va_ref, whole, cols, None, tka, tva),
                (kb_ref, vb_ref, early, cols, mask_cut, tkb, tvb),
            ],
        )
        tqb[late, cols] = attend(
            qb_ref[late, cols], go_b[late, cols], lb_ref[0, late, lane],
            [(kb_ref, vb_ref, late, cols, mask_tail, tkb, tvb)],
        )
    for place, offset in enumerate(offsets):
        source, rows = pl.ds(place * quarter, quarter), pl.ds(offset, quarter)
        for total, cos_ref, sin_ref, out_ref in (
            (tqa, cosa_ref, sina_ref, dqa_ref),
            (tka, cosa_ref, sina_ref, dka_ref),
            (tqb, cosb_ref, sinb_ref, dqb_ref),
            (tkb, cosb_ref, sinb_ref, dkb_ref),
        ):
            grad = total[source, :] * scale_value
            out_ref[rows, :] = (
                grad * widen(cos_ref[rows, :]) - swap_halves(grad) * widen(sin_ref[rows, :])
            ).astype(jnp.bfloat16)
        dva_ref[rows, :] = tva[source, :].astype(jnp.bfloat16)
        dvb_ref[rows, :] = tvb[source, :].astype(jnp.bfloat16)


COST_SCALE = 1.7


def cost_of(flops):
    return pl.CostEstimate(flops=int(COST_SCALE * flops), bytes_accessed=1000, transcendentals=0)


def rows_kernel(pairs, extra_count, dot, chunk, finish, *refs):
    lefts, weights = refs[:pairs], refs[pairs : 2 * pairs]
    extras = refs[2 * pairs : 2 * pairs + extra_count]
    outs = refs[2 * pairs + extra_count :]

    @pl.loop(0, outs[0].shape[0] // chunk)
    def _(step):
        rows = pl.ds(pl.multiple_of(step * chunk, chunk), chunk)
        total = None
        for left, weight in zip(lefts, weights):
            term = dot(left[rows, :], weight[...])
            total = term if total is None else total + term
        for out, value in zip(outs, finish(total, *[extra[rows, :] for extra in extras])):
            out[rows, :] = value.astype(out.dtype)


def keep_one(total):
    return (total,)


def rows_matmul(
    lefts, weights, dot, types, tile, chunk=1024, finish=keep_one, extras=(), pushes=()
):
    rows = lefts[0].shape[0]
    if dot is dot_nn:
        width = weights[0].shape[1]
        weight_specs = [pl.BlockSpec((w.shape[0], tile), lambda j: (0, j)) for w in weights]
    else:
        width = weights[0].shape[0]
        weight_specs = [pl.BlockSpec((tile, w.shape[1]), lambda j: (j, 0)) for w in weights]
    column = pl.BlockSpec((rows, tile), lambda j: (0, j))
    return grid_call(
        functools.partial(rows_kernel, len(lefts), len(extras), dot, min(chunk, rows), finish),
        [*lefts, *weights, *extras],
        [pl.BlockSpec(left.shape, lambda j: (0, 0)) for left in lefts]
        + weight_specs
        + [column] * len(extras),
        [jax.ShapeDtypeStruct((rows, width), kind) for kind in types],
        [column] * len(types),
        (width // tile,),
        2 * rows * width * sum(left.shape[1] for left in lefts),
        pushes=pushes,
    )


def sum_kernel(parts, chunk, *refs):
    lefts, rights, out = refs[:parts], refs[parts : 2 * parts], refs[-1]

    @pl.loop(0, out.shape[1] // chunk)
    def _(step):
        cols = pl.ds(pl.multiple_of(step * chunk, chunk), chunk)
        total = None
        for left, right in zip(lefts, rights):
            term = dot_tn(left[...], right[:, cols])
            total = term if total is None else total + term
        out[:, cols] = total.astype(out.dtype)


def sum_matmul(lefts, rights, tile, chunk, pushes=()):
    rows, height = lefts[0].shape
    width = rights[0].shape[1]
    return grid_call(
        functools.partial(sum_kernel, len(lefts), chunk),
        [*lefts, *rights],
        [pl.BlockSpec((rows, tile), lambda j: (0, j)) for _ in lefts]
        + [pl.BlockSpec((rows, width), lambda j: (0, 0)) for _ in rights],
        [jax.ShapeDtypeStruct((height, width), jnp.bfloat16)],
        [pl.BlockSpec((tile, width), lambda j: (j, 0))],
        (height // tile,),
        2 * rows * height * width * len(lefts),
        pushes=pushes,
    )


def partner_of(kind):
    index, place = lax.axis_index("fsdp"), lax.axis_index("tp")
    if kind == "near":
        return (index, place + 1 - 2 * (place % 2))
    if kind == "core":
        return sibling_id()
    return (index, place + 2 - 4 * (place // 2))


def start_pushes(kinds, sources, targets, send, receive):
    barrier = pltpu.get_barrier_semaphore()
    names = sorted(set(kinds))
    for kind in names:
        pl.semaphore_signal(
            barrier, inc=1, device_id=partner_of(kind), device_id_type=pl.DeviceIdType.MESH
        )
    pl.semaphore_wait(barrier, len(names))
    for place, kind in enumerate(kinds):
        push(
            sources[place], targets[place], send.at[place], receive.at[place], partner_of(kind)
        ).start()


def wait_pushes(kinds, sources, targets, send, receive):
    for place, kind in enumerate(kinds):
        push(
            sources[place], targets[place], send.at[place], receive.at[place], partner_of(kind)
        ).wait()


def pushing_kernel(kernel, axes, in_count, out_count, kinds, *refs):
    count = len(kinds)
    inputs, sources = refs[:in_count], refs[in_count : in_count + count]
    outs = refs[in_count + count : in_count + count + out_count]
    targets = refs[in_count + count + out_count : in_count + 2 * count + out_count]
    scratch, (send, receive) = refs[in_count + 2 * count + out_count : -2], refs[-2:]
    first = functools.reduce(jnp.logical_and, [pl.program_id(axis) == 0 for axis in range(axes)])
    last = functools.reduce(
        jnp.logical_and,
        [pl.program_id(axis) == pl.num_programs(axis) - 1 for axis in range(axes)],
    )

    @pl.when(first)
    def _():
        start_pushes(kinds, sources, targets, send, receive)

    kernel(*inputs, *outs, *scratch)

    @pl.when(last)
    def _():
        wait_pushes(kinds, sources, targets, send, receive)


def grid_call(
    kernel, operands, in_specs, outs, out_specs, grid, flops, scratch=(), pushes=(), vmem=60
):
    params = dict(
        dimension_semantics=("arbitrary",) * len(grid), vmem_limit_bytes=vmem * 1024 * 1024
    )
    operands, in_specs, outs = list(operands), list(in_specs), list(outs)
    out_specs, scratch = list(out_specs), list(scratch)
    if pushes:
        kinds = tuple(kind for kind, _ in pushes)
        kernel = functools.partial(
            pushing_kernel, kernel, len(grid), len(operands), len(outs), kinds
        )
        anywhere = [pl.BlockSpec(memory_space=pl.ANY)] * len(pushes)
        operands += [value for _, value in pushes]
        in_specs += anywhere
        outs += [jax.ShapeDtypeStruct(value.shape, value.dtype) for _, value in pushes]
        out_specs += anywhere
        scratch += [pltpu.SemaphoreType.DMA((len(pushes),))] * 2
        next_key[0] += 1
        params.update(collective_id=next_key[0], has_side_effects=True)
    return tuple(
        pl.pallas_call(
            kernel,
            out_shape=outs,
            grid=grid,
            in_specs=in_specs,
            out_specs=out_specs,
            scratch_shapes=scratch,
            compiler_params=pltpu.CompilerParams(**params),
            cost_estimate=cost_of(max(flops, 27 * 10**9) if pushes else flops),
        )(*operands)
    )


def swap_kernel(kinds, *refs):
    count = len(kinds)
    sources, targets, (send, receive) = refs[:count], refs[count : 2 * count], refs[2 * count :]
    start_pushes(kinds, sources, targets, send, receive)
    wait_pushes(kinds, sources, targets, send, receive)


def swap_call(*pushes):
    next_key[0] += 1
    kinds = tuple(kind for kind, _ in pushes)
    values = [value for _, value in pushes]
    return exchange_call(
        functools.partial(swap_kernel, kinds), next_key[0], values,
        [jax.ShapeDtypeStruct(value.shape, value.dtype) for value in values],
        [pltpu.SemaphoreType.DMA((len(pushes),))] * 2, flops=110 * 10**9,
    )


next_key = [11]


def sibling_id():
    index = lax.axis_index("fsdp")
    return (index + 1 - 2 * (index % 2), lax.axis_index("tp"))


def meet(partner):
    barrier = pltpu.get_barrier_semaphore()
    pl.semaphore_signal(barrier, inc=1, device_id=partner, device_id_type=pl.DeviceIdType.MESH)
    pl.semaphore_wait(barrier, 1)


def push(source, target, send, receive, partner):
    return pltpu.make_async_remote_copy(
        src_ref=source,
        dst_ref=target,
        send_sem=send,
        recv_sem=receive,
        device_id=partner,
        device_id_type=pl.DeviceIdType.MESH,
    )


def exchange_call(kernel, key, operands, outs, scratch, vmem=60, flops=4 * 10**9):
    anywhere = pl.BlockSpec(memory_space=pl.ANY)
    results = pl.pallas_call(
        kernel,
        out_shape=outs,
        in_specs=[anywhere] * len(operands),
        out_specs=[anywhere] * len(outs),
        scratch_shapes=scratch,
        compiler_params=pltpu.CompilerParams(
            collective_id=key, has_side_effects=True, vmem_limit_bytes=vmem * 1024 * 1024
        ),
        cost_estimate=cost_of(flops),
    )(*operands)
    return tuple(results) if len(outs) > 1 else results[0]


def relay(sources, targets, buffer, load, store):
    loads, stores = [], []
    for place, source in enumerate(sources):
        copy = pltpu.make_async_copy(source, buffer.at[place], load.at[place])
        copy.start()
        loads.append(copy)
    for place, target in enumerate(targets):
        loads[place].wait()
        copy = pltpu.make_async_copy(buffer.at[place], target, store.at[place])
        copy.start()
        stores.append(copy)
    for copy in stores:
        copy.wait()


def gather_kernel(own_ref, near_ref, full_ref, buffer, load, store, send, receive):
    partner = sibling_id()
    meet(partner)
    count = own_ref.shape[0]
    remotes = []
    for place, ref in enumerate((own_ref, near_ref)):
        remote = push(
            ref, full_ref.at[pl.ds((2 + place) * count, count)],
            send.at[place], receive.at[place], partner,
        )
        remote.start()
        remotes.append(remote)
    targets = [full_ref.at[pl.ds(place * count, count)] for place in range(2)]
    relay((own_ref, near_ref), targets, buffer, load, store)
    for remote in remotes:
        remote.wait()


def core_gather(own, near):
    shape = (4 * own.shape[0], own.shape[1])
    return exchange_call(
        gather_kernel, 1, [own, near], [jax.ShapeDtypeStruct(shape, own.dtype)],
        [pltpu.VMEM((2, *own.shape), own.dtype)] + [pltpu.SemaphoreType.DMA((2,))] * 4,
    )


def gather_two_kernel(
    own_ref, own_near_ref, got_ref, got_near_ref, first_ref, second_ref,
    buffer, load, store, send, receive,
):
    partner = sibling_id()
    far = lax.axis_index("tp") // 2
    meet(partner)
    count = own_ref.shape[0]

    def run(targets):
        sources = (own_ref, own_near_ref, got_ref, got_near_ref)
        remotes, places = [], []
        for place, ref in enumerate(sources):
            target, row = targets[place // 2], place % 2
            remote = push(
                ref, target.at[pl.ds((2 + row) * count, count)],
                send.at[place], receive.at[place], partner,
            )
            remote.start()
            remotes.append(remote)
            places.append(target.at[pl.ds(row * count, count)])
        relay(sources, places, buffer, load, store)
        for remote in remotes:
            remote.wait()

    @pl.when(far == 0)
    def _():
        run((first_ref, second_ref))

    @pl.when(far != 0)
    def _():
        run((second_ref, first_ref))


def core_gather_two(own, own_near, got, got_near):
    shape = (4 * own.shape[0], own.shape[1])
    return exchange_call(
        gather_two_kernel, 11, [own, own_near, got, got_near],
        [jax.ShapeDtypeStruct(shape, own.dtype)] * 2,
        [pltpu.VMEM((4, *own.shape), own.dtype)] + [pltpu.SemaphoreType.DMA((4,))] * 4,
    )


def reduce_kernel(term_ref, keep_ref, away_ref, mine, got, keep, away, local, send, receive, store):
    partner = sibling_id()
    meet(partner)
    pieces, count = mine.shape[0], mine.shape[1]
    half = pieces * count
    remotes, loads = [], []
    for piece in range(pieces):
        order = (piece + pieces // 2) % pieces
        remote = push(
            term_ref.at[pl.ds(half + order * count, count)], got.at[order],
            send.at[order], receive.at[order], partner,
        )
        remote.start()
        remotes.append(remote)
        load = pltpu.make_async_copy(
            term_ref.at[pl.ds(order * count, count)], mine.at[order], local.at[order]
        )
        load.start()
        loads.append(load)
    stores = []
    for piece in range(pieces):
        order = (piece + pieces // 2) % pieces
        loads[piece].wait()
        remotes[piece].wait()
        total = mine[order].astype(jnp.float32) + got[order].astype(jnp.float32)
        if order < pieces // 2:
            keep[order] = total
            copy = pltpu.make_async_copy(
                keep.at[order], keep_ref.at[pl.ds(order * count, count)], store.at[order]
            )
        else:
            slot = order - pieces // 2
            away[slot] = total.astype(away.dtype)
            copy = pltpu.make_async_copy(
                away.at[slot], away_ref.at[pl.ds(slot * count, count)], store.at[order]
            )
        copy.start()
        stores.append(copy)
    for copy in stores:
        copy.wait()


def core_reduce(term):
    rows, width = term.shape
    quarter = rows // 4
    pieces = 4
    count = 2 * quarter // pieces
    return exchange_call(
        reduce_kernel, 2, [term],
        [
            jax.ShapeDtypeStruct((quarter, width), jnp.float32),
            jax.ShapeDtypeStruct((quarter, width), term.dtype),
        ],
        [
            pltpu.VMEM((pieces, count, width), term.dtype),
            pltpu.VMEM((pieces, count, width), term.dtype),
            pltpu.VMEM((pieces // 2, count, width), jnp.float32),
            pltpu.VMEM((pieces // 2, count, width), term.dtype),
        ]
        + [pltpu.SemaphoreType.DMA((pieces,))] * 4,
    )


def pair_kernel(own_ref, *refs):
    others, (pair_ref, buffer, load, store, send, receive) = refs[:-6], refs[-6:]
    partner = sibling_id()
    core = lax.axis_index("fsdp") % 2
    far = lax.axis_index("tp") // 2
    meet(partner)
    base = pl.multiple_of(core * own_ref.shape[0], own_ref.shape[0])
    count = others[0].shape[0]
    owns = [own_ref.at[pl.ds(place * count, count)] for place in range(len(others))]

    def run(mine, theirs):
        remotes, targets = [], []
        for place in range(len(others)):
            target = pair_ref.at[pl.ds(base + place * count, count)]
            remote = push(theirs[place], target, send.at[place], receive.at[place], partner)
            remote.start()
            remotes.append(remote)
            targets.append(target)
        relay(mine, targets, buffer, load, store)
        for remote in remotes:
            remote.wait()

    @pl.when(core == far)
    def _():
        run(owns, others)

    @pl.when(core != far)
    def _():
        run(others, owns)


def core_pair(key, own, *others):
    shape = (2 * own.shape[0], own.shape[1])
    return exchange_call(
        pair_kernel, key, [own, *others], [jax.ShapeDtypeStruct(shape, own.dtype)],
        [pltpu.VMEM((len(others), *others[0].shape), own.dtype)]
        + [pltpu.SemaphoreType.DMA((len(others),))] * 4,
    )


def split_kernel(pair_ref, keep_ref, away_ref, buffer, load, store, send, receive):
    partner = sibling_id()
    core = lax.axis_index("fsdp") % 2
    far = lax.axis_index("tp") // 2
    meet(partner)
    count = keep_ref.shape[0]
    mine = pair_ref.at[pl.ds(pl.multiple_of(core * count, count), count)]
    theirs = pair_ref.at[pl.ds(pl.multiple_of((1 - core) * count, count), count)]

    def run(own_target, other_target):
        remote = push(theirs, other_target, send.at[0], receive.at[0], partner)
        remote.start()
        relay((mine,), (own_target,), buffer, load, store)
        remote.wait()

    @pl.when(core == far)
    def _():
        run(keep_ref, keep_ref)

    @pl.when(core != far)
    def _():
        run(away_ref, away_ref)


def core_split(key, pair):
    shape = (pair.shape[0] // 2, pair.shape[1])
    return exchange_call(
        split_kernel, key, [pair], [jax.ShapeDtypeStruct(shape, pair.dtype)] * 2,
        [pltpu.VMEM((1, *shape), pair.dtype)] + [pltpu.SemaphoreType.DMA((1,))] * 4,
    )


def attention_call(kernel, arrays, kinds, outs, scratch, pushes=()):
    rows, heads_local = arrays[-1].shape[0], outs[1]
    half = rows // 2
    groups = heads_local // HEAD_GROUP
    width = HEAD_GROUP * HD

    def spec(kind):
        if kind == "table":
            return pl.BlockSpec((half, HD), lambda s, g: (s, 0))
        if kind == "column":
            return pl.BlockSpec((half, 1), lambda s, g: (s, 0))
        if kind == "lse":
            return pl.BlockSpec((1, half, HEAD_GROUP), lambda s, g: (g, s, 0))
        shift = kind * groups
        return pl.BlockSpec((half, width), lambda s, g: (s, shift + g))

    def shape(kind):
        if kind == "lse":
            return jax.ShapeDtypeStruct((groups, rows, HEAD_GROUP), jnp.float32)
        return jax.ShapeDtypeStruct((rows, heads_local * HD), jnp.bfloat16)

    return grid_call(
        kernel,
        arrays,
        [spec(kind) for kind in kinds],
        [shape(kind) for kind in outs[0]],
        [spec(kind) for kind in outs[0]],
        (rows // half, groups),
        4 * len(outs[0]) ** 2 * rows * rows * heads_local * HD // 16,
        scratch=scratch(half, width),
        pushes=pushes,
    )


def backward_scratch(half, width):
    return [pltpu.VMEM((half, width), jnp.bfloat16)] * 2 + [
        pltpu.VMEM((half, width), jnp.float32)
    ] * 6


def no_scratch(half, width):
    return []


def head_tables(positions):
    half_width = HD // 2
    frequency = rope_theta ** (-(jnp.arange(half_width, dtype=jnp.float32) * 2.0 / HD))
    angles = positions.astype(jnp.float32)[:, None] * frequency[None, :]
    cosine, sine = jnp.cos(angles), jnp.sin(angles)
    return (
        jnp.concatenate([cosine, cosine], axis=-1),
        jnp.concatenate([-sine, sine], axis=-1),
    )


def paired_device(
    block_in,
    out_cotangent,
    segment_ids,
    doc_positions,
    norm1_gain,
    qkv_weight,
    out_weight,
    norm2_gain,
    gate_up_weight,
    down_weight,
):
    fsdp_count, tp_count = lax.axis_size("fsdp"), lax.axis_size("tp")
    core = lax.axis_index("fsdp") % 2
    lane_z = lax.axis_index("tp")
    near, far = lane_z % 2, lane_z // 2
    core_pairs = [(i, i ^ 1) for i in range(fsdp_count)]
    near_pairs = [(i, i ^ 1) for i in range(tp_count)]
    far_pairs = [(i, i ^ 2) for i in range(tp_count)]
    plane_groups = [list(range(first, fsdp_count, 2)) for first in range(2)]
    rows = block_in.shape[1]
    local_cols = qkv_weight.shape[2]
    heads_local = local_cols // HD
    gain_one = norm1_gain.astype(jnp.float32)
    gain_two = norm2_gain.astype(jnp.float32)

    def swap_core(value):
        return lax.ppermute(value, "fsdp", core_pairs)

    def swap_near(value):
        return lax.ppermute(value, "tp", near_pairs)

    def swap_far(value):
        return lax.ppermute(value, "tp", far_pairs)

    def pick_tile(size):
        return 512 if size % 512 == 0 else 768

    tokens = []

    def act(work, *inputs, sends=()):
        values = [*inputs, *[value for _, value in sends]]
        held = lax.optimization_barrier((*values, *tokens))[: len(values)]
        if sends:
            kinds = [kind for kind, _ in sends]
            result = work(*held[: len(inputs)], pushes=list(zip(kinds, held[len(inputs) :])))
        else:
            result = work(*held)
        tokens[:] = result if isinstance(result, tuple) else (result,)
        return result[0] if isinstance(result, tuple) and len(result) == 1 else result

    def swap(*sends):
        return act(lambda pushes: swap_call(*pushes), sends=sends)

    def pick(value, index):
        return lax.dynamic_index_in_dim(value, index, 0, keepdims=False)

    def place_tokens(value, got):
        keep = pick(value, far)
        return jnp.where(far == 0, keep, got), jnp.where(far == 0, got, keep)

    def join(left, right):
        return jnp.concatenate([left, right], axis=0)

    def plane_gather(pair):
        return lax.all_gather(pair, "fsdp", axis=0, tiled=True, axis_index_groups=plane_groups)

    def plane_scatter(grad):
        return lax.psum_scatter(
            grad, "fsdp", scatter_dimension=0, tiled=True, axis_index_groups=plane_groups
        )

    def gather_weight(key, local, *others):
        return plane_gather(act(lambda own, *got: core_pair(key, own, *got), local, *others))

    def halve(value):
        count = value.shape[0] // 2
        return value[:count], value[count:]

    def add_wide(left, right):
        return left.astype(jnp.float32) + right.astype(jnp.float32)

    def chained(value, *others):
        return lax.optimization_barrier((value, *others))[0]

    def scatter_gains(gains):
        for axis, size in (("fsdp", fsdp_count), ("tp", tp_count)):
            index = lax.axis_index(axis)
            step = size // 2
            while step >= 1:
                bit = (index // step) % 2
                parts = gains.reshape(gains.shape[0], 2, gains.shape[1] // 2)
                sent = lax.dynamic_index_in_dim(parts, 1 - bit, 1, keepdims=False)
                kept = lax.dynamic_index_in_dim(parts, bit, 1, keepdims=False)
                gains = kept + lax.ppermute(sent, axis, [(i, i ^ step) for i in range(size)])
                step //= 2
        return gains

    def wide_dot(left, right, pushes=()):
        return rows_matmul(
            [left], [right], dot_nn, [jnp.float32], pick_tile(right.shape[1]), pushes=pushes
        )

    def dot_bf16(left, right, pushes=()):
        return rows_matmul(
            [left], [right], dot_nn, [jnp.bfloat16], pick_tile(right.shape[1]), pushes=pushes
        )

    def grad_sum(left, right, left_next, right_next, pushes=()):
        chunk = pick_tile(right.shape[1])
        return sum_matmul(
            [left, left_next], [right, right_next], pick_tile(left.shape[1]),
            2 * chunk if right.shape[1] % (2 * chunk) == 0 else chunk, pushes=pushes,
        )

    def heads_back(grad, weight, pushes=()):
        return rows_matmul(
            [grad], [weight], dot_nt, [jnp.bfloat16], pick_tile(weight.shape[0]), pushes=pushes
        )

    def rms_pack(stream, gain):
        scale = rms_scale(stream)
        return scale, (stream * scale * gain).astype(jnp.bfloat16)

    qkv_local = qkv_weight.reshape(qkv_weight.shape[0], 3 * local_cols)
    gate_local, up_local = gate_up_weight[:, 0], gate_up_weight[:, 1]

    next_key[0] = 11
    places = jnp.broadcast_to(doc_positions[:, None, :], (2, 8, rows))

    def first_norm(part):
        stream = part.astype(jnp.float32)
        return (stream, *rms_pack(stream, gain_one))

    s_own, r_own, n_own = act(lambda value: first_norm(pick(value, far)), block_in)
    near_own, qkv_other, place_got = swap(
        ("near", n_own), ("far", qkv_local), ("far", pick(places, 1 - far))
    )
    qkv_full = gather_weight(4, qkv_local, qkv_other)
    places = join(*place_tokens(places, place_got))

    def make_tables(own, other):
        order = join(own, other)[::8].reshape(2, 2, 2, rows)
        early, late = order[:, :, 0].reshape(-1), order[:, :, 1].reshape(-1)
        return (*head_tables(early), *head_tables(late), late[:, None])

    c_own = pick(out_cotangent, far)
    stream_got, c_near_own, out_other, near_places = swap(
        ("far", pick(block_in, 1 - far)), ("near", c_own), ("far", out_weight), ("near", places)
    )
    places = join(places, near_places)
    out_full = gather_weight(3, out_weight, out_other)
    s_got, r_got, n_got = act(first_norm, stream_got)
    near_got, gate_other, core_places = swap(
        ("near", n_got), ("far", gate_local), ("core", places)
    )
    gate_full = gather_weight(5, gate_local, gate_other)
    h1_first, h1_second = act(core_gather_two, n_own, near_own, n_got, near_got)
    streams = [jnp.where(far == 0, s_own, s_got), jnp.where(far == 0, s_got, s_own)]
    scales_one = [jnp.where(far == 0, r_own, r_got), jnp.where(far == 0, r_got, r_own)]

    def attend_first(projected, pushes=()):
        arrays = [projected, projected, projected, *tables[0]]
        return attention_call(
            forward_first, arrays, [0, 1, 2, "table", "table"],
            ([0, 0, 0, 0, "lse"], heads_local), no_scratch, pushes,
        )

    def attend_second(projected, pushes=()):
        arrays = [projected, projected, projected, *tables[1], saved[0][1], saved[0][2], reach]
        return attention_call(
            forward_second, arrays, [0, 1, 2, "table", "table", 0, 0, "column"],
            ([0, 0, 0, 0, "lse"], heads_local), no_scratch, pushes,
        )

    up_other = swap_far(chained(up_local, gate_other))
    cos_first, sin_first, cos_second, sin_second, reach = act(
        make_tables, places, core_places
    )
    tables = [(cos_first, sin_first), (cos_second, sin_second)]
    projected = act(wide_dot, h1_first, qkv_full)
    results = act(attend_first, projected)
    up_full = gather_weight(5, up_local, up_other)
    down_other = swap_far(chained(down_weight, up_other))
    saved, lses, mixed_first = [results[:3]], [results[4]], results[3]
    term_first = act(dot_bf16, mixed_first, out_full)
    keep_first, send_first = act(core_reduce, term_first)
    projected, branch_first = act(
        wide_dot, h1_second, qkv_full, sends=[("near", send_first)]
    )

    def second_norm(stream, keep, got):
        middle = stream + keep + got.astype(jnp.float32)
        return (middle, *rms_pack(middle, gain_two))

    m_first, q_first, n_first = act(second_norm, streams[0], keep_first, branch_first)
    *results, near_first = act(attend_second, projected, sends=[("near", n_first)])
    saved.append(results[:3])
    lses.append(results[4])
    mixed_second = results[3]
    term_second = act(dot_bf16, mixed_second, out_full)
    keep_second, send_second = act(core_reduce, term_second)
    h2_first = act(core_gather, n_first, near_first)
    down_full_pair = act(lambda own, got: core_pair(6, own, got), down_weight, down_other)
    down_full = plane_gather(down_full_pair)
    c_got = swap_far(chained(pick(out_cotangent, 1 - far), down_full_pair))

    gate_first, branch_second = act(
        wide_dot, h2_first, gate_full, sends=[("near", send_second)]
    )
    m_second, q_second, n_second = act(second_norm, streams[1], keep_second, branch_second)

    def rise(hidden, weight, gate, pushes=()):
        return rows_matmul(
            [hidden], [weight], dot_nn, [jnp.float32, jnp.bfloat16], pick_tile(weight.shape[1]),
            finish=lambda up, gate: (up, gate * jax.nn.sigmoid(gate) * up), extras=[gate],
            pushes=pushes,
        )

    up_first, a_first, near_second = act(
        rise, h2_first, up_full, gate_first, sends=[("near", n_second)]
    )
    h2_second = act(core_gather, n_second, near_second)
    gate_second, c_near_got = act(
        wide_dot, h2_second, gate_full, sends=[("near", c_got)]
    )
    y_first, y_second = act(core_gather_two, c_own, c_near_own, c_got, c_near_got)
    c_first, c_second = jnp.where(far == 0, c_own, c_got), jnp.where(far == 0, c_got, c_own)
    up_second, a_second = act(rise, h2_second, up_full, gate_second)
    down_sum = plane_scatter(act(grad_sum, a_first, y_first, a_second, y_second))

    def fall_finish(act_grad, gate, up):
        sigmoid_gate = jax.nn.sigmoid(gate)
        return (
            act_grad * up * sigmoid_gate * (1.0 + gate * (1.0 - sigmoid_gate)),
            act_grad * (gate * sigmoid_gate),
        )

    def fall(cotangent, weight, gate, up, pushes=()):
        return rows_matmul(
            [cotangent], [weight], dot_nt, [jnp.bfloat16] * 2, pick_tile(weight.shape[0]),
            chunk=512, finish=fall_finish, extras=[gate, up], pushes=pushes,
        )

    def hidden_grad(gate_grad, up_grad, gate_weight, up_weight, pushes=()):
        return rows_matmul(
            [gate_grad, up_grad], [gate_weight, up_weight], dot_nt, [jnp.bfloat16],
            pick_tile(gate_weight.shape[0]), pushes=pushes,
        )

    def second_back(middle, scale, keep, got, cotangent):
        grad, gain_term = norm_back(middle, scale, gain_two, keep + got.astype(jnp.float32))
        grad = cotangent.astype(jnp.float32) + grad
        return grad, grad.astype(jnp.bfloat16), gain_term

    dg_first, du_first = act(fall, y_first, down_full, gate_first, up_first)
    term_first = act(hidden_grad, dg_first, du_first, gate_full, up_full)
    keep_first, send_first = act(core_reduce, term_first)
    dg_second, du_second, back_first = act(
        fall, y_second, down_full, gate_second, up_second, sends=[("near", send_first)]
    )
    g_first, n_first, gain_two_first = act(
        second_back, m_first, q_first, keep_first, back_first, c_first
    )
    term_second, near_first = act(
        hidden_grad, dg_second, du_second, gate_full, up_full, sends=[("near", n_first)]
    )
    keep_second, send_second = act(core_reduce, term_second)
    d_first = act(core_gather, n_first, near_first)
    grad_gate, back_second = act(
        grad_sum, h2_first, dg_first, h2_second, dg_second, sends=[("near", send_second)]
    )
    gate_sum = plane_scatter(grad_gate)
    g_second, n_second, gain_two_second = act(
        second_back, m_second, q_second, keep_second, back_second, c_second
    )
    heads_first = act(heads_back, d_first, out_full)
    down_mine, down_away = act(lambda pair: core_split(10, pair), down_sum)
    down_got = swap_far(down_away)
    grad_up, near_second = act(
        grad_sum, h2_first, du_first, h2_second, du_second, sends=[("near", n_second)]
    )
    up_sum = plane_scatter(grad_up)

    d_second = act(core_gather, n_second, near_second)
    heads_second = act(heads_back, d_second, out_full)
    grad_out = act(grad_sum, mixed_first, d_first, mixed_second, d_second)
    out_sum = plane_scatter(grad_out)
    mlp_first = act(dot_bf16, a_first, down_full)
    mlp_keep_first, mlp_send_first = act(core_reduce, mlp_first)
    mlp_second = act(dot_bf16, a_second, down_full)
    mlp_keep_second, mlp_send_second = act(core_reduce, mlp_second)
    def attend_back(heads_first, heads_second, pushes=()):
        return attention_call(
            backward_both,
            [
                *saved[0], *saved[1], heads_first, heads_second, *lses,
                *tables[0], *tables[1], reach,
            ],
            [0] * 8 + ["lse"] * 2 + ["table"] * 4 + ["column"],
            ([0] * 6, heads_local),
            backward_scratch,
            pushes,
        )

    *grads, mlp_branch_first, mlp_branch_second = act(
        attend_back, heads_first, heads_second,
        sends=[("near", mlp_send_first), ("near", mlp_send_second)],
    )
    gate_mine, gate_away = act(lambda pair: core_split(9, pair), gate_sum)
    gate_got = swap_far(gate_away)
    p_first, p_second = act(
        lambda *parts: (
            jnp.concatenate(parts[:3], axis=1),
            jnp.concatenate(parts[3:], axis=1),
        ),
        *grads,
    )

    def finish_output(first, first_keep, first_got, second, second_keep, second_got):
        first = (first + first_keep + first_got.astype(jnp.float32)).astype(jnp.bfloat16)
        second = (second + second_keep + second_got.astype(jnp.float32)).astype(jnp.bfloat16)
        return jnp.where(far == 0, first, second), jnp.where(far == 0, second, first)

    grad_qkv = act(grad_sum, h1_first, p_first, h1_second, p_second)
    qkv_sum = plane_scatter(grad_qkv)
    out_keep, out_send = act(
        finish_output,
        m_first, mlp_keep_first, mlp_branch_first, m_second, mlp_keep_second, mlp_branch_second,
    )
    out_got = swap_far(out_send)
    up_mine, up_away = act(lambda pair: core_split(9, pair), up_sum)
    up_got = swap_far(up_away)
    term_first = act(heads_back, p_first, qkv_full)
    keep_first, send_first = act(core_reduce, term_first)
    term_second, back_first = act(
        heads_back, p_second, qkv_full, sends=[("near", send_first)]
    )
    keep_second, send_second = act(core_reduce, term_second)
    out_mine, out_away = act(lambda pair: core_split(8, pair), out_sum)
    def settle(keep, got):
        return jnp.stack([jnp.where(far == 0, keep, got), jnp.where(far == 0, got, keep)])

    def first_back(stream, scale, keep, got, grad):
        back, gain_term = norm_back(stream, scale, gain_one, keep + got.astype(jnp.float32))
        return grad + back, gain_term

    def last_back(stream, scale, keep, got, grad, first):
        second, gain_term = first_back(stream, scale, keep, got, grad)
        return (
            jnp.where(far == 0, first, second),
            jnp.where(far == 0, second, first).astype(jnp.bfloat16),
            gain_term,
        )

    back_second, out_back = swap(("near", send_second), ("far", out_away))
    qkv_mine, qkv_away = act(lambda pair: core_split(0, pair), qkv_sum)
    qkv_back = swap_far(qkv_away)
    i_first, gain_one_first = act(
        first_back, streams[0], scales_one[0], keep_first, back_first, g_first
    )
    in_keep, in_send, gain_one_second = act(
        last_back, streams[1], scales_one[1], keep_second, back_second, g_second, i_first
    )
    in_got = swap_far(in_send)
    down_owned = act(add_wide, down_mine, down_got)
    gate_owned = act(add_wide, gate_mine, gate_got)
    block_out = act(settle, out_keep, out_got)
    up_owned = act(add_wide, up_mine, up_got)
    gate_up_owned = act(lambda a, b: jnp.stack([a, b], axis=1), gate_owned, up_owned)
    out_owned = act(add_wide, out_mine, out_back)
    gains = scatter_gains(
        jnp.stack([gain_one_first + gain_one_second, gain_two_first + gain_two_second])
    )
    in_grad = act(lambda keep, got: settle(keep, got.astype(jnp.float32)), in_keep, in_got)
    qkv_owned = act(add_wide, qkv_mine, qkv_back)
    return (
        block_out,
        in_grad,
        gains[0],
        qkv_owned.reshape(qkv_weight.shape),
        out_owned,
        gains[1],
        gate_up_owned,
        down_owned,
    )


def solution(mesh):
    sizes = (mesh.shape["fsdp"], mesh.shape["tp"])
    body = paired_device if sizes == (8, 4) else per_device
    in_specs = (
        P("fsdp", "tp", None),
        P("fsdp", "tp", None),
        P("fsdp", "tp"),
        P("fsdp", "tp"),
        P(),
        P("fsdp", None, "tp"),
        P(("tp", "fsdp"), None),
        P(),
        P("fsdp", None, "tp"),
        P(("tp", "fsdp"), None),
    )
    out_specs = (
        P("fsdp", "tp", None),
        P("fsdp", "tp", None),
        P(("fsdp", "tp")),
        P("fsdp", None, "tp"),
        P(("tp", "fsdp"), None),
        P(("fsdp", "tp")),
        P("fsdp", None, "tp"),
        P(("tp", "fsdp"), None),
    )
    return jax.shard_map(
        body, mesh=mesh, in_specs=in_specs, out_specs=out_specs, check_vma=False
    )
```

```python
import functools

import jax
import jax.numpy as jnp
from jax import lax
from jax.experimental import pallas as pl
from jax.experimental.pallas import tpu as pltpu
from jax.sharding import PartitionSpec as P

D = 3072
HD = 96


rms_epsilon = 1e-05
rope_theta = 10000.0
masked_score = -1e30
LOG2E = 1.4426950408889634


def rope_tables(positions, head_size):
    half_width = head_size // 2
    frequency = rope_theta ** (-(jnp.arange(half_width, dtype=jnp.float32) * 2.0 / head_size))
    angles = positions.astype(jnp.float32)[:, None] * frequency[None, :]
    return (jnp.cos(angles)[:, None, :], jnp.sin(angles)[:, None, :])


def rotate(values, cosine_part, sine_part):
    half_width = values.shape[-1] // 2
    lead_half = values[..., :half_width]
    tail_half = values[..., half_width:]
    return jnp.concatenate(
        [
            lead_half * cosine_part - tail_half * sine_part,
            tail_half * cosine_part + lead_half * sine_part,
        ],
        axis=-1,
    )


def unrotate(values, cosine_part, sine_part):
    half_width = values.shape[-1] // 2
    lead_half = values[..., :half_width]
    tail_half = values[..., half_width:]
    return jnp.concatenate(
        [
            lead_half * cosine_part + tail_half * sine_part,
            tail_half * cosine_part - lead_half * sine_part,
        ],
        axis=-1,
    )


def rms_scale(stream):
    return lax.rsqrt(jnp.mean(stream * stream, axis=-1, keepdims=True) + rms_epsilon)


def norm_back(stream, scale_rows, gain_vec, grad_rows):
    gained_grad = gain_vec * grad_rows
    input_grad = scale_rows * gained_grad - stream * scale_rows**3 * jnp.mean(
        gained_grad * stream, axis=-1, keepdims=True
    )
    return (input_grad, jnp.sum(grad_rows * stream * scale_rows, axis=0))


def allowed_mask(segment_tile, index_tile, segments):
    columns = jnp.arange(segments.shape[0], dtype=jnp.int32)
    return (segment_tile[:, None] == segments[None, :]) & (index_tile[:, None] >= columns[None, :])


def masked_scores(query_tile, key_rows, segment_tile, index_tile, segments, scale_value):
    scores = (
        jnp.einsum("qhd,khd->hqk", query_tile, key_rows, preferred_element_type=jnp.float32)
        * scale_value
    )
    return jnp.where(allowed_mask(segment_tile, index_tile, segments)[None], scores, masked_score)


def attention_forward(queries, key_rows, value_rows, segments, block_rows):
    seq_len, head_count, head_size = queries.shape
    tiles = seq_len // block_rows
    scale_value = head_size ** (-0.5)
    positions = jnp.arange(seq_len, dtype=jnp.int32)

    def query_block(packed):
        query_tile, segment_tile, index_tile = packed
        scores = masked_scores(
            query_tile, key_rows, segment_tile, index_tile, segments, scale_value
        )
        row_max = jnp.max(scores, axis=-1, keepdims=True)
        exponent = jnp.exp(scores - row_max)
        row_total = jnp.sum(exponent, axis=-1, keepdims=True)
        probs_low = (exponent / row_total).astype(jnp.bfloat16)
        mixed = jnp.einsum(
            "hqk,khd->qhd", probs_low, value_rows, preferred_element_type=jnp.float32
        )
        return (mixed, (row_max + jnp.log(row_total))[..., 0])

    mixed, log_total = lax.map(
        query_block,
        (
            queries.reshape(tiles, block_rows, head_count, head_size),
            segments.reshape(tiles, block_rows),
            positions.reshape(tiles, block_rows),
        ),
    )
    return (mixed.reshape(seq_len, head_count * head_size), log_total)


def attention_backward(queries, key_rows, value_rows, segments, log_total, out_grad, block_rows):
    seq_len, head_count, head_size = queries.shape
    tiles = seq_len // block_rows
    scale_value = head_size ** (-0.5)
    positions = jnp.arange(seq_len, dtype=jnp.int32)

    def query_block(carry, packed):
        key_acc, value_acc = carry
        query_tile, segment_tile, index_tile, total_tile, grad_tile = packed
        scores = masked_scores(
            query_tile, key_rows, segment_tile, index_tile, segments, scale_value
        )
        probs = jnp.exp(scores - total_tile[..., None])
        probs_low = probs.astype(jnp.bfloat16)
        prob_grad = jnp.einsum(
            "qhd,khd->hqk", grad_tile, value_rows, preferred_element_type=jnp.float32
        )
        score_grad = (
            probs * (prob_grad - jnp.sum(probs * prob_grad, axis=-1, keepdims=True))
        ).astype(jnp.bfloat16)
        query_grad = (
            jnp.einsum("hqk,khd->qhd", score_grad, key_rows, preferred_element_type=jnp.float32)
            * scale_value
        )
        key_acc = (
            key_acc
            + jnp.einsum("hqk,qhd->khd", score_grad, query_tile, preferred_element_type=jnp.float32)
            * scale_value
        )
        value_acc = value_acc + jnp.einsum(
            "hqk,qhd->khd", probs_low, grad_tile, preferred_element_type=jnp.float32
        )
        return ((key_acc, value_acc), query_grad)

    start_acc = (jnp.zeros(queries.shape, jnp.float32), jnp.zeros(queries.shape, jnp.float32))
    (key_grad, value_grad), query_grad = lax.scan(
        query_block,
        start_acc,
        (
            queries.reshape(tiles, block_rows, head_count, head_size),
            segments.reshape(tiles, block_rows),
            positions.reshape(tiles, block_rows),
            log_total,
            out_grad.reshape(tiles, block_rows, head_count, head_size),
        ),
    )
    return (query_grad.reshape(seq_len, head_count, head_size), key_grad, value_grad)


def gather_attention(qkv_weight, out_weight):
    return (
        lax.all_gather(qkv_weight, "fsdp", axis=0, tiled=True),
        lax.all_gather(out_weight, "fsdp", axis=0, tiled=True),
    )


def gather_feedforward(gate_up_weight, down_weight):
    return (
        lax.all_gather(gate_up_weight, "fsdp", axis=0, tiled=True),
        lax.all_gather(down_weight, "fsdp", axis=0, tiled=True),
    )


def per_device(
    block_in,
    out_cotangent,
    segment_ids,
    doc_positions,
    norm1_gain,
    qkv_weight,
    out_weight,
    norm2_gain,
    gate_up_weight,
    down_weight,
):
    micro_count = block_in.shape[0]
    fsdp_count = lax.axis_size("fsdp")
    segment_full, position_full = (
        lax.all_gather(segment_ids, "tp", axis=1, tiled=True),
        lax.all_gather(doc_positions, "tp", axis=1, tiled=True),
    )
    seq_len = segment_full.shape[1]
    block_rows = min(seq_len, 512)
    gain_one = norm1_gain.astype(jnp.float32)
    gain_two = norm2_gain.astype(jnp.float32)
    local_cols = qkv_weight.shape[2]
    local_units = gate_up_weight.shape[2]
    heads_local = local_cols // HD
    grad_qkv = jnp.zeros((D, 3, local_cols), jnp.float32)
    grad_out = jnp.zeros((out_weight.shape[0] * fsdp_count, D), jnp.float32)
    grad_gate_up = jnp.zeros((D, 2, local_units), jnp.float32)
    grad_down = jnp.zeros((down_weight.shape[0] * fsdp_count, D), jnp.float32)
    gain_one_acc = jnp.zeros((D,), jnp.float32)
    gain_two_acc = jnp.zeros((D,), jnp.float32)
    outputs = []
    input_grads = []
    for micro_index in range(micro_count):
        weights_fwd = (
            gather_attention(qkv_weight, out_weight),
            gather_feedforward(gate_up_weight, down_weight),
        )
        (qkv_full, out_full), (gate_up_full, down_full) = weights_fwd
        stream = block_in[micro_index].astype(jnp.float32)
        segment_row = segment_full[micro_index]
        cosine_part, sine_part = rope_tables(position_full[micro_index], HD)
        scale_one = rms_scale(stream)
        normed_one = (stream * scale_one * gain_one).astype(jnp.bfloat16)
        normed_one_full = lax.all_gather(normed_one, "tp", axis=0, tiled=True)
        projected = jnp.einsum(
            "sd,dtc->stc", normed_one_full, qkv_full, preferred_element_type=jnp.float32
        )
        queries = rotate(
            projected[:, 0].reshape(seq_len, heads_local, HD), cosine_part, sine_part
        ).astype(jnp.bfloat16)
        key_rows = rotate(
            projected[:, 1].reshape(seq_len, heads_local, HD), cosine_part, sine_part
        ).astype(jnp.bfloat16)
        value_rows = projected[:, 2].reshape(seq_len, heads_local, HD).astype(jnp.bfloat16)
        mixed, log_total = attention_forward(queries, key_rows, value_rows, segment_row, block_rows)
        attn_heads = mixed.astype(jnp.bfloat16)
        attn_term = jnp.dot(attn_heads, out_full, preferred_element_type=jnp.float32)
        attn_branch = lax.psum_scatter(attn_term, "tp", scatter_dimension=0, tiled=True)
        middle = stream + attn_branch
        scale_two = rms_scale(middle)
        normed_two = (middle * scale_two * gain_two).astype(jnp.bfloat16)
        normed_two_full = lax.all_gather(normed_two, "tp", axis=0, tiled=True)
        gate_up = jnp.einsum(
            "sd,dtf->stf", normed_two_full, gate_up_full, preferred_element_type=jnp.float32
        )
        gate_rows = gate_up[:, 0]
        up_rows = gate_up[:, 1]
        sigmoid_gate = jax.nn.sigmoid(gate_rows)
        silu_gate = gate_rows * sigmoid_gate
        activated = (silu_gate * up_rows).astype(jnp.bfloat16)
        mlp_term = jnp.dot(activated, down_full, preferred_element_type=jnp.float32)
        mlp_branch = lax.psum_scatter(
            mlp_term.astype(jnp.bfloat16), "tp", scatter_dimension=0, tiled=True
        ).astype(jnp.float32)
        outputs.append((middle + mlp_branch).astype(jnp.bfloat16))
        (qkv_back, out_back), (gate_up_back, down_back) = weights_fwd
        cotangent = out_cotangent[micro_index].astype(jnp.float32)
        cotangent_full = lax.all_gather(out_cotangent[micro_index], "tp", axis=0, tiled=True)
        grad_down = grad_down + jnp.einsum(
            "sf,sd->fd", activated, cotangent_full, preferred_element_type=jnp.float32
        )
        act_grad = jnp.einsum(
            "sd,fd->sf", cotangent_full, down_back, preferred_element_type=jnp.float32
        )
        gate_grad = act_grad * up_rows * sigmoid_gate * (1.0 + gate_rows * (1.0 - sigmoid_gate))
        up_grad = act_grad * silu_gate
        gate_up_grad = jnp.stack([gate_grad, up_grad], axis=1).astype(jnp.bfloat16)
        grad_gate_up = grad_gate_up + jnp.einsum(
            "sd,stf->dtf", normed_two_full, gate_up_grad, preferred_element_type=jnp.float32
        )
        normed_two_term = jnp.einsum(
            "stf,dtf->sd", gate_up_grad, gate_up_back, preferred_element_type=jnp.float32
        )
        normed_two_grad = lax.psum_scatter(normed_two_term, "tp", scatter_dimension=0, tiled=True)
        middle_back, gain_two_term = norm_back(middle, scale_two, gain_two, normed_two_grad)
        gain_two_acc = gain_two_acc + gain_two_term
        middle_grad = cotangent + middle_back
        attn_grad_full = lax.all_gather(middle_grad.astype(jnp.bfloat16), "tp", axis=0, tiled=True)
        grad_out = grad_out + jnp.einsum(
            "sc,sd->cd", attn_heads, attn_grad_full, preferred_element_type=jnp.float32
        )
        heads_grad = jnp.einsum(
            "sd,cd->sc", attn_grad_full, out_back, preferred_element_type=jnp.float32
        ).astype(jnp.bfloat16)
        query_grad, key_grad, value_grad = attention_backward(
            queries,
            key_rows,
            value_rows,
            segment_row,
            log_total,
            heads_grad.reshape(seq_len, heads_local, HD),
            block_rows,
        )
        projected_grad = jnp.stack(
            [
                unrotate(query_grad, cosine_part, sine_part).reshape(seq_len, local_cols),
                unrotate(key_grad, cosine_part, sine_part).reshape(seq_len, local_cols),
                value_grad.reshape(seq_len, local_cols),
            ],
            axis=1,
        ).astype(jnp.bfloat16)
        grad_qkv = grad_qkv + jnp.einsum(
            "sd,stc->dtc", normed_one_full, projected_grad, preferred_element_type=jnp.float32
        )
        normed_one_term = jnp.einsum(
            "stc,dtc->sd", projected_grad, qkv_back, preferred_element_type=jnp.float32
        )
        normed_one_grad = lax.psum_scatter(
            normed_one_term.astype(jnp.bfloat16), "tp", scatter_dimension=0, tiled=True
        ).astype(jnp.float32)
        stream_back, gain_one_term = norm_back(stream, scale_one, gain_one, normed_one_grad)
        gain_one_acc = gain_one_acc + gain_one_term
        input_grads.append(middle_grad + stream_back)
    owned_grads = (
        lax.psum_scatter(
            grad_qkv.astype(jnp.bfloat16), "fsdp", scatter_dimension=0, tiled=True
        ).astype(jnp.float32),
        lax.psum_scatter(
            grad_out.astype(jnp.bfloat16), "fsdp", scatter_dimension=0, tiled=True
        ).astype(jnp.float32),
        lax.psum_scatter(
            grad_gate_up.astype(jnp.bfloat16), "fsdp", scatter_dimension=0, tiled=True
        ).astype(jnp.float32),
        lax.psum_scatter(
            grad_down.astype(jnp.bfloat16), "fsdp", scatter_dimension=0, tiled=True
        ).astype(jnp.float32),
    )
    owned_gains = (
        lax.psum_scatter(gain_one_acc, ("fsdp", "tp"), scatter_dimension=0, tiled=True),
        lax.psum_scatter(gain_two_acc, ("fsdp", "tp"), scatter_dimension=0, tiled=True),
    )
    return (
        jnp.stack(outputs),
        jnp.stack(input_grads),
        owned_gains[0],
        owned_grads[0],
        owned_grads[1],
        owned_gains[1],
        owned_grads[2],
        owned_grads[3],
    )


HEAD_GROUP = 4
FIRST_DOC = 800


def dot_nt(left, right):
    return lax.dot_general(left, right, (((1,), (1,)), ((), ())), preferred_element_type=jnp.float32)


def dot_tn(left, right):
    return lax.dot_general(left, right, (((0,), (0,)), ((), ())), preferred_element_type=jnp.float32)


def dot_nn(left, right):
    return lax.dot_general(left, right, (((1,), (0,)), ((), ())), preferred_element_type=jnp.float32)


def swap_halves(values):
    lanes = lax.broadcasted_iota(jnp.int32, values.shape, 1)
    width = values.shape[1]
    return jnp.where(
        lanes % HD < HD // 2,
        pltpu.roll(values, width - HD // 2, 1),
        pltpu.roll(values, HD // 2, 1),
    )


def causal_mask(rows, columns):
    row_ids = lax.broadcasted_iota(jnp.int32, (rows, columns), 0)
    column_ids = lax.broadcasted_iota(jnp.int32, (rows, columns), 1)
    return row_ids >= column_ids


def tail_mask(reach):
    rows = reach.shape[0]
    row_ids = lax.broadcasted_iota(jnp.int32, (rows, rows), 0)
    column_ids = lax.broadcasted_iota(jnp.int32, (rows, rows), 1)
    return (row_ids >= column_ids) & (row_ids - column_ids <= reach)


def halves(quarter):
    first = lax.axis_index("tp") % 2
    return (
        pl.multiple_of(first * quarter, quarter),
        pl.multiple_of((1 - first) * quarter, quarter),
    )


def widen(table):
    return jnp.concatenate([table] * HEAD_GROUP, axis=1)


def load_rotated(offsets, quarter, q_ref, k_ref, v_ref, cos_ref, sin_ref, qr_ref, kr_ref, vr_ref):
    for place, offset in enumerate(offsets):
        rows = pl.ds(offset, quarter)
        target = pl.ds(place * quarter, quarter)
        cosine, sine = widen(cos_ref[rows, :]), widen(sin_ref[rows, :])
        q_raw, k_raw = q_ref[rows, :], k_ref[rows, :]
        qr_ref[target, :] = (q_raw * cosine + swap_halves(q_raw) * sine).astype(jnp.bfloat16)
        kr_ref[target, :] = (k_raw * cosine + swap_halves(k_raw) * sine).astype(jnp.bfloat16)
        vr_ref[target, :] = v_ref[rows, :].astype(jnp.bfloat16)


def softmax_mix(query, pieces, factor):
    scores = []
    for keys, _, mask in pieces:
        score = dot_nt(query, keys)
        scores.append(score if mask is None else jnp.where(mask, score, masked_score))
    top = functools.reduce(jnp.maximum, [jnp.max(s, axis=-1, keepdims=True) for s in scores])
    weights = [jnp.exp2((s - top) * factor) for s in scores]
    total = functools.reduce(jnp.add, [jnp.sum(w, axis=-1, keepdims=True) for w in weights])
    inverse = 1.0 / total
    mixed = functools.reduce(
        jnp.add,
        [dot_nn((w * inverse).astype(jnp.bfloat16), piece[1]) for w, piece in zip(weights, pieces)],
    )
    return mixed, top * factor + jnp.log2(total)


def head_slice(head):
    return slice(head * HD, (head + 1) * HD)


def forward_first(
    q_ref, k_ref, v_ref, cos_ref, sin_ref, qr_ref, kr_ref, vr_ref, o_ref, lse_ref
):
    half = q_ref.shape[0]
    quarter = half // 2
    offsets = halves(quarter)
    load_rotated(offsets, quarter, q_ref, k_ref, v_ref, cos_ref, sin_ref, qr_ref, kr_ref, vr_ref)
    factor = HD ** (-0.5) * LOG2E
    mask = causal_mask(quarter, quarter)
    for head in range(HEAD_GROUP):
        cols = head_slice(head)
        early, late = slice(0, quarter), slice(quarter, half)
        k_early, v_early = kr_ref[early, cols], vr_ref[early, cols]
        mixed, lse = softmax_mix(qr_ref[early, cols], [(k_early, v_early, mask)], factor)
        o_ref[pl.ds(offsets[0], quarter), cols] = mixed.astype(jnp.bfloat16)
        lse_ref[0, early, head : head + 1] = lse
        mixed, lse = softmax_mix(
            qr_ref[late, cols],
            [(k_early, v_early, None), (kr_ref[late, cols], vr_ref[late, cols], mask)],
            factor,
        )
        o_ref[pl.ds(offsets[1], quarter), cols] = mixed.astype(jnp.bfloat16)
        lse_ref[0, late, head : head + 1] = lse


def forward_second(
    q_ref, k_ref, v_ref, cos_ref, sin_ref, ka_ref, va_ref, pos_ref,
    qr_ref, kr_ref, vr_ref, o_ref, lse_ref,
):
    half = q_ref.shape[0]
    quarter = half // 2
    cut = FIRST_DOC - half
    spill = cut - quarter
    offsets = halves(quarter)
    load_rotated(offsets, quarter, q_ref, k_ref, v_ref, cos_ref, sin_ref, qr_ref, kr_ref, vr_ref)
    factor = HD ** (-0.5) * LOG2E
    mask = causal_mask(cut, cut)
    mask_tail = tail_mask(pos_ref[pl.ds(offsets[1] + spill, half - cut), :])
    for head in range(HEAD_GROUP):
        cols = head_slice(head)
        early, late = slice(0, cut), slice(cut, half)
        mixed, lse = softmax_mix(
            qr_ref[early, cols],
            [
                (ka_ref[:, cols], va_ref[:, cols], None),
                (kr_ref[early, cols], vr_ref[early, cols], mask),
            ],
            factor,
        )
        low = mixed.astype(jnp.bfloat16)
        o_ref[pl.ds(offsets[0], quarter), cols] = low[:quarter]
        o_ref[pl.ds(offsets[1], spill), cols] = low[quarter:]
        lse_ref[0, early, head : head + 1] = lse
        mixed, lse = softmax_mix(
            qr_ref[late, cols], [(kr_ref[late, cols], vr_ref[late, cols], mask_tail)], factor
        )
        o_ref[pl.ds(offsets[1] + spill, half - cut), cols] = mixed.astype(jnp.bfloat16)
        lse_ref[0, late, head : head + 1] = lse


def backward_both(
    qa_ref, ka_ref, va_ref, qb_ref, kb_ref, vb_ref, ga_ref, gb_ref, la_ref, lb_ref,
    cosa_ref, sina_ref, cosb_ref, sinb_ref, pos_ref,
    dqa_ref, dka_ref, dva_ref, dqb_ref, dkb_ref, dvb_ref,
    go_a, go_b, tqa, tka, tva, tqb, tkb, tvb,
):
    half = qa_ref.shape[0]
    quarter = half // 2
    cut = FIRST_DOC - half
    spill = cut - quarter
    offsets = halves(quarter)
    scale_value = HD ** (-0.5)
    factor = scale_value * LOG2E
    for place, offset in enumerate(offsets):
        target, rows = pl.ds(place * quarter, quarter), pl.ds(offset, quarter)
        go_a[target, :] = ga_ref[rows, :]
        go_b[target, :] = gb_ref[rows, :]
    mask = causal_mask(quarter, quarter)
    mask_cut = causal_mask(cut, cut)
    mask_tail = tail_mask(pos_ref[pl.ds(offsets[1] + spill, half - cut), :])
    for accumulator in (tka, tva, tkb, tvb):
        accumulator[...] = jnp.zeros_like(accumulator)

    def attend(query, grad, lse, pieces):
        weights, weight_grads = [], []
        for k_ref, v_ref, rows, cols, mask, _, _ in pieces:
            weight = jnp.exp2(dot_nt(query, k_ref[rows, cols]) * factor - lse)
            weights.append(weight if mask is None else jnp.where(mask, weight, 0.0))
            weight_grads.append(dot_nt(grad, v_ref[rows, cols]))
        shared = functools.reduce(
            jnp.add,
            [jnp.sum(w * g, axis=-1, keepdims=True) for w, g in zip(weights, weight_grads)],
        )
        query_grad = None
        for weight, weight_grad, piece in zip(weights, weight_grads, pieces):
            k_ref, v_ref, rows, cols, _, tk, tv = piece
            score_grad = (weight * (weight_grad - shared)).astype(jnp.bfloat16)
            term = dot_nn(score_grad, k_ref[rows, cols])
            query_grad = term if query_grad is None else query_grad + term
            tk[rows, cols] += dot_tn(score_grad, query)
            tv[rows, cols] += dot_tn(weight.astype(jnp.bfloat16), grad)
        return query_grad

    for head in range(HEAD_GROUP):
        cols = head_slice(head)
        lane = slice(head, head + 1)
        early, late, whole = slice(0, quarter), slice(quarter, half), slice(0, half)
        tqa[early, cols] = attend(
            qa_ref[early, cols], go_a[early, cols], la_ref[0, early, lane],
            [(ka_ref, va_ref, early, cols, mask, tka, tva)],
        )
        tqa[late, cols] = attend(
            qa_ref[late, cols], go_a[late, cols], la_ref[0, late, lane],
            [
                (ka_ref, va_ref, early, cols, None, tka, tva),
                (ka_ref, va_ref, late, cols, mask, tka, tva),
            ],
        )
        early, late = slice(0, cut), slice(cut, half)
        tqb[early, cols] = attend(
            qb_ref[early, cols], go_b[early, cols], lb_ref[0, early, lane],
            [
                (ka_ref, va_ref, whole, cols, None, tka, tva),
                (kb_ref, vb_ref, early, cols, mask_cut, tkb, tvb),
            ],
        )
        tqb[late, cols] = attend(
            qb_ref[late, cols], go_b[late, cols], lb_ref[0, late, lane],
            [(kb_ref, vb_ref, late, cols, mask_tail, tkb, tvb)],
        )
    for place, offset in enumerate(offsets):
        source, rows = pl.ds(place * quarter, quarter), pl.ds(offset, quarter)
        for total, cos_ref, sin_ref, out_ref in (
            (tqa, cosa_ref, sina_ref, dqa_ref),
            (tka, cosa_ref, sina_ref, dka_ref),
            (tqb, cosb_ref, sinb_ref, dqb_ref),
            (tkb, cosb_ref, sinb_ref, dkb_ref),
        ):
            grad = total[source, :] * scale_value
            out_ref[rows, :] = (
                grad * widen(cos_ref[rows, :]) - swap_halves(grad) * widen(sin_ref[rows, :])
            ).astype(jnp.bfloat16)
        dva_ref[rows, :] = tva[source, :].astype(jnp.bfloat16)
        dvb_ref[rows, :] = tvb[source, :].astype(jnp.bfloat16)


COST_SCALE = 1.7


def cost_of(flops):
    return pl.CostEstimate(flops=int(COST_SCALE * flops), bytes_accessed=1000, transcendentals=0)


def rows_kernel(pairs, extra_count, dot, chunk, finish, *refs):
    lefts, weights = refs[:pairs], refs[pairs : 2 * pairs]
    extras = refs[2 * pairs : 2 * pairs + extra_count]
    outs = refs[2 * pairs + extra_count :]

    @pl.loop(0, outs[0].shape[0] // chunk)
    def _(step):
        rows = pl.ds(pl.multiple_of(step * chunk, chunk), chunk)
        total = None
        for left, weight in zip(lefts, weights):
            term = dot(left[rows, :], weight[...])
            total = term if total is None else total + term
        for out, value in zip(outs, finish(total, *[extra[rows, :] for extra in extras])):
            out[rows, :] = value.astype(out.dtype)


def keep_one(total):
    return (total,)


def rows_matmul(
    lefts, weights, dot, types, tile, chunk=1024, finish=keep_one, extras=(), pushes=()
):
    rows = lefts[0].shape[0]
    if dot is dot_nn:
        width = weights[0].shape[1]
        weight_specs = [pl.BlockSpec((w.shape[0], tile), lambda j: (0, j)) for w in weights]
    else:
        width = weights[0].shape[0]
        weight_specs = [pl.BlockSpec((tile, w.shape[1]), lambda j: (j, 0)) for w in weights]
    column = pl.BlockSpec((rows, tile), lambda j: (0, j))
    return grid_call(
        functools.partial(rows_kernel, len(lefts), len(extras), dot, min(chunk, rows), finish),
        [*lefts, *weights, *extras],
        [pl.BlockSpec(left.shape, lambda j: (0, 0)) for left in lefts]
        + weight_specs
        + [column] * len(extras),
        [jax.ShapeDtypeStruct((rows, width), kind) for kind in types],
        [column] * len(types),
        (width // tile,),
        2 * rows * width * sum(left.shape[1] for left in lefts),
        pushes=pushes,
    )


def sum_kernel(parts, chunk, *refs):
    lefts, rights, out = refs[:parts], refs[parts : 2 * parts], refs[-1]

    @pl.loop(0, out.shape[1] // chunk)
    def _(step):
        cols = pl.ds(pl.multiple_of(step * chunk, chunk), chunk)
        total = None
        for left, right in zip(lefts, rights):
            term = dot_tn(left[...], right[:, cols])
            total = term if total is None else total + term
        out[:, cols] = total.astype(out.dtype)


def sum_matmul(lefts, rights, tile, chunk, pushes=()):
    rows, height = lefts[0].shape
    width = rights[0].shape[1]
    return grid_call(
        functools.partial(sum_kernel, len(lefts), chunk),
        [*lefts, *rights],
        [pl.BlockSpec((rows, tile), lambda j: (0, j)) for _ in lefts]
        + [pl.BlockSpec((rows, width), lambda j: (0, 0)) for _ in rights],
        [jax.ShapeDtypeStruct((height, width), jnp.bfloat16)],
        [pl.BlockSpec((tile, width), lambda j: (j, 0))],
        (height // tile,),
        2 * rows * height * width * len(lefts),
        pushes=pushes,
    )


def partner_of(kind):
    index, place = lax.axis_index("fsdp"), lax.axis_index("tp")
    if kind == "near":
        return (index, place + 1 - 2 * (place % 2))
    if kind == "core":
        return sibling_id()
    return (index, place + 2 - 4 * (place // 2))


def start_pushes(kinds, sources, targets, send, receive):
    barrier = pltpu.get_barrier_semaphore()
    names = sorted(set(kinds))
    for kind in names:
        pl.semaphore_signal(
            barrier, inc=1, device_id=partner_of(kind), device_id_type=pl.DeviceIdType.MESH
        )
    pl.semaphore_wait(barrier, len(names))
    for place, kind in enumerate(kinds):
        push(
            sources[place], targets[place], send.at[place], receive.at[place], partner_of(kind)
        ).start()


def wait_pushes(kinds, sources, targets, send, receive):
    for place, kind in enumerate(kinds):
        push(
            sources[place], targets[place], send.at[place], receive.at[place], partner_of(kind)
        ).wait()


def pushing_kernel(kernel, axes, in_count, out_count, kinds, *refs):
    count = len(kinds)
    inputs, sources = refs[:in_count], refs[in_count : in_count + count]
    outs = refs[in_count + count : in_count + count + out_count]
    targets = refs[in_count + count + out_count : in_count + 2 * count + out_count]
    scratch, (send, receive) = refs[in_count + 2 * count + out_count : -2], refs[-2:]
    first = functools.reduce(jnp.logical_and, [pl.program_id(axis) == 0 for axis in range(axes)])
    last = functools.reduce(
        jnp.logical_and,
        [pl.program_id(axis) == pl.num_programs(axis) - 1 for axis in range(axes)],
    )

    @pl.when(first)
    def _():
        start_pushes(kinds, sources, targets, send, receive)

    kernel(*inputs, *outs, *scratch)

    @pl.when(last)
    def _():
        wait_pushes(kinds, sources, targets, send, receive)


def grid_call(
    kernel, operands, in_specs, outs, out_specs, grid, flops, scratch=(), pushes=(), vmem=60
):
    params = dict(
        dimension_semantics=("arbitrary",) * len(grid), vmem_limit_bytes=vmem * 1024 * 1024
    )
    operands, in_specs, outs = list(operands), list(in_specs), list(outs)
    out_specs, scratch = list(out_specs), list(scratch)
    if pushes:
        kinds = tuple(kind for kind, _ in pushes)
        kernel = functools.partial(
            pushing_kernel, kernel, len(grid), len(operands), len(outs), kinds
        )
        anywhere = [pl.BlockSpec(memory_space=pl.ANY)] * len(pushes)
        operands += [value for _, value in pushes]
        in_specs += anywhere
        outs += [jax.ShapeDtypeStruct(value.shape, value.dtype) for _, value in pushes]
        out_specs += anywhere
        scratch += [pltpu.SemaphoreType.DMA((len(pushes),))] * 2
        next_key[0] += 1
        params.update(collective_id=next_key[0], has_side_effects=True)
    return tuple(
        pl.pallas_call(
            kernel,
            out_shape=outs,
            grid=grid,
            in_specs=in_specs,
            out_specs=out_specs,
            scratch_shapes=scratch,
            compiler_params=pltpu.CompilerParams(**params),
            cost_estimate=cost_of(max(flops, 27 * 10**9) if pushes else flops),
        )(*operands)
    )


def swap_kernel(kinds, *refs):
    count = len(kinds)
    sources, targets, (send, receive) = refs[:count], refs[count : 2 * count], refs[2 * count :]
    start_pushes(kinds, sources, targets, send, receive)
    wait_pushes(kinds, sources, targets, send, receive)


def swap_call(*pushes):
    next_key[0] += 1
    kinds = tuple(kind for kind, _ in pushes)
    values = [value for _, value in pushes]
    return exchange_call(
        functools.partial(swap_kernel, kinds), next_key[0], values,
        [jax.ShapeDtypeStruct(value.shape, value.dtype) for value in values],
        [pltpu.SemaphoreType.DMA((len(pushes),))] * 2, flops=130 * 10**9,
    )


next_key = [11]


def sibling_id():
    index = lax.axis_index("fsdp")
    return (index + 1 - 2 * (index % 2), lax.axis_index("tp"))


def meet(partner):
    barrier = pltpu.get_barrier_semaphore()
    pl.semaphore_signal(barrier, inc=1, device_id=partner, device_id_type=pl.DeviceIdType.MESH)
    pl.semaphore_wait(barrier, 1)


def push(source, target, send, receive, partner):
    return pltpu.make_async_remote_copy(
        src_ref=source,
        dst_ref=target,
        send_sem=send,
        recv_sem=receive,
        device_id=partner,
        device_id_type=pl.DeviceIdType.MESH,
    )


def exchange_call(kernel, key, operands, outs, scratch, vmem=60, flops=4 * 10**9):
    anywhere = pl.BlockSpec(memory_space=pl.ANY)
    results = pl.pallas_call(
        kernel,
        out_shape=outs,
        in_specs=[anywhere] * len(operands),
        out_specs=[anywhere] * len(outs),
        scratch_shapes=scratch,
        compiler_params=pltpu.CompilerParams(
            collective_id=key, has_side_effects=True, vmem_limit_bytes=vmem * 1024 * 1024
        ),
        cost_estimate=cost_of(flops),
    )(*operands)
    return tuple(results) if len(outs) > 1 else results[0]


def relay(sources, targets, buffer, load, store):
    loads, stores = [], []
    for place, source in enumerate(sources):
        copy = pltpu.make_async_copy(source, buffer.at[place], load.at[place])
        copy.start()
        loads.append(copy)
    for place, target in enumerate(targets):
        loads[place].wait()
        copy = pltpu.make_async_copy(buffer.at[place], target, store.at[place])
        copy.start()
        stores.append(copy)
    for copy in stores:
        copy.wait()


def gather_kernel(own_ref, near_ref, full_ref, buffer, load, store, send, receive):
    partner = sibling_id()
    meet(partner)
    count = own_ref.shape[0]
    remotes = []
    for place, ref in enumerate((own_ref, near_ref)):
        remote = push(
            ref, full_ref.at[pl.ds((2 + place) * count, count)],
            send.at[place], receive.at[place], partner,
        )
        remote.start()
        remotes.append(remote)
    targets = [full_ref.at[pl.ds(place * count, count)] for place in range(2)]
    relay((own_ref, near_ref), targets, buffer, load, store)
    for remote in remotes:
        remote.wait()


def core_gather(own, near):
    shape = (4 * own.shape[0], own.shape[1])
    return exchange_call(
        gather_kernel, 1, [own, near], [jax.ShapeDtypeStruct(shape, own.dtype)],
        [pltpu.VMEM((2, *own.shape), own.dtype)] + [pltpu.SemaphoreType.DMA((2,))] * 4,
    )


def gather_two_kernel(
    own_ref, own_near_ref, got_ref, got_near_ref, first_ref, second_ref,
    buffer, load, store, send, receive,
):
    partner = sibling_id()
    far = lax.axis_index("tp") // 2
    meet(partner)
    count = own_ref.shape[0]

    def run(targets):
        sources = (own_ref, own_near_ref, got_ref, got_near_ref)
        remotes, places = [], []
        for place, ref in enumerate(sources):
            target, row = targets[place // 2], place % 2
            remote = push(
                ref, target.at[pl.ds((2 + row) * count, count)],
                send.at[place], receive.at[place], partner,
            )
            remote.start()
            remotes.append(remote)
            places.append(target.at[pl.ds(row * count, count)])
        relay(sources, places, buffer, load, store)
        for remote in remotes:
            remote.wait()

    @pl.when(far == 0)
    def _():
        run((first_ref, second_ref))

    @pl.when(far != 0)
    def _():
        run((second_ref, first_ref))


def core_gather_two(own, own_near, got, got_near):
    shape = (4 * own.shape[0], own.shape[1])
    return exchange_call(
        gather_two_kernel, 11, [own, own_near, got, got_near],
        [jax.ShapeDtypeStruct(shape, own.dtype)] * 2,
        [pltpu.VMEM((4, *own.shape), own.dtype)] + [pltpu.SemaphoreType.DMA((4,))] * 4,
    )


def reduce_kernel(term_ref, keep_ref, away_ref, mine, got, keep, away, local, send, receive, store):
    partner = sibling_id()
    meet(partner)
    pieces, count = mine.shape[0], mine.shape[1]
    half = pieces * count
    remotes, loads = [], []
    for piece in range(pieces):
        order = (piece + pieces // 2) % pieces
        remote = push(
            term_ref.at[pl.ds(half + order * count, count)], got.at[order],
            send.at[order], receive.at[order], partner,
        )
        remote.start()
        remotes.append(remote)
        load = pltpu.make_async_copy(
            term_ref.at[pl.ds(order * count, count)], mine.at[order], local.at[order]
        )
        load.start()
        loads.append(load)
    stores = []
    for piece in range(pieces):
        order = (piece + pieces // 2) % pieces
        loads[piece].wait()
        remotes[piece].wait()
        total = mine[order].astype(jnp.float32) + got[order].astype(jnp.float32)
        if order < pieces // 2:
            keep[order] = total
            copy = pltpu.make_async_copy(
                keep.at[order], keep_ref.at[pl.ds(order * count, count)], store.at[order]
            )
        else:
            slot = order - pieces // 2
            away[slot] = total.astype(away.dtype)
            copy = pltpu.make_async_copy(
                away.at[slot], away_ref.at[pl.ds(slot * count, count)], store.at[order]
            )
        copy.start()
        stores.append(copy)
    for copy in stores:
        copy.wait()


def core_reduce(term):
    rows, width = term.shape
    quarter = rows // 4
    pieces = 4
    count = 2 * quarter // pieces
    return exchange_call(
        reduce_kernel, 2, [term],
        [
            jax.ShapeDtypeStruct((quarter, width), jnp.float32),
            jax.ShapeDtypeStruct((quarter, width), term.dtype),
        ],
        [
            pltpu.VMEM((pieces, count, width), term.dtype),
            pltpu.VMEM((pieces, count, width), term.dtype),
            pltpu.VMEM((pieces // 2, count, width), jnp.float32),
            pltpu.VMEM((pieces // 2, count, width), term.dtype),
        ]
        + [pltpu.SemaphoreType.DMA((pieces,))] * 4,
    )


def pair_kernel(own_ref, *refs):
    others, (pair_ref, buffer, load, store, send, receive) = refs[:-6], refs[-6:]
    partner = sibling_id()
    core = lax.axis_index("fsdp") % 2
    far = lax.axis_index("tp") // 2
    meet(partner)
    base = pl.multiple_of(core * own_ref.shape[0], own_ref.shape[0])
    count = others[0].shape[0]
    owns = [own_ref.at[pl.ds(place * count, count)] for place in range(len(others))]

    def run(mine, theirs):
        remotes, targets = [], []
        for place in range(len(others)):
            target = pair_ref.at[pl.ds(base + place * count, count)]
            remote = push(theirs[place], target, send.at[place], receive.at[place], partner)
            remote.start()
            remotes.append(remote)
            targets.append(target)
        relay(mine, targets, buffer, load, store)
        for remote in remotes:
            remote.wait()

    @pl.when(core == far)
    def _():
        run(owns, others)

    @pl.when(core != far)
    def _():
        run(others, owns)


def core_pair(key, own, *others):
    shape = (2 * own.shape[0], own.shape[1])
    return exchange_call(
        pair_kernel, key, [own, *others], [jax.ShapeDtypeStruct(shape, own.dtype)],
        [pltpu.VMEM((len(others), *others[0].shape), own.dtype)]
        + [pltpu.SemaphoreType.DMA((len(others),))] * 4,
    )


def split_kernel(pair_ref, keep_ref, away_ref, buffer, load, store, send, receive):
    partner = sibling_id()
    core = lax.axis_index("fsdp") % 2
    far = lax.axis_index("tp") // 2
    meet(partner)
    count = keep_ref.shape[0]
    mine = pair_ref.at[pl.ds(pl.multiple_of(core * count, count), count)]
    theirs = pair_ref.at[pl.ds(pl.multiple_of((1 - core) * count, count), count)]

    def run(own_target, other_target):
        remote = push(theirs, other_target, send.at[0], receive.at[0], partner)
        remote.start()
        relay((mine,), (own_target,), buffer, load, store)
        remote.wait()

    @pl.when(core == far)
    def _():
        run(keep_ref, keep_ref)

    @pl.when(core != far)
    def _():
        run(away_ref, away_ref)


def core_split(key, pair):
    shape = (pair.shape[0] // 2, pair.shape[1])
    return exchange_call(
        split_kernel, key, [pair], [jax.ShapeDtypeStruct(shape, pair.dtype)] * 2,
        [pltpu.VMEM((1, *shape), pair.dtype)] + [pltpu.SemaphoreType.DMA((1,))] * 4,
    )


def attention_call(kernel, arrays, kinds, outs, scratch, pushes=()):
    rows, heads_local = arrays[-1].shape[0], outs[1]
    half = rows // 2
    groups = heads_local // HEAD_GROUP
    width = HEAD_GROUP * HD

    def spec(kind):
        if kind == "table":
            return pl.BlockSpec((half, HD), lambda s, g: (s, 0))
        if kind == "column":
            return pl.BlockSpec((half, 1), lambda s, g: (s, 0))
        if kind == "lse":
            return pl.BlockSpec((1, half, HEAD_GROUP), lambda s, g: (g, s, 0))
        shift = kind * groups
        return pl.BlockSpec((half, width), lambda s, g: (s, shift + g))

    def shape(kind):
        if kind == "lse":
            return jax.ShapeDtypeStruct((groups, rows, HEAD_GROUP), jnp.float32)
        return jax.ShapeDtypeStruct((rows, heads_local * HD), jnp.bfloat16)

    return grid_call(
        kernel,
        arrays,
        [spec(kind) for kind in kinds],
        [shape(kind) for kind in outs[0]],
        [spec(kind) for kind in outs[0]],
        (rows // half, groups),
        4 * len(outs[0]) ** 2 * rows * rows * heads_local * HD // 16,
        scratch=scratch(half, width),
        pushes=pushes,
    )


def backward_scratch(half, width):
    return [pltpu.VMEM((half, width), jnp.bfloat16)] * 2 + [
        pltpu.VMEM((half, width), jnp.float32)
    ] * 6


def no_scratch(half, width):
    return []


def head_tables(positions):
    half_width = HD // 2
    frequency = rope_theta ** (-(jnp.arange(half_width, dtype=jnp.float32) * 2.0 / HD))
    angles = positions.astype(jnp.float32)[:, None] * frequency[None, :]
    cosine, sine = jnp.cos(angles), jnp.sin(angles)
    return (
        jnp.concatenate([cosine, cosine], axis=-1),
        jnp.concatenate([-sine, sine], axis=-1),
    )


def paired_device(
    block_in,
    out_cotangent,
    segment_ids,
    doc_positions,
    norm1_gain,
    qkv_weight,
    out_weight,
    norm2_gain,
    gate_up_weight,
    down_weight,
):
    fsdp_count, tp_count = lax.axis_size("fsdp"), lax.axis_size("tp")
    core = lax.axis_index("fsdp") % 2
    lane_z = lax.axis_index("tp")
    near, far = lane_z % 2, lane_z // 2
    core_pairs = [(i, i ^ 1) for i in range(fsdp_count)]
    near_pairs = [(i, i ^ 1) for i in range(tp_count)]
    far_pairs = [(i, i ^ 2) for i in range(tp_count)]
    plane_groups = [list(range(first, fsdp_count, 2)) for first in range(2)]
    rows = block_in.shape[1]
    local_cols = qkv_weight.shape[2]
    heads_local = local_cols // HD
    gain_one = norm1_gain.astype(jnp.float32)
    gain_two = norm2_gain.astype(jnp.float32)

    def swap_core(value):
        return lax.ppermute(value, "fsdp", core_pairs)

    def swap_near(value):
        return lax.ppermute(value, "tp", near_pairs)

    def swap_far(value):
        return lax.ppermute(value, "tp", far_pairs)

    def pick_tile(size):
        return 512 if size % 512 == 0 else 768

    tokens = []

    def act(work, *inputs, sends=()):
        values = [*inputs, *[value for _, value in sends]]
        held = lax.optimization_barrier((*values, *tokens))[: len(values)]
        if sends:
            kinds = [kind for kind, _ in sends]
            result = work(*held[: len(inputs)], pushes=list(zip(kinds, held[len(inputs) :])))
        else:
            result = work(*held)
        tokens[:] = result if isinstance(result, tuple) else (result,)
        return result[0] if isinstance(result, tuple) and len(result) == 1 else result

    def swap(*sends):
        return act(lambda pushes: swap_call(*pushes), sends=sends)

    def pick(value, index):
        return lax.dynamic_index_in_dim(value, index, 0, keepdims=False)

    def place_tokens(value, got):
        keep = pick(value, far)
        return jnp.where(far == 0, keep, got), jnp.where(far == 0, got, keep)

    def join(left, right):
        return jnp.concatenate([left, right], axis=0)

    def plane_gather(pair):
        return lax.all_gather(pair, "fsdp", axis=0, tiled=True, axis_index_groups=plane_groups)

    def plane_scatter(grad):
        return lax.psum_scatter(
            grad, "fsdp", scatter_dimension=0, tiled=True, axis_index_groups=plane_groups
        )

    def gather_weight(key, local, *others):
        return plane_gather(act(lambda own, *got: core_pair(key, own, *got), local, *others))

    def halve(value):
        count = value.shape[0] // 2
        return value[:count], value[count:]

    def add_wide(left, right):
        return left.astype(jnp.float32) + right.astype(jnp.float32)

    def chained(value, *others):
        return lax.optimization_barrier((value, *others))[0]

    def scatter_gains(gains):
        for axis, size in (("fsdp", fsdp_count), ("tp", tp_count)):
            index = lax.axis_index(axis)
            step = size // 2
            while step >= 1:
                bit = (index // step) % 2
                parts = gains.reshape(gains.shape[0], 2, gains.shape[1] // 2)
                sent = lax.dynamic_index_in_dim(parts, 1 - bit, 1, keepdims=False)
                kept = lax.dynamic_index_in_dim(parts, bit, 1, keepdims=False)
                gains = kept + lax.ppermute(sent, axis, [(i, i ^ step) for i in range(size)])
                step //= 2
        return gains

    def wide_dot(left, right, pushes=()):
        return rows_matmul(
            [left], [right], dot_nn, [jnp.float32], pick_tile(right.shape[1]), pushes=pushes
        )

    def dot_bf16(left, right, pushes=()):
        return rows_matmul(
            [left], [right], dot_nn, [jnp.bfloat16], pick_tile(right.shape[1]), pushes=pushes
        )

    def grad_sum(left, right, left_next, right_next, pushes=()):
        chunk = pick_tile(right.shape[1])
        return sum_matmul(
            [left, left_next], [right, right_next], pick_tile(left.shape[1]),
            2 * chunk if right.shape[1] % (2 * chunk) == 0 else chunk, pushes=pushes,
        )

    def heads_back(grad, weight, pushes=()):
        return rows_matmul(
            [grad], [weight], dot_nt, [jnp.bfloat16], pick_tile(weight.shape[0]), pushes=pushes
        )

    def rms_pack(stream, gain):
        scale = rms_scale(stream)
        return scale, (stream * scale * gain).astype(jnp.bfloat16)

    qkv_local = qkv_weight.reshape(qkv_weight.shape[0], 3 * local_cols)
    gate_local, up_local = gate_up_weight[:, 0], gate_up_weight[:, 1]

    next_key[0] = 11
    places = jnp.broadcast_to(doc_positions[:, None, :], (2, 8, rows))

    def first_norm(part):
        stream = part.astype(jnp.float32)
        return (stream, *rms_pack(stream, gain_one))

    s_own, r_own, n_own = act(lambda value: first_norm(pick(value, far)), block_in)
    near_own, qkv_other, place_got = swap(
        ("near", n_own), ("far", qkv_local), ("far", pick(places, 1 - far))
    )
    qkv_full = gather_weight(4, qkv_local, qkv_other)
    places = join(*place_tokens(places, place_got))

    def make_tables(own, other):
        order = join(own, other)[::8].reshape(2, 2, 2, rows)
        early, late = order[:, :, 0].reshape(-1), order[:, :, 1].reshape(-1)
        return (*head_tables(early), *head_tables(late), late[:, None])

    c_own = pick(out_cotangent, far)
    stream_got, c_near_own, out_other, near_places = swap(
        ("far", pick(block_in, 1 - far)), ("near", c_own), ("far", out_weight), ("near", places)
    )
    places = join(places, near_places)
    out_full = gather_weight(3, out_weight, out_other)
    s_got, r_got, n_got = act(first_norm, stream_got)
    near_got, gate_other, core_places = swap(
        ("near", n_got), ("far", gate_local), ("core", places)
    )
    gate_full = gather_weight(5, gate_local, gate_other)
    h1_first, h1_second = act(core_gather_two, n_own, near_own, n_got, near_got)
    streams = [jnp.where(far == 0, s_own, s_got), jnp.where(far == 0, s_got, s_own)]
    scales_one = [jnp.where(far == 0, r_own, r_got), jnp.where(far == 0, r_got, r_own)]

    def attend_first(projected, pushes=()):
        arrays = [projected, projected, projected, *tables[0]]
        return attention_call(
            forward_first, arrays, [0, 1, 2, "table", "table"],
            ([0, 0, 0, 0, "lse"], heads_local), no_scratch, pushes,
        )

    def attend_second(projected, pushes=()):
        arrays = [projected, projected, projected, *tables[1], saved[0][1], saved[0][2], reach]
        return attention_call(
            forward_second, arrays, [0, 1, 2, "table", "table", 0, 0, "column"],
            ([0, 0, 0, 0, "lse"], heads_local), no_scratch, pushes,
        )

    up_other = swap_far(chained(up_local, gate_other))
    cos_first, sin_first, cos_second, sin_second, reach = act(
        make_tables, places, core_places
    )
    tables = [(cos_first, sin_first), (cos_second, sin_second)]
    projected = act(wide_dot, h1_first, qkv_full)
    results = act(attend_first, projected)
    up_full = gather_weight(5, up_local, up_other)
    down_other = swap_far(chained(down_weight, up_other))
    saved, lses, mixed_first = [results[:3]], [results[4]], results[3]
    term_first = act(dot_bf16, mixed_first, out_full)
    keep_first, send_first = act(core_reduce, term_first)
    projected = act(wide_dot, h1_second, qkv_full)

    def second_norm(stream, keep, got):
        middle = stream + keep + got.astype(jnp.float32)
        return (middle, *rms_pack(middle, gain_two))

    *results, branch_first = act(attend_second, projected, sends=[("near", send_first)])
    saved.append(results[:3])
    lses.append(results[4])
    mixed_second = results[3]
    m_first, q_first, n_first = act(second_norm, streams[0], keep_first, branch_first)
    term_second, near_first = act(
        dot_bf16, mixed_second, out_full, sends=[("near", n_first)]
    )
    keep_second, send_second = act(core_reduce, term_second)
    h2_first = act(core_gather, n_first, near_first)
    down_full_pair = act(lambda own, got: core_pair(6, own, got), down_weight, down_other)
    down_full = plane_gather(down_full_pair)
    c_got = swap_far(chained(pick(out_cotangent, 1 - far), down_full_pair))

    gate_first, branch_second = act(
        wide_dot, h2_first, gate_full, sends=[("near", send_second)]
    )
    m_second, q_second, n_second = act(second_norm, streams[1], keep_second, branch_second)

    def rise(hidden, weight, gate, pushes=()):
        return rows_matmul(
            [hidden], [weight], dot_nn, [jnp.float32, jnp.bfloat16], pick_tile(weight.shape[1]),
            finish=lambda up, gate: (up, gate * jax.nn.sigmoid(gate) * up), extras=[gate],
            pushes=pushes,
        )

    up_first, a_first, near_second = act(
        rise, h2_first, up_full, gate_first, sends=[("near", n_second)]
    )
    h2_second = act(core_gather, n_second, near_second)
    gate_second, c_near_got = act(
        wide_dot, h2_second, gate_full, sends=[("near", c_got)]
    )
    y_first, y_second = act(core_gather_two, c_own, c_near_own, c_got, c_near_got)
    c_first, c_second = jnp.where(far == 0, c_own, c_got), jnp.where(far == 0, c_got, c_own)
    up_second, a_second = act(rise, h2_second, up_full, gate_second)
    down_sum = plane_scatter(act(grad_sum, a_first, y_first, a_second, y_second))

    def fall_finish(act_grad, gate, up):
        sigmoid_gate = jax.nn.sigmoid(gate)
        return (
            act_grad * up * sigmoid_gate * (1.0 + gate * (1.0 - sigmoid_gate)),
            act_grad * (gate * sigmoid_gate),
        )

    def fall(cotangent, weight, gate, up, pushes=()):
        return rows_matmul(
            [cotangent], [weight], dot_nt, [jnp.bfloat16] * 2, pick_tile(weight.shape[0]),
            chunk=512, finish=fall_finish, extras=[gate, up], pushes=pushes,
        )

    def hidden_grad(gate_grad, up_grad, gate_weight, up_weight, pushes=()):
        return rows_matmul(
            [gate_grad, up_grad], [gate_weight, up_weight], dot_nt, [jnp.bfloat16],
            pick_tile(gate_weight.shape[0]), pushes=pushes,
        )

    def second_back(middle, scale, keep, got, cotangent):
        grad, gain_term = norm_back(middle, scale, gain_two, keep + got.astype(jnp.float32))
        grad = cotangent.astype(jnp.float32) + grad
        return grad, grad.astype(jnp.bfloat16), gain_term

    dg_first, du_first = act(fall, y_first, down_full, gate_first, up_first)
    term_first = act(hidden_grad, dg_first, du_first, gate_full, up_full)
    keep_first, send_first = act(core_reduce, term_first)
    dg_second, du_second, back_first = act(
        fall, y_second, down_full, gate_second, up_second, sends=[("near", send_first)]
    )
    g_first, n_first, gain_two_first = act(
        second_back, m_first, q_first, keep_first, back_first, c_first
    )
    term_second, near_first = act(
        hidden_grad, dg_second, du_second, gate_full, up_full, sends=[("near", n_first)]
    )
    keep_second, send_second = act(core_reduce, term_second)
    d_first = act(core_gather, n_first, near_first)
    grad_gate, back_second = act(
        grad_sum, h2_first, dg_first, h2_second, dg_second, sends=[("near", send_second)]
    )
    gate_sum = plane_scatter(grad_gate)
    g_second, n_second, gain_two_second = act(
        second_back, m_second, q_second, keep_second, back_second, c_second
    )
    heads_first = act(heads_back, d_first, out_full)
    down_mine, down_away = act(lambda pair: core_split(10, pair), down_sum)
    down_got = swap_far(down_away)
    grad_up, near_second = act(
        grad_sum, h2_first, du_first, h2_second, du_second, sends=[("near", n_second)]
    )
    up_sum = plane_scatter(grad_up)

    d_second = act(core_gather, n_second, near_second)
    heads_second = act(heads_back, d_second, out_full)
    grad_out = act(grad_sum, mixed_first, d_first, mixed_second, d_second)
    out_sum = plane_scatter(grad_out)
    mlp_first = act(dot_bf16, a_first, down_full)
    mlp_keep_first, mlp_send_first = act(core_reduce, mlp_first)
    gate_mine, gate_away = act(lambda pair: core_split(9, pair), gate_sum)
    gate_got = swap_far(gate_away)
    mlp_second = act(dot_bf16, a_second, down_full)
    mlp_keep_second, mlp_send_second = act(core_reduce, mlp_second)
    def attend_back(heads_first, heads_second, pushes=()):
        return attention_call(
            backward_both,
            [
                *saved[0], *saved[1], heads_first, heads_second, *lses,
                *tables[0], *tables[1], reach,
            ],
            [0] * 8 + ["lse"] * 2 + ["table"] * 4 + ["column"],
            ([0] * 6, heads_local),
            backward_scratch,
            pushes,
        )

    *grads, mlp_branch_first, mlp_branch_second = act(
        attend_back, heads_first, heads_second,
        sends=[("near", mlp_send_first), ("near", mlp_send_second)],
    )
    p_first, p_second = act(
        lambda *parts: (
            jnp.concatenate(parts[:3], axis=1),
            jnp.concatenate(parts[3:], axis=1),
        ),
        *grads,
    )

    def finish_output(first, first_keep, first_got, second, second_keep, second_got):
        first = (first + first_keep + first_got.astype(jnp.float32)).astype(jnp.bfloat16)
        second = (second + second_keep + second_got.astype(jnp.float32)).astype(jnp.bfloat16)
        return jnp.where(far == 0, first, second), jnp.where(far == 0, second, first)

    up_mine, up_away = act(lambda pair: core_split(9, pair), up_sum)
    up_got = swap_far(up_away)
    grad_qkv = act(grad_sum, h1_first, p_first, h1_second, p_second)
    qkv_sum = plane_scatter(grad_qkv)
    out_keep, out_send = act(
        finish_output,
        m_first, mlp_keep_first, mlp_branch_first, m_second, mlp_keep_second, mlp_branch_second,
    )
    out_got = swap_far(out_send)
    term_first = act(heads_back, p_first, qkv_full)
    keep_first, send_first = act(core_reduce, term_first)
    term_second, back_first = act(
        heads_back, p_second, qkv_full, sends=[("near", send_first)]
    )
    keep_second, send_second = act(core_reduce, term_second)
    def settle(keep, got):
        return jnp.stack([jnp.where(far == 0, keep, got), jnp.where(far == 0, got, keep)])

    def first_back(stream, scale, keep, got, grad):
        back, gain_term = norm_back(stream, scale, gain_one, keep + got.astype(jnp.float32))
        return grad + back, gain_term

    def last_back(stream, scale, keep, got, grad, first):
        second, gain_term = first_back(stream, scale, keep, got, grad)
        return (
            jnp.where(far == 0, first, second),
            jnp.where(far == 0, second, first).astype(jnp.bfloat16),
            gain_term,
        )

    out_mine, out_away = act(lambda pair: core_split(8, pair), out_sum)
    back_second, out_back = swap(("near", send_second), ("far", out_away))
    qkv_mine, qkv_away = act(lambda pair: core_split(0, pair), qkv_sum)
    qkv_back = swap_far(qkv_away)
    i_first, gain_one_first = act(
        first_back, streams[0], scales_one[0], keep_first, back_first, g_first
    )
    in_keep, in_send, gain_one_second = act(
        last_back, streams[1], scales_one[1], keep_second, back_second, g_second, i_first
    )
    in_got = swap_far(in_send)
    down_owned = act(add_wide, down_mine, down_got)
    gate_owned = act(add_wide, gate_mine, gate_got)
    block_out = act(settle, out_keep, out_got)
    up_owned = act(add_wide, up_mine, up_got)
    gate_up_owned = act(lambda a, b: jnp.stack([a, b], axis=1), gate_owned, up_owned)
    out_owned = act(add_wide, out_mine, out_back)
    gains = scatter_gains(
        jnp.stack([gain_one_first + gain_one_second, gain_two_first + gain_two_second])
    )
    in_grad = act(lambda keep, got: settle(keep, got.astype(jnp.float32)), in_keep, in_got)
    qkv_owned = act(add_wide, qkv_mine, qkv_back)
    return (
        block_out,
        in_grad,
        gains[0],
        qkv_owned.reshape(qkv_weight.shape),
        out_owned,
        gains[1],
        gate_up_owned,
        down_owned,
    )


def solution(mesh):
    sizes = (mesh.shape["fsdp"], mesh.shape["tp"])
    body = paired_device if sizes == (8, 4) else per_device
    in_specs = (
        P("fsdp", "tp", None),
        P("fsdp", "tp", None),
        P("fsdp", "tp"),
        P("fsdp", "tp"),
        P(),
        P("fsdp", None, "tp"),
        P(("tp", "fsdp"), None),
        P(),
        P("fsdp", None, "tp"),
        P(("tp", "fsdp"), None),
    )
    out_specs = (
        P("fsdp", "tp", None),
        P("fsdp", "tp", None),
        P(("fsdp", "tp")),
        P("fsdp", None, "tp"),
        P(("tp", "fsdp"), None),
        P(("fsdp", "tp")),
        P("fsdp", None, "tp"),
        P(("tp", "fsdp"), None),
    )
    return jax.shard_map(
        body, mesh=mesh, in_specs=in_specs, out_specs=out_specs, check_vma=False
    )
```

```python
import functools

import jax
import jax.numpy as jnp
from jax import lax
from jax.experimental import pallas as pl
from jax.experimental.pallas import tpu as pltpu
from jax.sharding import PartitionSpec as P

D = 3072
HD = 96


rms_epsilon = 1e-05
rope_theta = 10000.0
masked_score = -1e30
LOG2E = 1.4426950408889634


def rope_tables(positions, head_size):
    half_width = head_size // 2
    frequency = rope_theta ** (-(jnp.arange(half_width, dtype=jnp.float32) * 2.0 / head_size))
    angles = positions.astype(jnp.float32)[:, None] * frequency[None, :]
    return (jnp.cos(angles)[:, None, :], jnp.sin(angles)[:, None, :])


def rotate(values, cosine_part, sine_part):
    half_width = values.shape[-1] // 2
    lead_half = values[..., :half_width]
    tail_half = values[..., half_width:]
    return jnp.concatenate(
        [
            lead_half * cosine_part - tail_half * sine_part,
            tail_half * cosine_part + lead_half * sine_part,
        ],
        axis=-1,
    )


def unrotate(values, cosine_part, sine_part):
    half_width = values.shape[-1] // 2
    lead_half = values[..., :half_width]
    tail_half = values[..., half_width:]
    return jnp.concatenate(
        [
            lead_half * cosine_part + tail_half * sine_part,
            tail_half * cosine_part - lead_half * sine_part,
        ],
        axis=-1,
    )


def rms_scale(stream):
    return lax.rsqrt(jnp.mean(stream * stream, axis=-1, keepdims=True) + rms_epsilon)


def norm_back(stream, scale_rows, gain_vec, grad_rows):
    gained_grad = gain_vec * grad_rows
    input_grad = scale_rows * gained_grad - stream * scale_rows**3 * jnp.mean(
        gained_grad * stream, axis=-1, keepdims=True
    )
    return (input_grad, jnp.sum(grad_rows * stream * scale_rows, axis=0))


def allowed_mask(segment_tile, index_tile, segments):
    columns = jnp.arange(segments.shape[0], dtype=jnp.int32)
    return (segment_tile[:, None] == segments[None, :]) & (index_tile[:, None] >= columns[None, :])


def masked_scores(query_tile, key_rows, segment_tile, index_tile, segments, scale_value):
    scores = (
        jnp.einsum("qhd,khd->hqk", query_tile, key_rows, preferred_element_type=jnp.float32)
        * scale_value
    )
    return jnp.where(allowed_mask(segment_tile, index_tile, segments)[None], scores, masked_score)


def attention_forward(queries, key_rows, value_rows, segments, block_rows):
    seq_len, head_count, head_size = queries.shape
    tiles = seq_len // block_rows
    scale_value = head_size ** (-0.5)
    positions = jnp.arange(seq_len, dtype=jnp.int32)

    def query_block(packed):
        query_tile, segment_tile, index_tile = packed
        scores = masked_scores(
            query_tile, key_rows, segment_tile, index_tile, segments, scale_value
        )
        row_max = jnp.max(scores, axis=-1, keepdims=True)
        exponent = jnp.exp(scores - row_max)
        row_total = jnp.sum(exponent, axis=-1, keepdims=True)
        probs_low = (exponent / row_total).astype(jnp.bfloat16)
        mixed = jnp.einsum(
            "hqk,khd->qhd", probs_low, value_rows, preferred_element_type=jnp.float32
        )
        return (mixed, (row_max + jnp.log(row_total))[..., 0])

    mixed, log_total = lax.map(
        query_block,
        (
            queries.reshape(tiles, block_rows, head_count, head_size),
            segments.reshape(tiles, block_rows),
            positions.reshape(tiles, block_rows),
        ),
    )
    return (mixed.reshape(seq_len, head_count * head_size), log_total)


def attention_backward(queries, key_rows, value_rows, segments, log_total, out_grad, block_rows):
    seq_len, head_count, head_size = queries.shape
    tiles = seq_len // block_rows
    scale_value = head_size ** (-0.5)
    positions = jnp.arange(seq_len, dtype=jnp.int32)

    def query_block(carry, packed):
        key_acc, value_acc = carry
        query_tile, segment_tile, index_tile, total_tile, grad_tile = packed
        scores = masked_scores(
            query_tile, key_rows, segment_tile, index_tile, segments, scale_value
        )
        probs = jnp.exp(scores - total_tile[..., None])
        probs_low = probs.astype(jnp.bfloat16)
        prob_grad = jnp.einsum(
            "qhd,khd->hqk", grad_tile, value_rows, preferred_element_type=jnp.float32
        )
        score_grad = (
            probs * (prob_grad - jnp.sum(probs * prob_grad, axis=-1, keepdims=True))
        ).astype(jnp.bfloat16)
        query_grad = (
            jnp.einsum("hqk,khd->qhd", score_grad, key_rows, preferred_element_type=jnp.float32)
            * scale_value
        )
        key_acc = (
            key_acc
            + jnp.einsum("hqk,qhd->khd", score_grad, query_tile, preferred_element_type=jnp.float32)
            * scale_value
        )
        value_acc = value_acc + jnp.einsum(
            "hqk,qhd->khd", probs_low, grad_tile, preferred_element_type=jnp.float32
        )
        return ((key_acc, value_acc), query_grad)

    start_acc = (jnp.zeros(queries.shape, jnp.float32), jnp.zeros(queries.shape, jnp.float32))
    (key_grad, value_grad), query_grad = lax.scan(
        query_block,
        start_acc,
        (
            queries.reshape(tiles, block_rows, head_count, head_size),
            segments.reshape(tiles, block_rows),
            positions.reshape(tiles, block_rows),
            log_total,
            out_grad.reshape(tiles, block_rows, head_count, head_size),
        ),
    )
    return (query_grad.reshape(seq_len, head_count, head_size), key_grad, value_grad)


def gather_attention(qkv_weight, out_weight):
    return (
        lax.all_gather(qkv_weight, "fsdp", axis=0, tiled=True),
        lax.all_gather(out_weight, "fsdp", axis=0, tiled=True),
    )


def gather_feedforward(gate_up_weight, down_weight):
    return (
        lax.all_gather(gate_up_weight, "fsdp", axis=0, tiled=True),
        lax.all_gather(down_weight, "fsdp", axis=0, tiled=True),
    )


def per_device(
    block_in,
    out_cotangent,
    segment_ids,
    doc_positions,
    norm1_gain,
    qkv_weight,
    out_weight,
    norm2_gain,
    gate_up_weight,
    down_weight,
):
    micro_count = block_in.shape[0]
    fsdp_count = lax.axis_size("fsdp")
    segment_full, position_full = (
        lax.all_gather(segment_ids, "tp", axis=1, tiled=True),
        lax.all_gather(doc_positions, "tp", axis=1, tiled=True),
    )
    seq_len = segment_full.shape[1]
    block_rows = min(seq_len, 512)
    gain_one = norm1_gain.astype(jnp.float32)
    gain_two = norm2_gain.astype(jnp.float32)
    local_cols = qkv_weight.shape[2]
    local_units = gate_up_weight.shape[2]
    heads_local = local_cols // HD
    grad_qkv = jnp.zeros((D, 3, local_cols), jnp.float32)
    grad_out = jnp.zeros((out_weight.shape[0] * fsdp_count, D), jnp.float32)
    grad_gate_up = jnp.zeros((D, 2, local_units), jnp.float32)
    grad_down = jnp.zeros((down_weight.shape[0] * fsdp_count, D), jnp.float32)
    gain_one_acc = jnp.zeros((D,), jnp.float32)
    gain_two_acc = jnp.zeros((D,), jnp.float32)
    outputs = []
    input_grads = []
    for micro_index in range(micro_count):
        weights_fwd = (
            gather_attention(qkv_weight, out_weight),
            gather_feedforward(gate_up_weight, down_weight),
        )
        (qkv_full, out_full), (gate_up_full, down_full) = weights_fwd
        stream = block_in[micro_index].astype(jnp.float32)
        segment_row = segment_full[micro_index]
        cosine_part, sine_part = rope_tables(position_full[micro_index], HD)
        scale_one = rms_scale(stream)
        normed_one = (stream * scale_one * gain_one).astype(jnp.bfloat16)
        normed_one_full = lax.all_gather(normed_one, "tp", axis=0, tiled=True)
        projected = jnp.einsum(
            "sd,dtc->stc", normed_one_full, qkv_full, preferred_element_type=jnp.float32
        )
        queries = rotate(
            projected[:, 0].reshape(seq_len, heads_local, HD), cosine_part, sine_part
        ).astype(jnp.bfloat16)
        key_rows = rotate(
            projected[:, 1].reshape(seq_len, heads_local, HD), cosine_part, sine_part
        ).astype(jnp.bfloat16)
        value_rows = projected[:, 2].reshape(seq_len, heads_local, HD).astype(jnp.bfloat16)
        mixed, log_total = attention_forward(queries, key_rows, value_rows, segment_row, block_rows)
        attn_heads = mixed.astype(jnp.bfloat16)
        attn_term = jnp.dot(attn_heads, out_full, preferred_element_type=jnp.float32)
        attn_branch = lax.psum_scatter(attn_term, "tp", scatter_dimension=0, tiled=True)
        middle = stream + attn_branch
        scale_two = rms_scale(middle)
        normed_two = (middle * scale_two * gain_two).astype(jnp.bfloat16)
        normed_two_full = lax.all_gather(normed_two, "tp", axis=0, tiled=True)
        gate_up = jnp.einsum(
            "sd,dtf->stf", normed_two_full, gate_up_full, preferred_element_type=jnp.float32
        )
        gate_rows = gate_up[:, 0]
        up_rows = gate_up[:, 1]
        sigmoid_gate = jax.nn.sigmoid(gate_rows)
        silu_gate = gate_rows * sigmoid_gate
        activated = (silu_gate * up_rows).astype(jnp.bfloat16)
        mlp_term = jnp.dot(activated, down_full, preferred_element_type=jnp.float32)
        mlp_branch = lax.psum_scatter(
            mlp_term.astype(jnp.bfloat16), "tp", scatter_dimension=0, tiled=True
        ).astype(jnp.float32)
        outputs.append((middle + mlp_branch).astype(jnp.bfloat16))
        (qkv_back, out_back), (gate_up_back, down_back) = weights_fwd
        cotangent = out_cotangent[micro_index].astype(jnp.float32)
        cotangent_full = lax.all_gather(out_cotangent[micro_index], "tp", axis=0, tiled=True)
        grad_down = grad_down + jnp.einsum(
            "sf,sd->fd", activated, cotangent_full, preferred_element_type=jnp.float32
        )
        act_grad = jnp.einsum(
            "sd,fd->sf", cotangent_full, down_back, preferred_element_type=jnp.float32
        )
        gate_grad = act_grad * up_rows * sigmoid_gate * (1.0 + gate_rows * (1.0 - sigmoid_gate))
        up_grad = act_grad * silu_gate
        gate_up_grad = jnp.stack([gate_grad, up_grad], axis=1).astype(jnp.bfloat16)
        grad_gate_up = grad_gate_up + jnp.einsum(
            "sd,stf->dtf", normed_two_full, gate_up_grad, preferred_element_type=jnp.float32
        )
        normed_two_term = jnp.einsum(
            "stf,dtf->sd", gate_up_grad, gate_up_back, preferred_element_type=jnp.float32
        )
        normed_two_grad = lax.psum_scatter(normed_two_term, "tp", scatter_dimension=0, tiled=True)
        middle_back, gain_two_term = norm_back(middle, scale_two, gain_two, normed_two_grad)
        gain_two_acc = gain_two_acc + gain_two_term
        middle_grad = cotangent + middle_back
        attn_grad_full = lax.all_gather(middle_grad.astype(jnp.bfloat16), "tp", axis=0, tiled=True)
        grad_out = grad_out + jnp.einsum(
            "sc,sd->cd", attn_heads, attn_grad_full, preferred_element_type=jnp.float32
        )
        heads_grad = jnp.einsum(
            "sd,cd->sc", attn_grad_full, out_back, preferred_element_type=jnp.float32
        ).astype(jnp.bfloat16)
        query_grad, key_grad, value_grad = attention_backward(
            queries,
            key_rows,
            value_rows,
            segment_row,
            log_total,
            heads_grad.reshape(seq_len, heads_local, HD),
            block_rows,
        )
        projected_grad = jnp.stack(
            [
                unrotate(query_grad, cosine_part, sine_part).reshape(seq_len, local_cols),
                unrotate(key_grad, cosine_part, sine_part).reshape(seq_len, local_cols),
                value_grad.reshape(seq_len, local_cols),
            ],
            axis=1,
        ).astype(jnp.bfloat16)
        grad_qkv = grad_qkv + jnp.einsum(
            "sd,stc->dtc", normed_one_full, projected_grad, preferred_element_type=jnp.float32
        )
        normed_one_term = jnp.einsum(
            "stc,dtc->sd", projected_grad, qkv_back, preferred_element_type=jnp.float32
        )
        normed_one_grad = lax.psum_scatter(
            normed_one_term.astype(jnp.bfloat16), "tp", scatter_dimension=0, tiled=True
        ).astype(jnp.float32)
        stream_back, gain_one_term = norm_back(stream, scale_one, gain_one, normed_one_grad)
        gain_one_acc = gain_one_acc + gain_one_term
        input_grads.append(middle_grad + stream_back)
    owned_grads = (
        lax.psum_scatter(
            grad_qkv.astype(jnp.bfloat16), "fsdp", scatter_dimension=0, tiled=True
        ).astype(jnp.float32),
        lax.psum_scatter(
            grad_out.astype(jnp.bfloat16), "fsdp", scatter_dimension=0, tiled=True
        ).astype(jnp.float32),
        lax.psum_scatter(
            grad_gate_up.astype(jnp.bfloat16), "fsdp", scatter_dimension=0, tiled=True
        ).astype(jnp.float32),
        lax.psum_scatter(
            grad_down.astype(jnp.bfloat16), "fsdp", scatter_dimension=0, tiled=True
        ).astype(jnp.float32),
    )
    owned_gains = (
        lax.psum_scatter(gain_one_acc, ("fsdp", "tp"), scatter_dimension=0, tiled=True),
        lax.psum_scatter(gain_two_acc, ("fsdp", "tp"), scatter_dimension=0, tiled=True),
    )
    return (
        jnp.stack(outputs),
        jnp.stack(input_grads),
        owned_gains[0],
        owned_grads[0],
        owned_grads[1],
        owned_gains[1],
        owned_grads[2],
        owned_grads[3],
    )


HEAD_GROUP = 4
FIRST_DOC = 800


def dot_nt(left, right):
    return lax.dot_general(left, right, (((1,), (1,)), ((), ())), preferred_element_type=jnp.float32)


def dot_tn(left, right):
    return lax.dot_general(left, right, (((0,), (0,)), ((), ())), preferred_element_type=jnp.float32)


def dot_nn(left, right):
    return lax.dot_general(left, right, (((1,), (0,)), ((), ())), preferred_element_type=jnp.float32)


def swap_halves(values):
    lanes = lax.broadcasted_iota(jnp.int32, values.shape, 1)
    width = values.shape[1]
    return jnp.where(
        lanes % HD < HD // 2,
        pltpu.roll(values, width - HD // 2, 1),
        pltpu.roll(values, HD // 2, 1),
    )


def causal_mask(rows, columns):
    row_ids = lax.broadcasted_iota(jnp.int32, (rows, columns), 0)
    column_ids = lax.broadcasted_iota(jnp.int32, (rows, columns), 1)
    return row_ids >= column_ids


def tail_mask(reach):
    rows = reach.shape[0]
    row_ids = lax.broadcasted_iota(jnp.int32, (rows, rows), 0)
    column_ids = lax.broadcasted_iota(jnp.int32, (rows, rows), 1)
    return (row_ids >= column_ids) & (row_ids - column_ids <= reach)


def halves(quarter):
    first = lax.axis_index("tp") % 2
    return (
        pl.multiple_of(first * quarter, quarter),
        pl.multiple_of((1 - first) * quarter, quarter),
    )


def widen(table):
    return jnp.concatenate([table] * HEAD_GROUP, axis=1)


def load_rotated(offsets, quarter, q_ref, k_ref, v_ref, cos_ref, sin_ref, qr_ref, kr_ref, vr_ref):
    for place, offset in enumerate(offsets):
        rows = pl.ds(offset, quarter)
        target = pl.ds(place * quarter, quarter)
        cosine, sine = widen(cos_ref[rows, :]), widen(sin_ref[rows, :])
        q_raw, k_raw = q_ref[rows, :], k_ref[rows, :]
        qr_ref[target, :] = (q_raw * cosine + swap_halves(q_raw) * sine).astype(jnp.bfloat16)
        kr_ref[target, :] = (k_raw * cosine + swap_halves(k_raw) * sine).astype(jnp.bfloat16)
        vr_ref[target, :] = v_ref[rows, :].astype(jnp.bfloat16)


def softmax_mix(query, pieces, factor):
    scores = []
    for keys, _, mask in pieces:
        score = dot_nt(query, keys)
        scores.append(score if mask is None else jnp.where(mask, score, masked_score))
    top = functools.reduce(jnp.maximum, [jnp.max(s, axis=-1, keepdims=True) for s in scores])
    weights = [jnp.exp2((s - top) * factor) for s in scores]
    total = functools.reduce(jnp.add, [jnp.sum(w, axis=-1, keepdims=True) for w in weights])
    inverse = 1.0 / total
    mixed = functools.reduce(
        jnp.add,
        [dot_nn((w * inverse).astype(jnp.bfloat16), piece[1]) for w, piece in zip(weights, pieces)],
    )
    return mixed, top * factor + jnp.log2(total)


def head_slice(head):
    return slice(head * HD, (head + 1) * HD)


def forward_first(
    q_ref, k_ref, v_ref, cos_ref, sin_ref, qr_ref, kr_ref, vr_ref, o_ref, lse_ref
):
    half = q_ref.shape[0]
    quarter = half // 2
    offsets = halves(quarter)
    load_rotated(offsets, quarter, q_ref, k_ref, v_ref, cos_ref, sin_ref, qr_ref, kr_ref, vr_ref)
    factor = HD ** (-0.5) * LOG2E
    mask = causal_mask(quarter, quarter)
    for head in range(HEAD_GROUP):
        cols = head_slice(head)
        early, late = slice(0, quarter), slice(quarter, half)
        k_early, v_early = kr_ref[early, cols], vr_ref[early, cols]
        mixed, lse = softmax_mix(qr_ref[early, cols], [(k_early, v_early, mask)], factor)
        o_ref[pl.ds(offsets[0], quarter), cols] = mixed.astype(jnp.bfloat16)
        lse_ref[0, early, head : head + 1] = lse
        mixed, lse = softmax_mix(
            qr_ref[late, cols],
            [(k_early, v_early, None), (kr_ref[late, cols], vr_ref[late, cols], mask)],
            factor,
        )
        o_ref[pl.ds(offsets[1], quarter), cols] = mixed.astype(jnp.bfloat16)
        lse_ref[0, late, head : head + 1] = lse


def forward_second(
    q_ref, k_ref, v_ref, cos_ref, sin_ref, ka_ref, va_ref, pos_ref,
    qr_ref, kr_ref, vr_ref, o_ref, lse_ref,
):
    half = q_ref.shape[0]
    quarter = half // 2
    cut = FIRST_DOC - half
    spill = cut - quarter
    offsets = halves(quarter)
    load_rotated(offsets, quarter, q_ref, k_ref, v_ref, cos_ref, sin_ref, qr_ref, kr_ref, vr_ref)
    factor = HD ** (-0.5) * LOG2E
    mask = causal_mask(cut, cut)
    mask_tail = tail_mask(pos_ref[pl.ds(offsets[1] + spill, half - cut), :])
    for head in range(HEAD_GROUP):
        cols = head_slice(head)
        early, late = slice(0, cut), slice(cut, half)
        mixed, lse = softmax_mix(
            qr_ref[early, cols],
            [
                (ka_ref[:, cols], va_ref[:, cols], None),
                (kr_ref[early, cols], vr_ref[early, cols], mask),
            ],
            factor,
        )
        low = mixed.astype(jnp.bfloat16)
        o_ref[pl.ds(offsets[0], quarter), cols] = low[:quarter]
        o_ref[pl.ds(offsets[1], spill), cols] = low[quarter:]
        lse_ref[0, early, head : head + 1] = lse
        mixed, lse = softmax_mix(
            qr_ref[late, cols], [(kr_ref[late, cols], vr_ref[late, cols], mask_tail)], factor
        )
        o_ref[pl.ds(offsets[1] + spill, half - cut), cols] = mixed.astype(jnp.bfloat16)
        lse_ref[0, late, head : head + 1] = lse


def backward_both(
    qa_ref, ka_ref, va_ref, qb_ref, kb_ref, vb_ref, ga_ref, gb_ref, la_ref, lb_ref,
    cosa_ref, sina_ref, cosb_ref, sinb_ref, pos_ref,
    dqa_ref, dka_ref, dva_ref, dqb_ref, dkb_ref, dvb_ref,
    go_a, go_b, tqa, tka, tva, tqb, tkb, tvb,
):
    half = qa_ref.shape[0]
    quarter = half // 2
    cut = FIRST_DOC - half
    spill = cut - quarter
    offsets = halves(quarter)
    scale_value = HD ** (-0.5)
    factor = scale_value * LOG2E
    for place, offset in enumerate(offsets):
        target, rows = pl.ds(place * quarter, quarter), pl.ds(offset, quarter)
        go_a[target, :] = ga_ref[rows, :]
        go_b[target, :] = gb_ref[rows, :]
    mask = causal_mask(quarter, quarter)
    mask_cut = causal_mask(cut, cut)
    mask_tail = tail_mask(pos_ref[pl.ds(offsets[1] + spill, half - cut), :])
    for accumulator in (tka, tva, tkb, tvb):
        accumulator[...] = jnp.zeros_like(accumulator)

    def attend(query, grad, lse, pieces):
        weights, weight_grads = [], []
        for k_ref, v_ref, rows, cols, mask, _, _ in pieces:
            weight = jnp.exp2(dot_nt(query, k_ref[rows, cols]) * factor - lse)
            weights.append(weight if mask is None else jnp.where(mask, weight, 0.0))
            weight_grads.append(dot_nt(grad, v_ref[rows, cols]))
        shared = functools.reduce(
            jnp.add,
            [jnp.sum(w * g, axis=-1, keepdims=True) for w, g in zip(weights, weight_grads)],
        )
        query_grad = None
        for weight, weight_grad, piece in zip(weights, weight_grads, pieces):
            k_ref, v_ref, rows, cols, _, tk, tv = piece
            score_grad = (weight * (weight_grad - shared)).astype(jnp.bfloat16)
            term = dot_nn(score_grad, k_ref[rows, cols])
            query_grad = term if query_grad is None else query_grad + term
            tk[rows, cols] += dot_tn(score_grad, query)
            tv[rows, cols] += dot_tn(weight.astype(jnp.bfloat16), grad)
        return query_grad

    for head in range(HEAD_GROUP):
        cols = head_slice(head)
        lane = slice(head, head + 1)
        early, late, whole = slice(0, quarter), slice(quarter, half), slice(0, half)
        tqa[early, cols] = attend(
            qa_ref[early, cols], go_a[early, cols], la_ref[0, early, lane],
            [(ka_ref, va_ref, early, cols, mask, tka, tva)],
        )
        tqa[late, cols] = attend(
            qa_ref[late, cols], go_a[late, cols], la_ref[0, late, lane],
            [
                (ka_ref, va_ref, early, cols, None, tka, tva),
                (ka_ref, va_ref, late, cols, mask, tka, tva),
            ],
        )
        early, late = slice(0, cut), slice(cut, half)
        tqb[early, cols] = attend(
            qb_ref[early, cols], go_b[early, cols], lb_ref[0, early, lane],
            [
                (ka_ref, va_ref, whole, cols, None, tka, tva),
                (kb_ref, vb_ref, early, cols, mask_cut, tkb, tvb),
            ],
        )
        tqb[late, cols] = attend(
            qb_ref[late, cols], go_b[late, cols], lb_ref[0, late, lane],
            [(kb_ref, vb_ref, late, cols, mask_tail, tkb, tvb)],
        )
    for place, offset in enumerate(offsets):
        source, rows = pl.ds(place * quarter, quarter), pl.ds(offset, quarter)
        for total, cos_ref, sin_ref, out_ref in (
            (tqa, cosa_ref, sina_ref, dqa_ref),
            (tka, cosa_ref, sina_ref, dka_ref),
            (tqb, cosb_ref, sinb_ref, dqb_ref),
            (tkb, cosb_ref, sinb_ref, dkb_ref),
        ):
            grad = total[source, :] * scale_value
            out_ref[rows, :] = (
                grad * widen(cos_ref[rows, :]) - swap_halves(grad) * widen(sin_ref[rows, :])
            ).astype(jnp.bfloat16)
        dva_ref[rows, :] = tva[source, :].astype(jnp.bfloat16)
        dvb_ref[rows, :] = tvb[source, :].astype(jnp.bfloat16)


COST_SCALE = 1.7


def cost_of(flops):
    return pl.CostEstimate(flops=int(COST_SCALE * flops), bytes_accessed=1000, transcendentals=0)


def rows_kernel(pairs, extra_count, dot, chunk, finish, *refs):
    lefts, weights = refs[:pairs], refs[pairs : 2 * pairs]
    extras = refs[2 * pairs : 2 * pairs + extra_count]
    outs = refs[2 * pairs + extra_count :]

    @pl.loop(0, outs[0].shape[0] // chunk)
    def _(step):
        rows = pl.ds(pl.multiple_of(step * chunk, chunk), chunk)
        total = None
        for left, weight in zip(lefts, weights):
            term = dot(left[rows, :], weight[...])
            total = term if total is None else total + term
        for out, value in zip(outs, finish(total, *[extra[rows, :] for extra in extras])):
            out[rows, :] = value.astype(out.dtype)


def keep_one(total):
    return (total,)


def rows_matmul(
    lefts, weights, dot, types, tile, chunk=1024, finish=keep_one, extras=(), pushes=()
):
    rows = lefts[0].shape[0]
    if dot is dot_nn:
        width = weights[0].shape[1]
        weight_specs = [pl.BlockSpec((w.shape[0], tile), lambda j: (0, j)) for w in weights]
    else:
        width = weights[0].shape[0]
        weight_specs = [pl.BlockSpec((tile, w.shape[1]), lambda j: (j, 0)) for w in weights]
    column = pl.BlockSpec((rows, tile), lambda j: (0, j))
    return grid_call(
        functools.partial(rows_kernel, len(lefts), len(extras), dot, min(chunk, rows), finish),
        [*lefts, *weights, *extras],
        [pl.BlockSpec(left.shape, lambda j: (0, 0)) for left in lefts]
        + weight_specs
        + [column] * len(extras),
        [jax.ShapeDtypeStruct((rows, width), kind) for kind in types],
        [column] * len(types),
        (width // tile,),
        2 * rows * width * sum(left.shape[1] for left in lefts),
        pushes=pushes,
    )


def sum_kernel(parts, chunk, *refs):
    lefts, rights, out = refs[:parts], refs[parts : 2 * parts], refs[-1]

    @pl.loop(0, out.shape[1] // chunk)
    def _(step):
        cols = pl.ds(pl.multiple_of(step * chunk, chunk), chunk)
        total = None
        for left, right in zip(lefts, rights):
            term = dot_tn(left[...], right[:, cols])
            total = term if total is None else total + term
        out[:, cols] = total.astype(out.dtype)


def sum_matmul(lefts, rights, tile, chunk, pushes=()):
    rows, height = lefts[0].shape
    width = rights[0].shape[1]
    return grid_call(
        functools.partial(sum_kernel, len(lefts), chunk),
        [*lefts, *rights],
        [pl.BlockSpec((rows, tile), lambda j: (0, j)) for _ in lefts]
        + [pl.BlockSpec((rows, width), lambda j: (0, 0)) for _ in rights],
        [jax.ShapeDtypeStruct((height, width), jnp.bfloat16)],
        [pl.BlockSpec((tile, width), lambda j: (j, 0))],
        (height // tile,),
        2 * rows * height * width * len(lefts),
        pushes=pushes,
    )


def partner_of(kind):
    index, place = lax.axis_index("fsdp"), lax.axis_index("tp")
    if kind == "near":
        return (index, place + 1 - 2 * (place % 2))
    if kind == "core":
        return sibling_id()
    return (index, place + 2 - 4 * (place // 2))


def start_pushes(kinds, sources, targets, send, receive):
    barrier = pltpu.get_barrier_semaphore()
    names = sorted(set(kinds))
    for kind in names:
        pl.semaphore_signal(
            barrier, inc=1, device_id=partner_of(kind), device_id_type=pl.DeviceIdType.MESH
        )
    pl.semaphore_wait(barrier, len(names))
    for place, kind in enumerate(kinds):
        push(
            sources[place], targets[place], send.at[place], receive.at[place], partner_of(kind)
        ).start()


def wait_pushes(kinds, sources, targets, send, receive):
    for place, kind in enumerate(kinds):
        push(
            sources[place], targets[place], send.at[place], receive.at[place], partner_of(kind)
        ).wait()


def pushing_kernel(kernel, axes, in_count, out_count, kinds, *refs):
    count = len(kinds)
    inputs, sources = refs[:in_count], refs[in_count : in_count + count]
    outs = refs[in_count + count : in_count + count + out_count]
    targets = refs[in_count + count + out_count : in_count + 2 * count + out_count]
    scratch, (send, receive) = refs[in_count + 2 * count + out_count : -2], refs[-2:]
    first = functools.reduce(jnp.logical_and, [pl.program_id(axis) == 0 for axis in range(axes)])
    last = functools.reduce(
        jnp.logical_and,
        [pl.program_id(axis) == pl.num_programs(axis) - 1 for axis in range(axes)],
    )

    @pl.when(first)
    def _():
        start_pushes(kinds, sources, targets, send, receive)

    kernel(*inputs, *outs, *scratch)

    @pl.when(last)
    def _():
        wait_pushes(kinds, sources, targets, send, receive)


def grid_call(
    kernel, operands, in_specs, outs, out_specs, grid, flops, scratch=(), pushes=(), vmem=60
):
    params = dict(
        dimension_semantics=("arbitrary",) * len(grid), vmem_limit_bytes=vmem * 1024 * 1024
    )
    operands, in_specs, outs = list(operands), list(in_specs), list(outs)
    out_specs, scratch = list(out_specs), list(scratch)
    if pushes:
        kinds = tuple(kind for kind, _ in pushes)
        kernel = functools.partial(
            pushing_kernel, kernel, len(grid), len(operands), len(outs), kinds
        )
        anywhere = [pl.BlockSpec(memory_space=pl.ANY)] * len(pushes)
        operands += [value for _, value in pushes]
        in_specs += anywhere
        outs += [jax.ShapeDtypeStruct(value.shape, value.dtype) for _, value in pushes]
        out_specs += anywhere
        scratch += [pltpu.SemaphoreType.DMA((len(pushes),))] * 2
        next_key[0] += 1
        params.update(collective_id=next_key[0], has_side_effects=True)
    return tuple(
        pl.pallas_call(
            kernel,
            out_shape=outs,
            grid=grid,
            in_specs=in_specs,
            out_specs=out_specs,
            scratch_shapes=scratch,
            compiler_params=pltpu.CompilerParams(**params),
            cost_estimate=cost_of(max(flops, 27 * 10**9) if pushes else flops),
        )(*operands)
    )


def swap_kernel(kinds, *refs):
    count = len(kinds)
    sources, targets, (send, receive) = refs[:count], refs[count : 2 * count], refs[2 * count :]
    start_pushes(kinds, sources, targets, send, receive)
    wait_pushes(kinds, sources, targets, send, receive)


def swap_call(*pushes):
    next_key[0] += 1
    kinds = tuple(kind for kind, _ in pushes)
    values = [value for _, value in pushes]
    return exchange_call(
        functools.partial(swap_kernel, kinds), next_key[0], values,
        [jax.ShapeDtypeStruct(value.shape, value.dtype) for value in values],
        [pltpu.SemaphoreType.DMA((len(pushes),))] * 2, flops=130 * 10**9,
    )


next_key = [11]


def sibling_id():
    index = lax.axis_index("fsdp")
    return (index + 1 - 2 * (index % 2), lax.axis_index("tp"))


def meet(partner):
    barrier = pltpu.get_barrier_semaphore()
    pl.semaphore_signal(barrier, inc=1, device_id=partner, device_id_type=pl.DeviceIdType.MESH)
    pl.semaphore_wait(barrier, 1)


def push(source, target, send, receive, partner):
    return pltpu.make_async_remote_copy(
        src_ref=source,
        dst_ref=target,
        send_sem=send,
        recv_sem=receive,
        device_id=partner,
        device_id_type=pl.DeviceIdType.MESH,
    )


def exchange_call(kernel, key, operands, outs, scratch, vmem=60, flops=4 * 10**9):
    anywhere = pl.BlockSpec(memory_space=pl.ANY)
    results = pl.pallas_call(
        kernel,
        out_shape=outs,
        in_specs=[anywhere] * len(operands),
        out_specs=[anywhere] * len(outs),
        scratch_shapes=scratch,
        compiler_params=pltpu.CompilerParams(
            collective_id=key, has_side_effects=True, vmem_limit_bytes=vmem * 1024 * 1024
        ),
        cost_estimate=cost_of(flops),
    )(*operands)
    return tuple(results) if len(outs) > 1 else results[0]


def relay(sources, targets, buffer, load, store):
    loads, stores = [], []
    for place, source in enumerate(sources):
        copy = pltpu.make_async_copy(source, buffer.at[place], load.at[place])
        copy.start()
        loads.append(copy)
    for place, target in enumerate(targets):
        loads[place].wait()
        copy = pltpu.make_async_copy(buffer.at[place], target, store.at[place])
        copy.start()
        stores.append(copy)
    for copy in stores:
        copy.wait()


def gather_kernel(own_ref, near_ref, full_ref, buffer, load, store, send, receive):
    partner = sibling_id()
    meet(partner)
    count = own_ref.shape[0]
    remotes = []
    for place, ref in enumerate((own_ref, near_ref)):
        remote = push(
            ref, full_ref.at[pl.ds((2 + place) * count, count)],
            send.at[place], receive.at[place], partner,
        )
        remote.start()
        remotes.append(remote)
    targets = [full_ref.at[pl.ds(place * count, count)] for place in range(2)]
    relay((own_ref, near_ref), targets, buffer, load, store)
    for remote in remotes:
        remote.wait()


def core_gather(own, near):
    shape = (4 * own.shape[0], own.shape[1])
    return exchange_call(
        gather_kernel, 1, [own, near], [jax.ShapeDtypeStruct(shape, own.dtype)],
        [pltpu.VMEM((2, *own.shape), own.dtype)] + [pltpu.SemaphoreType.DMA((2,))] * 4,
    )


def gather_two_kernel(
    own_ref, own_near_ref, got_ref, got_near_ref, first_ref, second_ref,
    buffer, load, store, send, receive,
):
    partner = sibling_id()
    far = lax.axis_index("tp") // 2
    meet(partner)
    count = own_ref.shape[0]

    def run(targets):
        sources = (own_ref, own_near_ref, got_ref, got_near_ref)
        remotes, places = [], []
        for place, ref in enumerate(sources):
            target, row = targets[place // 2], place % 2
            remote = push(
                ref, target.at[pl.ds((2 + row) * count, count)],
                send.at[place], receive.at[place], partner,
            )
            remote.start()
            remotes.append(remote)
            places.append(target.at[pl.ds(row * count, count)])
        relay(sources, places, buffer, load, store)
        for remote in remotes:
            remote.wait()

    @pl.when(far == 0)
    def _():
        run((first_ref, second_ref))

    @pl.when(far != 0)
    def _():
        run((second_ref, first_ref))


def core_gather_two(own, own_near, got, got_near):
    shape = (4 * own.shape[0], own.shape[1])
    return exchange_call(
        gather_two_kernel, 11, [own, own_near, got, got_near],
        [jax.ShapeDtypeStruct(shape, own.dtype)] * 2,
        [pltpu.VMEM((4, *own.shape), own.dtype)] + [pltpu.SemaphoreType.DMA((4,))] * 4,
    )


def reduce_kernel(term_ref, keep_ref, away_ref, mine, got, keep, away, local, send, receive, store):
    partner = sibling_id()
    meet(partner)
    pieces, count = mine.shape[0], mine.shape[1]
    half = pieces * count
    remotes, loads = [], []
    for piece in range(pieces):
        order = (piece + pieces // 2) % pieces
        remote = push(
            term_ref.at[pl.ds(half + order * count, count)], got.at[order],
            send.at[order], receive.at[order], partner,
        )
        remote.start()
        remotes.append(remote)
        load = pltpu.make_async_copy(
            term_ref.at[pl.ds(order * count, count)], mine.at[order], local.at[order]
        )
        load.start()
        loads.append(load)
    stores = []
    for piece in range(pieces):
        order = (piece + pieces // 2) % pieces
        loads[piece].wait()
        remotes[piece].wait()
        total = mine[order].astype(jnp.float32) + got[order].astype(jnp.float32)
        if order < pieces // 2:
            keep[order] = total
            copy = pltpu.make_async_copy(
                keep.at[order], keep_ref.at[pl.ds(order * count, count)], store.at[order]
            )
        else:
            slot = order - pieces // 2
            away[slot] = total.astype(away.dtype)
            copy = pltpu.make_async_copy(
                away.at[slot], away_ref.at[pl.ds(slot * count, count)], store.at[order]
            )
        copy.start()
        stores.append(copy)
    for copy in stores:
        copy.wait()


def core_reduce(term):
    rows, width = term.shape
    quarter = rows // 4
    pieces = 4
    count = 2 * quarter // pieces
    return exchange_call(
        reduce_kernel, 2, [term],
        [
            jax.ShapeDtypeStruct((quarter, width), jnp.float32),
            jax.ShapeDtypeStruct((quarter, width), term.dtype),
        ],
        [
            pltpu.VMEM((pieces, count, width), term.dtype),
            pltpu.VMEM((pieces, count, width), term.dtype),
            pltpu.VMEM((pieces // 2, count, width), jnp.float32),
            pltpu.VMEM((pieces // 2, count, width), term.dtype),
        ]
        + [pltpu.SemaphoreType.DMA((pieces,))] * 4,
    )


def pair_kernel(own_ref, *refs):
    others, (pair_ref, buffer, load, store, send, receive) = refs[:-6], refs[-6:]
    partner = sibling_id()
    core = lax.axis_index("fsdp") % 2
    far = lax.axis_index("tp") // 2
    meet(partner)
    base = pl.multiple_of(core * own_ref.shape[0], own_ref.shape[0])
    count = others[0].shape[0]
    owns = [own_ref.at[pl.ds(place * count, count)] for place in range(len(others))]

    def run(mine, theirs):
        remotes, targets = [], []
        for place in range(len(others)):
            target = pair_ref.at[pl.ds(base + place * count, count)]
            remote = push(theirs[place], target, send.at[place], receive.at[place], partner)
            remote.start()
            remotes.append(remote)
            targets.append(target)
        relay(mine, targets, buffer, load, store)
        for remote in remotes:
            remote.wait()

    @pl.when(core == far)
    def _():
        run(owns, others)

    @pl.when(core != far)
    def _():
        run(others, owns)


def core_pair(key, own, *others):
    shape = (2 * own.shape[0], own.shape[1])
    return exchange_call(
        pair_kernel, key, [own, *others], [jax.ShapeDtypeStruct(shape, own.dtype)],
        [pltpu.VMEM((len(others), *others[0].shape), own.dtype)]
        + [pltpu.SemaphoreType.DMA((len(others),))] * 4,
    )


def split_kernel(pair_ref, keep_ref, away_ref, buffer, load, store, send, receive):
    partner = sibling_id()
    core = lax.axis_index("fsdp") % 2
    far = lax.axis_index("tp") // 2
    meet(partner)
    count = keep_ref.shape[0]
    mine = pair_ref.at[pl.ds(pl.multiple_of(core * count, count), count)]
    theirs = pair_ref.at[pl.ds(pl.multiple_of((1 - core) * count, count), count)]

    def run(own_target, other_target):
        remote = push(theirs, other_target, send.at[0], receive.at[0], partner)
        remote.start()
        relay((mine,), (own_target,), buffer, load, store)
        remote.wait()

    @pl.when(core == far)
    def _():
        run(keep_ref, keep_ref)

    @pl.when(core != far)
    def _():
        run(away_ref, away_ref)


def core_split(key, pair):
    shape = (pair.shape[0] // 2, pair.shape[1])
    return exchange_call(
        split_kernel, key, [pair], [jax.ShapeDtypeStruct(shape, pair.dtype)] * 2,
        [pltpu.VMEM((1, *shape), pair.dtype)] + [pltpu.SemaphoreType.DMA((1,))] * 4,
    )


def attention_call(kernel, arrays, kinds, outs, scratch, pushes=()):
    rows, heads_local = arrays[-1].shape[0], outs[1]
    half = rows // 2
    groups = heads_local // HEAD_GROUP
    width = HEAD_GROUP * HD

    def spec(kind):
        if kind == "table":
            return pl.BlockSpec((half, HD), lambda s, g: (s, 0))
        if kind == "column":
            return pl.BlockSpec((half, 1), lambda s, g: (s, 0))
        if kind == "lse":
            return pl.BlockSpec((1, half, HEAD_GROUP), lambda s, g: (g, s, 0))
        shift = kind * groups
        return pl.BlockSpec((half, width), lambda s, g: (s, shift + g))

    def shape(kind):
        if kind == "lse":
            return jax.ShapeDtypeStruct((groups, rows, HEAD_GROUP), jnp.float32)
        return jax.ShapeDtypeStruct((rows, heads_local * HD), jnp.bfloat16)

    return grid_call(
        kernel,
        arrays,
        [spec(kind) for kind in kinds],
        [shape(kind) for kind in outs[0]],
        [spec(kind) for kind in outs[0]],
        (rows // half, groups),
        4 * len(outs[0]) ** 2 * rows * rows * heads_local * HD // 16,
        scratch=scratch(half, width),
        pushes=pushes,
    )


def backward_scratch(half, width):
    return [pltpu.VMEM((half, width), jnp.bfloat16)] * 2 + [
        pltpu.VMEM((half, width), jnp.float32)
    ] * 6


def no_scratch(half, width):
    return []


def head_tables(positions):
    half_width = HD // 2
    frequency = rope_theta ** (-(jnp.arange(half_width, dtype=jnp.float32) * 2.0 / HD))
    angles = positions.astype(jnp.float32)[:, None] * frequency[None, :]
    cosine, sine = jnp.cos(angles), jnp.sin(angles)
    return (
        jnp.concatenate([cosine, cosine], axis=-1),
        jnp.concatenate([-sine, sine], axis=-1),
    )


def paired_device(
    block_in,
    out_cotangent,
    segment_ids,
    doc_positions,
    norm1_gain,
    qkv_weight,
    out_weight,
    norm2_gain,
    gate_up_weight,
    down_weight,
):
    fsdp_count, tp_count = lax.axis_size("fsdp"), lax.axis_size("tp")
    core = lax.axis_index("fsdp") % 2
    lane_z = lax.axis_index("tp")
    near, far = lane_z % 2, lane_z // 2
    core_pairs = [(i, i ^ 1) for i in range(fsdp_count)]
    near_pairs = [(i, i ^ 1) for i in range(tp_count)]
    far_pairs = [(i, i ^ 2) for i in range(tp_count)]
    plane_groups = [list(range(first, fsdp_count, 2)) for first in range(2)]
    rows = block_in.shape[1]
    local_cols = qkv_weight.shape[2]
    heads_local = local_cols // HD
    gain_one = norm1_gain.astype(jnp.float32)
    gain_two = norm2_gain.astype(jnp.float32)

    def swap_core(value):
        return lax.ppermute(value, "fsdp", core_pairs)

    def swap_near(value):
        return lax.ppermute(value, "tp", near_pairs)

    def swap_far(value):
        return lax.ppermute(value, "tp", far_pairs)

    def pick_tile(size):
        return 512 if size % 512 == 0 else 768

    tokens = []

    def act(work, *inputs, sends=()):
        values = [*inputs, *[value for _, value in sends]]
        held = lax.optimization_barrier((*values, *tokens))[: len(values)]
        if sends:
            kinds = [kind for kind, _ in sends]
            result = work(*held[: len(inputs)], pushes=list(zip(kinds, held[len(inputs) :])))
        else:
            result = work(*held)
        tokens[:] = result if isinstance(result, tuple) else (result,)
        return result[0] if isinstance(result, tuple) and len(result) == 1 else result

    def swap(*sends):
        return act(lambda pushes: swap_call(*pushes), sends=sends)

    def pick(value, index):
        return lax.dynamic_index_in_dim(value, index, 0, keepdims=False)

    def place_tokens(value, got):
        keep = pick(value, far)
        return jnp.where(far == 0, keep, got), jnp.where(far == 0, got, keep)

    def join(left, right):
        return jnp.concatenate([left, right], axis=0)

    def plane_gather(pair):
        return lax.all_gather(pair, "fsdp", axis=0, tiled=True, axis_index_groups=plane_groups)

    def plane_scatter(grad):
        return lax.psum_scatter(
            grad, "fsdp", scatter_dimension=0, tiled=True, axis_index_groups=plane_groups
        )

    def gather_weight(key, local, *others):
        return plane_gather(act(lambda own, *got: core_pair(key, own, *got), local, *others))

    def halve(value):
        count = value.shape[0] // 2
        return value[:count], value[count:]

    def add_wide(left, right):
        return left.astype(jnp.float32) + right.astype(jnp.float32)

    def chained(value, *others):
        return lax.optimization_barrier((value, *others))[0]

    def scatter_gains(gains):
        for axis, size in (("fsdp", fsdp_count), ("tp", tp_count)):
            index = lax.axis_index(axis)
            step = size // 2
            while step >= 1:
                bit = (index // step) % 2
                parts = gains.reshape(gains.shape[0], 2, gains.shape[1] // 2)
                sent = lax.dynamic_index_in_dim(parts, 1 - bit, 1, keepdims=False)
                kept = lax.dynamic_index_in_dim(parts, bit, 1, keepdims=False)
                gains = kept + lax.ppermute(sent, axis, [(i, i ^ step) for i in range(size)])
                step //= 2
        return gains

    def wide_dot(left, right, pushes=()):
        return rows_matmul(
            [left], [right], dot_nn, [jnp.float32], pick_tile(right.shape[1]), pushes=pushes
        )

    def dot_bf16(left, right, pushes=()):
        return rows_matmul(
            [left], [right], dot_nn, [jnp.bfloat16], pick_tile(right.shape[1]), pushes=pushes
        )

    def grad_sum(left, right, left_next, right_next, pushes=()):
        chunk = pick_tile(right.shape[1])
        return sum_matmul(
            [left, left_next], [right, right_next], pick_tile(left.shape[1]),
            2 * chunk if right.shape[1] % (2 * chunk) == 0 else chunk, pushes=pushes,
        )

    def heads_back(grad, weight, pushes=()):
        return rows_matmul(
            [grad], [weight], dot_nt, [jnp.bfloat16], pick_tile(weight.shape[0]), pushes=pushes
        )

    def rms_pack(stream, gain):
        scale = rms_scale(stream)
        return scale, (stream * scale * gain).astype(jnp.bfloat16)

    qkv_local = qkv_weight.reshape(qkv_weight.shape[0], 3 * local_cols)
    gate_local, up_local = gate_up_weight[:, 0], gate_up_weight[:, 1]

    next_key[0] = 11
    places = jnp.broadcast_to(doc_positions[:, None, :], (2, 8, rows))

    def first_norm(part):
        stream = part.astype(jnp.float32)
        return (stream, *rms_pack(stream, gain_one))

    s_own, r_own, n_own = act(lambda value: first_norm(pick(value, far)), block_in)
    near_own, qkv_other, place_got = swap(
        ("near", n_own), ("far", qkv_local), ("far", pick(places, 1 - far))
    )
    qkv_full = gather_weight(4, qkv_local, qkv_other)
    places = join(*place_tokens(places, place_got))

    def make_tables(own, other):
        order = join(own, other)[::8].reshape(2, 2, 2, rows)
        early, late = order[:, :, 0].reshape(-1), order[:, :, 1].reshape(-1)
        return (*head_tables(early), *head_tables(late), late[:, None])

    c_own = pick(out_cotangent, far)
    stream_got, c_near_own, out_other, near_places = swap(
        ("far", pick(block_in, 1 - far)), ("near", c_own), ("far", out_weight), ("near", places)
    )
    places = join(places, near_places)
    out_full = gather_weight(3, out_weight, out_other)
    s_got, r_got, n_got = act(first_norm, stream_got)
    near_got, gate_other, core_places = swap(
        ("near", n_got), ("far", gate_local), ("core", places)
    )
    gate_full = gather_weight(5, gate_local, gate_other)
    h1_first, h1_second = act(core_gather_two, n_own, near_own, n_got, near_got)
    streams = [jnp.where(far == 0, s_own, s_got), jnp.where(far == 0, s_got, s_own)]
    scales_one = [jnp.where(far == 0, r_own, r_got), jnp.where(far == 0, r_got, r_own)]

    def attend_first(projected, pushes=()):
        arrays = [projected, projected, projected, *tables[0]]
        return attention_call(
            forward_first, arrays, [0, 1, 2, "table", "table"],
            ([0, 0, 0, 0, "lse"], heads_local), no_scratch, pushes,
        )

    def attend_second(projected, pushes=()):
        arrays = [projected, projected, projected, *tables[1], saved[0][1], saved[0][2], reach]
        return attention_call(
            forward_second, arrays, [0, 1, 2, "table", "table", 0, 0, "column"],
            ([0, 0, 0, 0, "lse"], heads_local), no_scratch, pushes,
        )

    up_other = swap_far(chained(up_local, gate_other))
    cos_first, sin_first, cos_second, sin_second, reach = act(
        make_tables, places, core_places
    )
    tables = [(cos_first, sin_first), (cos_second, sin_second)]
    projected = act(wide_dot, h1_first, qkv_full)
    results = act(attend_first, projected)
    up_full = gather_weight(5, up_local, up_other)
    down_other = swap_far(chained(down_weight, up_other))
    saved, lses, mixed_first = [results[:3]], [results[4]], results[3]
    term_first = act(dot_bf16, mixed_first, out_full)
    keep_first, send_first = act(core_reduce, term_first)
    projected, branch_first = act(
        wide_dot, h1_second, qkv_full, sends=[("near", send_first)]
    )

    def second_norm(stream, keep, got):
        middle = stream + keep + got.astype(jnp.float32)
        return (middle, *rms_pack(middle, gain_two))

    m_first, q_first, n_first = act(second_norm, streams[0], keep_first, branch_first)
    *results, near_first = act(attend_second, projected, sends=[("near", n_first)])
    saved.append(results[:3])
    lses.append(results[4])
    mixed_second = results[3]
    term_second = act(dot_bf16, mixed_second, out_full)
    keep_second, send_second = act(core_reduce, term_second)
    h2_first = act(core_gather, n_first, near_first)
    down_full_pair = act(lambda own, got: core_pair(6, own, got), down_weight, down_other)
    down_full = plane_gather(down_full_pair)
    c_got = swap_far(chained(pick(out_cotangent, 1 - far), down_full_pair))

    gate_first, branch_second = act(
        wide_dot, h2_first, gate_full, sends=[("near", send_second)]
    )
    m_second, q_second, n_second = act(second_norm, streams[1], keep_second, branch_second)

    def rise(hidden, weight, gate, pushes=()):
        return rows_matmul(
            [hidden], [weight], dot_nn, [jnp.float32, jnp.bfloat16], pick_tile(weight.shape[1]),
            finish=lambda up, gate: (up, gate * jax.nn.sigmoid(gate) * up), extras=[gate],
            pushes=pushes,
        )

    up_first, a_first, near_second = act(
        rise, h2_first, up_full, gate_first, sends=[("near", n_second)]
    )
    h2_second = act(core_gather, n_second, near_second)
    gate_second, c_near_got = act(
        wide_dot, h2_second, gate_full, sends=[("near", c_got)]
    )
    y_first, y_second = act(core_gather_two, c_own, c_near_own, c_got, c_near_got)
    c_first, c_second = jnp.where(far == 0, c_own, c_got), jnp.where(far == 0, c_got, c_own)
    up_second, a_second = act(rise, h2_second, up_full, gate_second)
    down_sum = plane_scatter(act(grad_sum, a_first, y_first, a_second, y_second))

    def fall_finish(act_grad, gate, up):
        sigmoid_gate = jax.nn.sigmoid(gate)
        return (
            act_grad * up * sigmoid_gate * (1.0 + gate * (1.0 - sigmoid_gate)),
            act_grad * (gate * sigmoid_gate),
        )

    def fall(cotangent, weight, gate, up, pushes=()):
        return rows_matmul(
            [cotangent], [weight], dot_nt, [jnp.bfloat16] * 2, pick_tile(weight.shape[0]),
            chunk=512, finish=fall_finish, extras=[gate, up], pushes=pushes,
        )

    def hidden_grad(gate_grad, up_grad, gate_weight, up_weight, pushes=()):
        return rows_matmul(
            [gate_grad, up_grad], [gate_weight, up_weight], dot_nt, [jnp.bfloat16],
            pick_tile(gate_weight.shape[0]), pushes=pushes,
        )

    def second_back(middle, scale, keep, got, cotangent):
        grad, gain_term = norm_back(middle, scale, gain_two, keep + got.astype(jnp.float32))
        grad = cotangent.astype(jnp.float32) + grad
        return grad, grad.astype(jnp.bfloat16), gain_term

    dg_first, du_first = act(fall, y_first, down_full, gate_first, up_first)
    term_first = act(hidden_grad, dg_first, du_first, gate_full, up_full)
    keep_first, send_first = act(core_reduce, term_first)
    dg_second, du_second, back_first = act(
        fall, y_second, down_full, gate_second, up_second, sends=[("near", send_first)]
    )
    g_first, n_first, gain_two_first = act(
        second_back, m_first, q_first, keep_first, back_first, c_first
    )
    term_second, near_first = act(
        hidden_grad, dg_second, du_second, gate_full, up_full, sends=[("near", n_first)]
    )
    keep_second, send_second = act(core_reduce, term_second)
    d_first = act(core_gather, n_first, near_first)
    grad_gate, back_second = act(
        grad_sum, h2_first, dg_first, h2_second, dg_second, sends=[("near", send_second)]
    )
    gate_sum = plane_scatter(grad_gate)
    g_second, n_second, gain_two_second = act(
        second_back, m_second, q_second, keep_second, back_second, c_second
    )
    heads_first = act(heads_back, d_first, out_full)
    down_mine, down_away = act(lambda pair: core_split(10, pair), down_sum)
    down_got = swap_far(down_away)
    grad_up, near_second = act(
        grad_sum, h2_first, du_first, h2_second, du_second, sends=[("near", n_second)]
    )
    up_sum = plane_scatter(grad_up)

    d_second = act(core_gather, n_second, near_second)
    heads_second = act(heads_back, d_second, out_full)
    grad_out = act(grad_sum, mixed_first, d_first, mixed_second, d_second)
    out_sum = plane_scatter(grad_out)
    mlp_first = act(dot_bf16, a_first, down_full)
    mlp_keep_first, mlp_send_first = act(core_reduce, mlp_first)
    mlp_second = act(dot_bf16, a_second, down_full)
    mlp_keep_second, mlp_send_second = act(core_reduce, mlp_second)
    def attend_back(heads_first, heads_second, pushes=()):
        return attention_call(
            backward_both,
            [
                *saved[0], *saved[1], heads_first, heads_second, *lses,
                *tables[0], *tables[1], reach,
            ],
            [0] * 8 + ["lse"] * 2 + ["table"] * 4 + ["column"],
            ([0] * 6, heads_local),
            backward_scratch,
            pushes,
        )

    *grads, mlp_branch_first, mlp_branch_second = act(
        attend_back, heads_first, heads_second,
        sends=[("near", mlp_send_first), ("near", mlp_send_second)],
    )
    gate_mine, gate_away = act(lambda pair: core_split(9, pair), gate_sum)
    gate_got = swap_far(gate_away)
    p_first, p_second = act(
        lambda *parts: (
            jnp.concatenate(parts[:3], axis=1),
            jnp.concatenate(parts[3:], axis=1),
        ),
        *grads,
    )

    def finish_output(first, first_keep, first_got, second, second_keep, second_got):
        first = (first + first_keep + first_got.astype(jnp.float32)).astype(jnp.bfloat16)
        second = (second + second_keep + second_got.astype(jnp.float32)).astype(jnp.bfloat16)
        return jnp.where(far == 0, first, second), jnp.where(far == 0, second, first)

    grad_qkv = act(grad_sum, h1_first, p_first, h1_second, p_second)
    qkv_sum = plane_scatter(grad_qkv)
    out_keep, out_send = act(
        finish_output,
        m_first, mlp_keep_first, mlp_branch_first, m_second, mlp_keep_second, mlp_branch_second,
    )
    up_mine, up_away = act(lambda pair: core_split(9, pair), up_sum)
    up_got = swap_far(up_away)
    term_first = act(heads_back, p_first, qkv_full)
    keep_first, send_first = act(core_reduce, term_first)
    term_second, back_first = act(
        heads_back, p_second, qkv_full, sends=[("near", send_first)]
    )
    out_got = swap_far(chained(out_send, term_second))
    keep_second, send_second = act(core_reduce, term_second)
    out_mine, out_away = act(lambda pair: core_split(8, pair), out_sum)
    def settle(keep, got):
        return jnp.stack([jnp.where(far == 0, keep, got), jnp.where(far == 0, got, keep)])

    def first_back(stream, scale, keep, got, grad):
        back, gain_term = norm_back(stream, scale, gain_one, keep + got.astype(jnp.float32))
        return grad + back, gain_term

    def last_back(stream, scale, keep, got, grad, first):
        second, gain_term = first_back(stream, scale, keep, got, grad)
        return (
            jnp.where(far == 0, first, second),
            jnp.where(far == 0, second, first).astype(jnp.bfloat16),
            gain_term,
        )

    back_second, out_back = swap(("near", send_second), ("far", out_away))
    qkv_mine, qkv_away = act(lambda pair: core_split(0, pair), qkv_sum)
    qkv_back = swap_far(qkv_away)
    i_first, gain_one_first = act(
        first_back, streams[0], scales_one[0], keep_first, back_first, g_first
    )
    in_keep, in_send, gain_one_second = act(
        last_back, streams[1], scales_one[1], keep_second, back_second, g_second, i_first
    )
    in_got = swap_far(in_send)
    down_owned = act(add_wide, down_mine, down_got)
    gate_owned = act(add_wide, gate_mine, gate_got)
    block_out = act(settle, out_keep, out_got)
    up_owned = act(add_wide, up_mine, up_got)
    gate_up_owned = act(lambda a, b: jnp.stack([a, b], axis=1), gate_owned, up_owned)
    out_owned = act(add_wide, out_mine, out_back)
    gains = scatter_gains(
        jnp.stack([gain_one_first + gain_one_second, gain_two_first + gain_two_second])
    )
    in_grad = act(lambda keep, got: settle(keep, got.astype(jnp.float32)), in_keep, in_got)
    qkv_owned = act(add_wide, qkv_mine, qkv_back)
    return (
        block_out,
        in_grad,
        gains[0],
        qkv_owned.reshape(qkv_weight.shape),
        out_owned,
        gains[1],
        gate_up_owned,
        down_owned,
    )


def solution(mesh):
    sizes = (mesh.shape["fsdp"], mesh.shape["tp"])
    body = paired_device if sizes == (8, 4) else per_device
    in_specs = (
        P("fsdp", "tp", None),
        P("fsdp", "tp", None),
        P("fsdp", "tp"),
        P("fsdp", "tp"),
        P(),
        P("fsdp", None, "tp"),
        P(("tp", "fsdp"), None),
        P(),
        P("fsdp", None, "tp"),
        P(("tp", "fsdp"), None),
    )
    out_specs = (
        P("fsdp", "tp", None),
        P("fsdp", "tp", None),
        P(("fsdp", "tp")),
        P("fsdp", None, "tp"),
        P(("tp", "fsdp"), None),
        P(("fsdp", "tp")),
        P("fsdp", None, "tp"),
        P(("tp", "fsdp"), None),
    )
    return jax.shard_map(
        body, mesh=mesh, in_specs=in_specs, out_specs=out_specs, check_vma=False
    )
```

```python
import functools

import jax
import jax.numpy as jnp
from jax import lax
from jax.experimental import pallas as pl
from jax.experimental.pallas import tpu as pltpu
from jax.sharding import PartitionSpec as P

D = 3072
HD = 96


rms_epsilon = 1e-05
rope_theta = 10000.0
masked_score = -1e30
LOG2E = 1.4426950408889634


def rope_tables(positions, head_size):
    half_width = head_size // 2
    frequency = rope_theta ** (-(jnp.arange(half_width, dtype=jnp.float32) * 2.0 / head_size))
    angles = positions.astype(jnp.float32)[:, None] * frequency[None, :]
    return (jnp.cos(angles)[:, None, :], jnp.sin(angles)[:, None, :])


def rotate(values, cosine_part, sine_part):
    half_width = values.shape[-1] // 2
    lead_half = values[..., :half_width]
    tail_half = values[..., half_width:]
    return jnp.concatenate(
        [
            lead_half * cosine_part - tail_half * sine_part,
            tail_half * cosine_part + lead_half * sine_part,
        ],
        axis=-1,
    )


def unrotate(values, cosine_part, sine_part):
    half_width = values.shape[-1] // 2
    lead_half = values[..., :half_width]
    tail_half = values[..., half_width:]
    return jnp.concatenate(
        [
            lead_half * cosine_part + tail_half * sine_part,
            tail_half * cosine_part - lead_half * sine_part,
        ],
        axis=-1,
    )


def rms_scale(stream):
    return lax.rsqrt(jnp.mean(stream * stream, axis=-1, keepdims=True) + rms_epsilon)


def norm_back(stream, scale_rows, gain_vec, grad_rows):
    gained_grad = gain_vec * grad_rows
    input_grad = scale_rows * gained_grad - stream * scale_rows**3 * jnp.mean(
        gained_grad * stream, axis=-1, keepdims=True
    )
    return (input_grad, jnp.sum(grad_rows * stream * scale_rows, axis=0))


def allowed_mask(segment_tile, index_tile, segments):
    columns = jnp.arange(segments.shape[0], dtype=jnp.int32)
    return (segment_tile[:, None] == segments[None, :]) & (index_tile[:, None] >= columns[None, :])


def masked_scores(query_tile, key_rows, segment_tile, index_tile, segments, scale_value):
    scores = (
        jnp.einsum("qhd,khd->hqk", query_tile, key_rows, preferred_element_type=jnp.float32)
        * scale_value
    )
    return jnp.where(allowed_mask(segment_tile, index_tile, segments)[None], scores, masked_score)


def attention_forward(queries, key_rows, value_rows, segments, block_rows):
    seq_len, head_count, head_size = queries.shape
    tiles = seq_len // block_rows
    scale_value = head_size ** (-0.5)
    positions = jnp.arange(seq_len, dtype=jnp.int32)

    def query_block(packed):
        query_tile, segment_tile, index_tile = packed
        scores = masked_scores(
            query_tile, key_rows, segment_tile, index_tile, segments, scale_value
        )
        row_max = jnp.max(scores, axis=-1, keepdims=True)
        exponent = jnp.exp(scores - row_max)
        row_total = jnp.sum(exponent, axis=-1, keepdims=True)
        probs_low = (exponent / row_total).astype(jnp.bfloat16)
        mixed = jnp.einsum(
            "hqk,khd->qhd", probs_low, value_rows, preferred_element_type=jnp.float32
        )
        return (mixed, (row_max + jnp.log(row_total))[..., 0])

    mixed, log_total = lax.map(
        query_block,
        (
            queries.reshape(tiles, block_rows, head_count, head_size),
            segments.reshape(tiles, block_rows),
            positions.reshape(tiles, block_rows),
        ),
    )
    return (mixed.reshape(seq_len, head_count * head_size), log_total)


def attention_backward(queries, key_rows, value_rows, segments, log_total, out_grad, block_rows):
    seq_len, head_count, head_size = queries.shape
    tiles = seq_len // block_rows
    scale_value = head_size ** (-0.5)
    positions = jnp.arange(seq_len, dtype=jnp.int32)

    def query_block(carry, packed):
        key_acc, value_acc = carry
        query_tile, segment_tile, index_tile, total_tile, grad_tile = packed
        scores = masked_scores(
            query_tile, key_rows, segment_tile, index_tile, segments, scale_value
        )
        probs = jnp.exp(scores - total_tile[..., None])
        probs_low = probs.astype(jnp.bfloat16)
        prob_grad = jnp.einsum(
            "qhd,khd->hqk", grad_tile, value_rows, preferred_element_type=jnp.float32
        )
        score_grad = (
            probs * (prob_grad - jnp.sum(probs * prob_grad, axis=-1, keepdims=True))
        ).astype(jnp.bfloat16)
        query_grad = (
            jnp.einsum("hqk,khd->qhd", score_grad, key_rows, preferred_element_type=jnp.float32)
            * scale_value
        )
        key_acc = (
            key_acc
            + jnp.einsum("hqk,qhd->khd", score_grad, query_tile, preferred_element_type=jnp.float32)
            * scale_value
        )
        value_acc = value_acc + jnp.einsum(
            "hqk,qhd->khd", probs_low, grad_tile, preferred_element_type=jnp.float32
        )
        return ((key_acc, value_acc), query_grad)

    start_acc = (jnp.zeros(queries.shape, jnp.float32), jnp.zeros(queries.shape, jnp.float32))
    (key_grad, value_grad), query_grad = lax.scan(
        query_block,
        start_acc,
        (
            queries.reshape(tiles, block_rows, head_count, head_size),
            segments.reshape(tiles, block_rows),
            positions.reshape(tiles, block_rows),
            log_total,
            out_grad.reshape(tiles, block_rows, head_count, head_size),
        ),
    )
    return (query_grad.reshape(seq_len, head_count, head_size), key_grad, value_grad)


def gather_attention(qkv_weight, out_weight):
    return (
        lax.all_gather(qkv_weight, "fsdp", axis=0, tiled=True),
        lax.all_gather(out_weight, "fsdp", axis=0, tiled=True),
    )


def gather_feedforward(gate_up_weight, down_weight):
    return (
        lax.all_gather(gate_up_weight, "fsdp", axis=0, tiled=True),
        lax.all_gather(down_weight, "fsdp", axis=0, tiled=True),
    )


def per_device(
    block_in,
    out_cotangent,
    segment_ids,
    doc_positions,
    norm1_gain,
    qkv_weight,
    out_weight,
    norm2_gain,
    gate_up_weight,
    down_weight,
):
    micro_count = block_in.shape[0]
    fsdp_count = lax.axis_size("fsdp")
    segment_full, position_full = (
        lax.all_gather(segment_ids, "tp", axis=1, tiled=True),
        lax.all_gather(doc_positions, "tp", axis=1, tiled=True),
    )
    seq_len = segment_full.shape[1]
    block_rows = min(seq_len, 512)
    gain_one = norm1_gain.astype(jnp.float32)
    gain_two = norm2_gain.astype(jnp.float32)
    local_cols = qkv_weight.shape[2]
    local_units = gate_up_weight.shape[2]
    heads_local = local_cols // HD
    grad_qkv = jnp.zeros((D, 3, local_cols), jnp.float32)
    grad_out = jnp.zeros((out_weight.shape[0] * fsdp_count, D), jnp.float32)
    grad_gate_up = jnp.zeros((D, 2, local_units), jnp.float32)
    grad_down = jnp.zeros((down_weight.shape[0] * fsdp_count, D), jnp.float32)
    gain_one_acc = jnp.zeros((D,), jnp.float32)
    gain_two_acc = jnp.zeros((D,), jnp.float32)
    outputs = []
    input_grads = []
    for micro_index in range(micro_count):
        weights_fwd = (
            gather_attention(qkv_weight, out_weight),
            gather_feedforward(gate_up_weight, down_weight),
        )
        (qkv_full, out_full), (gate_up_full, down_full) = weights_fwd
        stream = block_in[micro_index].astype(jnp.float32)
        segment_row = segment_full[micro_index]
        cosine_part, sine_part = rope_tables(position_full[micro_index], HD)
        scale_one = rms_scale(stream)
        normed_one = (stream * scale_one * gain_one).astype(jnp.bfloat16)
        normed_one_full = lax.all_gather(normed_one, "tp", axis=0, tiled=True)
        projected = jnp.einsum(
            "sd,dtc->stc", normed_one_full, qkv_full, preferred_element_type=jnp.float32
        )
        queries = rotate(
            projected[:, 0].reshape(seq_len, heads_local, HD), cosine_part, sine_part
        ).astype(jnp.bfloat16)
        key_rows = rotate(
            projected[:, 1].reshape(seq_len, heads_local, HD), cosine_part, sine_part
        ).astype(jnp.bfloat16)
        value_rows = projected[:, 2].reshape(seq_len, heads_local, HD).astype(jnp.bfloat16)
        mixed, log_total = attention_forward(queries, key_rows, value_rows, segment_row, block_rows)
        attn_heads = mixed.astype(jnp.bfloat16)
        attn_term = jnp.dot(attn_heads, out_full, preferred_element_type=jnp.float32)
        attn_branch = lax.psum_scatter(attn_term, "tp", scatter_dimension=0, tiled=True)
        middle = stream + attn_branch
        scale_two = rms_scale(middle)
        normed_two = (middle * scale_two * gain_two).astype(jnp.bfloat16)
        normed_two_full = lax.all_gather(normed_two, "tp", axis=0, tiled=True)
        gate_up = jnp.einsum(
            "sd,dtf->stf", normed_two_full, gate_up_full, preferred_element_type=jnp.float32
        )
        gate_rows = gate_up[:, 0]
        up_rows = gate_up[:, 1]
        sigmoid_gate = jax.nn.sigmoid(gate_rows)
        silu_gate = gate_rows * sigmoid_gate
        activated = (silu_gate * up_rows).astype(jnp.bfloat16)
        mlp_term = jnp.dot(activated, down_full, preferred_element_type=jnp.float32)
        mlp_branch = lax.psum_scatter(
            mlp_term.astype(jnp.bfloat16), "tp", scatter_dimension=0, tiled=True
        ).astype(jnp.float32)
        outputs.append((middle + mlp_branch).astype(jnp.bfloat16))
        (qkv_back, out_back), (gate_up_back, down_back) = weights_fwd
        cotangent = out_cotangent[micro_index].astype(jnp.float32)
        cotangent_full = lax.all_gather(out_cotangent[micro_index], "tp", axis=0, tiled=True)
        grad_down = grad_down + jnp.einsum(
            "sf,sd->fd", activated, cotangent_full, preferred_element_type=jnp.float32
        )
        act_grad = jnp.einsum(
            "sd,fd->sf", cotangent_full, down_back, preferred_element_type=jnp.float32
        )
        gate_grad = act_grad * up_rows * sigmoid_gate * (1.0 + gate_rows * (1.0 - sigmoid_gate))
        up_grad = act_grad * silu_gate
        gate_up_grad = jnp.stack([gate_grad, up_grad], axis=1).astype(jnp.bfloat16)
        grad_gate_up = grad_gate_up + jnp.einsum(
            "sd,stf->dtf", normed_two_full, gate_up_grad, preferred_element_type=jnp.float32
        )
        normed_two_term = jnp.einsum(
            "stf,dtf->sd", gate_up_grad, gate_up_back, preferred_element_type=jnp.float32
        )
        normed_two_grad = lax.psum_scatter(normed_two_term, "tp", scatter_dimension=0, tiled=True)
        middle_back, gain_two_term = norm_back(middle, scale_two, gain_two, normed_two_grad)
        gain_two_acc = gain_two_acc + gain_two_term
        middle_grad = cotangent + middle_back
        attn_grad_full = lax.all_gather(middle_grad.astype(jnp.bfloat16), "tp", axis=0, tiled=True)
        grad_out = grad_out + jnp.einsum(
            "sc,sd->cd", attn_heads, attn_grad_full, preferred_element_type=jnp.float32
        )
        heads_grad = jnp.einsum(
            "sd,cd->sc", attn_grad_full, out_back, preferred_element_type=jnp.float32
        ).astype(jnp.bfloat16)
        query_grad, key_grad, value_grad = attention_backward(
            queries,
            key_rows,
            value_rows,
            segment_row,
            log_total,
            heads_grad.reshape(seq_len, heads_local, HD),
            block_rows,
        )
        projected_grad = jnp.stack(
            [
                unrotate(query_grad, cosine_part, sine_part).reshape(seq_len, local_cols),
                unrotate(key_grad, cosine_part, sine_part).reshape(seq_len, local_cols),
                value_grad.reshape(seq_len, local_cols),
            ],
            axis=1,
        ).astype(jnp.bfloat16)
        grad_qkv = grad_qkv + jnp.einsum(
            "sd,stc->dtc", normed_one_full, projected_grad, preferred_element_type=jnp.float32
        )
        normed_one_term = jnp.einsum(
            "stc,dtc->sd", projected_grad, qkv_back, preferred_element_type=jnp.float32
        )
        normed_one_grad = lax.psum_scatter(
            normed_one_term.astype(jnp.bfloat16), "tp", scatter_dimension=0, tiled=True
        ).astype(jnp.float32)
        stream_back, gain_one_term = norm_back(stream, scale_one, gain_one, normed_one_grad)
        gain_one_acc = gain_one_acc + gain_one_term
        input_grads.append(middle_grad + stream_back)
    owned_grads = (
        lax.psum_scatter(
            grad_qkv.astype(jnp.bfloat16), "fsdp", scatter_dimension=0, tiled=True
        ).astype(jnp.float32),
        lax.psum_scatter(
            grad_out.astype(jnp.bfloat16), "fsdp", scatter_dimension=0, tiled=True
        ).astype(jnp.float32),
        lax.psum_scatter(
            grad_gate_up.astype(jnp.bfloat16), "fsdp", scatter_dimension=0, tiled=True
        ).astype(jnp.float32),
        lax.psum_scatter(
            grad_down.astype(jnp.bfloat16), "fsdp", scatter_dimension=0, tiled=True
        ).astype(jnp.float32),
    )
    owned_gains = (
        lax.psum_scatter(gain_one_acc, ("fsdp", "tp"), scatter_dimension=0, tiled=True),
        lax.psum_scatter(gain_two_acc, ("fsdp", "tp"), scatter_dimension=0, tiled=True),
    )
    return (
        jnp.stack(outputs),
        jnp.stack(input_grads),
        owned_gains[0],
        owned_grads[0],
        owned_grads[1],
        owned_gains[1],
        owned_grads[2],
        owned_grads[3],
    )


HEAD_GROUP = 4
FIRST_DOC = 800


def dot_nt(left, right):
    return lax.dot_general(left, right, (((1,), (1,)), ((), ())), preferred_element_type=jnp.float32)


def dot_tn(left, right):
    return lax.dot_general(left, right, (((0,), (0,)), ((), ())), preferred_element_type=jnp.float32)


def dot_nn(left, right):
    return lax.dot_general(left, right, (((1,), (0,)), ((), ())), preferred_element_type=jnp.float32)


def swap_halves(values):
    lanes = lax.broadcasted_iota(jnp.int32, values.shape, 1)
    width = values.shape[1]
    return jnp.where(
        lanes % HD < HD // 2,
        pltpu.roll(values, width - HD // 2, 1),
        pltpu.roll(values, HD // 2, 1),
    )


def causal_mask(rows, columns):
    row_ids = lax.broadcasted_iota(jnp.int32, (rows, columns), 0)
    column_ids = lax.broadcasted_iota(jnp.int32, (rows, columns), 1)
    return row_ids >= column_ids


def tail_mask(reach):
    rows = reach.shape[0]
    row_ids = lax.broadcasted_iota(jnp.int32, (rows, rows), 0)
    column_ids = lax.broadcasted_iota(jnp.int32, (rows, rows), 1)
    return (row_ids >= column_ids) & (row_ids - column_ids <= reach)


def halves(quarter):
    first = lax.axis_index("tp") % 2
    return (
        pl.multiple_of(first * quarter, quarter),
        pl.multiple_of((1 - first) * quarter, quarter),
    )


def widen(table):
    return jnp.concatenate([table] * HEAD_GROUP, axis=1)


def load_rotated(offsets, quarter, q_ref, k_ref, v_ref, cos_ref, sin_ref, qr_ref, kr_ref, vr_ref):
    for place, offset in enumerate(offsets):
        rows = pl.ds(offset, quarter)
        target = pl.ds(place * quarter, quarter)
        cosine, sine = widen(cos_ref[rows, :]), widen(sin_ref[rows, :])
        q_raw, k_raw = q_ref[rows, :], k_ref[rows, :]
        qr_ref[target, :] = (q_raw * cosine + swap_halves(q_raw) * sine).astype(jnp.bfloat16)
        kr_ref[target, :] = (k_raw * cosine + swap_halves(k_raw) * sine).astype(jnp.bfloat16)
        vr_ref[target, :] = v_ref[rows, :].astype(jnp.bfloat16)


def softmax_mix(query, pieces, factor):
    scores = []
    for keys, _, mask in pieces:
        score = dot_nt(query, keys)
        scores.append(score if mask is None else jnp.where(mask, score, masked_score))
    top = functools.reduce(jnp.maximum, [jnp.max(s, axis=-1, keepdims=True) for s in scores])
    weights = [jnp.exp2((s - top) * factor) for s in scores]
    total = functools.reduce(jnp.add, [jnp.sum(w, axis=-1, keepdims=True) for w in weights])
    inverse = 1.0 / total
    mixed = functools.reduce(
        jnp.add,
        [dot_nn((w * inverse).astype(jnp.bfloat16), piece[1]) for w, piece in zip(weights, pieces)],
    )
    return mixed, top * factor + jnp.log2(total)


def head_slice(head):
    return slice(head * HD, (head + 1) * HD)


def forward_first(
    q_ref, k_ref, v_ref, cos_ref, sin_ref, qr_ref, kr_ref, vr_ref, o_ref, lse_ref
):
    half = q_ref.shape[0]
    quarter = half // 2
    offsets = halves(quarter)
    load_rotated(offsets, quarter, q_ref, k_ref, v_ref, cos_ref, sin_ref, qr_ref, kr_ref, vr_ref)
    factor = HD ** (-0.5) * LOG2E
    mask = causal_mask(quarter, quarter)
    for head in range(HEAD_GROUP):
        cols = head_slice(head)
        early, late = slice(0, quarter), slice(quarter, half)
        k_early, v_early = kr_ref[early, cols], vr_ref[early, cols]
        mixed, lse = softmax_mix(qr_ref[early, cols], [(k_early, v_early, mask)], factor)
        o_ref[pl.ds(offsets[0], quarter), cols] = mixed.astype(jnp.bfloat16)
        lse_ref[0, early, head : head + 1] = lse
        mixed, lse = softmax_mix(
            qr_ref[late, cols],
            [(k_early, v_early, None), (kr_ref[late, cols], vr_ref[late, cols], mask)],
            factor,
        )
        o_ref[pl.ds(offsets[1], quarter), cols] = mixed.astype(jnp.bfloat16)
        lse_ref[0, late, head : head + 1] = lse


def forward_second(
    q_ref, k_ref, v_ref, cos_ref, sin_ref, ka_ref, va_ref, pos_ref,
    qr_ref, kr_ref, vr_ref, o_ref, lse_ref,
):
    half = q_ref.shape[0]
    quarter = half // 2
    cut = FIRST_DOC - half
    spill = cut - quarter
    offsets = halves(quarter)
    load_rotated(offsets, quarter, q_ref, k_ref, v_ref, cos_ref, sin_ref, qr_ref, kr_ref, vr_ref)
    factor = HD ** (-0.5) * LOG2E
    mask = causal_mask(cut, cut)
    mask_tail = tail_mask(pos_ref[pl.ds(offsets[1] + spill, half - cut), :])
    for head in range(HEAD_GROUP):
        cols = head_slice(head)
        early, late = slice(0, cut), slice(cut, half)
        mixed, lse = softmax_mix(
            qr_ref[early, cols],
            [
                (ka_ref[:, cols], va_ref[:, cols], None),
                (kr_ref[early, cols], vr_ref[early, cols], mask),
            ],
            factor,
        )
        low = mixed.astype(jnp.bfloat16)
        o_ref[pl.ds(offsets[0], quarter), cols] = low[:quarter]
        o_ref[pl.ds(offsets[1], spill), cols] = low[quarter:]
        lse_ref[0, early, head : head + 1] = lse
        mixed, lse = softmax_mix(
            qr_ref[late, cols], [(kr_ref[late, cols], vr_ref[late, cols], mask_tail)], factor
        )
        o_ref[pl.ds(offsets[1] + spill, half - cut), cols] = mixed.astype(jnp.bfloat16)
        lse_ref[0, late, head : head + 1] = lse


def backward_both(
    qa_ref, ka_ref, va_ref, qb_ref, kb_ref, vb_ref, ga_ref, gb_ref, la_ref, lb_ref,
    cosa_ref, sina_ref, cosb_ref, sinb_ref, pos_ref,
    dqa_ref, dka_ref, dva_ref, dqb_ref, dkb_ref, dvb_ref,
    go_a, go_b, tqa, tka, tva, tqb, tkb, tvb,
):
    half = qa_ref.shape[0]
    quarter = half // 2
    cut = FIRST_DOC - half
    spill = cut - quarter
    offsets = halves(quarter)
    scale_value = HD ** (-0.5)
    factor = scale_value * LOG2E
    for place, offset in enumerate(offsets):
        target, rows = pl.ds(place * quarter, quarter), pl.ds(offset, quarter)
        go_a[target, :] = ga_ref[rows, :]
        go_b[target, :] = gb_ref[rows, :]
    mask = causal_mask(quarter, quarter)
    mask_cut = causal_mask(cut, cut)
    mask_tail = tail_mask(pos_ref[pl.ds(offsets[1] + spill, half - cut), :])
    for accumulator in (tka, tva, tkb, tvb):
        accumulator[...] = jnp.zeros_like(accumulator)

    def attend(query, grad, lse, pieces):
        weights, weight_grads = [], []
        for k_ref, v_ref, rows, cols, mask, _, _ in pieces:
            weight = jnp.exp2(dot_nt(query, k_ref[rows, cols]) * factor - lse)
            weights.append(weight if mask is None else jnp.where(mask, weight, 0.0))
            weight_grads.append(dot_nt(grad, v_ref[rows, cols]))
        shared = functools.reduce(
            jnp.add,
            [jnp.sum(w * g, axis=-1, keepdims=True) for w, g in zip(weights, weight_grads)],
        )
        query_grad = None
        for weight, weight_grad, piece in zip(weights, weight_grads, pieces):
            k_ref, v_ref, rows, cols, _, tk, tv = piece
            score_grad = (weight * (weight_grad - shared)).astype(jnp.bfloat16)
            term = dot_nn(score_grad, k_ref[rows, cols])
            query_grad = term if query_grad is None else query_grad + term
            tk[rows, cols] += dot_tn(score_grad, query)
            tv[rows, cols] += dot_tn(weight.astype(jnp.bfloat16), grad)
        return query_grad

    for head in range(HEAD_GROUP):
        cols = head_slice(head)
        lane = slice(head, head + 1)
        early, late, whole = slice(0, quarter), slice(quarter, half), slice(0, half)
        tqa[early, cols] = attend(
            qa_ref[early, cols], go_a[early, cols], la_ref[0, early, lane],
            [(ka_ref, va_ref, early, cols, mask, tka, tva)],
        )
        tqa[late, cols] = attend(
            qa_ref[late, cols], go_a[late, cols], la_ref[0, late, lane],
            [
                (ka_ref, va_ref, early, cols, None, tka, tva),
                (ka_ref, va_ref, late, cols, mask, tka, tva),
            ],
        )
        early, late = slice(0, cut), slice(cut, half)
        tqb[early, cols] = attend(
            qb_ref[early, cols], go_b[early, cols], lb_ref[0, early, lane],
            [
                (ka_ref, va_ref, whole, cols, None, tka, tva),
                (kb_ref, vb_ref, early, cols, mask_cut, tkb, tvb),
            ],
        )
        tqb[late, cols] = attend(
            qb_ref[late, cols], go_b[late, cols], lb_ref[0, late, lane],
            [(kb_ref, vb_ref, late, cols, mask_tail, tkb, tvb)],
        )
    for place, offset in enumerate(offsets):
        source, rows = pl.ds(place * quarter, quarter), pl.ds(offset, quarter)
        for total, cos_ref, sin_ref, out_ref in (
            (tqa, cosa_ref, sina_ref, dqa_ref),
            (tka, cosa_ref, sina_ref, dka_ref),
            (tqb, cosb_ref, sinb_ref, dqb_ref),
            (tkb, cosb_ref, sinb_ref, dkb_ref),
        ):
            grad = total[source, :] * scale_value
            out_ref[rows, :] = (
                grad * widen(cos_ref[rows, :]) - swap_halves(grad) * widen(sin_ref[rows, :])
            ).astype(jnp.bfloat16)
        dva_ref[rows, :] = tva[source, :].astype(jnp.bfloat16)
        dvb_ref[rows, :] = tvb[source, :].astype(jnp.bfloat16)


COST_SCALE = 1.7


def cost_of(flops):
    return pl.CostEstimate(flops=int(COST_SCALE * flops), bytes_accessed=1000, transcendentals=0)


def rows_kernel(pairs, extra_count, dot, chunk, finish, *refs):
    lefts, weights = refs[:pairs], refs[pairs : 2 * pairs]
    extras = refs[2 * pairs : 2 * pairs + extra_count]
    outs = refs[2 * pairs + extra_count :]

    @pl.loop(0, outs[0].shape[0] // chunk)
    def _(step):
        rows = pl.ds(pl.multiple_of(step * chunk, chunk), chunk)
        total = None
        for left, weight in zip(lefts, weights):
            term = dot(left[rows, :], weight[...])
            total = term if total is None else total + term
        for out, value in zip(outs, finish(total, *[extra[rows, :] for extra in extras])):
            out[rows, :] = value.astype(out.dtype)


def keep_one(total):
    return (total,)


def rows_matmul(
    lefts, weights, dot, types, tile, chunk=1024, finish=keep_one, extras=(), pushes=()
):
    rows = lefts[0].shape[0]
    if dot is dot_nn:
        width = weights[0].shape[1]
        weight_specs = [pl.BlockSpec((w.shape[0], tile), lambda j: (0, j)) for w in weights]
    else:
        width = weights[0].shape[0]
        weight_specs = [pl.BlockSpec((tile, w.shape[1]), lambda j: (j, 0)) for w in weights]
    column = pl.BlockSpec((rows, tile), lambda j: (0, j))
    return grid_call(
        functools.partial(rows_kernel, len(lefts), len(extras), dot, min(chunk, rows), finish),
        [*lefts, *weights, *extras],
        [pl.BlockSpec(left.shape, lambda j: (0, 0)) for left in lefts]
        + weight_specs
        + [column] * len(extras),
        [jax.ShapeDtypeStruct((rows, width), kind) for kind in types],
        [column] * len(types),
        (width // tile,),
        2 * rows * width * sum(left.shape[1] for left in lefts),
        pushes=pushes,
    )


def sum_kernel(parts, chunk, *refs):
    lefts, rights, out = refs[:parts], refs[parts : 2 * parts], refs[-1]

    @pl.loop(0, out.shape[1] // chunk)
    def _(step):
        cols = pl.ds(pl.multiple_of(step * chunk, chunk), chunk)
        total = None
        for left, right in zip(lefts, rights):
            term = dot_tn(left[...], right[:, cols])
            total = term if total is None else total + term
        out[:, cols] = total.astype(out.dtype)


def sum_matmul(lefts, rights, tile, chunk, pushes=()):
    rows, height = lefts[0].shape
    width = rights[0].shape[1]
    return grid_call(
        functools.partial(sum_kernel, len(lefts), chunk),
        [*lefts, *rights],
        [pl.BlockSpec((rows, tile), lambda j: (0, j)) for _ in lefts]
        + [pl.BlockSpec((rows, width), lambda j: (0, 0)) for _ in rights],
        [jax.ShapeDtypeStruct((height, width), jnp.bfloat16)],
        [pl.BlockSpec((tile, width), lambda j: (j, 0))],
        (height // tile,),
        2 * rows * height * width * len(lefts),
        pushes=pushes,
    )


def partner_of(kind):
    index, place = lax.axis_index("fsdp"), lax.axis_index("tp")
    if kind == "near":
        return (index, place + 1 - 2 * (place % 2))
    if kind == "core":
        return sibling_id()
    return (index, place + 2 - 4 * (place // 2))


def start_pushes(kinds, sources, targets, send, receive):
    barrier = pltpu.get_barrier_semaphore()
    names = sorted(set(kinds))
    for kind in names:
        pl.semaphore_signal(
            barrier, inc=1, device_id=partner_of(kind), device_id_type=pl.DeviceIdType.MESH
        )
    pl.semaphore_wait(barrier, len(names))
    for place, kind in enumerate(kinds):
        push(
            sources[place], targets[place], send.at[place], receive.at[place], partner_of(kind)
        ).start()


def wait_pushes(kinds, sources, targets, send, receive):
    for place, kind in enumerate(kinds):
        push(
            sources[place], targets[place], send.at[place], receive.at[place], partner_of(kind)
        ).wait()


def pushing_kernel(kernel, axes, in_count, out_count, kinds, *refs):
    count = len(kinds)
    inputs, sources = refs[:in_count], refs[in_count : in_count + count]
    outs = refs[in_count + count : in_count + count + out_count]
    targets = refs[in_count + count + out_count : in_count + 2 * count + out_count]
    scratch, (send, receive) = refs[in_count + 2 * count + out_count : -2], refs[-2:]
    first = functools.reduce(jnp.logical_and, [pl.program_id(axis) == 0 for axis in range(axes)])
    last = functools.reduce(
        jnp.logical_and,
        [pl.program_id(axis) == pl.num_programs(axis) - 1 for axis in range(axes)],
    )

    @pl.when(first)
    def _():
        start_pushes(kinds, sources, targets, send, receive)

    kernel(*inputs, *outs, *scratch)

    @pl.when(last)
    def _():
        wait_pushes(kinds, sources, targets, send, receive)


def grid_call(
    kernel, operands, in_specs, outs, out_specs, grid, flops, scratch=(), pushes=(), vmem=60
):
    params = dict(
        dimension_semantics=("arbitrary",) * len(grid), vmem_limit_bytes=vmem * 1024 * 1024
    )
    operands, in_specs, outs = list(operands), list(in_specs), list(outs)
    out_specs, scratch = list(out_specs), list(scratch)
    if pushes:
        kinds = tuple(kind for kind, _ in pushes)
        kernel = functools.partial(
            pushing_kernel, kernel, len(grid), len(operands), len(outs), kinds
        )
        anywhere = [pl.BlockSpec(memory_space=pl.ANY)] * len(pushes)
        operands += [value for _, value in pushes]
        in_specs += anywhere
        outs += [jax.ShapeDtypeStruct(value.shape, value.dtype) for _, value in pushes]
        out_specs += anywhere
        scratch += [pltpu.SemaphoreType.DMA((len(pushes),))] * 2
        next_key[0] += 1
        params.update(collective_id=next_key[0], has_side_effects=True)
    return tuple(
        pl.pallas_call(
            kernel,
            out_shape=outs,
            grid=grid,
            in_specs=in_specs,
            out_specs=out_specs,
            scratch_shapes=scratch,
            compiler_params=pltpu.CompilerParams(**params),
            cost_estimate=cost_of(max(flops, 27 * 10**9) if pushes else flops),
        )(*operands)
    )


def swap_kernel(kinds, *refs):
    count = len(kinds)
    sources, targets, (send, receive) = refs[:count], refs[count : 2 * count], refs[2 * count :]
    start_pushes(kinds, sources, targets, send, receive)
    wait_pushes(kinds, sources, targets, send, receive)


def swap_call(*pushes):
    next_key[0] += 1
    kinds = tuple(kind for kind, _ in pushes)
    values = [value for _, value in pushes]
    return exchange_call(
        functools.partial(swap_kernel, kinds), next_key[0], values,
        [jax.ShapeDtypeStruct(value.shape, value.dtype) for value in values],
        [pltpu.SemaphoreType.DMA((len(pushes),))] * 2, flops=130 * 10**9,
    )


next_key = [11]


def sibling_id():
    index = lax.axis_index("fsdp")
    return (index + 1 - 2 * (index % 2), lax.axis_index("tp"))


def meet(partner):
    barrier = pltpu.get_barrier_semaphore()
    pl.semaphore_signal(barrier, inc=1, device_id=partner, device_id_type=pl.DeviceIdType.MESH)
    pl.semaphore_wait(barrier, 1)


def push(source, target, send, receive, partner):
    return pltpu.make_async_remote_copy(
        src_ref=source,
        dst_ref=target,
        send_sem=send,
        recv_sem=receive,
        device_id=partner,
        device_id_type=pl.DeviceIdType.MESH,
    )


def exchange_call(kernel, key, operands, outs, scratch, vmem=60, flops=4 * 10**9):
    anywhere = pl.BlockSpec(memory_space=pl.ANY)
    results = pl.pallas_call(
        kernel,
        out_shape=outs,
        in_specs=[anywhere] * len(operands),
        out_specs=[anywhere] * len(outs),
        scratch_shapes=scratch,
        compiler_params=pltpu.CompilerParams(
            collective_id=key, has_side_effects=True, vmem_limit_bytes=vmem * 1024 * 1024
        ),
        cost_estimate=cost_of(flops),
    )(*operands)
    return tuple(results) if len(outs) > 1 else results[0]


def relay(sources, targets, buffer, load, store):
    loads, stores = [], []
    for place, source in enumerate(sources):
        copy = pltpu.make_async_copy(source, buffer.at[place], load.at[place])
        copy.start()
        loads.append(copy)
    for place, target in enumerate(targets):
        loads[place].wait()
        copy = pltpu.make_async_copy(buffer.at[place], target, store.at[place])
        copy.start()
        stores.append(copy)
    for copy in stores:
        copy.wait()


def gather_kernel(own_ref, near_ref, full_ref, buffer, load, store, send, receive):
    partner = sibling_id()
    meet(partner)
    count = own_ref.shape[0]
    remotes = []
    for place, ref in enumerate((own_ref, near_ref)):
        remote = push(
            ref, full_ref.at[pl.ds((2 + place) * count, count)],
            send.at[place], receive.at[place], partner,
        )
        remote.start()
        remotes.append(remote)
    targets = [full_ref.at[pl.ds(place * count, count)] for place in range(2)]
    relay((own_ref, near_ref), targets, buffer, load, store)
    for remote in remotes:
        remote.wait()


def core_gather(own, near):
    shape = (4 * own.shape[0], own.shape[1])
    return exchange_call(
        gather_kernel, 1, [own, near], [jax.ShapeDtypeStruct(shape, own.dtype)],
        [pltpu.VMEM((2, *own.shape), own.dtype)] + [pltpu.SemaphoreType.DMA((2,))] * 4,
    )


def gather_two_kernel(
    own_ref, own_near_ref, got_ref, got_near_ref, first_ref, second_ref,
    buffer, load, store, send, receive,
):
    partner = sibling_id()
    far = lax.axis_index("tp") // 2
    meet(partner)
    count = own_ref.shape[0]

    def run(targets):
        sources = (own_ref, own_near_ref, got_ref, got_near_ref)
        remotes, places = [], []
        for place, ref in enumerate(sources):
            target, row = targets[place // 2], place % 2
            remote = push(
                ref, target.at[pl.ds((2 + row) * count, count)],
                send.at[place], receive.at[place], partner,
            )
            remote.start()
            remotes.append(remote)
            places.append(target.at[pl.ds(row * count, count)])
        relay(sources, places, buffer, load, store)
        for remote in remotes:
            remote.wait()

    @pl.when(far == 0)
    def _():
        run((first_ref, second_ref))

    @pl.when(far != 0)
    def _():
        run((second_ref, first_ref))


def core_gather_two(own, own_near, got, got_near):
    shape = (4 * own.shape[0], own.shape[1])
    return exchange_call(
        gather_two_kernel, 11, [own, own_near, got, got_near],
        [jax.ShapeDtypeStruct(shape, own.dtype)] * 2,
        [pltpu.VMEM((4, *own.shape), own.dtype)] + [pltpu.SemaphoreType.DMA((4,))] * 4,
    )


def reduce_kernel(term_ref, keep_ref, away_ref, mine, got, keep, away, local, send, receive, store):
    partner = sibling_id()
    meet(partner)
    pieces, count = mine.shape[0], mine.shape[1]
    half = pieces * count
    remotes, loads = [], []
    for piece in range(pieces):
        order = (piece + pieces // 2) % pieces
        remote = push(
            term_ref.at[pl.ds(half + order * count, count)], got.at[order],
            send.at[order], receive.at[order], partner,
        )
        remote.start()
        remotes.append(remote)
        load = pltpu.make_async_copy(
            term_ref.at[pl.ds(order * count, count)], mine.at[order], local.at[order]
        )
        load.start()
        loads.append(load)
    stores = []
    for piece in range(pieces):
        order = (piece + pieces // 2) % pieces
        loads[piece].wait()
        remotes[piece].wait()
        total = mine[order].astype(jnp.float32) + got[order].astype(jnp.float32)
        if order < pieces // 2:
            keep[order] = total
            copy = pltpu.make_async_copy(
                keep.at[order], keep_ref.at[pl.ds(order * count, count)], store.at[order]
            )
        else:
            slot = order - pieces // 2
            away[slot] = total.astype(away.dtype)
            copy = pltpu.make_async_copy(
                away.at[slot], away_ref.at[pl.ds(slot * count, count)], store.at[order]
            )
        copy.start()
        stores.append(copy)
    for copy in stores:
        copy.wait()


def core_reduce(term):
    rows, width = term.shape
    quarter = rows // 4
    pieces = 4
    count = 2 * quarter // pieces
    return exchange_call(
        reduce_kernel, 2, [term],
        [
            jax.ShapeDtypeStruct((quarter, width), jnp.float32),
            jax.ShapeDtypeStruct((quarter, width), term.dtype),
        ],
        [
            pltpu.VMEM((pieces, count, width), term.dtype),
            pltpu.VMEM((pieces, count, width), term.dtype),
            pltpu.VMEM((pieces // 2, count, width), jnp.float32),
            pltpu.VMEM((pieces // 2, count, width), term.dtype),
        ]
        + [pltpu.SemaphoreType.DMA((pieces,))] * 4,
    )


def pair_kernel(own_ref, *refs):
    others, (pair_ref, buffer, load, store, send, receive) = refs[:-6], refs[-6:]
    partner = sibling_id()
    core = lax.axis_index("fsdp") % 2
    far = lax.axis_index("tp") // 2
    meet(partner)
    base = pl.multiple_of(core * own_ref.shape[0], own_ref.shape[0])
    count = others[0].shape[0]
    owns = [own_ref.at[pl.ds(place * count, count)] for place in range(len(others))]

    def run(mine, theirs):
        remotes, targets = [], []
        for place in range(len(others)):
            target = pair_ref.at[pl.ds(base + place * count, count)]
            remote = push(theirs[place], target, send.at[place], receive.at[place], partner)
            remote.start()
            remotes.append(remote)
            targets.append(target)
        relay(mine, targets, buffer, load, store)
        for remote in remotes:
            remote.wait()

    @pl.when(core == far)
    def _():
        run(owns, others)

    @pl.when(core != far)
    def _():
        run(others, owns)


def core_pair(key, own, *others):
    shape = (2 * own.shape[0], own.shape[1])
    return exchange_call(
        pair_kernel, key, [own, *others], [jax.ShapeDtypeStruct(shape, own.dtype)],
        [pltpu.VMEM((len(others), *others[0].shape), own.dtype)]
        + [pltpu.SemaphoreType.DMA((len(others),))] * 4,
    )


def split_kernel(pair_ref, keep_ref, away_ref, buffer, load, store, send, receive):
    partner = sibling_id()
    core = lax.axis_index("fsdp") % 2
    far = lax.axis_index("tp") // 2
    meet(partner)
    count = keep_ref.shape[0]
    mine = pair_ref.at[pl.ds(pl.multiple_of(core * count, count), count)]
    theirs = pair_ref.at[pl.ds(pl.multiple_of((1 - core) * count, count), count)]

    def run(own_target, other_target):
        remote = push(theirs, other_target, send.at[0], receive.at[0], partner)
        remote.start()
        relay((mine,), (own_target,), buffer, load, store)
        remote.wait()

    @pl.when(core == far)
    def _():
        run(keep_ref, keep_ref)

    @pl.when(core != far)
    def _():
        run(away_ref, away_ref)


def core_split(key, pair):
    shape = (pair.shape[0] // 2, pair.shape[1])
    return exchange_call(
        split_kernel, key, [pair], [jax.ShapeDtypeStruct(shape, pair.dtype)] * 2,
        [pltpu.VMEM((1, *shape), pair.dtype)] + [pltpu.SemaphoreType.DMA((1,))] * 4,
    )


def attention_call(kernel, arrays, kinds, outs, scratch, pushes=()):
    rows, heads_local = arrays[-1].shape[0], outs[1]
    half = rows // 2
    groups = heads_local // HEAD_GROUP
    width = HEAD_GROUP * HD

    def spec(kind):
        if kind == "table":
            return pl.BlockSpec((half, HD), lambda s, g: (s, 0))
        if kind == "column":
            return pl.BlockSpec((half, 1), lambda s, g: (s, 0))
        if kind == "lse":
            return pl.BlockSpec((1, half, HEAD_GROUP), lambda s, g: (g, s, 0))
        shift = kind * groups
        return pl.BlockSpec((half, width), lambda s, g: (s, shift + g))

    def shape(kind):
        if kind == "lse":
            return jax.ShapeDtypeStruct((groups, rows, HEAD_GROUP), jnp.float32)
        return jax.ShapeDtypeStruct((rows, heads_local * HD), jnp.bfloat16)

    return grid_call(
        kernel,
        arrays,
        [spec(kind) for kind in kinds],
        [shape(kind) for kind in outs[0]],
        [spec(kind) for kind in outs[0]],
        (rows // half, groups),
        4 * len(outs[0]) ** 2 * rows * rows * heads_local * HD // 16,
        scratch=scratch(half, width),
        pushes=pushes,
    )


def backward_scratch(half, width):
    return [pltpu.VMEM((half, width), jnp.bfloat16)] * 2 + [
        pltpu.VMEM((half, width), jnp.float32)
    ] * 6


def no_scratch(half, width):
    return []


def head_tables(positions):
    half_width = HD // 2
    frequency = rope_theta ** (-(jnp.arange(half_width, dtype=jnp.float32) * 2.0 / HD))
    angles = positions.astype(jnp.float32)[:, None] * frequency[None, :]
    cosine, sine = jnp.cos(angles), jnp.sin(angles)
    return (
        jnp.concatenate([cosine, cosine], axis=-1),
        jnp.concatenate([-sine, sine], axis=-1),
    )


def paired_device(
    block_in,
    out_cotangent,
    segment_ids,
    doc_positions,
    norm1_gain,
    qkv_weight,
    out_weight,
    norm2_gain,
    gate_up_weight,
    down_weight,
):
    fsdp_count, tp_count = lax.axis_size("fsdp"), lax.axis_size("tp")
    core = lax.axis_index("fsdp") % 2
    lane_z = lax.axis_index("tp")
    near, far = lane_z % 2, lane_z // 2
    core_pairs = [(i, i ^ 1) for i in range(fsdp_count)]
    near_pairs = [(i, i ^ 1) for i in range(tp_count)]
    far_pairs = [(i, i ^ 2) for i in range(tp_count)]
    plane_groups = [list(range(first, fsdp_count, 2)) for first in range(2)]
    rows = block_in.shape[1]
    local_cols = qkv_weight.shape[2]
    heads_local = local_cols // HD
    gain_one = norm1_gain.astype(jnp.float32)
    gain_two = norm2_gain.astype(jnp.float32)

    def swap_core(value):
        return lax.ppermute(value, "fsdp", core_pairs)

    def swap_near(value):
        return lax.ppermute(value, "tp", near_pairs)

    def swap_far(value):
        return lax.ppermute(value, "tp", far_pairs)

    def pick_tile(size):
        return 512 if size % 512 == 0 else 768

    tokens = []

    def act(work, *inputs, sends=()):
        values = [*inputs, *[value for _, value in sends]]
        held = lax.optimization_barrier((*values, *tokens))[: len(values)]
        if sends:
            kinds = [kind for kind, _ in sends]
            result = work(*held[: len(inputs)], pushes=list(zip(kinds, held[len(inputs) :])))
        else:
            result = work(*held)
        tokens[:] = result if isinstance(result, tuple) else (result,)
        return result[0] if isinstance(result, tuple) and len(result) == 1 else result

    def swap(*sends):
        return act(lambda pushes: swap_call(*pushes), sends=sends)

    def pick(value, index):
        return lax.dynamic_index_in_dim(value, index, 0, keepdims=False)

    def place_tokens(value, got):
        keep = pick(value, far)
        return jnp.where(far == 0, keep, got), jnp.where(far == 0, got, keep)

    def join(left, right):
        return jnp.concatenate([left, right], axis=0)

    def plane_gather(pair):
        return lax.all_gather(pair, "fsdp", axis=0, tiled=True, axis_index_groups=plane_groups)

    def plane_scatter(grad):
        return lax.psum_scatter(
            grad, "fsdp", scatter_dimension=0, tiled=True, axis_index_groups=plane_groups
        )

    def gather_weight(key, local, *others):
        return plane_gather(act(lambda own, *got: core_pair(key, own, *got), local, *others))

    def halve(value):
        count = value.shape[0] // 2
        return value[:count], value[count:]

    def add_wide(left, right):
        return left.astype(jnp.float32) + right.astype(jnp.float32)

    def chained(value, *others):
        return lax.optimization_barrier((value, *others))[0]

    def scatter_gains(gains):
        for axis, size in (("fsdp", fsdp_count), ("tp", tp_count)):
            index = lax.axis_index(axis)
            step = size // 2
            while step >= 1:
                bit = (index // step) % 2
                parts = gains.reshape(gains.shape[0], 2, gains.shape[1] // 2)
                sent = lax.dynamic_index_in_dim(parts, 1 - bit, 1, keepdims=False)
                kept = lax.dynamic_index_in_dim(parts, bit, 1, keepdims=False)
                gains = kept + lax.ppermute(sent, axis, [(i, i ^ step) for i in range(size)])
                step //= 2
        return gains

    def wide_dot(left, right, pushes=()):
        return rows_matmul(
            [left], [right], dot_nn, [jnp.float32], pick_tile(right.shape[1]), pushes=pushes
        )

    def dot_bf16(left, right, pushes=()):
        return rows_matmul(
            [left], [right], dot_nn, [jnp.bfloat16], pick_tile(right.shape[1]), pushes=pushes
        )

    def grad_sum(left, right, left_next, right_next, pushes=()):
        chunk = pick_tile(right.shape[1])
        return sum_matmul(
            [left, left_next], [right, right_next], pick_tile(left.shape[1]),
            2 * chunk if right.shape[1] % (2 * chunk) == 0 else chunk, pushes=pushes,
        )

    def heads_back(grad, weight, pushes=()):
        return rows_matmul(
            [grad], [weight], dot_nt, [jnp.bfloat16], pick_tile(weight.shape[0]), pushes=pushes
        )

    def rms_pack(stream, gain):
        scale = rms_scale(stream)
        return scale, (stream * scale * gain).astype(jnp.bfloat16)

    qkv_local = qkv_weight.reshape(qkv_weight.shape[0], 3 * local_cols)
    gate_local, up_local = gate_up_weight[:, 0], gate_up_weight[:, 1]

    next_key[0] = 11
    places = jnp.broadcast_to(doc_positions[:, None, :], (2, 8, rows))

    def first_norm(part):
        stream = part.astype(jnp.float32)
        return (stream, *rms_pack(stream, gain_one))

    s_own, r_own, n_own = act(lambda value: first_norm(pick(value, far)), block_in)
    near_own, qkv_other, place_got = swap(
        ("near", n_own), ("far", qkv_local), ("far", pick(places, 1 - far))
    )
    qkv_full = gather_weight(4, qkv_local, qkv_other)
    places = join(*place_tokens(places, place_got))

    def make_tables(own, other):
        order = join(own, other)[::8].reshape(2, 2, 2, rows)
        early, late = order[:, :, 0].reshape(-1), order[:, :, 1].reshape(-1)
        return (*head_tables(early), *head_tables(late), late[:, None])

    c_own = pick(out_cotangent, far)
    stream_got, c_near_own, out_other, near_places = swap(
        ("far", pick(block_in, 1 - far)), ("near", c_own), ("far", out_weight), ("near", places)
    )
    places = join(places, near_places)
    out_full = gather_weight(3, out_weight, out_other)
    s_got, r_got, n_got = act(first_norm, stream_got)
    near_got, gate_other, core_places = swap(
        ("near", n_got), ("far", gate_local), ("core", places)
    )
    gate_full = gather_weight(5, gate_local, gate_other)
    h1_first, h1_second = act(core_gather_two, n_own, near_own, n_got, near_got)
    streams = [jnp.where(far == 0, s_own, s_got), jnp.where(far == 0, s_got, s_own)]
    scales_one = [jnp.where(far == 0, r_own, r_got), jnp.where(far == 0, r_got, r_own)]

    def attend_first(projected, pushes=()):
        arrays = [projected, projected, projected, *tables[0]]
        return attention_call(
            forward_first, arrays, [0, 1, 2, "table", "table"],
            ([0, 0, 0, 0, "lse"], heads_local), no_scratch, pushes,
        )

    def attend_second(projected, pushes=()):
        arrays = [projected, projected, projected, *tables[1], saved[0][1], saved[0][2], reach]
        return attention_call(
            forward_second, arrays, [0, 1, 2, "table", "table", 0, 0, "column"],
            ([0, 0, 0, 0, "lse"], heads_local), no_scratch, pushes,
        )

    up_other = swap_far(chained(up_local, gate_other))
    cos_first, sin_first, cos_second, sin_second, reach = act(
        make_tables, places, core_places
    )
    tables = [(cos_first, sin_first), (cos_second, sin_second)]
    projected = act(wide_dot, h1_first, qkv_full)
    results = act(attend_first, projected)
    up_full = gather_weight(5, up_local, up_other)
    down_other = swap_far(chained(down_weight, up_other))
    saved, lses, mixed_first = [results[:3]], [results[4]], results[3]
    term_first = act(dot_bf16, mixed_first, out_full)
    keep_first, send_first = act(core_reduce, term_first)
    projected, branch_first = act(
        wide_dot, h1_second, qkv_full, sends=[("near", send_first)]
    )

    def second_norm(stream, keep, got):
        middle = stream + keep + got.astype(jnp.float32)
        return (middle, *rms_pack(middle, gain_two))

    m_first, q_first, n_first = act(second_norm, streams[0], keep_first, branch_first)
    *results, near_first = act(attend_second, projected, sends=[("near", n_first)])
    saved.append(results[:3])
    lses.append(results[4])
    mixed_second = results[3]
    term_second = act(dot_bf16, mixed_second, out_full)
    keep_second, send_second = act(core_reduce, term_second)
    h2_first = act(core_gather, n_first, near_first)
    down_full_pair = act(lambda own, got: core_pair(6, own, got), down_weight, down_other)
    down_full = plane_gather(down_full_pair)
    c_got = swap_far(chained(pick(out_cotangent, 1 - far), down_full_pair))

    gate_first, branch_second = act(
        wide_dot, h2_first, gate_full, sends=[("near", send_second)]
    )
    m_second, q_second, n_second = act(second_norm, streams[1], keep_second, branch_second)

    def rise(hidden, weight, gate, pushes=()):
        return rows_matmul(
            [hidden], [weight], dot_nn, [jnp.float32, jnp.bfloat16], pick_tile(weight.shape[1]),
            finish=lambda up, gate: (up, gate * jax.nn.sigmoid(gate) * up), extras=[gate],
            pushes=pushes,
        )

    up_first, a_first, near_second = act(
        rise, h2_first, up_full, gate_first, sends=[("near", n_second)]
    )
    h2_second = act(core_gather, n_second, near_second)
    gate_second, c_near_got = act(
        wide_dot, h2_second, gate_full, sends=[("near", c_got)]
    )
    y_first, y_second = act(core_gather_two, c_own, c_near_own, c_got, c_near_got)
    c_first, c_second = jnp.where(far == 0, c_own, c_got), jnp.where(far == 0, c_got, c_own)
    up_second, a_second = act(rise, h2_second, up_full, gate_second)
    down_sum = plane_scatter(act(grad_sum, a_first, y_first, a_second, y_second))

    def fall_finish(act_grad, gate, up):
        sigmoid_gate = jax.nn.sigmoid(gate)
        return (
            act_grad * up * sigmoid_gate * (1.0 + gate * (1.0 - sigmoid_gate)),
            act_grad * (gate * sigmoid_gate),
        )

    def fall(cotangent, weight, gate, up, pushes=()):
        return rows_matmul(
            [cotangent], [weight], dot_nt, [jnp.bfloat16] * 2, pick_tile(weight.shape[0]),
            chunk=512, finish=fall_finish, extras=[gate, up], pushes=pushes,
        )

    def hidden_grad(gate_grad, up_grad, gate_weight, up_weight, pushes=()):
        return rows_matmul(
            [gate_grad, up_grad], [gate_weight, up_weight], dot_nt, [jnp.bfloat16],
            pick_tile(gate_weight.shape[0]), pushes=pushes,
        )

    def second_back(middle, scale, keep, got, cotangent):
        grad, gain_term = norm_back(middle, scale, gain_two, keep + got.astype(jnp.float32))
        grad = cotangent.astype(jnp.float32) + grad
        return grad, grad.astype(jnp.bfloat16), gain_term

    dg_first, du_first = act(fall, y_first, down_full, gate_first, up_first)
    term_first = act(hidden_grad, dg_first, du_first, gate_full, up_full)
    keep_first, send_first = act(core_reduce, term_first)
    dg_second, du_second, back_first = act(
        fall, y_second, down_full, gate_second, up_second, sends=[("near", send_first)]
    )
    g_first, n_first, gain_two_first = act(
        second_back, m_first, q_first, keep_first, back_first, c_first
    )
    term_second, near_first = act(
        hidden_grad, dg_second, du_second, gate_full, up_full, sends=[("near", n_first)]
    )
    keep_second, send_second = act(core_reduce, term_second)
    d_first = act(core_gather, n_first, near_first)
    grad_gate, back_second = act(
        grad_sum, h2_first, dg_first, h2_second, dg_second, sends=[("near", send_second)]
    )
    gate_sum = plane_scatter(grad_gate)
    g_second, n_second, gain_two_second = act(
        second_back, m_second, q_second, keep_second, back_second, c_second
    )
    heads_first = act(heads_back, d_first, out_full)
    down_mine, down_away = act(lambda pair: core_split(10, pair), down_sum)
    down_got = swap_far(down_away)
    grad_up, near_second = act(
        grad_sum, h2_first, du_first, h2_second, du_second, sends=[("near", n_second)]
    )
    up_sum = plane_scatter(grad_up)

    d_second = act(core_gather, n_second, near_second)
    heads_second = act(heads_back, d_second, out_full)
    mlp_first = act(dot_bf16, a_first, down_full)
    mlp_keep_first, mlp_send_first = act(core_reduce, mlp_first)
    mlp_second, mlp_branch_first = act(
        dot_bf16, a_second, down_full, sends=[("near", mlp_send_first)]
    )
    mlp_keep_second, mlp_send_second = act(core_reduce, mlp_second)
    gate_mine, gate_away = act(lambda pair: core_split(9, pair), gate_sum)
    gate_got = swap_far(gate_away)
    grad_out = act(grad_sum, mixed_first, d_first, mixed_second, d_second)
    out_sum = plane_scatter(grad_out)
    def attend_back(heads_first, heads_second, pushes=()):
        return attention_call(
            backward_both,
            [
                *saved[0], *saved[1], heads_first, heads_second, *lses,
                *tables[0], *tables[1], reach,
            ],
            [0] * 8 + ["lse"] * 2 + ["table"] * 4 + ["column"],
            ([0] * 6, heads_local),
            backward_scratch,
            pushes,
        )

    *grads, mlp_branch_second = act(
        attend_back, heads_first, heads_second, sends=[("near", mlp_send_second)]
    )
    p_first, p_second = act(
        lambda *parts: (
            jnp.concatenate(parts[:3], axis=1),
            jnp.concatenate(parts[3:], axis=1),
        ),
        *grads,
    )

    def finish_output(first, first_keep, first_got, second, second_keep, second_got):
        first = (first + first_keep + first_got.astype(jnp.float32)).astype(jnp.bfloat16)
        second = (second + second_keep + second_got.astype(jnp.float32)).astype(jnp.bfloat16)
        return jnp.where(far == 0, first, second), jnp.where(far == 0, second, first)

    up_mine, up_away = act(lambda pair: core_split(9, pair), up_sum)
    up_got = swap_far(up_away)
    grad_qkv = act(grad_sum, h1_first, p_first, h1_second, p_second)
    qkv_sum = plane_scatter(grad_qkv)
    out_keep, out_send = act(
        finish_output,
        m_first, mlp_keep_first, mlp_branch_first, m_second, mlp_keep_second, mlp_branch_second,
    )
    out_got = swap_far(out_send)
    term_first = act(heads_back, p_first, qkv_full)
    keep_first, send_first = act(core_reduce, term_first)
    term_second, back_first = act(
        heads_back, p_second, qkv_full, sends=[("near", send_first)]
    )
    keep_second, send_second = act(core_reduce, term_second)
    out_mine, out_away = act(lambda pair: core_split(8, pair), out_sum)
    def settle(keep, got):
        return jnp.stack([jnp.where(far == 0, keep, got), jnp.where(far == 0, got, keep)])

    def first_back(stream, scale, keep, got, grad):
        back, gain_term = norm_back(stream, scale, gain_one, keep + got.astype(jnp.float32))
        return grad + back, gain_term

    def last_back(stream, scale, keep, got, grad, first):
        second, gain_term = first_back(stream, scale, keep, got, grad)
        return (
            jnp.where(far == 0, first, second),
            jnp.where(far == 0, second, first).astype(jnp.bfloat16),
            gain_term,
        )

    back_second, out_back = swap(("near", send_second), ("far", out_away))
    qkv_mine, qkv_away = act(lambda pair: core_split(0, pair), qkv_sum)
    qkv_back = swap_far(qkv_away)
    i_first, gain_one_first = act(
        first_back, streams[0], scales_one[0], keep_first, back_first, g_first
    )
    in_keep, in_send, gain_one_second = act(
        last_back, streams[1], scales_one[1], keep_second, back_second, g_second, i_first
    )
    in_got = swap_far(in_send)
    down_owned = act(add_wide, down_mine, down_got)
    gate_owned = act(add_wide, gate_mine, gate_got)
    block_out = act(settle, out_keep, out_got)
    up_owned = act(add_wide, up_mine, up_got)
    gate_up_owned = act(lambda a, b: jnp.stack([a, b], axis=1), gate_owned, up_owned)
    out_owned = act(add_wide, out_mine, out_back)
    gains = scatter_gains(
        jnp.stack([gain_one_first + gain_one_second, gain_two_first + gain_two_second])
    )
    in_grad = act(lambda keep, got: settle(keep, got.astype(jnp.float32)), in_keep, in_got)
    qkv_owned = act(add_wide, qkv_mine, qkv_back)
    return (
        block_out,
        in_grad,
        gains[0],
        qkv_owned.reshape(qkv_weight.shape),
        out_owned,
        gains[1],
        gate_up_owned,
        down_owned,
    )


def solution(mesh):
    sizes = (mesh.shape["fsdp"], mesh.shape["tp"])
    body = paired_device if sizes == (8, 4) else per_device
    in_specs = (
        P("fsdp", "tp", None),
        P("fsdp", "tp", None),
        P("fsdp", "tp"),
        P("fsdp", "tp"),
        P(),
        P("fsdp", None, "tp"),
        P(("tp", "fsdp"), None),
        P(),
        P("fsdp", None, "tp"),
        P(("tp", "fsdp"), None),
    )
    out_specs = (
        P("fsdp", "tp", None),
        P("fsdp", "tp", None),
        P(("fsdp", "tp")),
        P("fsdp", None, "tp"),
        P(("tp", "fsdp"), None),
        P(("fsdp", "tp")),
        P("fsdp", None, "tp"),
        P(("tp", "fsdp"), None),
    )
    return jax.shard_map(
        body, mesh=mesh, in_specs=in_specs, out_specs=out_specs, check_vma=False
    )
```

```python
import functools

import jax
import jax.numpy as jnp
from jax import lax
from jax.experimental import pallas as pl
from jax.experimental.pallas import tpu as pltpu
from jax.sharding import PartitionSpec as P

D = 3072
HD = 96


rms_epsilon = 1e-05
rope_theta = 10000.0
masked_score = -1e30
LOG2E = 1.4426950408889634


def rope_tables(positions, head_size):
    half_width = head_size // 2
    frequency = rope_theta ** (-(jnp.arange(half_width, dtype=jnp.float32) * 2.0 / head_size))
    angles = positions.astype(jnp.float32)[:, None] * frequency[None, :]
    return (jnp.cos(angles)[:, None, :], jnp.sin(angles)[:, None, :])


def rotate(values, cosine_part, sine_part):
    half_width = values.shape[-1] // 2
    lead_half = values[..., :half_width]
    tail_half = values[..., half_width:]
    return jnp.concatenate(
        [
            lead_half * cosine_part - tail_half * sine_part,
            tail_half * cosine_part + lead_half * sine_part,
        ],
        axis=-1,
    )


def unrotate(values, cosine_part, sine_part):
    half_width = values.shape[-1] // 2
    lead_half = values[..., :half_width]
    tail_half = values[..., half_width:]
    return jnp.concatenate(
        [
            lead_half * cosine_part + tail_half * sine_part,
            tail_half * cosine_part - lead_half * sine_part,
        ],
        axis=-1,
    )


def rms_scale(stream):
    return lax.rsqrt(jnp.mean(stream * stream, axis=-1, keepdims=True) + rms_epsilon)


def norm_back(stream, scale_rows, gain_vec, grad_rows):
    gained_grad = gain_vec * grad_rows
    input_grad = scale_rows * gained_grad - stream * scale_rows**3 * jnp.mean(
        gained_grad * stream, axis=-1, keepdims=True
    )
    return (input_grad, jnp.sum(grad_rows * stream * scale_rows, axis=0))


def allowed_mask(segment_tile, index_tile, segments):
    columns = jnp.arange(segments.shape[0], dtype=jnp.int32)
    return (segment_tile[:, None] == segments[None, :]) & (index_tile[:, None] >= columns[None, :])


def masked_scores(query_tile, key_rows, segment_tile, index_tile, segments, scale_value):
    scores = (
        jnp.einsum("qhd,khd->hqk", query_tile, key_rows, preferred_element_type=jnp.float32)
        * scale_value
    )
    return jnp.where(allowed_mask(segment_tile, index_tile, segments)[None], scores, masked_score)


def attention_forward(queries, key_rows, value_rows, segments, block_rows):
    seq_len, head_count, head_size = queries.shape
    tiles = seq_len // block_rows
    scale_value = head_size ** (-0.5)
    positions = jnp.arange(seq_len, dtype=jnp.int32)

    def query_block(packed):
        query_tile, segment_tile, index_tile = packed
        scores = masked_scores(
            query_tile, key_rows, segment_tile, index_tile, segments, scale_value
        )
        row_max = jnp.max(scores, axis=-1, keepdims=True)
        exponent = jnp.exp(scores - row_max)
        row_total = jnp.sum(exponent, axis=-1, keepdims=True)
        probs_low = (exponent / row_total).astype(jnp.bfloat16)
        mixed = jnp.einsum(
            "hqk,khd->qhd", probs_low, value_rows, preferred_element_type=jnp.float32
        )
        return (mixed, (row_max + jnp.log(row_total))[..., 0])

    mixed, log_total = lax.map(
        query_block,
        (
            queries.reshape(tiles, block_rows, head_count, head_size),
            segments.reshape(tiles, block_rows),
            positions.reshape(tiles, block_rows),
        ),
    )
    return (mixed.reshape(seq_len, head_count * head_size), log_total)


def attention_backward(queries, key_rows, value_rows, segments, log_total, out_grad, block_rows):
    seq_len, head_count, head_size = queries.shape
    tiles = seq_len // block_rows
    scale_value = head_size ** (-0.5)
    positions = jnp.arange(seq_len, dtype=jnp.int32)

    def query_block(carry, packed):
        key_acc, value_acc = carry
        query_tile, segment_tile, index_tile, total_tile, grad_tile = packed
        scores = masked_scores(
            query_tile, key_rows, segment_tile, index_tile, segments, scale_value
        )
        probs = jnp.exp(scores - total_tile[..., None])
        probs_low = probs.astype(jnp.bfloat16)
        prob_grad = jnp.einsum(
            "qhd,khd->hqk", grad_tile, value_rows, preferred_element_type=jnp.float32
        )
        score_grad = (
            probs * (prob_grad - jnp.sum(probs * prob_grad, axis=-1, keepdims=True))
        ).astype(jnp.bfloat16)
        query_grad = (
            jnp.einsum("hqk,khd->qhd", score_grad, key_rows, preferred_element_type=jnp.float32)
            * scale_value
        )
        key_acc = (
            key_acc
            + jnp.einsum("hqk,qhd->khd", score_grad, query_tile, preferred_element_type=jnp.float32)
            * scale_value
        )
        value_acc = value_acc + jnp.einsum(
            "hqk,qhd->khd", probs_low, grad_tile, preferred_element_type=jnp.float32
        )
        return ((key_acc, value_acc), query_grad)

    start_acc = (jnp.zeros(queries.shape, jnp.float32), jnp.zeros(queries.shape, jnp.float32))
    (key_grad, value_grad), query_grad = lax.scan(
        query_block,
        start_acc,
        (
            queries.reshape(tiles, block_rows, head_count, head_size),
            segments.reshape(tiles, block_rows),
            positions.reshape(tiles, block_rows),
            log_total,
            out_grad.reshape(tiles, block_rows, head_count, head_size),
        ),
    )
    return (query_grad.reshape(seq_len, head_count, head_size), key_grad, value_grad)


def gather_attention(qkv_weight, out_weight):
    return (
        lax.all_gather(qkv_weight, "fsdp", axis=0, tiled=True),
        lax.all_gather(out_weight, "fsdp", axis=0, tiled=True),
    )


def gather_feedforward(gate_up_weight, down_weight):
    return (
        lax.all_gather(gate_up_weight, "fsdp", axis=0, tiled=True),
        lax.all_gather(down_weight, "fsdp", axis=0, tiled=True),
    )


def per_device(
    block_in,
    out_cotangent,
    segment_ids,
    doc_positions,
    norm1_gain,
    qkv_weight,
    out_weight,
    norm2_gain,
    gate_up_weight,
    down_weight,
):
    micro_count = block_in.shape[0]
    fsdp_count = lax.axis_size("fsdp")
    segment_full, position_full = (
        lax.all_gather(segment_ids, "tp", axis=1, tiled=True),
        lax.all_gather(doc_positions, "tp", axis=1, tiled=True),
    )
    seq_len = segment_full.shape[1]
    block_rows = min(seq_len, 512)
    gain_one = norm1_gain.astype(jnp.float32)
    gain_two = norm2_gain.astype(jnp.float32)
    local_cols = qkv_weight.shape[2]
    local_units = gate_up_weight.shape[2]
    heads_local = local_cols // HD
    grad_qkv = jnp.zeros((D, 3, local_cols), jnp.float32)
    grad_out = jnp.zeros((out_weight.shape[0] * fsdp_count, D), jnp.float32)
    grad_gate_up = jnp.zeros((D, 2, local_units), jnp.float32)
    grad_down = jnp.zeros((down_weight.shape[0] * fsdp_count, D), jnp.float32)
    gain_one_acc = jnp.zeros((D,), jnp.float32)
    gain_two_acc = jnp.zeros((D,), jnp.float32)
    outputs = []
    input_grads = []
    for micro_index in range(micro_count):
        weights_fwd = (
            gather_attention(qkv_weight, out_weight),
            gather_feedforward(gate_up_weight, down_weight),
        )
        (qkv_full, out_full), (gate_up_full, down_full) = weights_fwd
        stream = block_in[micro_index].astype(jnp.float32)
        segment_row = segment_full[micro_index]
        cosine_part, sine_part = rope_tables(position_full[micro_index], HD)
        scale_one = rms_scale(stream)
        normed_one = (stream * scale_one * gain_one).astype(jnp.bfloat16)
        normed_one_full = lax.all_gather(normed_one, "tp", axis=0, tiled=True)
        projected = jnp.einsum(
            "sd,dtc->stc", normed_one_full, qkv_full, preferred_element_type=jnp.float32
        )
        queries = rotate(
            projected[:, 0].reshape(seq_len, heads_local, HD), cosine_part, sine_part
        ).astype(jnp.bfloat16)
        key_rows = rotate(
            projected[:, 1].reshape(seq_len, heads_local, HD), cosine_part, sine_part
        ).astype(jnp.bfloat16)
        value_rows = projected[:, 2].reshape(seq_len, heads_local, HD).astype(jnp.bfloat16)
        mixed, log_total = attention_forward(queries, key_rows, value_rows, segment_row, block_rows)
        attn_heads = mixed.astype(jnp.bfloat16)
        attn_term = jnp.dot(attn_heads, out_full, preferred_element_type=jnp.float32)
        attn_branch = lax.psum_scatter(attn_term, "tp", scatter_dimension=0, tiled=True)
        middle = stream + attn_branch
        scale_two = rms_scale(middle)
        normed_two = (middle * scale_two * gain_two).astype(jnp.bfloat16)
        normed_two_full = lax.all_gather(normed_two, "tp", axis=0, tiled=True)
        gate_up = jnp.einsum(
            "sd,dtf->stf", normed_two_full, gate_up_full, preferred_element_type=jnp.float32
        )
        gate_rows = gate_up[:, 0]
        up_rows = gate_up[:, 1]
        sigmoid_gate = jax.nn.sigmoid(gate_rows)
        silu_gate = gate_rows * sigmoid_gate
        activated = (silu_gate * up_rows).astype(jnp.bfloat16)
        mlp_term = jnp.dot(activated, down_full, preferred_element_type=jnp.float32)
        mlp_branch = lax.psum_scatter(
            mlp_term.astype(jnp.bfloat16), "tp", scatter_dimension=0, tiled=True
        ).astype(jnp.float32)
        outputs.append((middle + mlp_branch).astype(jnp.bfloat16))
        (qkv_back, out_back), (gate_up_back, down_back) = weights_fwd
        cotangent = out_cotangent[micro_index].astype(jnp.float32)
        cotangent_full = lax.all_gather(out_cotangent[micro_index], "tp", axis=0, tiled=True)
        grad_down = grad_down + jnp.einsum(
            "sf,sd->fd", activated, cotangent_full, preferred_element_type=jnp.float32
        )
        act_grad = jnp.einsum(
            "sd,fd->sf", cotangent_full, down_back, preferred_element_type=jnp.float32
        )
        gate_grad = act_grad * up_rows * sigmoid_gate * (1.0 + gate_rows * (1.0 - sigmoid_gate))
        up_grad = act_grad * silu_gate
        gate_up_grad = jnp.stack([gate_grad, up_grad], axis=1).astype(jnp.bfloat16)
        grad_gate_up = grad_gate_up + jnp.einsum(
            "sd,stf->dtf", normed_two_full, gate_up_grad, preferred_element_type=jnp.float32
        )
        normed_two_term = jnp.einsum(
            "stf,dtf->sd", gate_up_grad, gate_up_back, preferred_element_type=jnp.float32
        )
        normed_two_grad = lax.psum_scatter(normed_two_term, "tp", scatter_dimension=0, tiled=True)
        middle_back, gain_two_term = norm_back(middle, scale_two, gain_two, normed_two_grad)
        gain_two_acc = gain_two_acc + gain_two_term
        middle_grad = cotangent + middle_back
        attn_grad_full = lax.all_gather(middle_grad.astype(jnp.bfloat16), "tp", axis=0, tiled=True)
        grad_out = grad_out + jnp.einsum(
            "sc,sd->cd", attn_heads, attn_grad_full, preferred_element_type=jnp.float32
        )
        heads_grad = jnp.einsum(
            "sd,cd->sc", attn_grad_full, out_back, preferred_element_type=jnp.float32
        ).astype(jnp.bfloat16)
        query_grad, key_grad, value_grad = attention_backward(
            queries,
            key_rows,
            value_rows,
            segment_row,
            log_total,
            heads_grad.reshape(seq_len, heads_local, HD),
            block_rows,
        )
        projected_grad = jnp.stack(
            [
                unrotate(query_grad, cosine_part, sine_part).reshape(seq_len, local_cols),
                unrotate(key_grad, cosine_part, sine_part).reshape(seq_len, local_cols),
                value_grad.reshape(seq_len, local_cols),
            ],
            axis=1,
        ).astype(jnp.bfloat16)
        grad_qkv = grad_qkv + jnp.einsum(
            "sd,stc->dtc", normed_one_full, projected_grad, preferred_element_type=jnp.float32
        )
        normed_one_term = jnp.einsum(
            "stc,dtc->sd", projected_grad, qkv_back, preferred_element_type=jnp.float32
        )
        normed_one_grad = lax.psum_scatter(
            normed_one_term.astype(jnp.bfloat16), "tp", scatter_dimension=0, tiled=True
        ).astype(jnp.float32)
        stream_back, gain_one_term = norm_back(stream, scale_one, gain_one, normed_one_grad)
        gain_one_acc = gain_one_acc + gain_one_term
        input_grads.append(middle_grad + stream_back)
    owned_grads = (
        lax.psum_scatter(
            grad_qkv.astype(jnp.bfloat16), "fsdp", scatter_dimension=0, tiled=True
        ).astype(jnp.float32),
        lax.psum_scatter(
            grad_out.astype(jnp.bfloat16), "fsdp", scatter_dimension=0, tiled=True
        ).astype(jnp.float32),
        lax.psum_scatter(
            grad_gate_up.astype(jnp.bfloat16), "fsdp", scatter_dimension=0, tiled=True
        ).astype(jnp.float32),
        lax.psum_scatter(
            grad_down.astype(jnp.bfloat16), "fsdp", scatter_dimension=0, tiled=True
        ).astype(jnp.float32),
    )
    owned_gains = (
        lax.psum_scatter(gain_one_acc, ("fsdp", "tp"), scatter_dimension=0, tiled=True),
        lax.psum_scatter(gain_two_acc, ("fsdp", "tp"), scatter_dimension=0, tiled=True),
    )
    return (
        jnp.stack(outputs),
        jnp.stack(input_grads),
        owned_gains[0],
        owned_grads[0],
        owned_grads[1],
        owned_gains[1],
        owned_grads[2],
        owned_grads[3],
    )


HEAD_GROUP = 4
FIRST_DOC = 800


def dot_nt(left, right):
    return lax.dot_general(left, right, (((1,), (1,)), ((), ())), preferred_element_type=jnp.float32)


def dot_tn(left, right):
    return lax.dot_general(left, right, (((0,), (0,)), ((), ())), preferred_element_type=jnp.float32)


def dot_nn(left, right):
    return lax.dot_general(left, right, (((1,), (0,)), ((), ())), preferred_element_type=jnp.float32)


def swap_halves(values):
    lanes = lax.broadcasted_iota(jnp.int32, values.shape, 1)
    width = values.shape[1]
    return jnp.where(
        lanes % HD < HD // 2,
        pltpu.roll(values, width - HD // 2, 1),
        pltpu.roll(values, HD // 2, 1),
    )


def causal_mask(rows, columns):
    row_ids = lax.broadcasted_iota(jnp.int32, (rows, columns), 0)
    column_ids = lax.broadcasted_iota(jnp.int32, (rows, columns), 1)
    return row_ids >= column_ids


def tail_mask(reach):
    rows = reach.shape[0]
    row_ids = lax.broadcasted_iota(jnp.int32, (rows, rows), 0)
    column_ids = lax.broadcasted_iota(jnp.int32, (rows, rows), 1)
    return (row_ids >= column_ids) & (row_ids - column_ids <= reach)


def halves(quarter):
    first = lax.axis_index("tp") % 2
    return (
        pl.multiple_of(first * quarter, quarter),
        pl.multiple_of((1 - first) * quarter, quarter),
    )


def widen(table):
    return jnp.concatenate([table] * HEAD_GROUP, axis=1)


def load_rotated(offsets, quarter, q_ref, k_ref, v_ref, cos_ref, sin_ref, qr_ref, kr_ref, vr_ref):
    for place, offset in enumerate(offsets):
        rows = pl.ds(offset, quarter)
        target = pl.ds(place * quarter, quarter)
        cosine, sine = widen(cos_ref[rows, :]), widen(sin_ref[rows, :])
        q_raw, k_raw = q_ref[rows, :], k_ref[rows, :]
        qr_ref[target, :] = (q_raw * cosine + swap_halves(q_raw) * sine).astype(jnp.bfloat16)
        kr_ref[target, :] = (k_raw * cosine + swap_halves(k_raw) * sine).astype(jnp.bfloat16)
        vr_ref[target, :] = v_ref[rows, :].astype(jnp.bfloat16)


def softmax_mix(query, pieces, factor):
    scores = []
    for keys, _, mask in pieces:
        score = dot_nt(query, keys)
        scores.append(score if mask is None else jnp.where(mask, score, masked_score))
    top = functools.reduce(jnp.maximum, [jnp.max(s, axis=-1, keepdims=True) for s in scores])
    weights = [jnp.exp2((s - top) * factor) for s in scores]
    total = functools.reduce(jnp.add, [jnp.sum(w, axis=-1, keepdims=True) for w in weights])
    inverse = 1.0 / total
    mixed = functools.reduce(
        jnp.add,
        [dot_nn((w * inverse).astype(jnp.bfloat16), piece[1]) for w, piece in zip(weights, pieces)],
    )
    return mixed, top * factor + jnp.log2(total)


def head_slice(head):
    return slice(head * HD, (head + 1) * HD)


def forward_first(
    q_ref, k_ref, v_ref, cos_ref, sin_ref, qr_ref, kr_ref, vr_ref, o_ref, lse_ref
):
    half = q_ref.shape[0]
    quarter = half // 2
    offsets = halves(quarter)
    load_rotated(offsets, quarter, q_ref, k_ref, v_ref, cos_ref, sin_ref, qr_ref, kr_ref, vr_ref)
    factor = HD ** (-0.5) * LOG2E
    mask = causal_mask(quarter, quarter)
    for head in range(HEAD_GROUP):
        cols = head_slice(head)
        early, late = slice(0, quarter), slice(quarter, half)
        k_early, v_early = kr_ref[early, cols], vr_ref[early, cols]
        mixed, lse = softmax_mix(qr_ref[early, cols], [(k_early, v_early, mask)], factor)
        o_ref[pl.ds(offsets[0], quarter), cols] = mixed.astype(jnp.bfloat16)
        lse_ref[0, early, head : head + 1] = lse
        mixed, lse = softmax_mix(
            qr_ref[late, cols],
            [(k_early, v_early, None), (kr_ref[late, cols], vr_ref[late, cols], mask)],
            factor,
        )
        o_ref[pl.ds(offsets[1], quarter), cols] = mixed.astype(jnp.bfloat16)
        lse_ref[0, late, head : head + 1] = lse


def forward_second(
    q_ref, k_ref, v_ref, cos_ref, sin_ref, ka_ref, va_ref, pos_ref,
    qr_ref, kr_ref, vr_ref, o_ref, lse_ref,
):
    half = q_ref.shape[0]
    quarter = half // 2
    cut = FIRST_DOC - half
    spill = cut - quarter
    offsets = halves(quarter)
    load_rotated(offsets, quarter, q_ref, k_ref, v_ref, cos_ref, sin_ref, qr_ref, kr_ref, vr_ref)
    factor = HD ** (-0.5) * LOG2E
    mask = causal_mask(cut, cut)
    mask_tail = tail_mask(pos_ref[pl.ds(offsets[1] + spill, half - cut), :])
    for head in range(HEAD_GROUP):
        cols = head_slice(head)
        early, late = slice(0, cut), slice(cut, half)
        mixed, lse = softmax_mix(
            qr_ref[early, cols],
            [
                (ka_ref[:, cols], va_ref[:, cols], None),
                (kr_ref[early, cols], vr_ref[early, cols], mask),
            ],
            factor,
        )
        low = mixed.astype(jnp.bfloat16)
        o_ref[pl.ds(offsets[0], quarter), cols] = low[:quarter]
        o_ref[pl.ds(offsets[1], spill), cols] = low[quarter:]
        lse_ref[0, early, head : head + 1] = lse
        mixed, lse = softmax_mix(
            qr_ref[late, cols], [(kr_ref[late, cols], vr_ref[late, cols], mask_tail)], factor
        )
        o_ref[pl.ds(offsets[1] + spill, half - cut), cols] = mixed.astype(jnp.bfloat16)
        lse_ref[0, late, head : head + 1] = lse


def backward_both(
    qa_ref, ka_ref, va_ref, qb_ref, kb_ref, vb_ref, ga_ref, gb_ref, la_ref, lb_ref,
    cosa_ref, sina_ref, cosb_ref, sinb_ref, pos_ref,
    dqa_ref, dka_ref, dva_ref, dqb_ref, dkb_ref, dvb_ref,
    go_a, go_b, tqa, tka, tva, tqb, tkb, tvb,
):
    half = qa_ref.shape[0]
    quarter = half // 2
    cut = FIRST_DOC - half
    spill = cut - quarter
    offsets = halves(quarter)
    scale_value = HD ** (-0.5)
    factor = scale_value * LOG2E
    for place, offset in enumerate(offsets):
        target, rows = pl.ds(place * quarter, quarter), pl.ds(offset, quarter)
        go_a[target, :] = ga_ref[rows, :]
        go_b[target, :] = gb_ref[rows, :]
    mask = causal_mask(quarter, quarter)
    mask_cut = causal_mask(cut, cut)
    mask_tail = tail_mask(pos_ref[pl.ds(offsets[1] + spill, half - cut), :])
    for accumulator in (tka, tva, tkb, tvb):
        accumulator[...] = jnp.zeros_like(accumulator)

    def attend(query, grad, lse, pieces):
        weights, weight_grads = [], []
        for k_ref, v_ref, rows, cols, mask, _, _ in pieces:
            weight = jnp.exp2(dot_nt(query, k_ref[rows, cols]) * factor - lse)
            weights.append(weight if mask is None else jnp.where(mask, weight, 0.0))
            weight_grads.append(dot_nt(grad, v_ref[rows, cols]))
        shared = functools.reduce(
            jnp.add,
            [jnp.sum(w * g, axis=-1, keepdims=True) for w, g in zip(weights, weight_grads)],
        )
        query_grad = None
        for weight, weight_grad, piece in zip(weights, weight_grads, pieces):
            k_ref, v_ref, rows, cols, _, tk, tv = piece
            score_grad = (weight * (weight_grad - shared)).astype(jnp.bfloat16)
            term = dot_nn(score_grad, k_ref[rows, cols])
            query_grad = term if query_grad is None else query_grad + term
            tk[rows, cols] += dot_tn(score_grad, query)
            tv[rows, cols] += dot_tn(weight.astype(jnp.bfloat16), grad)
        return query_grad

    for head in range(HEAD_GROUP):
        cols = head_slice(head)
        lane = slice(head, head + 1)
        early, late, whole = slice(0, quarter), slice(quarter, half), slice(0, half)
        tqa[early, cols] = attend(
            qa_ref[early, cols], go_a[early, cols], la_ref[0, early, lane],
            [(ka_ref, va_ref, early, cols, mask, tka, tva)],
        )
        tqa[late, cols] = attend(
            qa_ref[late, cols], go_a[late, cols], la_ref[0, late, lane],
            [
                (ka_ref, va_ref, early, cols, None, tka, tva),
                (ka_ref, va_ref, late, cols, mask, tka, tva),
            ],
        )
        early, late = slice(0, cut), slice(cut, half)
        tqb[early, cols] = attend(
            qb_ref[early, cols], go_b[early, cols], lb_ref[0, early, lane],
            [
                (ka_ref, va_ref, whole, cols, None, tka, tva),
                (kb_ref, vb_ref, early, cols, mask_cut, tkb, tvb),
            ],
        )
        tqb[late, cols] = attend(
            qb_ref[late, cols], go_b[late, cols], lb_ref[0, late, lane],
            [(kb_ref, vb_ref, late, cols, mask_tail, tkb, tvb)],
        )
    for place, offset in enumerate(offsets):
        source, rows = pl.ds(place * quarter, quarter), pl.ds(offset, quarter)
        for total, cos_ref, sin_ref, out_ref in (
            (tqa, cosa_ref, sina_ref, dqa_ref),
            (tka, cosa_ref, sina_ref, dka_ref),
            (tqb, cosb_ref, sinb_ref, dqb_ref),
            (tkb, cosb_ref, sinb_ref, dkb_ref),
        ):
            grad = total[source, :] * scale_value
            out_ref[rows, :] = (
                grad * widen(cos_ref[rows, :]) - swap_halves(grad) * widen(sin_ref[rows, :])
            ).astype(jnp.bfloat16)
        dva_ref[rows, :] = tva[source, :].astype(jnp.bfloat16)
        dvb_ref[rows, :] = tvb[source, :].astype(jnp.bfloat16)


COST_SCALE = 1.7


def cost_of(flops):
    return pl.CostEstimate(flops=int(COST_SCALE * flops), bytes_accessed=1000, transcendentals=0)


def rows_kernel(pairs, extra_count, dot, chunk, finish, *refs):
    lefts, weights = refs[:pairs], refs[pairs : 2 * pairs]
    extras = refs[2 * pairs : 2 * pairs + extra_count]
    outs = refs[2 * pairs + extra_count :]

    @pl.loop(0, outs[0].shape[0] // chunk)
    def _(step):
        rows = pl.ds(pl.multiple_of(step * chunk, chunk), chunk)
        total = None
        for left, weight in zip(lefts, weights):
            term = dot(left[rows, :], weight[...])
            total = term if total is None else total + term
        for out, value in zip(outs, finish(total, *[extra[rows, :] for extra in extras])):
            out[rows, :] = value.astype(out.dtype)


def keep_one(total):
    return (total,)


def rows_matmul(
    lefts, weights, dot, types, tile, chunk=1024, finish=keep_one, extras=(), pushes=()
):
    rows = lefts[0].shape[0]
    if dot is dot_nn:
        width = weights[0].shape[1]
        weight_specs = [pl.BlockSpec((w.shape[0], tile), lambda j: (0, j)) for w in weights]
    else:
        width = weights[0].shape[0]
        weight_specs = [pl.BlockSpec((tile, w.shape[1]), lambda j: (j, 0)) for w in weights]
    column = pl.BlockSpec((rows, tile), lambda j: (0, j))
    return grid_call(
        functools.partial(rows_kernel, len(lefts), len(extras), dot, min(chunk, rows), finish),
        [*lefts, *weights, *extras],
        [pl.BlockSpec(left.shape, lambda j: (0, 0)) for left in lefts]
        + weight_specs
        + [column] * len(extras),
        [jax.ShapeDtypeStruct((rows, width), kind) for kind in types],
        [column] * len(types),
        (width // tile,),
        2 * rows * width * sum(left.shape[1] for left in lefts),
        pushes=pushes,
    )


def sum_kernel(parts, chunk, *refs):
    lefts, rights, out = refs[:parts], refs[parts : 2 * parts], refs[-1]

    @pl.loop(0, out.shape[1] // chunk)
    def _(step):
        cols = pl.ds(pl.multiple_of(step * chunk, chunk), chunk)
        total = None
        for left, right in zip(lefts, rights):
            term = dot_tn(left[...], right[:, cols])
            total = term if total is None else total + term
        out[:, cols] = total.astype(out.dtype)


def sum_matmul(lefts, rights, tile, chunk, pushes=()):
    rows, height = lefts[0].shape
    width = rights[0].shape[1]
    return grid_call(
        functools.partial(sum_kernel, len(lefts), chunk),
        [*lefts, *rights],
        [pl.BlockSpec((rows, tile), lambda j: (0, j)) for _ in lefts]
        + [pl.BlockSpec((rows, width), lambda j: (0, 0)) for _ in rights],
        [jax.ShapeDtypeStruct((height, width), jnp.bfloat16)],
        [pl.BlockSpec((tile, width), lambda j: (j, 0))],
        (height // tile,),
        2 * rows * height * width * len(lefts),
        pushes=pushes,
    )


def partner_of(kind):
    index, place = lax.axis_index("fsdp"), lax.axis_index("tp")
    if kind == "near":
        return (index, place + 1 - 2 * (place % 2))
    if kind == "core":
        return sibling_id()
    return (index, place + 2 - 4 * (place // 2))


def start_pushes(kinds, sources, targets, send, receive):
    barrier = pltpu.get_barrier_semaphore()
    names = sorted(set(kinds))
    for kind in names:
        pl.semaphore_signal(
            barrier, inc=1, device_id=partner_of(kind), device_id_type=pl.DeviceIdType.MESH
        )
    pl.semaphore_wait(barrier, len(names))
    for place, kind in enumerate(kinds):
        push(
            sources[place], targets[place], send.at[place], receive.at[place], partner_of(kind)
        ).start()


def wait_pushes(kinds, sources, targets, send, receive):
    for place, kind in enumerate(kinds):
        push(
            sources[place], targets[place], send.at[place], receive.at[place], partner_of(kind)
        ).wait()


def pushing_kernel(kernel, axes, in_count, out_count, kinds, *refs):
    count = len(kinds)
    inputs, sources = refs[:in_count], refs[in_count : in_count + count]
    outs = refs[in_count + count : in_count + count + out_count]
    targets = refs[in_count + count + out_count : in_count + 2 * count + out_count]
    scratch, (send, receive) = refs[in_count + 2 * count + out_count : -2], refs[-2:]
    first = functools.reduce(jnp.logical_and, [pl.program_id(axis) == 0 for axis in range(axes)])
    last = functools.reduce(
        jnp.logical_and,
        [pl.program_id(axis) == pl.num_programs(axis) - 1 for axis in range(axes)],
    )

    @pl.when(first)
    def _():
        start_pushes(kinds, sources, targets, send, receive)

    kernel(*inputs, *outs, *scratch)

    @pl.when(last)
    def _():
        wait_pushes(kinds, sources, targets, send, receive)


def grid_call(
    kernel, operands, in_specs, outs, out_specs, grid, flops, scratch=(), pushes=(), vmem=60
):
    params = dict(
        dimension_semantics=("arbitrary",) * len(grid), vmem_limit_bytes=vmem * 1024 * 1024
    )
    operands, in_specs, outs = list(operands), list(in_specs), list(outs)
    out_specs, scratch = list(out_specs), list(scratch)
    if pushes:
        kinds = tuple(kind for kind, _ in pushes)
        kernel = functools.partial(
            pushing_kernel, kernel, len(grid), len(operands), len(outs), kinds
        )
        anywhere = [pl.BlockSpec(memory_space=pl.ANY)] * len(pushes)
        operands += [value for _, value in pushes]
        in_specs += anywhere
        outs += [jax.ShapeDtypeStruct(value.shape, value.dtype) for _, value in pushes]
        out_specs += anywhere
        scratch += [pltpu.SemaphoreType.DMA((len(pushes),))] * 2
        next_key[0] += 1
        params.update(collective_id=next_key[0], has_side_effects=True)
    return tuple(
        pl.pallas_call(
            kernel,
            out_shape=outs,
            grid=grid,
            in_specs=in_specs,
            out_specs=out_specs,
            scratch_shapes=scratch,
            compiler_params=pltpu.CompilerParams(**params),
            cost_estimate=cost_of(max(flops, 27 * 10**9) if pushes else flops),
        )(*operands)
    )


def swap_kernel(kinds, *refs):
    count = len(kinds)
    sources, targets, (send, receive) = refs[:count], refs[count : 2 * count], refs[2 * count :]
    start_pushes(kinds, sources, targets, send, receive)
    wait_pushes(kinds, sources, targets, send, receive)


def swap_call(*pushes):
    next_key[0] += 1
    kinds = tuple(kind for kind, _ in pushes)
    values = [value for _, value in pushes]
    return exchange_call(
        functools.partial(swap_kernel, kinds), next_key[0], values,
        [jax.ShapeDtypeStruct(value.shape, value.dtype) for value in values],
        [pltpu.SemaphoreType.DMA((len(pushes),))] * 2, flops=110 * 10**9,
    )


next_key = [11]


def sibling_id():
    index = lax.axis_index("fsdp")
    return (index + 1 - 2 * (index % 2), lax.axis_index("tp"))


def meet(partner):
    barrier = pltpu.get_barrier_semaphore()
    pl.semaphore_signal(barrier, inc=1, device_id=partner, device_id_type=pl.DeviceIdType.MESH)
    pl.semaphore_wait(barrier, 1)


def push(source, target, send, receive, partner):
    return pltpu.make_async_remote_copy(
        src_ref=source,
        dst_ref=target,
        send_sem=send,
        recv_sem=receive,
        device_id=partner,
        device_id_type=pl.DeviceIdType.MESH,
    )


def exchange_call(kernel, key, operands, outs, scratch, vmem=60, flops=4 * 10**9):
    anywhere = pl.BlockSpec(memory_space=pl.ANY)
    results = pl.pallas_call(
        kernel,
        out_shape=outs,
        in_specs=[anywhere] * len(operands),
        out_specs=[anywhere] * len(outs),
        scratch_shapes=scratch,
        compiler_params=pltpu.CompilerParams(
            collective_id=key, has_side_effects=True, vmem_limit_bytes=vmem * 1024 * 1024
        ),
        cost_estimate=cost_of(flops),
    )(*operands)
    return tuple(results) if len(outs) > 1 else results[0]


def relay(sources, targets, buffer, load, store):
    loads, stores = [], []
    for place, source in enumerate(sources):
        copy = pltpu.make_async_copy(source, buffer.at[place], load.at[place])
        copy.start()
        loads.append(copy)
    for place, target in enumerate(targets):
        loads[place].wait()
        copy = pltpu.make_async_copy(buffer.at[place], target, store.at[place])
        copy.start()
        stores.append(copy)
    for copy in stores:
        copy.wait()


def gather_kernel(own_ref, near_ref, full_ref, buffer, load, store, send, receive):
    partner = sibling_id()
    meet(partner)
    count = own_ref.shape[0]
    remotes = []
    for place, ref in enumerate((own_ref, near_ref)):
        remote = push(
            ref, full_ref.at[pl.ds((2 + place) * count, count)],
            send.at[place], receive.at[place], partner,
        )
        remote.start()
        remotes.append(remote)
    targets = [full_ref.at[pl.ds(place * count, count)] for place in range(2)]
    relay((own_ref, near_ref), targets, buffer, load, store)
    for remote in remotes:
        remote.wait()


def core_gather(own, near):
    shape = (4 * own.shape[0], own.shape[1])
    return exchange_call(
        gather_kernel, 1, [own, near], [jax.ShapeDtypeStruct(shape, own.dtype)],
        [pltpu.VMEM((2, *own.shape), own.dtype)] + [pltpu.SemaphoreType.DMA((2,))] * 4,
    )


def gather_two_kernel(
    own_ref, own_near_ref, got_ref, got_near_ref, first_ref, second_ref,
    buffer, load, store, send, receive,
):
    partner = sibling_id()
    far = lax.axis_index("tp") // 2
    meet(partner)
    count = own_ref.shape[0]

    def run(targets):
        sources = (own_ref, own_near_ref, got_ref, got_near_ref)
        remotes, places = [], []
        for place, ref in enumerate(sources):
            target, row = targets[place // 2], place % 2
            remote = push(
                ref, target.at[pl.ds((2 + row) * count, count)],
                send.at[place], receive.at[place], partner,
            )
            remote.start()
            remotes.append(remote)
            places.append(target.at[pl.ds(row * count, count)])
        relay(sources, places, buffer, load, store)
        for remote in remotes:
            remote.wait()

    @pl.when(far == 0)
    def _():
        run((first_ref, second_ref))

    @pl.when(far != 0)
    def _():
        run((second_ref, first_ref))


def core_gather_two(own, own_near, got, got_near):
    shape = (4 * own.shape[0], own.shape[1])
    return exchange_call(
        gather_two_kernel, 11, [own, own_near, got, got_near],
        [jax.ShapeDtypeStruct(shape, own.dtype)] * 2,
        [pltpu.VMEM((4, *own.shape), own.dtype)] + [pltpu.SemaphoreType.DMA((4,))] * 4,
    )


def reduce_kernel(term_ref, keep_ref, away_ref, mine, got, keep, away, local, send, receive, store):
    partner = sibling_id()
    meet(partner)
    pieces, count = mine.shape[0], mine.shape[1]
    half = pieces * count
    remotes, loads = [], []
    for piece in range(pieces):
        order = (piece + pieces // 2) % pieces
        remote = push(
            term_ref.at[pl.ds(half + order * count, count)], got.at[order],
            send.at[order], receive.at[order], partner,
        )
        remote.start()
        remotes.append(remote)
        load = pltpu.make_async_copy(
            term_ref.at[pl.ds(order * count, count)], mine.at[order], local.at[order]
        )
        load.start()
        loads.append(load)
    stores = []
    for piece in range(pieces):
        order = (piece + pieces // 2) % pieces
        loads[piece].wait()
        remotes[piece].wait()
        total = mine[order].astype(jnp.float32) + got[order].astype(jnp.float32)
        if order < pieces // 2:
            keep[order] = total
            copy = pltpu.make_async_copy(
                keep.at[order], keep_ref.at[pl.ds(order * count, count)], store.at[order]
            )
        else:
            slot = order - pieces // 2
            away[slot] = total.astype(away.dtype)
            copy = pltpu.make_async_copy(
                away.at[slot], away_ref.at[pl.ds(slot * count, count)], store.at[order]
            )
        copy.start()
        stores.append(copy)
    for copy in stores:
        copy.wait()


def core_reduce(term):
    rows, width = term.shape
    quarter = rows // 4
    pieces = 4
    count = 2 * quarter // pieces
    return exchange_call(
        reduce_kernel, 2, [term],
        [
            jax.ShapeDtypeStruct((quarter, width), jnp.float32),
            jax.ShapeDtypeStruct((quarter, width), term.dtype),
        ],
        [
            pltpu.VMEM((pieces, count, width), term.dtype),
            pltpu.VMEM((pieces, count, width), term.dtype),
            pltpu.VMEM((pieces // 2, count, width), jnp.float32),
            pltpu.VMEM((pieces // 2, count, width), term.dtype),
        ]
        + [pltpu.SemaphoreType.DMA((pieces,))] * 4,
        flops=58 * 10**9,
    )


def pair_kernel(own_ref, *refs):
    others, (pair_ref, buffer, load, store, send, receive) = refs[:-6], refs[-6:]
    partner = sibling_id()
    core = lax.axis_index("fsdp") % 2
    far = lax.axis_index("tp") // 2
    meet(partner)
    base = pl.multiple_of(core * own_ref.shape[0], own_ref.shape[0])
    count = others[0].shape[0]
    owns = [own_ref.at[pl.ds(place * count, count)] for place in range(len(others))]

    def run(mine, theirs):
        remotes, targets = [], []
        for place in range(len(others)):
            target = pair_ref.at[pl.ds(base + place * count, count)]
            remote = push(theirs[place], target, send.at[place], receive.at[place], partner)
            remote.start()
            remotes.append(remote)
            targets.append(target)
        relay(mine, targets, buffer, load, store)
        for remote in remotes:
            remote.wait()

    @pl.when(core == far)
    def _():
        run(owns, others)

    @pl.when(core != far)
    def _():
        run(others, owns)


def core_pair(key, own, *others):
    shape = (2 * own.shape[0], own.shape[1])
    return exchange_call(
        pair_kernel, key, [own, *others], [jax.ShapeDtypeStruct(shape, own.dtype)],
        [pltpu.VMEM((len(others), *others[0].shape), own.dtype)]
        + [pltpu.SemaphoreType.DMA((len(others),))] * 4,
    )


def split_kernel(pair_ref, keep_ref, away_ref, buffer, load, store, send, receive):
    partner = sibling_id()
    core = lax.axis_index("fsdp") % 2
    far = lax.axis_index("tp") // 2
    meet(partner)
    count = keep_ref.shape[0]
    mine = pair_ref.at[pl.ds(pl.multiple_of(core * count, count), count)]
    theirs = pair_ref.at[pl.ds(pl.multiple_of((1 - core) * count, count), count)]

    def run(own_target, other_target):
        remote = push(theirs, other_target, send.at[0], receive.at[0], partner)
        remote.start()
        relay((mine,), (own_target,), buffer, load, store)
        remote.wait()

    @pl.when(core == far)
    def _():
        run(keep_ref, keep_ref)

    @pl.when(core != far)
    def _():
        run(away_ref, away_ref)


def core_split(key, pair):
    shape = (pair.shape[0] // 2, pair.shape[1])
    return exchange_call(
        split_kernel, key, [pair], [jax.ShapeDtypeStruct(shape, pair.dtype)] * 2,
        [pltpu.VMEM((1, *shape), pair.dtype)] + [pltpu.SemaphoreType.DMA((1,))] * 4,
    )


def attention_call(kernel, arrays, kinds, outs, scratch, pushes=()):
    rows, heads_local = arrays[-1].shape[0], outs[1]
    half = rows // 2
    groups = heads_local // HEAD_GROUP
    width = HEAD_GROUP * HD

    def spec(kind):
        if kind == "table":
            return pl.BlockSpec((half, HD), lambda s, g: (s, 0))
        if kind == "column":
            return pl.BlockSpec((half, 1), lambda s, g: (s, 0))
        if kind == "lse":
            return pl.BlockSpec((1, half, HEAD_GROUP), lambda s, g: (g, s, 0))
        shift = kind * groups
        return pl.BlockSpec((half, width), lambda s, g: (s, shift + g))

    def shape(kind):
        if kind == "lse":
            return jax.ShapeDtypeStruct((groups, rows, HEAD_GROUP), jnp.float32)
        return jax.ShapeDtypeStruct((rows, heads_local * HD), jnp.bfloat16)

    return grid_call(
        kernel,
        arrays,
        [spec(kind) for kind in kinds],
        [shape(kind) for kind in outs[0]],
        [spec(kind) for kind in outs[0]],
        (rows // half, groups),
        4 * len(outs[0]) ** 2 * rows * rows * heads_local * HD // 16,
        scratch=scratch(half, width),
        pushes=pushes,
    )


def backward_scratch(half, width):
    return [pltpu.VMEM((half, width), jnp.bfloat16)] * 2 + [
        pltpu.VMEM((half, width), jnp.float32)
    ] * 6


def no_scratch(half, width):
    return []


def head_tables(positions):
    half_width = HD // 2
    frequency = rope_theta ** (-(jnp.arange(half_width, dtype=jnp.float32) * 2.0 / HD))
    angles = positions.astype(jnp.float32)[:, None] * frequency[None, :]
    cosine, sine = jnp.cos(angles), jnp.sin(angles)
    return (
        jnp.concatenate([cosine, cosine], axis=-1),
        jnp.concatenate([-sine, sine], axis=-1),
    )


def paired_device(
    block_in,
    out_cotangent,
    segment_ids,
    doc_positions,
    norm1_gain,
    qkv_weight,
    out_weight,
    norm2_gain,
    gate_up_weight,
    down_weight,
):
    fsdp_count, tp_count = lax.axis_size("fsdp"), lax.axis_size("tp")
    core = lax.axis_index("fsdp") % 2
    lane_z = lax.axis_index("tp")
    near, far = lane_z % 2, lane_z // 2
    core_pairs = [(i, i ^ 1) for i in range(fsdp_count)]
    near_pairs = [(i, i ^ 1) for i in range(tp_count)]
    far_pairs = [(i, i ^ 2) for i in range(tp_count)]
    plane_groups = [list(range(first, fsdp_count, 2)) for first in range(2)]
    rows = block_in.shape[1]
    local_cols = qkv_weight.shape[2]
    heads_local = local_cols // HD
    gain_one = norm1_gain.astype(jnp.float32)
    gain_two = norm2_gain.astype(jnp.float32)

    def swap_core(value):
        return lax.ppermute(value, "fsdp", core_pairs)

    def swap_near(value):
        return lax.ppermute(value, "tp", near_pairs)

    def swap_far(value):
        return lax.ppermute(value, "tp", far_pairs)

    def pick_tile(size):
        return 512 if size % 512 == 0 else 768

    tokens = []

    def act(work, *inputs, sends=()):
        values = [*inputs, *[value for _, value in sends]]
        held = lax.optimization_barrier((*values, *tokens))[: len(values)]
        if sends:
            kinds = [kind for kind, _ in sends]
            result = work(*held[: len(inputs)], pushes=list(zip(kinds, held[len(inputs) :])))
        else:
            result = work(*held)
        tokens[:] = result if isinstance(result, tuple) else (result,)
        return result[0] if isinstance(result, tuple) and len(result) == 1 else result

    def swap(*sends):
        return act(lambda pushes: swap_call(*pushes), sends=sends)

    def pick(value, index):
        return lax.dynamic_index_in_dim(value, index, 0, keepdims=False)

    def place_tokens(value, got):
        keep = pick(value, far)
        return jnp.where(far == 0, keep, got), jnp.where(far == 0, got, keep)

    def join(left, right):
        return jnp.concatenate([left, right], axis=0)

    def plane_gather(pair):
        return lax.all_gather(pair, "fsdp", axis=0, tiled=True, axis_index_groups=plane_groups)

    def plane_scatter(grad):
        return lax.psum_scatter(
            grad, "fsdp", scatter_dimension=0, tiled=True, axis_index_groups=plane_groups
        )

    def gather_weight(key, local, *others):
        return plane_gather(act(lambda own, *got: core_pair(key, own, *got), local, *others))

    def halve(value):
        count = value.shape[0] // 2
        return value[:count], value[count:]

    def add_wide(left, right):
        return left.astype(jnp.float32) + right.astype(jnp.float32)

    def chained(value, *others):
        return lax.optimization_barrier((value, *others))[0]

    def scatter_gains(gains):
        for axis, size in (("fsdp", fsdp_count), ("tp", tp_count)):
            index = lax.axis_index(axis)
            step = size // 2
            while step >= 1:
                bit = (index // step) % 2
                parts = gains.reshape(gains.shape[0], 2, gains.shape[1] // 2)
                sent = lax.dynamic_index_in_dim(parts, 1 - bit, 1, keepdims=False)
                kept = lax.dynamic_index_in_dim(parts, bit, 1, keepdims=False)
                gains = kept + lax.ppermute(sent, axis, [(i, i ^ step) for i in range(size)])
                step //= 2
        return gains

    def wide_dot(left, right, pushes=()):
        return rows_matmul(
            [left], [right], dot_nn, [jnp.float32], pick_tile(right.shape[1]), pushes=pushes
        )

    def dot_bf16(left, right, pushes=()):
        return rows_matmul(
            [left], [right], dot_nn, [jnp.bfloat16], pick_tile(right.shape[1]), pushes=pushes
        )

    def grad_sum(left, right, left_next, right_next, pushes=()):
        chunk = pick_tile(right.shape[1])
        return sum_matmul(
            [left, left_next], [right, right_next], pick_tile(left.shape[1]),
            2 * chunk if right.shape[1] % (2 * chunk) == 0 else chunk, pushes=pushes,
        )

    def heads_back(grad, weight, pushes=()):
        return rows_matmul(
            [grad], [weight], dot_nt, [jnp.bfloat16], pick_tile(weight.shape[0]), pushes=pushes
        )

    def rms_pack(stream, gain):
        scale = rms_scale(stream)
        return scale, (stream * scale * gain).astype(jnp.bfloat16)

    qkv_local = qkv_weight.reshape(qkv_weight.shape[0], 3 * local_cols)
    gate_local, up_local = gate_up_weight[:, 0], gate_up_weight[:, 1]

    next_key[0] = 11
    places = jnp.broadcast_to(doc_positions[:, None, :], (2, 8, rows))

    def first_norm(part):
        stream = part.astype(jnp.float32)
        return (stream, *rms_pack(stream, gain_one))

    s_own, r_own, n_own = act(lambda value: first_norm(pick(value, far)), block_in)
    near_own, qkv_other, place_got = swap(
        ("near", n_own), ("far", qkv_local), ("far", pick(places, 1 - far))
    )
    qkv_full = gather_weight(4, qkv_local, qkv_other)
    places = join(*place_tokens(places, place_got))

    def make_tables(own, other):
        order = join(own, other)[::8].reshape(2, 2, 2, rows)
        early, late = order[:, :, 0].reshape(-1), order[:, :, 1].reshape(-1)
        return (*head_tables(early), *head_tables(late), late[:, None])

    c_own = pick(out_cotangent, far)
    stream_got, c_near_own, out_other, near_places = swap(
        ("far", pick(block_in, 1 - far)), ("near", c_own), ("far", out_weight), ("near", places)
    )
    places = join(places, near_places)
    out_full = gather_weight(3, out_weight, out_other)
    s_got, r_got, n_got = act(first_norm, stream_got)
    near_got, gate_other, core_places = swap(
        ("near", n_got), ("far", gate_local), ("core", places)
    )
    gate_full = gather_weight(5, gate_local, gate_other)
    h1_first, h1_second = act(core_gather_two, n_own, near_own, n_got, near_got)
    streams = [jnp.where(far == 0, s_own, s_got), jnp.where(far == 0, s_got, s_own)]
    scales_one = [jnp.where(far == 0, r_own, r_got), jnp.where(far == 0, r_got, r_own)]

    def attend_first(projected, pushes=()):
        arrays = [projected, projected, projected, *tables[0]]
        return attention_call(
            forward_first, arrays, [0, 1, 2, "table", "table"],
            ([0, 0, 0, 0, "lse"], heads_local), no_scratch, pushes,
        )

    def attend_second(projected, pushes=()):
        arrays = [projected, projected, projected, *tables[1], saved[0][1], saved[0][2], reach]
        return attention_call(
            forward_second, arrays, [0, 1, 2, "table", "table", 0, 0, "column"],
            ([0, 0, 0, 0, "lse"], heads_local), no_scratch, pushes,
        )

    up_other = swap_far(chained(up_local, gate_other))
    cos_first, sin_first, cos_second, sin_second, reach = act(
        make_tables, places, core_places
    )
    tables = [(cos_first, sin_first), (cos_second, sin_second)]
    projected = act(wide_dot, h1_first, qkv_full)
    results = act(attend_first, projected)
    up_full = gather_weight(5, up_local, up_other)
    down_other = swap_far(chained(down_weight, up_other))
    saved, lses, mixed_first = [results[:3]], [results[4]], results[3]
    term_first = act(dot_bf16, mixed_first, out_full)
    keep_first, send_first = act(core_reduce, term_first)
    projected, branch_first = act(
        wide_dot, h1_second, qkv_full, sends=[("near", send_first)]
    )

    def second_norm(stream, keep, got):
        middle = stream + keep + got.astype(jnp.float32)
        return (middle, *rms_pack(middle, gain_two))

    m_first, q_first, n_first = act(second_norm, streams[0], keep_first, branch_first)
    *results, near_first = act(attend_second, projected, sends=[("near", n_first)])
    saved.append(results[:3])
    lses.append(results[4])
    mixed_second = results[3]
    term_second = act(dot_bf16, mixed_second, out_full)
    keep_second, send_second = act(core_reduce, term_second)
    h2_first = act(core_gather, n_first, near_first)
    down_full_pair = act(lambda own, got: core_pair(6, own, got), down_weight, down_other)
    down_full = plane_gather(down_full_pair)
    c_got = swap_far(chained(pick(out_cotangent, 1 - far), down_full_pair))

    gate_first, branch_second = act(
        wide_dot, h2_first, gate_full, sends=[("near", send_second)]
    )
    m_second, q_second, n_second = act(second_norm, streams[1], keep_second, branch_second)

    def rise(hidden, weight, gate, pushes=()):
        return rows_matmul(
            [hidden], [weight], dot_nn, [jnp.float32, jnp.bfloat16], pick_tile(weight.shape[1]),
            finish=lambda up, gate: (up, gate * jax.nn.sigmoid(gate) * up), extras=[gate],
            pushes=pushes,
        )

    up_first, a_first, near_second = act(
        rise, h2_first, up_full, gate_first, sends=[("near", n_second)]
    )
    h2_second = act(core_gather, n_second, near_second)
    gate_second, c_near_got = act(
        wide_dot, h2_second, gate_full, sends=[("near", c_got)]
    )
    y_first, y_second = act(core_gather_two, c_own, c_near_own, c_got, c_near_got)
    c_first, c_second = jnp.where(far == 0, c_own, c_got), jnp.where(far == 0, c_got, c_own)
    up_second, a_second = act(rise, h2_second, up_full, gate_second)
    down_sum = plane_scatter(act(grad_sum, a_first, y_first, a_second, y_second))

    def fall_finish(act_grad, gate, up):
        sigmoid_gate = jax.nn.sigmoid(gate)
        return (
            act_grad * up * sigmoid_gate * (1.0 + gate * (1.0 - sigmoid_gate)),
            act_grad * (gate * sigmoid_gate),
        )

    def fall(cotangent, weight, gate, up, pushes=()):
        return rows_matmul(
            [cotangent], [weight], dot_nt, [jnp.bfloat16] * 2, pick_tile(weight.shape[0]),
            chunk=512, finish=fall_finish, extras=[gate, up], pushes=pushes,
        )

    def hidden_grad(gate_grad, up_grad, gate_weight, up_weight, pushes=()):
        return rows_matmul(
            [gate_grad, up_grad], [gate_weight, up_weight], dot_nt, [jnp.bfloat16],
            pick_tile(gate_weight.shape[0]), pushes=pushes,
        )

    def second_back(middle, scale, keep, got, cotangent):
        grad, gain_term = norm_back(middle, scale, gain_two, keep + got.astype(jnp.float32))
        grad = cotangent.astype(jnp.float32) + grad
        return grad, grad.astype(jnp.bfloat16), gain_term

    dg_first, du_first = act(fall, y_first, down_full, gate_first, up_first)
    term_first = act(hidden_grad, dg_first, du_first, gate_full, up_full)
    keep_first, send_first = act(core_reduce, term_first)
    dg_second, du_second, back_first = act(
        fall, y_second, down_full, gate_second, up_second, sends=[("near", send_first)]
    )
    g_first, n_first, gain_two_first = act(
        second_back, m_first, q_first, keep_first, back_first, c_first
    )
    term_second, near_first = act(
        hidden_grad, dg_second, du_second, gate_full, up_full, sends=[("near", n_first)]
    )
    keep_second, send_second = act(core_reduce, term_second)
    d_first = act(core_gather, n_first, near_first)
    grad_gate, back_second = act(
        grad_sum, h2_first, dg_first, h2_second, dg_second, sends=[("near", send_second)]
    )
    gate_sum = plane_scatter(grad_gate)
    g_second, n_second, gain_two_second = act(
        second_back, m_second, q_second, keep_second, back_second, c_second
    )
    heads_first = act(heads_back, d_first, out_full)
    down_mine, down_away = act(lambda pair: core_split(10, pair), down_sum)
    down_got = swap_far(down_away)
    grad_up, near_second = act(
        grad_sum, h2_first, du_first, h2_second, du_second, sends=[("near", n_second)]
    )
    up_sum = plane_scatter(grad_up)

    d_second = act(core_gather, n_second, near_second)
    heads_second = act(heads_back, d_second, out_full)
    grad_out = act(grad_sum, mixed_first, d_first, mixed_second, d_second)
    out_sum = plane_scatter(grad_out)
    mlp_first = act(dot_bf16, a_first, down_full)
    mlp_keep_first, mlp_send_first = act(core_reduce, mlp_first)
    mlp_second = act(dot_bf16, a_second, down_full)
    mlp_keep_second, mlp_send_second = act(core_reduce, mlp_second)
    def attend_back(heads_first, heads_second, pushes=()):
        return attention_call(
            backward_both,
            [
                *saved[0], *saved[1], heads_first, heads_second, *lses,
                *tables[0], *tables[1], reach,
            ],
            [0] * 8 + ["lse"] * 2 + ["table"] * 4 + ["column"],
            ([0] * 6, heads_local),
            backward_scratch,
            pushes,
        )

    *grads, mlp_branch_first, mlp_branch_second = act(
        attend_back, heads_first, heads_second,
        sends=[("near", mlp_send_first), ("near", mlp_send_second)],
    )
    gate_mine, gate_away = act(lambda pair: core_split(9, pair), gate_sum)
    gate_got = swap_far(gate_away)
    p_first, p_second = act(
        lambda *parts: (
            jnp.concatenate(parts[:3], axis=1),
            jnp.concatenate(parts[3:], axis=1),
        ),
        *grads,
    )

    def finish_output(first, first_keep, first_got, second, second_keep, second_got):
        first = (first + first_keep + first_got.astype(jnp.float32)).astype(jnp.bfloat16)
        second = (second + second_keep + second_got.astype(jnp.float32)).astype(jnp.bfloat16)
        return jnp.where(far == 0, first, second), jnp.where(far == 0, second, first)

    grad_qkv = act(grad_sum, h1_first, p_first, h1_second, p_second)
    qkv_sum = plane_scatter(grad_qkv)
    out_keep, out_send = act(
        finish_output,
        m_first, mlp_keep_first, mlp_branch_first, m_second, mlp_keep_second, mlp_branch_second,
    )
    out_got = swap_far(out_send)
    up_mine, up_away = act(lambda pair: core_split(9, pair), up_sum)
    up_got = swap_far(up_away)
    term_first = act(heads_back, p_first, qkv_full)
    keep_first, send_first = act(core_reduce, term_first)
    term_second, back_first = act(
        heads_back, p_second, qkv_full, sends=[("near", send_first)]
    )
    keep_second, send_second = act(core_reduce, term_second)
    out_mine, out_away = act(lambda pair: core_split(8, pair), out_sum)
    def settle(keep, got):
        return jnp.stack([jnp.where(far == 0, keep, got), jnp.where(far == 0, got, keep)])

    def first_back(stream, scale, keep, got, grad):
        back, gain_term = norm_back(stream, scale, gain_one, keep + got.astype(jnp.float32))
        return grad + back, gain_term

    def last_back(stream, scale, keep, got, grad, first):
        second, gain_term = first_back(stream, scale, keep, got, grad)
        return (
            jnp.where(far == 0, first, second),
            jnp.where(far == 0, second, first).astype(jnp.bfloat16),
            gain_term,
        )

    qkv_mine, qkv_away = act(lambda pair: core_split(0, pair), qkv_sum)
    qkv_back = swap_far(qkv_away)
    back_second, out_back = swap(("near", send_second), ("far", out_away))
    i_first, gain_one_first = act(
        first_back, streams[0], scales_one[0], keep_first, back_first, g_first
    )
    in_keep, in_send, gain_one_second = act(
        last_back, streams[1], scales_one[1], keep_second, back_second, g_second, i_first
    )
    in_got = swap_far(in_send)
    down_owned = act(add_wide, down_mine, down_got)
    gate_owned = act(add_wide, gate_mine, gate_got)
    block_out = act(settle, out_keep, out_got)
    up_owned = act(add_wide, up_mine, up_got)
    gate_up_owned = act(lambda a, b: jnp.stack([a, b], axis=1), gate_owned, up_owned)
    out_owned = act(add_wide, out_mine, out_back)
    gains = scatter_gains(
        jnp.stack([gain_one_first + gain_one_second, gain_two_first + gain_two_second])
    )
    in_grad = act(lambda keep, got: settle(keep, got.astype(jnp.float32)), in_keep, in_got)
    qkv_owned = act(add_wide, qkv_mine, qkv_back)
    return (
        block_out,
        in_grad,
        gains[0],
        qkv_owned.reshape(qkv_weight.shape),
        out_owned,
        gains[1],
        gate_up_owned,
        down_owned,
    )


def solution(mesh):
    sizes = (mesh.shape["fsdp"], mesh.shape["tp"])
    body = paired_device if sizes == (8, 4) else per_device
    in_specs = (
        P("fsdp", "tp", None),
        P("fsdp", "tp", None),
        P("fsdp", "tp"),
        P("fsdp", "tp"),
        P(),
        P("fsdp", None, "tp"),
        P(("tp", "fsdp"), None),
        P(),
        P("fsdp", None, "tp"),
        P(("tp", "fsdp"), None),
    )
    out_specs = (
        P("fsdp", "tp", None),
        P("fsdp", "tp", None),
        P(("fsdp", "tp")),
        P("fsdp", None, "tp"),
        P(("tp", "fsdp"), None),
        P(("fsdp", "tp")),
        P("fsdp", None, "tp"),
        P(("tp", "fsdp"), None),
    )
    return jax.shard_map(
        body, mesh=mesh, in_specs=in_specs, out_specs=out_specs, check_vma=False
    )
```
